32 devices in a mesh: narrow: 4 (over y, core), wide: 8 (over z, x).
Axes of the slice: x: 2, y: 2, z: 4, core: 2. Of those that a mesh axis runs over, the one named last changes fastest.
Arguments:
- inputs: bfloat16 [9216, 768], P('wide'), may hold values from -6 to 6
- counts: int32 [16], P('wide'), may hold values from 196 to 576, as said below
- routes: int32 [9216, 2], P('wide'), may hold values from 0 to 3, as said below
- slot_ids: int32 [9216, 2], P('wide'), may hold values from 0 to 606, as said below
- norm_first: float32 [768], replicated, may hold values from 0.5 to 1.5
- attn_in: bfloat16 [3, 768, 768], P(None, None, 'narrow'), may hold values from -0.21875 to 0.21875
- attn_out: bfloat16 [768, 768], P('narrow'), may hold values from -2.5 to 2.5
- norm_second: float32 [768], replicated, may hold values from 0.5 to 1.5
- router: bfloat16 [768, 4], replicated, may hold values from -0.15625 to 0.15625
- expert_in: bfloat16 [8, 768, 3072], P('wide', None, 'narrow'), as said below
- expert_out: bfloat16 [8, 3072, 768], P('wide', 'narrow'), as said below
- cotangent: bfloat16 [9216, 768], P('wide'), may hold values from -6 to 6
Outputs:
- output: bfloat16 [9216, 768], P('wide')
- input_grad: float32 [9216, 768], P('wide')
- norm_first_grad: float32 [768], replicated
- attn_in_grad: float32 [3, 768, 768], P(None, None, 'narrow')
- attn_out_grad: float32 [768, 768], P('narrow')
- norm_second_grad: float32 [768], replicated
- router_grad: float32 [768, 4], replicated
- expert_in_grad: float32 [8, 768, 3072], P('wide', None, 'narrow')
- expert_out_grad: float32 [8, 3072, 768], P('wide', 'narrow')
The draws below stay inside these ranges and needn't reach their ends.
Inputs may be any that keep to these rules, and one draw needn't show every extreme that they name: Each is 196 or 576; image slot i holds rows i * 576 to i * 576 + counts[i] - 1, the rest of the slot is padding; every index of wide has at least one slot of 576; both values occur in every draw. The two routes of a row differ. `slot_ids`: within the 1152 rows of one index of wide, the kept pairs sent to one expert hold the distinct slots 0, 1, 2, ... in a priority order that puts all first routes before all second routes; a pair holds 606 (dropped) when its expert already has 606 pairs from those rows, and every pair of a padding row holds 606. In every draw one expert receives 606 pairs from every index of wide. `expert_in`: entries 2e and 2e+1 along the first dimension are equal. `expert_out`: entries 2e and 2e+1 along the first dimension are equal.
All inputs are finite; a program needn't handle non-finite values.
Results may differ from the reference program's by a relative error of at most 0.015.
Values may be sent and summed in bfloat16 or wider, within the bound.
A program may use at most 192 MiB of HBM per device.

```python
import jax
import jax.numpy as jnp
from jax import lax

D = 768
HEADS = 12
FF = 3072
PATCHES = 576
SHORT = 196
IMG_DEV = 2
HEAD_DIM = 64
EXPERTS = 4
ROWS_DEV = 1152
TOKENS = 9216
IMAGES = 16
CAP = 606
N_WIDE = 8


def device_slots(expert_ids, order_keys, pair_live):
    order = jnp.argsort(order_keys, stable=True)
    sorted_ids = expert_ids[order]
    one_hot = (sorted_ids[:, None] == jnp.arange(EXPERTS, dtype=jnp.int32)[None, :]).astype(jnp.int32)
    earlier = jnp.cumsum(one_hot, axis=0) - one_hot
    position = jnp.sum(earlier * one_hot, axis=1)
    slot_sorted = jnp.where(pair_live[order] & (position < CAP), position, CAP).astype(jnp.int32)
    return jnp.zeros_like(slot_sorted).at[order].set(slot_sorted)


def routing_tables(key):
    base = jax.random.fold_in(key, 4242)
    k_count, k_hot, k_first, k_other, k_second, k_order, k_perm, k_pick = jax.random.split(base, 8)
    bits = jax.random.randint(k_count, (N_WIDE, IMG_DEV), 0, 2).astype(jnp.int32)
    pick = jax.random.randint(k_pick, (N_WIDE,), 0, IMG_DEV).astype(jnp.int32)
    slot_index = jnp.arange(IMG_DEV, dtype=jnp.int32)[None, :]
    bits = jnp.where(slot_index == pick[:, None], 1, bits)
    bits = jnp.where((jnp.arange(N_WIDE, dtype=jnp.int32)[:, None] == 0) & (slot_index == (pick[0] + 1) % IMG_DEV), 0, bits)
    counts = (SHORT + bits.reshape(N_WIDE * IMG_DEV) * (PATCHES - SHORT)).astype(jnp.int32)
    count_table = counts.reshape(N_WIDE, IMG_DEV)
    before_rows = jnp.cumsum(count_table, axis=1) - count_table
    row_ids = jnp.arange(ROWS_DEV, dtype=jnp.int32)
    row_image = row_ids // PATCHES
    offset = row_ids % PATCHES
    row_valid = offset[None, :] < count_table[:, row_image]
    order_index = before_rows[:, row_image] + offset[None, :]
    hot_rows = row_valid & (order_index < CAP + 4)
    hot_expert = jax.random.randint(k_hot, (), 0, EXPERTS).astype(jnp.int32)
    shuffled = jax.random.permutation(k_perm, EXPERTS).astype(jnp.int32)
    draw_a = jax.random.randint(k_first, (N_WIDE, ROWS_DEV), 0, EXPERTS)
    draw_b = jax.random.randint(k_other, (N_WIDE, ROWS_DEV), 0, EXPERTS)
    first = jnp.where(hot_rows, hot_expert, shuffled[jnp.minimum(draw_a, draw_b)]).astype(jnp.int32)
    second = ((first + 1 + jax.random.randint(k_second, (N_WIDE, ROWS_DEV), 0, EXPERTS - 1)) % EXPERTS).astype(jnp.int32)
    score = jax.random.randint(k_order, (N_WIDE, ROWS_DEV), 0, 65536).astype(jnp.int32) * ROWS_DEV + row_ids[None, :]
    rank = jnp.argsort(jnp.argsort(score, axis=1, stable=True), axis=1, stable=True).astype(jnp.int32)
    pair_ids = jnp.concatenate([first, second], axis=1)
    pair_live = jnp.concatenate([row_valid, row_valid], axis=1)
    fallback = 2 * ROWS_DEV + jnp.concatenate([row_ids, row_ids + ROWS_DEV])[None, :]
    order_keys = jnp.where(pair_live, jnp.concatenate([rank, rank + ROWS_DEV], axis=1), fallback).astype(jnp.int32)
    slot_pairs = jax.vmap(device_slots)(pair_ids, order_keys, pair_live)
    routes = jnp.stack([first, second], axis=-1).reshape(TOKENS, 2)
    slot_ids = jnp.stack([slot_pairs[:, :ROWS_DEV], slot_pairs[:, ROWS_DEV:]], axis=-1).reshape(TOKENS, 2)
    return (counts, routes.astype(jnp.int32), slot_ids.astype(jnp.int32))


def draw_counts(key, part):
    return routing_tables(key)[0]


def draw_routes(key, part):
    return routing_tables(key)[1]


def draw_slot_ids(key, part):
    return routing_tables(key)[2]


def draw_expert_in(key, part):
    values = jax.random.normal(jax.random.fold_in(key, 71), (EXPERTS, D, FF), jnp.float32)
    values = jnp.clip(values, -6.0, 6.0) * D ** (-0.5)
    return jnp.repeat(values, 2, axis=0).astype(jnp.bfloat16)


def draw_expert_out(key, part):
    values = jax.random.normal(jax.random.fold_in(key, 73), (EXPERTS, FF, D), jnp.float32)
    values = jnp.clip(values, -6.0, 6.0) * (FF // 2) ** (-0.5)
    return jnp.repeat(values, 2, axis=0).astype(jnp.bfloat16)


def levels(key, shape, cuts, smallest, high):
    def one(axis_at, parts):
        steps = jax.random.uniform(jax.random.fold_in(jax.random.fold_in(key, 6), axis_at), (parts,), jnp.float32, smallest / len(cuts), high / len(cuts))
        return jnp.repeat(jnp.exp(steps), shape[axis_at] // parts).reshape((-1,) + (1,) * (len(shape) - axis_at - 1))

    level = one(*cuts[0])
    for cut in cuts[1:]:
        level = level * one(*cut)
    return level


def normal_values(key, shape, width, most, cuts=(), held_as=jnp.bfloat16):
    drawn = width * jax.random.normal(key, shape, jnp.float32)
    if cuts:
        drawn = drawn * levels(key, shape, cuts, -0.22, 0.18)
    return jnp.clip(drawn, -most, most).astype(held_as)


def setup_inputs(seed: int = 0) -> dict:
    keys = jax.random.split(jax.random.key(seed), 13)
    inputs = normal_values(keys[0], (TOKENS, D), 1.0, 6.0, ((0, 8),))
    counts = draw_counts(jax.random.fold_in(keys[12], 71), 0)
    routes = draw_routes(jax.random.fold_in(keys[12], 71), 0)
    slot_ids = draw_slot_ids(jax.random.fold_in(keys[12], 71), 0)
    norm_first = jnp.clip(1.0 + 0.1 * jax.random.normal(keys[4], (D,), jnp.float32), 0.5, 1.5)
    attn_in = normal_values(keys[5], (3, D, D), D ** -0.5, 0.21875, ((2, 4),))
    attn_out = normal_values(keys[6], (D, D), (max(D // 128, 1)) ** -0.5, 2.5, ((0, 4),))
    norm_second = jnp.clip(1.0 + 0.1 * jax.random.normal(keys[7], (D,), jnp.float32), 0.5, 1.5)
    router = normal_values(keys[8], (D, EXPERTS), (2 * D) ** -0.5, 0.15625)
    expert_in = draw_expert_in(jax.random.fold_in(keys[12], 71), 0)
    expert_out = draw_expert_out(jax.random.fold_in(keys[12], 71), 0)
    cotangent = normal_values(keys[11], (TOKENS, D), 1.0, 6.0, ((0, 8),))
    return dict(inputs=inputs, counts=counts, routes=routes, slot_ids=slot_ids, norm_first=norm_first, attn_in=attn_in, attn_out=attn_out, norm_second=norm_second, router=router, expert_in=expert_in, expert_out=expert_out, cotangent=cotangent)


@jax.custom_vjp
def low(v):
    return lax.optimization_barrier(v.astype(jnp.bfloat16)).astype(jnp.float32)

@jax.custom_vjp
def low_back(v):
    return v

def low_keep(v):
    return (low(v), None)

def low_pass(kept, grad):
    return (grad,)

def back_keep(v):
    return (v, None)

def back_low(kept, grad):
    return (low(grad),)
low.defvjp(low_keep, low_pass)
low_back.defvjp(back_keep, back_low)
NORM_EPSILON = 1e-06
MASKED_SCORE = -1e+30

def layer_norm(values, gain):
    center = values - lax.optimization_barrier(jnp.mean(values, -1, keepdims=True))
    return center * lax.rsqrt(lax.optimization_barrier(jnp.mean(center * center, -1, keepdims=True)) + NORM_EPSILON) * gain

def matmul(left, right):
    return jnp.dot(left, right, precision=lax.Precision.HIGHEST)

def attend_image(carry, block):
    query, key_rows, value_rows, key_valid = block
    scores = low_back(jnp.einsum('qhd,khd->hqk', query, key_rows, precision=lax.Precision.HIGHEST)) * HEAD_DIM ** (-0.5)
    scores = jnp.where(key_valid[None, None, :], scores, MASKED_SCORE)
    softmax_w = low(jax.nn.softmax(scores, axis=-1))
    attended = low(low_back(jnp.einsum('hqk,khd->qhd', softmax_w, value_rows, precision=lax.Precision.HIGHEST)))
    return (carry, attended)

def expert_block(block):
    dispatched, weight_in, weight_out = block
    pre_act = low_back(matmul(dispatched, weight_in))
    hidden = low(jax.nn.gelu(pre_act, approximate=False))
    return low(low_back(matmul(hidden, weight_out)))

def forward(inputs, norm_first, attn_in, attn_out, norm_second, router, expert_in, expert_out, counts, routes, slot_ids):
    row_ids = jnp.arange(TOKENS, dtype=jnp.int32)
    row_image = row_ids // PATCHES
    row_valid = row_ids % PATCHES < counts[row_image]
    row_mask = row_valid.astype(jnp.float32)[:, None]
    normed = low(layer_norm(inputs, norm_first))
    query = low(low_back(matmul(normed, attn_in[0])))
    key_rows = low(low_back(matmul(normed, attn_in[1])))
    value_rows = low(low_back(matmul(normed, attn_in[2])))
    blocks = (query.reshape(IMAGES, PATCHES, HEADS, HEAD_DIM), key_rows.reshape(IMAGES, PATCHES, HEADS, HEAD_DIM), value_rows.reshape(IMAGES, PATCHES, HEADS, HEAD_DIM), row_valid.reshape(IMAGES, PATCHES))
    carry_zero, attended = lax.scan(jax.checkpoint(attend_image), jnp.zeros((), jnp.float32), blocks)
    attention = low_back(matmul(attended.reshape(TOKENS, D), attn_out))
    mixed = inputs + row_mask * attention
    routed = low(layer_norm(mixed, norm_second))
    expert_prob = jax.nn.softmax(low_back(matmul(routed, router)), axis=-1)
    picked = jnp.take_along_axis(expert_prob, routes, axis=1)
    gate_values = picked / lax.optimization_barrier(jnp.sum(picked, axis=1, keepdims=True))
    source_dev = (row_ids // ROWS_DEV)[:, None]
    empty_row = EXPERTS * N_WIDE * CAP
    target = jnp.where(slot_ids < CAP, (routes * N_WIDE + source_dev) * CAP + slot_ids, empty_row).astype(jnp.int32)
    buffer_rows = jnp.zeros((empty_row + 1, D), jnp.float32).at[target[:, 0]].add(routed).at[target[:, 1]].add(routed)
    dispatched = low_back(buffer_rows[:empty_row]).reshape(EXPERTS, N_WIDE * CAP, D)
    results = lax.map(jax.checkpoint(expert_block), (dispatched, expert_in, expert_out))
    result_table = jnp.concatenate([results.reshape(empty_row, D), jnp.zeros((1, D), jnp.float32)], axis=0)
    combined = gate_values[:, 0:1] * result_table[target[:, 0]] + gate_values[:, 1:2] * result_table[target[:, 1]]
    return mixed + combined

def reference(inputs, counts, routes, slot_ids, norm_first, attn_in, attn_out, norm_second, router, expert_in, expert_out, cotangent):

    def closed(inputs_f, first_f, attn_in_f, attn_out_f, second_f, router_f, expert_in_f, expert_out_f):
        return forward(inputs_f, first_f, attn_in_f, attn_out_f, second_f, router_f, expert_in_f, expert_out_f, counts, routes, slot_ids)
    output, pullback = jax.vjp(closed, inputs.astype(jnp.float32), norm_first.astype(jnp.float32), attn_in.astype(jnp.float32), attn_out.astype(jnp.float32), norm_second.astype(jnp.float32), router.astype(jnp.float32), expert_in[0::2].astype(jnp.float32), expert_out[0::2].astype(jnp.float32))
    grads = pullback(cotangent.astype(jnp.float32))
    expert_in_grad = jnp.repeat(grads[6], 2, axis=0)
    expert_out_grad = jnp.repeat(grads[7], 2, axis=0)
    return (output.astype(jnp.bfloat16), grads[0], grads[1], grads[2], grads[3], grads[4], grads[5], expert_in_grad, expert_out_grad)
```

```python
import functools

import jax
import jax.numpy as jnp
from jax import lax
from jax.experimental import pallas as pl
from jax.experimental.pallas import tpu as pltpu
from jax.sharding import PartitionSpec as P

HEAD_DIM = 64


NORM_EPSILON = 1e-06
MASKED_SCORE = -1e30


BY_MESH = pl.DeviceIdType.MESH
VMEM_BYTES = 64 * 1024 * 1024 - 65536


def round_up(value, multiple):
    return -(-value // multiple) * multiple


def dot_rows(left, right):
    return lax.dot_general(left, right, (((1,), (0,)), ((), ())), preferred_element_type=jnp.float32)


def dot_cols(left, right):
    return lax.dot_general(left, right, (((1,), (1,)), ((), ())), preferred_element_type=jnp.float32)


def normal_parts(values):
    t = 1.0 / (1.0 + (0.3275911 * 0.7071067811865476) * jnp.abs(values))
    bell = jnp.exp(-0.5 * values * values)
    poly = t * (
        0.254829592
        + t * (-0.284496736 + t * (1.421413741 + t * (-1.453152027 + t * 1.061405429)))
    )
    tail = 0.5 * poly * bell
    return jnp.where(values >= 0.0, 1.0 - tail, tail), 0.3989422804014327 * values * bell


Z_OUT, Y_OUT, C_OWN, C_FAR, R_CORE, R_CHIP, R_HOME, R_PAIR = 0, 2, 4, 6, 8, 10, 12, 14
GATES, G_CORE, G_CHIP, G_HOME = 16, 17, 18, 19
END_CHIP, END_OWN, END_FAR = 20, 22, 24
SEM_ROWS = 26


def exchange_kernel(
    experts,
    low_ref,
    cot_ref,
    key_row,
    key_col,
    gate_col,
    in_ref,
    out_ref,
    grad_ref,
    mix_ref,
    pair_ref,
    rows_ref,
    cots_ref,
    hid_ref,
    pre_ref,
    send_rows,
    gate_send,
    gate_recv,
    gate_tall,
    pair_tall,
    pair_part,
    pair_core,
    pair_sum,
    pair_chip,
    pair_home,
    pair_back,
    core_send,
    core_recv,
    kept,
    chip_send,
    chip_recv,
    back,
    hot_ref,
    total,
    sent,
    came,
):
    rows, width = low_ref.shape
    cap = rows_ref.shape[1]
    half = cap // 2
    side = width // 2
    half_rows = rows // 2
    units = in_ref.shape[1]
    wide_cap = gate_send.shape[2]
    n = lax.axis_index("narrow")
    w = lax.axis_index("wide")
    core = lax.rem(n, 2)
    chip = n // 2
    me = w // 2
    parity = lax.rem(w, 2)
    near = n + 1 - 2 * core
    across = lax.rem(n + 2, 4)
    my_half = pl.ds(pl.multiple_of(core * half, 16), half)
    other_half = pl.ds(pl.multiple_of((1 - core) * half, 16), half)
    my_side = pl.ds(pl.multiple_of(chip * side, 128), side)
    other_side = pl.ds(pl.multiple_of((1 - chip) * side, 128), side)
    my_rows = pl.ds(pl.multiple_of(core * half_rows, 16), half_rows)

    def to(narrow, wide):
        return {"narrow": narrow, "wide": wide}

    def home_of(e):
        return 2 * e + parity

    def send_to(i):
        return lax.rem(me + jnp.where(2 * me >= experts, i, experts - i), experts)

    def take(i):
        return lax.rem(me + jnp.where(2 * me < experts, i, experts - i), experts)

    def move(src, dst, row, sent_at, came_at, where):
        return pltpu.make_async_remote_copy(
            src_ref=src,
            dst_ref=dst,
            send_sem=sent.at[row, sent_at],
            recv_sem=came.at[row, came_at],
            device_id=where,
            device_id_type=BY_MESH,
        )

    barrier = pltpu.get_barrier_semaphore()
    for peer in (near, across):
        pl.semaphore_signal(barrier, inc=1, device_id=to(peer, w), device_id_type=BY_MESH)

    @pl.loop(1, experts)
    def _(i):
        pl.semaphore_signal(
            barrier, inc=1, device_id=to(n, home_of(send_to(i))), device_id_type=BY_MESH
        )

    pl.semaphore_wait(barrier, experts + 1)

    landing = (rows_ref, cots_ref)

    def z_copy(a, e, landed):
        return move(
            send_rows.at[a, e],
            landing[a].at[landed, my_half, my_side],
            Z_OUT + a,
            e,
            landed,
            to(n, home_of(e)),
        )

    def build(e):
        slot = e * cap + core * half + lax.broadcasted_iota(jnp.int32, (half, rows), 0)
        hit = (key_row[0:1, :] == slot) | (key_row[1:2, :] == slot)
        hot = jnp.where(hit, 1.0, 0.0).astype(jnp.bfloat16)
        for a, source in enumerate((low_ref, cot_ref)):
            piece = dot_rows(hot, source[:, my_side]).astype(jnp.bfloat16)

            @pl.when(e == me)
            def _():
                landing[a][me, my_half, my_side] = piece

            @pl.when(e != me)
            def _():
                send_rows[a, e] = piece
                z_copy(a, e, me).start()

    @pl.loop(0, experts)
    def _(i):
        build(send_to(i + 1))

    def gate_copy(e, landed):
        return move(gate_send.at[e], gate_recv.at[landed], GATES, e, landed, to(n, home_of(e)))

    @pl.loop(0, experts)
    def _(i):
        e = send_to(i + 1)

        @pl.loop(0, wide_cap // 128)
        def _(j):
            lanes = pl.ds(pl.multiple_of(j * 128, 128), 128)
            slot = e * cap + j * 128 + lax.broadcasted_iota(jnp.int32, (rows, 128), 1)
            picked = jnp.where(key_col[:, 0:1] == slot, gate_col[:, 0:1], 0.0) + jnp.where(
                key_col[:, 1:2] == slot, gate_col[:, 1:2], 0.0
            )
            line = jnp.broadcast_to(jnp.sum(picked, 0, keepdims=True), (8, 128))

            @pl.when(e == me)
            def _():
                gate_recv[me, :, lanes] = line

            @pl.when(e != me)
            def _():
                gate_send[e, :, lanes] = line

        @pl.when(e != me)
        def _():
            gate_copy(e, me).start()

    def spread(a, s, row, rows_part, cols_part, where):
        ref = landing[a].at[s, rows_part, cols_part]
        return move(ref, ref, row + a, s, s, where)

    def stage_a(i):
        s = take(i)
        for a in range(2):

            @pl.when(i > 0)
            def _():
                z_copy(a, s, s).wait_recv()

            spread(a, s, Y_OUT, my_half, my_side, to(across, w)).start()
            spread(a, s, C_OWN, my_half, my_side, to(near, w)).start()

    def stage_b(i):
        s = take(i)
        for a in range(2):
            spread(a, s, Y_OUT, my_half, other_side, to(across, w)).wait_recv()
            spread(a, s, C_FAR, my_half, other_side, to(near, w)).start()

    def stage_c(i):
        s = take(i)
        for a in range(2):
            spread(a, s, C_OWN, other_half, my_side, to(near, w)).wait_recv()
            spread(a, s, C_FAR, other_half, other_side, to(near, w)).wait_recv()

    pair_tall[...] = jnp.zeros_like(pair_tall)

    def pair_move(step, s):
        src, dst, row, where = (
            (pair_part, pair_core, G_CORE, to(near, w)),
            (pair_sum, pair_chip, G_CHIP, to(across, w)),
        )[step]
        return move(src.at[s], dst.at[s], row, s, s, where)

    def pair_return(s, landed):
        return move(
            pair_home.at[s], pair_back.at[landed], G_HOME, s, landed, to(n, home_of(s))
        )

    def core_move(k, s):
        return move(
            core_send.at[k, s], core_recv.at[k, s], R_CORE + k, s, s, to(near, w)
        )

    def chip_move(k, s):
        return move(
            chip_send.at[k, s], chip_recv.at[k, s], R_CHIP + k, s, s, to(across, w)
        )

    def home_move(k, s, landed):
        return move(
            core_send.at[k, s, :, slice(0, side)],
            back.at[k, landed, my_half, :],
            R_HOME + k,
            s,
            landed,
            to(n, home_of(s)),
        )

    def pair_forward(k, e, part):
        ref = back.at[k, e, part, :]
        return move(ref, ref, R_PAIR + k, e, e, to(near, w))

    chunk = 256 if units % 256 == 0 else units

    def compute(i):
        s = take(i)

        @pl.when(i > 0)
        def _():
            gate_copy(s, s).wait_recv()

        gate_tall[...] = jnp.transpose(gate_recv[s])

        @pl.loop(0, 2)
        def _(m):
            part = pl.ds(pl.multiple_of(m * half, 16), half)
            left = rows_ref[s, part, :]
            cots = cots_ref[s, part, :]
            gate = gate_tall[part, 0:1]
            pair = jnp.zeros((half, 1), jnp.float32)
            for j in range(units // chunk):
                cols = slice(j * chunk, (j + 1) * chunk)
                pre = dot_rows(left, in_ref[:, cols])
                free = dot_cols(cots, out_ref[cols, :])
                cdf, slope = normal_parts(pre)
                hidden = (pre * cdf).astype(jnp.bfloat16)
                hid_ref[s, part, cols] = hidden
                pre_ref[s, part, cols] = (gate * free * (cdf + slope)).astype(jnp.bfloat16)
                pair += jnp.sum(hidden.astype(jnp.float32) * free, 1, keepdims=True)
            pair_tall[part, :] = jnp.broadcast_to(pair, (half, 128))

        pair_part[s] = jnp.transpose(pair_tall[...])[0:8]
        pair_move(0, s).start()

    def first_reduce(k, s):
        left, weight, dot = ((pre_ref, in_ref, dot_cols), (hid_ref, out_ref, dot_rows))[k]
        for mine in (False, True):
            part = my_half if mine else other_half
            piece = dot(left[s, part, :], weight[...])
            if k == 1:
                piece = piece * gate_tall[part, 0:1]
            if mine:
                kept[k, s] = piece
            else:
                core_send[k, s] = piece.astype(jnp.bfloat16)
                core_move(k, s).start()

    def gate_cots(s):
        cots_ref[s] = (gate_tall[0:cap, 0:1] * cots_ref[s].astype(jnp.float32)).astype(jnp.bfloat16)

    def wait_spread_sends(i):
        s = take(i)
        for a in range(2):
            spread(a, s, Y_OUT, my_half, my_side, to(across, w)).wait_send()
            spread(a, s, C_OWN, my_half, my_side, to(near, w)).wait_send()
            spread(a, s, C_FAR, my_half, other_side, to(near, w)).wait_send()

    stage_a(0)

    @pl.loop(0, experts)
    def _(i):
        @pl.when(i + 1 < experts)
        def _():
            stage_a(i + 1)

        stage_b(i)
        stage_c(i)
        compute(i)
        s = take(i)
        first_reduce(0, s)
        first_reduce(1, s)
        wait_spread_sends(i)
        gate_cots(s)

    @pl.loop(0, experts)
    def _(i):
        s = take(i)
        for k in range(2):
            core_move(k, s).wait_recv()
            chip_send[k, s] = (
                kept[k, s, :, other_side] + core_recv[k, s, :, other_side].astype(jnp.float32)
            ).astype(jnp.bfloat16)
            chip_move(k, s).start()
        pair_move(0, s).wait_recv()
        pair_sum[s] = pair_part[s] + pair_core[s]
        pair_move(1, s).start()

    @pl.loop(0, experts)
    def _(i):
        s = take(i)
        for k in range(2):
            chip_move(k, s).wait_recv()
            core_move(k, s).wait_send()
            piece = (
                kept[k, s, :, my_side]
                + core_recv[k, s, :, my_side].astype(jnp.float32)
                + chip_recv[k, s].astype(jnp.float32)
            ).astype(jnp.bfloat16)

            @pl.when(s == me)
            def _():
                back[k, me, my_half, :] = piece

            @pl.when(s != me)
            def _():
                core_send[k, s, :, 0:side] = piece
                home_move(k, s, me).start()

        pair_move(1, s).wait_recv()
        line = pair_sum[s] + pair_chip[s]

        @pl.when(s == me)
        def _():
            pair_back[me] = line

        @pl.when(s != me)
        def _():
            pair_home[s] = line
            pair_return(s, me).start()

    total[...] = jnp.zeros_like(total)
    pair_ref[...] = jnp.zeros_like(pair_ref)

    @pl.loop(0, experts)
    def _(i):
        e = take(i)
        for k in range(2):

            @pl.when(i > 0)
            def _():
                home_move(k, e, e).wait_recv()

            pair_forward(k, e, my_half).start()

        @pl.when(i > 0)
        def _():
            pair_return(e, e).wait_recv()

    @pl.loop(0, experts)
    def _(i):
        e = take(i)

        @pl.loop(0, 4)
        def _(m):
            part = pl.ds(pl.multiple_of(m * (rows // 4), 16), rows // 4)
            slot = e * cap + lax.broadcasted_iota(jnp.int32, (rows // 4, cap), 1)
            hit = (key_col[part, 0:1] == slot) | (key_col[part, 1:2] == slot)
            hot_ref[part, :] = jnp.where(hit, 1.0, 0.0).astype(jnp.bfloat16)

        tall = jnp.transpose(pair_back[e])[0:cap, 0:1]
        high = tall.astype(jnp.bfloat16)
        rest = tall - high.astype(jnp.float32)
        middle = rest.astype(jnp.bfloat16)
        low = (rest - middle.astype(jnp.float32)).astype(jnp.bfloat16)
        lane = lax.broadcasted_iota(jnp.int32, (cap, 128), 1)
        spelled = jnp.where(
            lane == 0,
            high.astype(jnp.float32),
            jnp.where(
                lane == 1,
                middle.astype(jnp.float32),
                jnp.where(lane == 2, low.astype(jnp.float32), 0.0),
            ),
        ).astype(jnp.bfloat16)
        found = jnp.sum(dot_rows(hot_ref[...], spelled), 1, keepdims=True)
        lane_rows = lax.broadcasted_iota(jnp.int32, (rows, 128), 1)
        pair_ref[...] += jnp.where(lane_rows == e, found, 0.0)
        for k in range(2):
            pair_forward(k, e, other_half).wait_recv()
            total[k] += dot_rows(hot_ref[my_rows, :], back[k, e])

    ends = (grad_ref, mix_ref)

    def end_move(a, row, cols, where):
        ref = ends[a].at[my_rows, cols]
        return move(ref, ref, row + a, 0, 0, where)

    for a in range(2):
        ends[a][my_rows, my_side] = total[a].astype(jnp.bfloat16)
        end_move(a, END_CHIP, my_side, to(across, w)).start()
        end_move(a, END_OWN, my_side, to(near, w)).start()
    for a in range(2):
        end_move(a, END_CHIP, other_side, to(across, w)).wait_recv()
        end_move(a, END_FAR, other_side, to(near, w)).start()
    for a in range(2):
        end_move(a, END_OWN, my_side, to(near, w)).wait()
        end_move(a, END_FAR, other_side, to(near, w)).wait()
        end_move(a, END_CHIP, my_side, to(across, w)).wait_send()

    @pl.loop(0, experts)
    def _(i):
        s = take(i)
        for k in range(2):
            chip_move(k, s).wait_send()
            pair_forward(k, s, my_half).wait_send()
        pair_move(0, s).wait_send()
        pair_move(1, s).wait_send()

        @pl.when(i > 0)
        def _():
            for k in range(2):
                z_copy(k, s, me).wait_send()
                home_move(k, s, me).wait_send()
            gate_copy(s, me).wait_send()
            pair_return(s, me).wait_send()


def expert_exchange(low, cotangent, keys, gates, weight_in, weight_out, experts, cap):
    rows, width = low.shape
    units = weight_in.shape[1]
    half, side, wide_cap = cap // 2, width // 2, round_up(cap, 128)
    bf16, f32 = jnp.bfloat16, jnp.float32
    vmem = pl.BlockSpec(memory_space=pltpu.VMEM)
    return pl.pallas_call(
        functools.partial(exchange_kernel, experts),
        out_shape=[
            jax.ShapeDtypeStruct((rows, width), bf16),
            jax.ShapeDtypeStruct((rows, width), bf16),
            jax.ShapeDtypeStruct((rows, 128), f32),
            jax.ShapeDtypeStruct((experts, cap, width), bf16),
            jax.ShapeDtypeStruct((experts, cap, width), bf16),
            jax.ShapeDtypeStruct((experts, cap, units), bf16),
            jax.ShapeDtypeStruct((experts, cap, units), bf16),
        ],
        in_specs=[vmem] * 7,
        out_specs=[vmem] * 7,
        scratch_shapes=[
            pltpu.VMEM((2, experts, half, side), bf16),
            pltpu.VMEM((experts, 8, wide_cap), f32),
            pltpu.VMEM((experts, 8, wide_cap), f32),
            pltpu.VMEM((wide_cap, 8), f32),
            pltpu.VMEM((wide_cap, 128), f32),
            pltpu.VMEM((experts, 8, wide_cap), f32),
            pltpu.VMEM((experts, 8, wide_cap), f32),
            pltpu.VMEM((experts, 8, wide_cap), f32),
            pltpu.VMEM((experts, 8, wide_cap), f32),
            pltpu.VMEM((experts, 8, wide_cap), f32),
            pltpu.VMEM((experts, 8, wide_cap), f32),
            pltpu.VMEM((2, experts, half, width), bf16),
            pltpu.VMEM((2, experts, half, width), bf16),
            pltpu.VMEM((2, experts, half, width), f32),
            pltpu.VMEM((2, experts, half, side), bf16),
            pltpu.VMEM((2, experts, half, side), bf16),
            pltpu.VMEM((2, experts, cap, side), bf16),
            pltpu.VMEM((rows, cap), bf16),
            pltpu.VMEM((2, rows // 2, side), f32),
            pltpu.SemaphoreType.DMA((SEM_ROWS, experts)),
            pltpu.SemaphoreType.DMA((SEM_ROWS, experts)),
        ],
        compiler_params=pltpu.CompilerParams(
            collective_id=1, has_side_effects=True, vmem_limit_bytes=VMEM_BYTES
        ),
    )(low, cotangent, keys.T, keys, gates, weight_in, weight_out)


def swapped(x, axis, distance):
    return lax.ppermute(x, axis, [(i, i ^ 1 << distance) for i in range(lax.axis_size(axis))])


def norm_forward(values, gain):
    center = values - jnp.mean(values, -1, keepdims=True)
    scaled = lax.rsqrt(jnp.mean(center * center, -1, keepdims=True) + NORM_EPSILON)
    normed = center * scaled
    return (normed * gain, normed, scaled)


def norm_backward(grad_rows, gain, normed, scaled):
    grad_normed = grad_rows * gain
    gain_grad = jnp.sum(grad_rows * normed, 0)
    inner = (
        grad_normed
        - jnp.mean(grad_normed, -1, keepdims=True)
        - normed * jnp.mean(grad_normed * normed, -1, keepdims=True)
    )
    return (scaled * inner, gain_grad)


def gelu_exact(values):
    return jax.nn.gelu(values, approximate=False)


def image_scores(query, key_rows, key_valid, score_scale):
    scores = (
        jnp.einsum("qhd,khd->hqk", query, key_rows, preferred_element_type=jnp.float32)
        * score_scale
    )
    return jnp.where(key_valid[None, None, :], scores, MASKED_SCORE)


def attend_forward(query, key_rows, value_rows, key_valid, score_scale):
    scores = image_scores(query, key_rows, key_valid, score_scale)
    row_max = jnp.max(scores, -1, keepdims=True)
    log_total = row_max + jnp.log(jnp.sum(jnp.exp(scores - row_max), -1, keepdims=True))
    softmax_w = jnp.exp(scores - log_total).astype(jnp.bfloat16)
    out_block = jnp.einsum(
        "hqk,khd->qhd", softmax_w, value_rows, preferred_element_type=jnp.float32
    )
    return (out_block.astype(jnp.bfloat16), log_total)


def attend_backward(query, key_rows, value_rows, key_valid, log_total, out_grad, score_scale):
    scores = image_scores(query, key_rows, key_valid, score_scale)
    softmax_w = jnp.exp(scores - log_total)
    prob_change = jnp.einsum(
        "qhd,khd->hqk", out_grad, value_rows, preferred_element_type=jnp.float32
    )
    row_delta = jnp.sum(softmax_w * prob_change, -1, keepdims=True)
    score_grad = (score_scale * softmax_w * (prob_change - row_delta)).astype(jnp.bfloat16)
    query_grad = jnp.einsum(
        "hqk,khd->qhd", score_grad, key_rows, preferred_element_type=jnp.float32
    )
    key_grad = jnp.einsum("hqk,qhd->khd", score_grad, query, preferred_element_type=jnp.float32)
    value_grad = jnp.einsum(
        "hqk,qhd->khd", softmax_w.astype(jnp.bfloat16), out_grad, preferred_element_type=jnp.float32
    )
    return (
        query_grad.astype(jnp.bfloat16),
        key_grad.astype(jnp.bfloat16),
        value_grad.astype(jnp.bfloat16),
    )


def body(
    inputs,
    counts,
    routes,
    slot_ids,
    norm_first,
    attn_in,
    attn_out,
    norm_second,
    router,
    expert_in,
    expert_out,
    cotangent,
):
    rows_dev, feat_width = inputs.shape
    images = counts.shape[0]
    patches = rows_dev // images
    experts = router.shape[1]
    local_experts = expert_in.shape[0]
    wide_size = lax.axis_size("wide")
    half_slots = (105 * rows_dev + 100 * experts - 1) // (100 * experts)
    capacity = 2 * half_slots
    head_cols = attn_out.shape[0]
    local_heads = head_cols // HEAD_DIM
    score_scale = HEAD_DIM ** (-0.5)
    positions = jnp.arange(rows_dev, dtype=jnp.int32)
    owner_hot = (positions // patches)[:, None] == jnp.arange(images, dtype=jnp.int32)[None, :]
    lengths = jnp.sum(jnp.where(owner_hot, counts[None, :], 0), 1)
    row_live = positions % patches < lengths
    row_mask = row_live.astype(jnp.float32)[:, None]
    key_live = row_live.reshape(images, patches)
    source_rows = inputs.astype(jnp.float32)
    normed1, hat_first, rs_first = norm_forward(source_rows, norm_first)
    low_first = normed1.astype(jnp.bfloat16)
    projected = jnp.einsum(
        "rd,idc->irc", low_first, attn_in, preferred_element_type=jnp.float32
    ).astype(jnp.bfloat16)
    head_blocks = projected.reshape(3, images, patches, local_heads, HEAD_DIM)
    out_blocks = []
    total_blocks = []
    for slot_image in range(images):
        out_block, log_total = attend_forward(
            head_blocks[0, slot_image],
            head_blocks[1, slot_image],
            head_blocks[2, slot_image],
            key_live[slot_image],
            score_scale,
        )
        out_blocks.append(out_block)
        total_blocks.append(log_total)
    attended = jnp.stack(out_blocks).reshape(rows_dev, head_cols)
    attention = lax.psum(jnp.dot(attended, attn_out, preferred_element_type=jnp.float32), "narrow")
    mixed = source_rows + row_mask * attention
    normed2, hat_second, rs_second = norm_forward(mixed, norm_second)
    low_second = normed2.astype(jnp.bfloat16)
    logits = jnp.dot(low_second, router, preferred_element_type=jnp.float32)
    expert_prob = jax.nn.softmax(logits, axis=-1)
    expert_ids = jnp.arange(experts, dtype=jnp.int32)[None, :]
    first_hot = (routes[:, 0:1] == expert_ids).astype(jnp.float32)
    second_hot = (routes[:, 1:2] == expert_ids).astype(jnp.float32)
    picked = jnp.stack(
        [jnp.sum(expert_prob * first_hot, 1), jnp.sum(expert_prob * second_hot, 1)], 1
    )
    pick_total = jnp.sum(picked, 1, keepdims=True)
    gate_values = picked / pick_total
    slot_pad = round_up(capacity, 32)
    slot_keys = jnp.where(slot_ids < capacity, routes * slot_pad + slot_ids, -1)
    dispatch_grad, combined, pair_grads, received, arrived_grad, hidden, pre_grad = expert_exchange(
        low_second, cotangent, slot_keys, gate_values, expert_in[0], expert_out[0], experts, slot_pad
    )
    output = (mixed + combined.astype(jnp.float32)).astype(jnp.bfloat16)
    grad_rows = cotangent.astype(jnp.float32)
    by_expert = pair_grads[:, :experts]
    gate_grad = jnp.stack([jnp.sum(by_expert * first_hot, 1), jnp.sum(by_expert * second_hot, 1)], 1)
    copy_out_grad = jnp.einsum(
        "scf,scd->fd", hidden, arrived_grad, preferred_element_type=jnp.float32
    )[None]
    copy_in_grad = jnp.einsum(
        "scd,scf->df", received, pre_grad, preferred_element_type=jnp.float32
    )[None]
    dispatch_grad = dispatch_grad.astype(jnp.float32)
    other_in, other_out = (
        swapped(copy_in_grad.astype(jnp.bfloat16), "wide", 0).astype(copy_in_grad.dtype),
        swapped(copy_out_grad.astype(jnp.bfloat16), "wide", 0).astype(copy_out_grad.dtype),
    )
    expert_in_grad = copy_in_grad + other_in
    expert_out_grad = copy_out_grad + other_out
    weighted = jnp.sum(gate_grad * gate_values, 1, keepdims=True)
    picked_grad = (gate_grad - weighted) / pick_total
    prob_grad = picked_grad[:, 0:1] * first_hot + picked_grad[:, 1:2] * second_hot
    logit_grad = (
        expert_prob * (prob_grad - jnp.sum(expert_prob * prob_grad, 1, keepdims=True))
    ).astype(jnp.bfloat16)
    router_grad = jnp.einsum(
        "rd,re->de", low_second, logit_grad, preferred_element_type=jnp.float32
    )
    normed2_grad = dispatch_grad + jnp.einsum(
        "re,de->rd", logit_grad, router, preferred_element_type=jnp.float32
    )
    mixed_delta, norm_second_grad = norm_backward(normed2_grad, norm_second, hat_second, rs_second)
    mixed_grad = grad_rows + mixed_delta
    attention_grad = (row_mask * mixed_grad).astype(jnp.bfloat16)
    attn_out_grad = jnp.einsum(
        "rc,rd->cd", attended, attention_grad, preferred_element_type=jnp.float32
    )
    attended_grad = jnp.einsum(
        "rd,cd->rc", attention_grad, attn_out, preferred_element_type=jnp.float32
    ).astype(jnp.bfloat16)
    grad_blocks = attended_grad.reshape(images, patches, local_heads, HEAD_DIM)
    query_list = []
    key_list = []
    value_list = []
    for slot_image in range(images):
        query_grad, key_grad, value_grad = attend_backward(
            head_blocks[0, slot_image],
            head_blocks[1, slot_image],
            head_blocks[2, slot_image],
            key_live[slot_image],
            total_blocks[slot_image],
            grad_blocks[slot_image],
            score_scale,
        )
        query_list.append(query_grad)
        key_list.append(key_grad)
        value_list.append(value_grad)
    projected_grad = jnp.stack(
        [
            jnp.stack(query_list).reshape(rows_dev, head_cols),
            jnp.stack(key_list).reshape(rows_dev, head_cols),
            jnp.stack(value_list).reshape(rows_dev, head_cols),
        ]
    )
    attn_in_grad = jnp.einsum(
        "rd,irc->idc", low_first, projected_grad, preferred_element_type=jnp.float32
    )
    normed1_part = jnp.einsum(
        "irc,idc->rd", projected_grad, attn_in, preferred_element_type=jnp.float32
    )
    normed1_grad = lax.psum(normed1_part.astype(jnp.bfloat16), "narrow").astype(jnp.float32)
    source_delta, norm_first_grad = norm_backward(normed1_grad, norm_first, hat_first, rs_first)
    input_grad = mixed_grad + source_delta
    summed = lax.psum(
        (norm_first_grad, attn_in_grad, attn_out_grad, norm_second_grad, router_grad), "wide"
    )
    return (
        output,
        input_grad,
        summed[0],
        summed[1],
        summed[2],
        summed[3],
        summed[4],
        expert_in_grad,
        expert_out_grad,
    )


def solution(mesh):
    in_specs = (
        P("wide", None),
        P("wide"),
        P("wide", None),
        P("wide", None),
        P(),
        P(None, None, "narrow"),
        P("narrow", None),
        P(),
        P(),
        P("wide", None, "narrow"),
        P("wide", "narrow", None),
        P("wide", None),
    )
    out_specs = (
        P("wide", None),
        P("wide", None),
        P(),
        P(None, None, "narrow"),
        P("narrow", None),
        P(),
        P(),
        P("wide", None, "narrow"),
        P("wide", "narrow", None),
    )
    return jax.shard_map(body, mesh=mesh, in_specs=in_specs, out_specs=out_specs, check_vma=False)
```

```python
import functools

import jax
import jax.numpy as jnp
from jax import lax
from jax.experimental import pallas as pl
from jax.experimental.pallas import tpu as pltpu
from jax.sharding import PartitionSpec as P

HEAD_DIM = 64
NORM_EPSILON = 1e-06
MASKED_SCORE = -1e30
BY_MESH = pl.DeviceIdType.MESH
VMEM_BYTES = 64 * 1024 * 1024 - 65536


def round_up(value, multiple):
    return -(-value // multiple) * multiple


def dot_rows(left, right):
    return lax.dot_general(left, right, (((1,), (0,)), ((), ())), preferred_element_type=jnp.float32)


def dot_cols(left, right):
    return lax.dot_general(left, right, (((1,), (1,)), ((), ())), preferred_element_type=jnp.float32)


def normal_parts(values):
    t = 1.0 / (1.0 + (0.3275911 * 0.7071067811865476) * jnp.abs(values))
    bell = jnp.exp(-0.5 * values * values)
    poly = t * (
        0.254829592
        + t * (-0.284496736 + t * (1.421413741 + t * (-1.453152027 + t * 1.061405429)))
    )
    tail = 0.5 * poly * bell
    return jnp.where(values >= 0.0, 1.0 - tail, tail), 0.3989422804014327 * values * bell


def normalize(values, gain):
    center = values - jnp.mean(values, -1, keepdims=True)
    scaled = lax.rsqrt(jnp.mean(center * center, -1, keepdims=True) + NORM_EPSILON)
    normed = center * scaled
    return normed * gain, normed, scaled


class Place:
    def __init__(self, experts):
        self.experts = experts
        self.n = lax.axis_index("narrow")
        self.w = lax.axis_index("wide")
        self.core = lax.rem(self.n, 2)
        self.chip = self.n // 2
        self.me = self.w // 2
        self.parity = lax.rem(self.w, 2)
        self.near_n = self.n + 1 - 2 * self.core
        self.across_n = lax.rem(self.n + 2, 4)
        self.near = {"narrow": self.near_n, "wide": self.w}
        self.across = {"narrow": self.across_n, "wide": self.w}

    def home(self, e):
        return {"narrow": self.n, "wide": 2 * e + self.parity}

    def send_to(self, i):
        far_first = jnp.where(2 * self.me >= self.experts, i, self.experts - i)
        return lax.rem(self.me + far_first, self.experts)

    def take(self, i):
        near_first = jnp.where(2 * self.me < self.experts, i, self.experts - i)
        return lax.rem(self.me + near_first, self.experts)

    def part(self, which, size, align):
        return pl.ds(pl.multiple_of(which * size, align), size)

    def greet(self, others=()):
        barrier = pltpu.get_barrier_semaphore()
        for peer in (self.near, self.across, *others):
            pl.semaphore_signal(barrier, inc=1, device_id=peer, device_id_type=BY_MESH)

        @pl.loop(1, self.experts)
        def _(i):
            pl.semaphore_signal(
                barrier, inc=1, device_id=self.home(self.send_to(i)), device_id_type=BY_MESH
            )

        pl.semaphore_wait(barrier, self.experts + 1 + len(others))


def mover(sent, came):
    def move(src, dst, row, sent_at, came_at, where):
        return pltpu.make_async_remote_copy(
            src_ref=src,
            dst_ref=dst,
            send_sem=sent.at[row, sent_at],
            recv_sem=came.at[row, came_at],
            device_id=where,
            device_id_type=BY_MESH,
        )

    return move


class Dispatch:
    def __init__(self, place, move, base, send, landing):
        self.place, self.move, self.base = place, move, base
        self.send, self.landing = send, landing
        cap, width = landing.shape[1:]
        self.cap, self.half, self.side = cap, cap // 2, width // 2
        self.mine = place.part(place.core, self.half, 16)
        self.other = place.part(1 - place.core, self.half, 16)
        self.side_mine = place.part(place.chip, self.side, 128)
        self.side_other = place.part(1 - place.chip, self.side, 128)

    def z_copy(self, e, landed):
        return self.move(
            self.send.at[e],
            self.landing.at[landed, self.mine, self.side_mine],
            self.base,
            e,
            landed,
            self.place.home(e),
        )

    def build(self, i, key_row, source):
        place = self.place
        e = place.send_to(i)
        rows = source.shape[0]
        slot = e * self.cap + place.core * self.half
        slot = slot + lax.broadcasted_iota(jnp.int32, (self.half, rows), 0)
        hit = (key_row[0:1, :] == slot) | (key_row[1:2, :] == slot)
        hot = jnp.where(hit, 1.0, 0.0).astype(jnp.bfloat16)
        piece = dot_rows(hot, source[:, self.side_mine]).astype(jnp.bfloat16)

        @pl.when(e == place.me)
        def _():
            self.landing[place.me, self.mine, self.side_mine] = piece

        @pl.when(e != place.me)
        def _():
            self.send[e] = piece
            self.z_copy(e, place.me).start()

    def spread(self, step, s):
        rows, cols, where = (
            (self.mine, self.side_mine, self.place.across),
            (self.mine, self.side_mine, self.place.near),
            (self.mine, self.side_other, self.place.near),
        )[step]
        ref = self.landing.at[s, rows, cols]
        return self.move(ref, ref, self.base + 1 + step, s, s, where)

    def stage_a(self, i):
        s = self.place.take(i)

        @pl.when(i > 0)
        def _():
            self.z_copy(s, s).wait_recv()

        self.spread(0, s).start()
        self.spread(1, s).start()

    def stage_b(self, i):
        s = self.place.take(i)
        self.spread(0, s).wait_recv()
        self.spread(2, s).start()

    def stage_c(self, i):
        s = self.place.take(i)
        self.spread(1, s).wait_recv()
        self.spread(2, s).wait_recv()

    def finish(self):
        @pl.loop(0, self.place.experts)
        def _(i):
            s = self.place.take(i)
            for step in range(3):
                self.spread(step, s).wait_send()

            @pl.when(i > 0)
            def _():
                self.z_copy(s, self.place.me).wait_send()


FRONT_OWN, FRONT_FAR, FRONT_CHIP = 4, 5, 6
FRONT_ROWS = 7


def front_kernel(
    experts,
    counts,
    x_ref,
    cot_ref,
    key_row,
    routes_col,
    gain1_ref,
    qkv_w,
    out_w,
    gain2_ref,
    router_ref,
    cots_ref,
    heads_ref,
    attended_ref,
    stats_ref,
    mixed_ref,
    low2_ref,
    prob_ref,
    gate_ref,
    cot_send,
    low_ref,
    gather,
    out_all,
    sent,
    came,
):
    rows, width = x_ref.shape
    images = counts.shape[0]
    patches = rows // images
    head_cols = out_w.shape[0]
    heads = head_cols // HEAD_DIM
    scale = HEAD_DIM ** (-0.5)
    place = Place(experts)
    move = mover(sent, came)
    cots = Dispatch(place, move, 0, cot_send, cots_ref)
    place.greet()

    def share(ref, at):
        def copy(step):
            piece = ref(place.across_n if step == 2 else place.n)
            where = place.across if step == 0 else place.near
            row = (FRONT_CHIP, FRONT_OWN, FRONT_FAR)[step]
            return move(piece, piece, row, at, at, where)

        return copy

    out_share = share(lambda n: out_all.at[n, pl.ds(0, head_cols), :], images)
    out_all[:, head_cols:, :] = jnp.zeros_like(out_all[:, head_cols:, :])
    out_all[place.n, pl.ds(0, head_cols), :] = out_w[...]

    @pl.loop(0, experts)
    def _(i):
        cots.build(i + 1, key_row, cot_ref)

    out_share(0).start()
    out_share(1).start()
    cots.stage_a(0)

    tile = patches // 2

    @pl.loop(0, rows // tile)
    def _(t):
        part = pl.ds(pl.multiple_of(t * tile, 16), tile)
        normed, _, _ = normalize(x_ref[part, :].astype(jnp.float32), gain1_ref[0:1, :])
        low = normed.astype(jnp.bfloat16)
        low_ref[part, :] = low
        for i in range(3):
            block = dot_rows(low, qkv_w[i]).astype(jnp.bfloat16)
            for h in range(heads):
                heads_ref[i, h, part, :] = block[:, h * HEAD_DIM : (h + 1) * HEAD_DIM]

    stats_ref[...] = jnp.zeros_like(stats_ref)
    gather[place.n, :, head_cols:] = jnp.zeros_like(gather[place.n, :, head_cols:])

    def attend(image):
        keys_at = pl.ds(image * patches, patches)
        live = lax.broadcasted_iota(jnp.int32, (1, patches), 1) < counts[image]
        for h in range(heads):
            key_rows = heads_ref[1, h, keys_at, :]
            value_rows = heads_ref[2, h, keys_at, :]
            for t in range(patches // tile):
                part = pl.ds(image * patches + t * tile, tile)
                scores = dot_cols(heads_ref[0, h, part, :], key_rows) * scale
                scores = jnp.where(live, scores, MASKED_SCORE)
                top = jnp.max(scores, -1, keepdims=True)
                weights = jnp.exp(scores - top)
                total = jnp.sum(weights, -1, keepdims=True)
                probs = (weights * (1.0 / total)).astype(jnp.bfloat16)
                block = dot_rows(probs, value_rows).astype(jnp.bfloat16)
                gather[place.n, part, h * HEAD_DIM : (h + 1) * HEAD_DIM] = block
                stats_ref[part, h : h + 1] = top + jnp.log(total)

    shares = [
        share(lambda n, image=image: gather.at[n, pl.ds(image * patches, patches), :], image)
        for image in range(images)
    ]
    for image in range(images):
        attend(image)
        shares[image](0).start()
        shares[image](1).start()
        if image + 1 < experts:
            cots.stage_a(image + 1)
    attended_ref[...] = gather[place.n, :, 0:head_cols]
    out_share(0).wait_recv()
    out_share(2).start()
    cots.stage_b(0)
    out_share(1).wait_recv()
    out_share(2).wait_recv()

    def finish(image):
        shares[image](0).wait_recv()
        shares[image](2).start()
        shares[image](1).wait_recv()
        shares[image](2).wait_recv()

        @pl.loop(0, patches // tile)
        def _(t):
            part = pl.ds(pl.multiple_of(image * patches + t * tile, 16), tile)
            attention = dot_rows(gather[0, part, :], out_all[0])
            for n in range(1, 4):
                attention += dot_rows(gather[n, part, :], out_all[n])
            offset = t * tile + lax.broadcasted_iota(jnp.int32, (tile, 1), 0)
            mixed = x_ref[part, :].astype(jnp.float32) + jnp.where(
                offset < counts[image], attention, 0.0
            )
            mixed_ref[part, :] = mixed
            normed, _, _ = normalize(mixed, gain2_ref[0:1, :])
            low = normed.astype(jnp.bfloat16)
            low2_ref[part, :] = low
            lane = lax.broadcasted_iota(jnp.int32, (tile, 128), 1)
            logits = jnp.where(lane < experts, dot_rows(low, router_ref[...]), MASKED_SCORE)
            powers = jnp.exp(logits - jnp.max(logits, -1, keepdims=True))
            prob = powers / jnp.sum(powers, -1, keepdims=True)
            prob_ref[part, :] = prob
            picked = [
                jnp.sum(jnp.where(lane == routes_col[part, k : k + 1], prob, 0.0), 1, keepdims=True)
                for k in range(2)
            ]
            both = picked[0] + picked[1]
            gate_ref[part, :] = jnp.where(
                lane == 0, picked[0] / both, jnp.where(lane == 1, picked[1] / both, both)
            )

    for image in range(images):
        finish(image)

    @pl.loop(images + 1, experts)
    def _(i):
        cots.stage_a(i)

    @pl.loop(1, experts)
    def _(i):
        cots.stage_b(i)

    @pl.loop(0, experts)
    def _(i):
        cots.stage_c(i)

    cots.finish()
    for copy in (out_share, *shares):
        for step in range(3):
            copy(step).wait_send()


def front(counts, x, cot, key_row, routes, gain1, qkv_w, out_w, gain2, router, experts, cap):
    rows, width = x.shape
    head_cols = out_w.shape[0]
    heads = head_cols // HEAD_DIM
    images = counts.shape[0]
    bf16, f32 = jnp.bfloat16, jnp.float32
    vmem = pl.BlockSpec(memory_space=pltpu.VMEM)
    padded_cols = round_up(head_cols, 128)
    slots = max(experts, images + 1)
    return pl.pallas_call(
        functools.partial(front_kernel, experts),
        out_shape=[
            jax.ShapeDtypeStruct((experts, cap, width), bf16),
            jax.ShapeDtypeStruct((3, heads, rows, HEAD_DIM), bf16),
            jax.ShapeDtypeStruct((rows, head_cols), bf16),
            jax.ShapeDtypeStruct((rows, 128), f32),
            jax.ShapeDtypeStruct((rows, width), f32),
            jax.ShapeDtypeStruct((rows, width), bf16),
            jax.ShapeDtypeStruct((rows, 128), f32),
            jax.ShapeDtypeStruct((rows, 128), f32),
        ],
        in_specs=[pl.BlockSpec(memory_space=pltpu.SMEM)] + [vmem] * 9,
        out_specs=[vmem] * 8,
        scratch_shapes=[
            pltpu.VMEM((experts, cap // 2, width // 2), bf16),
            pltpu.VMEM((rows, width), bf16),
            pltpu.VMEM((4, rows, padded_cols), bf16),
            pltpu.VMEM((4, padded_cols, width), bf16),
            pltpu.SemaphoreType.DMA((FRONT_ROWS, slots)),
            pltpu.SemaphoreType.DMA((FRONT_ROWS, slots)),
        ],
        compiler_params=pltpu.CompilerParams(
            collective_id=2, has_side_effects=True, vmem_limit_bytes=VMEM_BYTES
        ),
    )(counts, x, cot, key_row, routes, gain1, qkv_w, out_w, gain2, router)


class Return:
    def __init__(self, place, move, base, core_send, core_recv, kept, chip_send, chip_recv, back):
        self.place, self.move, self.base = place, move, base
        self.core_send, self.core_recv, self.kept = core_send, core_recv, kept
        self.chip_send, self.chip_recv, self.back = chip_send, chip_recv, back
        self.half, self.side = chip_send.shape[1:]
        self.mine = place.part(place.core, self.half, 16)
        self.other = place.part(1 - place.core, self.half, 16)
        self.side_mine = place.part(place.chip, self.side, 128)
        self.side_other = place.part(1 - place.chip, self.side, 128)

    def core_move(self, s):
        return self.move(
            self.core_send.at[s], self.core_recv.at[s], self.base, s, s, self.place.near
        )

    def chip_move(self, s):
        return self.move(
            self.chip_send.at[s], self.chip_recv.at[s], self.base + 1, s, s, self.place.across
        )

    def home_move(self, s, landed):
        return self.move(
            self.core_send.at[s, :, pl.ds(0, self.side)],
            self.back.at[landed, self.mine, :],
            self.base + 2,
            s,
            landed,
            self.place.home(s),
        )

    def pair_move(self, e, part):
        ref = self.back.at[e, part, :]
        return self.move(ref, ref, self.base + 3, e, e, self.place.near)

    def first(self, s, product):
        self.core_send[s] = product(self.other).astype(jnp.bfloat16)
        self.core_move(s).start()
        self.kept[s] = product(self.mine)

    def second(self, s):
        self.core_move(s).wait_recv()
        self.chip_send[s] = (
            self.kept[s, :, self.side_other]
            + self.core_recv[s, :, self.side_other].astype(jnp.float32)
        ).astype(jnp.bfloat16)
        self.chip_move(s).start()

    def third(self, s):
        self.chip_move(s).wait_recv()
        self.core_move(s).wait_send()
        piece = (
            self.kept[s, :, self.side_mine]
            + self.core_recv[s, :, self.side_mine].astype(jnp.float32)
            + self.chip_recv[s].astype(jnp.float32)
        ).astype(jnp.bfloat16)

        @pl.when(s == self.place.me)
        def _():
            self.back[self.place.me, self.mine, :] = piece

        @pl.when(s != self.place.me)
        def _():
            self.core_send[s, :, 0 : self.side] = piece
            self.home_move(s, self.place.me).start()

    def fourth(self, i):
        e = self.place.take(i)

        @pl.when(e != self.place.me)
        def _():
            self.home_move(e, e).wait_recv()

        self.pair_move(e, self.mine).start()

    def ready(self, i):
        self.pair_move(self.place.take(i), self.other).wait_recv()

    def finish(self):
        @pl.loop(0, self.place.experts)
        def _(i):
            s = self.place.take(i)
            self.chip_move(s).wait_send()
            self.pair_move(s, self.mine).wait_send()

            @pl.when(i > 0)
            def _():
                self.home_move(s, self.place.me).wait_send()


class Quarters:
    def __init__(self, place, move, base, at, ref):
        self.place, self.move, self.base, self.at, self.ref = place, move, base, at, ref
        rows, width = ref.shape
        self.rows = place.part(place.core, rows // 2, 16)
        self.mine = place.part(place.chip, width // 2, 128)
        self.other = place.part(1 - place.chip, width // 2, 128)

    def copy(self, step):
        ref = self.ref.at[self.rows, self.other if step == 2 else self.mine]
        where = self.place.across if step == 0 else self.place.near
        return self.move(ref, ref, self.base + step, self.at, self.at, where)

    def start(self):
        self.copy(0).start()
        self.copy(1).start()

    def relay(self):
        self.copy(0).wait_recv()
        self.copy(2).start()

    def ready(self):
        self.copy(1).wait_recv()
        self.copy(2).wait_recv()

    def finish(self):
        for step in range(3):
            self.copy(step).wait_send()


M_GATES, M_CORE, M_CHIP, M_HOME, M_BACK, M_MIX, M_END = 4, 5, 6, 7, 8, 12, 13
M_ROWS = 16


def middle_kernel(
    experts,
    counts,
    low_ref,
    cot_ref,
    key_row,
    key_col,
    gate_col,
    in_ref,
    out_ref,
    cots_ref,
    mixed_ref,
    prob_ref,
    routes_col,
    gain_ref,
    router_ref,
    half_ref,
    rows_ref,
    hid_ref,
    pre_ref,
    mixed_grad,
    att_grad,
    router_grad,
    gain_grad,
    send_rows,
    gate_send,
    gate_recv,
    gate_tall,
    pair_tall,
    pair_part,
    pair_core,
    pair_sum,
    pair_chip,
    pair_home,
    pair_back,
    core_send,
    core_recv,
    kept,
    chip_send,
    chip_recv,
    back,
    mix_send,
    mix_recv,
    hot_ref,
    total,
    pair_ref,
    dis_ref,
    sent,
    came,
):
    rows, width = low_ref.shape
    images = counts.shape[0]
    patches = rows // images
    cap = rows_ref.shape[1]
    half = cap // 2
    units = in_ref.shape[1]
    wide_cap = gate_send.shape[2]
    place = Place(experts)
    move = mover(sent, came)
    me = place.me
    lows = Dispatch(place, move, 0, send_rows, rows_ref)

    dgrad = Return(
        place, move, M_BACK, core_send, core_recv, kept, chip_send, chip_recv, back
    )
    place.greet()

    @pl.loop(0, experts)
    def _(i):
        lows.build(i + 1, key_row, low_ref)

    lows.stage_a(0)

    def gate_copy(e, landed):
        return move(gate_send.at[e], gate_recv.at[landed], M_GATES, e, landed, place.home(e))

    @pl.loop(0, experts)
    def _(i):
        e = place.send_to(i + 1)

        @pl.loop(0, wide_cap // 128)
        def _(j):
            lanes = pl.ds(pl.multiple_of(j * 128, 128), 128)
            slot = e * cap + j * 128 + lax.broadcasted_iota(jnp.int32, (rows, 128), 1)
            picked = jnp.where(key_col[:, 0:1] == slot, gate_col[:, 0:1], 0.0) + jnp.where(
                key_col[:, 1:2] == slot, gate_col[:, 1:2], 0.0
            )
            line = jnp.broadcast_to(jnp.sum(picked, 0, keepdims=True), (8, 128))

            @pl.when(e == me)
            def _():
                gate_recv[me, :, lanes] = line

            @pl.when(e != me)
            def _():
                gate_send[e, :, lanes] = line

        @pl.when(e != me)
        def _():
            gate_copy(e, me).start()

    pair_tall[...] = jnp.zeros_like(pair_tall)

    def pair_move(step, s):
        src, dst, row, where = (
            (pair_part, pair_core, M_CORE, place.near),
            (pair_sum, pair_chip, M_CHIP, place.across),
        )[step]
        return move(src.at[s], dst.at[s], row, s, s, where)

    def pair_return(s, landed):
        return move(pair_home.at[s], pair_back.at[landed], M_HOME, s, landed, place.home(s))

    chunk = 256 if units % 256 == 0 else units

    def compute(s, m):
        part = pl.ds(m * half, half)
        left = rows_ref[s, part, :]
        cots = cots_ref[s, part, :]
        gate = gate_tall[part, 0:1]
        pair = jnp.zeros((half, 1), jnp.float32)
        for j in range(units // chunk):
            cols = slice(j * chunk, (j + 1) * chunk)
            pre = dot_rows(left, in_ref[:, cols])
            free = dot_cols(cots, out_ref[cols, :])
            cdf, slope = normal_parts(pre)
            hidden = pre * cdf
            hid_ref[s, part, cols] = (gate * hidden).astype(jnp.bfloat16)
            pre_ref[s, part, cols] = (gate * free * (cdf + slope)).astype(jnp.bfloat16)
            pair += jnp.sum(hidden * free, 1, keepdims=True)
        pair_tall[part, :] = jnp.broadcast_to(pair, (half, 128))

    def second(s):
        dgrad.second(s)
        pair_move(0, s).wait_recv()
        pair_sum[s] = pair_part[s] + pair_core[s]
        pair_move(1, s).start()

    def third(s):
        dgrad.third(s)
        pair_move(1, s).wait_recv()
        line = pair_sum[s] + pair_chip[s]

        @pl.when(s == me)
        def _():
            pair_back[me] = line

        @pl.when(s != me)
        def _():
            pair_home[s] = line
            pair_return(s, me).start()

    @pl.loop(0, experts)
    def _(i):
        s = place.take(i)

        @pl.when(i + 1 < experts)
        def _():
            lows.stage_a(i + 1)

        lows.stage_b(i)
        lows.stage_c(i)

        @pl.when(i > 0)
        def _():
            gate_copy(s, s).wait_recv()

        gate_tall[...] = jnp.transpose(gate_recv[s])
        compute(s, 0)

        @pl.when(i > 0)
        def _():
            second(place.take(i - 1))

        compute(s, 1)
        pair_part[s] = jnp.transpose(pair_tall[...])[0:8]
        pair_move(0, s).start()
        dgrad.first(s, lambda part: dot_cols(pre_ref[s, part, :], in_ref[...]))

        @pl.when(i > 0)
        def _():
            third(place.take(i - 1))

    last = place.take(experts - 1)
    second(last)

    third(last)

    def mix_move(s):
        return move(mix_send.at[s], mix_recv.at[s], M_MIX, s, s, place.near)

    @pl.loop(0, experts)
    def _(i):
        s = place.take(i)
        for part in (dgrad.other, dgrad.mine):
            piece = dot_rows(hid_ref[s, part, :], out_ref[...])
            if part is dgrad.other:
                mix_send[s] = piece.astype(jnp.bfloat16)
                mix_move(s).start()
            else:
                kept[s] = piece

    pair_ref[...] = jnp.zeros_like(pair_ref)

    def build_hot(e):
        @pl.loop(0, 4)
        def _(m):
            part = pl.ds(pl.multiple_of(m * (rows // 4), 16), rows // 4)
            slot = e * cap + lax.broadcasted_iota(jnp.int32, (rows // 4, cap), 1)
            hit = (key_col[part, 0:1] == slot) | (key_col[part, 1:2] == slot)
            hot_ref[part, :] = jnp.where(hit, 1.0, 0.0).astype(jnp.bfloat16)

    my_rows = place.part(place.core, rows // 2, 16)
    total[...] = jnp.zeros_like(total)

    @pl.loop(0, experts)
    def _(i):
        dgrad.fourth(i)
        e = place.take(i)
        build_hot(e)

        @pl.when(i > 0)
        def _():
            pair_return(e, e).wait_recv()

        tall = jnp.transpose(pair_back[e])[0:cap, 0:1]
        high = tall.astype(jnp.bfloat16).astype(jnp.float32)
        middle = (tall - high).astype(jnp.bfloat16).astype(jnp.float32)
        lane = lax.broadcasted_iota(jnp.int32, (cap, 128), 1)
        spelled = jnp.where(
            lane == 0, high, jnp.where(lane == 1, middle, jnp.where(lane == 2, tall - high - middle, 0.0))
        ).astype(jnp.bfloat16)
        found = jnp.sum(dot_rows(hot_ref[...], spelled), 1, keepdims=True)
        lane_rows = lax.broadcasted_iota(jnp.int32, (rows, 128), 1)
        pair_ref[...] += jnp.where(lane_rows == e, found, 0.0)
        dgrad.ready(i)
        total[...] += dot_rows(hot_ref[my_rows, :], dgrad.back[e])

    ends = Quarters(place, move, M_END, 0, dis_ref)
    dis_ref[ends.rows, ends.mine] = total[...].astype(jnp.bfloat16)
    ends.start()

    @pl.loop(0, experts)
    def _(i):
        s = place.take(i)
        mix_move(s).wait_recv()
        half_ref[s] = (kept[s] + mix_recv[s].astype(jnp.float32)).astype(jnp.bfloat16)

    ends.relay()
    ends.ready()

    tile = patches // 2
    router_grad[...] = jnp.zeros_like(router_grad)
    gain_grad[...] = jnp.zeros_like(gain_grad)

    @pl.loop(0, rows // tile)
    def _(t):
        part = pl.ds(pl.multiple_of(t * tile, 16), tile)
        lane = lax.broadcasted_iota(jnp.int32, (tile, 128), 1)
        by_expert = pair_ref[part, :]
        hots = [lane == routes_col[part, k : k + 1] for k in range(2)]
        pair = [jnp.sum(jnp.where(hot, by_expert, 0.0), 1, keepdims=True) for hot in hots]
        weighted = pair[0] * gate_col[part, 0:1] + pair[1] * gate_col[part, 1:2]
        both = gate_col[part, 2:3]
        prob = prob_ref[part, :]
        prob_grad = jnp.where(hots[0], (pair[0] - weighted) / both, 0.0) + jnp.where(
            hots[1], (pair[1] - weighted) / both, 0.0
        )
        logit_grad = (
            prob * (prob_grad - jnp.sum(prob * prob_grad, 1, keepdims=True))
        ).astype(jnp.bfloat16)
        router_grad[...] += lax.dot_general(
            logit_grad, low_ref[part, :], (((0,), (0,)), ((), ())), preferred_element_type=jnp.float32
        )
        normed_grad = dis_ref[part, :].astype(jnp.float32) + dot_cols(logit_grad, router_ref[...])
        _, hat, scaled = normalize(mixed_ref[part, :], gain_ref[0:1, :])
        gain_grad[...] += jnp.sum(normed_grad * hat, 0, keepdims=True)
        grad = normed_grad * gain_ref[0:1, :]
        inner = (
            grad - jnp.mean(grad, -1, keepdims=True) - hat * jnp.mean(grad * hat, -1, keepdims=True)
        )
        full = cot_ref[part, :].astype(jnp.float32) + scaled * inner
        mixed_grad[part, :] = full
        row = t * tile + lax.broadcasted_iota(jnp.int32, (tile, 1), 0)
        live = lax.rem(row, patches) < jnp.where(t * tile < patches, counts[0], counts[images - 1])
        att_grad[part, :] = jnp.where(live, full, 0.0).astype(jnp.bfloat16)

    ends.finish()
    dgrad.finish()
    lows.finish()

    @pl.loop(0, experts)
    def _(i):
        s = place.take(i)
        pair_move(0, s).wait_send()
        pair_move(1, s).wait_send()
        mix_move(s).wait_send()

        @pl.when(i > 0)
        def _():
            gate_copy(s, me).wait_send()
            pair_return(s, me).wait_send()


def middle(
    counts, low, cot, keys, gates, weight_in, weight_out, cots, mixed, prob, routes, gain, router, experts
):
    rows, width = low.shape
    units = weight_in.shape[1]
    cap = cots.shape[1]
    half, side, wide_cap = cap // 2, width // 2, round_up(cap, 128)
    bf16, f32 = jnp.bfloat16, jnp.float32
    vmem = pl.BlockSpec(memory_space=pltpu.VMEM)
    slots = jax.ShapeDtypeStruct((experts, cap, width), bf16)
    line = pltpu.VMEM((experts, 8, wide_cap), f32)
    return pl.pallas_call(
        functools.partial(middle_kernel, experts),
        out_shape=[
            jax.ShapeDtypeStruct((experts, half, width), bf16),
            slots,
            jax.ShapeDtypeStruct((experts, cap, units), bf16),
            jax.ShapeDtypeStruct((experts, cap, units), bf16),
            jax.ShapeDtypeStruct((rows, width), f32),
            jax.ShapeDtypeStruct((rows, width), bf16),
            jax.ShapeDtypeStruct((128, width), f32),
            jax.ShapeDtypeStruct((1, width), f32),
        ],
        in_specs=[pl.BlockSpec(memory_space=pltpu.SMEM)] + [vmem] * 13,
        out_specs=[vmem] * 8,
        scratch_shapes=[
            pltpu.VMEM((experts, half, side), bf16),
            line,
            line,
            pltpu.VMEM((wide_cap, 8), f32),
            pltpu.VMEM((wide_cap, 128), f32),
            line,
            line,
            line,
            line,
            line,
            line,
            pltpu.VMEM((experts, half, width), bf16),
            pltpu.VMEM((experts, half, width), bf16),
            pltpu.VMEM((experts, half, width), f32),
            pltpu.VMEM((experts, half, side), bf16),
            pltpu.VMEM((experts, half, side), bf16),
            pltpu.VMEM((experts, cap, side), bf16),
            pltpu.VMEM((experts, half, width), bf16),
            pltpu.VMEM((experts, half, width), bf16),
            pltpu.VMEM((rows, cap), bf16),
            pltpu.VMEM((rows // 2, side), f32),
            pltpu.VMEM((rows, 128), f32),
            pltpu.VMEM((rows, width), bf16),
            pltpu.SemaphoreType.DMA((M_ROWS, experts)),
            pltpu.SemaphoreType.DMA((M_ROWS, experts)),
        ],
        compiler_params=pltpu.CompilerParams(
            collective_id=1, has_side_effects=True, vmem_limit_bytes=VMEM_BYTES
        ),
    )(
        counts, low, cot, keys.T, keys, gates, weight_in, weight_out, cots, mixed, prob, routes, gain, router
    )


class Fold:
    def __init__(self, place, move, base, core_send, core_recv, kept, chip_send, chip_recv, whole):
        self.place, self.move, self.base = place, move, base
        self.core_send, self.core_recv, self.kept = core_send, core_recv, kept
        self.chip_send, self.chip_recv, self.whole = chip_send, chip_recv, whole
        self.half, self.side = chip_send.shape[1:]
        self.side_mine = place.part(place.chip, self.side, 128)
        self.side_other = place.part(1 - place.chip, self.side, 128)

    def rows(self, image, core):
        start = (2 * image + core) * self.half
        return pl.ds(pl.multiple_of(start, 16), self.half)

    def core_move(self, image):
        return self.move(
            self.core_send.at[image],
            self.core_recv.at[image],
            self.base,
            image,
            image,
            self.place.near,
        )

    def chip_move(self, image):
        return self.move(
            self.chip_send.at[image],
            self.chip_recv.at[image],
            self.base + 1,
            image,
            image,
            self.place.across,
        )

    def share(self, image, step):
        cols = self.side_other if step == 2 else self.side_mine
        ref = self.whole.at[self.rows(image, self.place.core), cols]
        where = self.place.across if step == 0 else self.place.near
        return self.move(ref, ref, self.base + 2 + step, image, image, where)

    def second(self, image):
        self.core_move(image).wait_recv()
        self.chip_send[image] = (
            self.kept[image, :, self.side_other]
            + self.core_recv[image, :, self.side_other].astype(jnp.float32)
        ).astype(jnp.bfloat16)
        self.chip_move(image).start()

    def third(self, image):
        self.chip_move(image).wait_recv()
        self.whole[self.rows(image, self.place.core), self.side_mine] = (
            self.kept[image, :, self.side_mine]
            + self.core_recv[image, :, self.side_mine].astype(jnp.float32)
            + self.chip_recv[image].astype(jnp.float32)
        ).astype(jnp.bfloat16)
        self.share(image, 0).start()
        self.share(image, 1).start()

    def relay(self, image):
        self.share(image, 0).wait_recv()
        self.share(image, 2).start()

    def ready(self, image):
        self.share(image, 1).wait_recv()
        self.share(image, 2).wait_recv()

    def finish(self, images):
        for image in range(images):
            self.core_move(image).wait_send()
            self.chip_move(image).wait_send()
            for step in range(3):
                self.share(image, step).wait_send()


class WideSum:
    def __init__(self, place, move, tables, pair_send, pair_recv, kept, group_send, group_recv, whole):
        self.place, self.move = place, move
        self.pair_sems, self.group_out, self.group_in = tables
        self.pair_send, self.pair_recv, self.kept = pair_send, pair_recv, kept
        self.group_send, self.group_recv, self.whole = group_send, group_recv, whole
        self.rows, self.cols = group_recv.shape[2:]
        self.half = pair_send.shape[1]
        self.real = kept.shape[1]
        self.pair = {"narrow": place.n, "wide": place.w + 1 - 2 * place.parity}

    def pair_move(self, p):
        return self.move[0](
            self.pair_send.at[p], self.pair_recv.at[p], 0, p, p, self.pair
        )

    def chunk(self, e):
        return (
            pl.ds(pl.multiple_of((e // 2) * self.rows, 16), self.rows),
            pl.ds(pl.multiple_of(lax.rem(e, 2) * self.cols, 128), self.cols),
        )

    def group_move(self, p, e, landed):
        rows, cols = self.chunk(e)
        return self.move[1](
            self.group_send.at[p, rows, cols],
            self.group_recv.at[p, landed],
            p,
            e,
            landed,
            self.place.home(e),
        )

    def group_share(self, p, owner, at, landed, where):
        rows, cols = self.chunk(owner)
        ref = self.whole.at[p, self.place.parity, rows, cols]
        pieces = self.pair_send.shape[0]
        return self.move[1](ref, ref, pieces + p, at, landed, where)

    def pair_share(self, p, parity):
        ref = self.whole.at[p, parity]
        return self.move[0](ref, ref, 1, p, p, self.pair)

    def first(self, p, halves):
        @pl.when(self.place.parity == 0)
        def _():
            self.kept[p] = halves[0]
            self.pair_send[p, 0 : self.real] = halves[1].astype(jnp.bfloat16)

        @pl.when(self.place.parity == 1)
        def _():
            self.kept[p] = halves[1]
            self.pair_send[p, 0 : self.real] = halves[0].astype(jnp.bfloat16)

        self.pair_move(p).start()

    def second(self, p):
        self.pair_move(p).wait_recv()
        self.group_send[p, 0 : self.real] = (
            self.kept[p] + self.pair_recv[p, 0 : self.real].astype(jnp.float32)
        ).astype(jnp.bfloat16)

        @pl.loop(1, self.place.experts)
        def _(i):
            self.group_move(p, self.place.send_to(i), self.place.me).start()

    def third(self, p):
        rows, cols = self.chunk(self.place.me)
        total = self.group_send[p, rows, cols].astype(jnp.float32)
        self.total[...] = total

        @pl.loop(1, self.place.experts)
        def _(i):
            s = self.place.take(i)
            self.group_move(p, s, s).wait_recv()
            self.total[...] += self.group_recv[p, s].astype(jnp.float32)

        self.whole[p, self.place.parity, rows, cols] = self.total[...].astype(jnp.bfloat16)

        @pl.loop(1, self.place.experts)
        def _(i):
            e = self.place.send_to(i)
            self.group_share(p, self.place.me, e, self.place.me, self.place.home(e)).start()

    def fourth(self, p):
        @pl.loop(1, self.place.experts)
        def _(i):
            s = self.place.take(i)
            self.group_share(p, s, s, s, self.place.home(s)).wait_recv()

        self.pair_share(p, self.place.parity).start()

    def ready(self, p):
        self.pair_share(p, 1 - self.place.parity).wait_recv()

    def finish(self):
        for p in range(self.pair_send.shape[0]):
            self.pair_move(p).wait_send()
            self.pair_share(p, self.place.parity).wait_send()

            @pl.loop(1, self.place.experts)
            def _(i):
                e = self.place.send_to(i)
                self.group_move(p, e, self.place.me).wait_send()
                self.group_share(p, self.place.me, e, self.place.me, self.place.home(e)).wait_send()


B_MIX, B_ENDMIX, B_FOLD, B_SMALL = 0, 3, 6, 11
B_ROWS = 14


def back_kernel(
    experts,
    counts,
    att_grad,
    mixed_grad,
    heads_ref,
    stats_ref,
    attended_ref,
    x_ref,
    gain_ref,
    qkv_w,
    out_w,
    mixed_ref,
    half_ref,
    key_col,
    router_part,
    gain2_part,
    out_ref,
    x_grad,
    whole_ref,
    small_out,
    low_ref,
    lines,
    head_grad,
    proj_grad,
    chip_recv,
    home_send,
    back,
    hot_ref,
    total,
    fold_send,
    fold_recv,
    fold_kept,
    fold_chip_send,
    fold_chip_recv,
    normed_ref,
    pair_send,
    pair_recv,
    pair_kept,
    group_send,
    group_recv,
    group_total,
    small_ref,
    small_near,
    small_far,
    small_pair,
    small_group,
    small_steps,
    sent,
    came,
    pair_sent,
    pair_came,
    group_sent,
    group_came,
):
    rows, width = att_grad.shape
    images = counts.shape[0]
    patches = rows // images
    head_cols = attended_ref.shape[1]
    heads = head_cols // HEAD_DIM
    scale = HEAD_DIM ** (-0.5)
    cap = back.shape[1]
    tile = patches // 2
    pieces = heads + 1
    place = Place(experts)
    move = mover(sent, came)
    me = place.me
    wide = WideSum(
        place,
        (mover(pair_sent, pair_came), mover(group_sent, group_came)),
        (None, None, None),
        pair_send,
        pair_recv,
        pair_kept,
        group_send,
        group_recv,
        whole_ref,
    )
    wide.total = group_total
    fold = Fold(
        place,
        move,
        B_FOLD,
        fold_send,
        fold_recv,
        fold_kept,
        fold_chip_send,
        fold_chip_recv,
        normed_ref,
    )
    place.greet((wide.pair,))

    half = half_ref.shape[1]
    side = width // 2
    mine = place.part(place.core, half, 16)
    other = place.part(1 - place.core, half, 16)
    side_mine = place.part(place.chip, side, 128)
    side_other = place.part(1 - place.chip, side, 128)

    def mix_chip(s):
        return move(half_ref.at[s, :, side_other], chip_recv.at[s], B_MIX, s, s, place.across)

    def mix_home(s, landed):
        return move(
            home_send.at[s], back.at[landed, mine, :], B_MIX + 1, s, landed, place.home(s)
        )

    def mix_near(e, part):
        ref = back.at[e, part, :]
        return move(ref, ref, B_MIX + 2, e, e, place.near)

    @pl.loop(0, experts)
    def _(i):
        mix_chip(place.take(experts - 1 - i)).start()

    def mix_back(i):
        s = place.take(experts - 1 - i)
        mix_chip(s).wait_recv()
        piece = (
            half_ref[s, :, side_mine].astype(jnp.float32) + chip_recv[s].astype(jnp.float32)
        ).astype(jnp.bfloat16)

        @pl.when(s == me)
        def _():
            back[me, mine, :] = piece

        @pl.when(s != me)
        def _():
            home_send[s] = piece
            mix_home(s, me).start()

    def mix_relay(i):
        e = place.take(i)

        @pl.when(e != me)
        def _():
            mix_home(e, e).wait_recv()

        mix_near(e, mine).start()

    my_rows = place.part(place.core, rows // 2, 16)

    def mix_sum(i):
        e = place.take(i)

        @pl.loop(0, 2)
        def _(m):
            part = pl.ds(pl.multiple_of((place.core * 2 + m) * (rows // 4), 16), rows // 4)
            put = pl.ds(pl.multiple_of(m * (rows // 4), 16), rows // 4)
            slot = e * cap + lax.broadcasted_iota(jnp.int32, (rows // 4, cap), 1)
            hit = (key_col[part, 0:1] == slot) | (key_col[part, 1:2] == slot)
            hot_ref[put, :] = jnp.where(hit, 1.0, 0.0).astype(jnp.bfloat16)

        mix_near(e, other).wait_recv()
        total[...] += dot_rows(hot_ref[...], back[e])

    ends = Quarters(place, move, B_ENDMIX, 0, out_ref)

    small_sizes = small_ref.shape
    small_ref[...] = jnp.zeros_like(small_ref)
    small_ref[0:experts] = router_part[0:experts]
    small_ref[experts : experts + 1] = gain2_part[...]

    def small_move(step):
        src, dst, where = (
            (small_ref, small_near, place.near),
            (small_steps.at[0], small_far, place.across),
            (small_steps.at[1], small_pair, wide.pair),
        )[step]
        return move(src, dst, B_SMALL, step, step, where)

    def small_home(e, landed):
        return move(
            small_steps.at[2], small_group.at[landed], B_SMALL + 1, e, landed, place.home(e)
        )

    share_row = lax.broadcasted_iota(jnp.int32, small_sizes, 0) == experts + 1

    def small_second():
        small_move(0).wait_recv()
        small_steps[0] = small_ref[...] + jnp.where(share_row, small_near[...], 0.0)
        small_move(1).start()

    def small_third():
        small_move(1).wait_recv()
        small_steps[1] = small_steps[0] + jnp.where(share_row, small_far[...], 0.0)
        small_move(2).start()

    def small_fourth():
        small_move(2).wait_recv()
        small_steps[2] = small_steps[1] + small_pair[...]
        small_group[me] = small_steps[2]

        @pl.loop(1, experts)
        def _(i):
            small_home(place.send_to(i), me).start()

    def small_last():
        @pl.loop(1, experts)
        def _(i):
            s = place.take(i)
            small_home(s, s).wait_recv()

        small_out[...] = jnp.zeros_like(small_out)

        @pl.loop(0, experts)
        def _(e):
            small_out[...] += small_group[e]

    real = pair_kept.shape[1]

    def contract(left, right):
        return lax.dot_general(
            left, right, (((0,), (0,)), ((), ())), preferred_element_type=jnp.float32
        )

    def zero_pads():
        if pair_send.shape[1] > real:
            pair_send[:, real:] = jnp.zeros_like(pair_send[:, real:])
            group_send[:, real:] = jnp.zeros_like(group_send[:, real:])

    zero_pads()
    product = contract(attended_ref[...], att_grad[...])
    wide.first(0, (product[0:real], product[real:]))

    @pl.loop(0, rows // tile)
    def _(t):
        part = pl.ds(pl.multiple_of(t * tile, 16), tile)
        normed, _, _ = normalize(x_ref[part, :].astype(jnp.float32), gain_ref[0:1, :])
        low_ref[part, :] = normed.astype(jnp.bfloat16)
        block = dot_cols(att_grad[part, :], out_w[...]).astype(jnp.bfloat16)
        for h in range(heads):
            head_grad[h, part, :] = block[:, h * HEAD_DIM : (h + 1) * HEAD_DIM]

    @pl.loop(0, images)
    def _(image):
        part = pl.ds(pl.multiple_of(image * patches, 16), patches)
        padded = round_up(patches, 128)
        column = jnp.concatenate(
            [stats_ref[part, :], jnp.zeros((padded - patches, 128), jnp.float32)], 0
        )
        lines[image] = jnp.transpose(column)[0:8, :]

    def attend_back(image, h):
        part = pl.ds(pl.multiple_of(image * patches, 16), patches)
        query = heads_ref[0, h, part, :]
        key_rows = heads_ref[1, h, part, :]
        out_grad = head_grad[h, part, :]
        live = lax.broadcasted_iota(jnp.int32, (patches, 1), 0) < counts[image]
        line = lines[image, pl.ds(h, 1), 0:patches]
        scores = jnp.where(live, dot_cols(key_rows, query) * scale, MASKED_SCORE)
        probs = jnp.exp(scores - line)
        change = dot_cols(heads_ref[2, h, part, :], out_grad)
        delta = jnp.sum(probs * change, 0, keepdims=True)
        score_grad = (scale * probs * (change - delta)).astype(jnp.bfloat16)
        proj_grad[2, h, part, :] = dot_rows(probs.astype(jnp.bfloat16), out_grad).astype(
            jnp.bfloat16
        )
        proj_grad[1, h, part, :] = dot_rows(score_grad, query).astype(jnp.bfloat16)
        proj_grad[0, h, part, :] = contract(score_grad, key_rows).astype(jnp.bfloat16)

    def piece(h):
        grads = jnp.concatenate([proj_grad[i, h] for i in range(3)], 1)
        product = contract(grads, low_ref[...])
        wide.first(h + 1, (product[0:real], product[real:]))

    def fold_first(image):
        for mine_too in (False, True):
            part = fold.rows(image, place.core if mine_too else 1 - place.core)
            normed_part = jnp.zeros((tile, width), jnp.float32)
            for i in range(3):
                grads = jnp.concatenate([proj_grad[i, h, part, :] for h in range(heads)], 1)
                normed_part += dot_cols(grads, qkv_w[i])
            if mine_too:
                fold_kept[image] = normed_part
            else:
                fold_send[image] = normed_part.astype(jnp.bfloat16)
                fold.core_move(image).start()
            _, hat, _ = normalize(x_ref[part, :].astype(jnp.float32), gain_ref[0:1, :])
            small_ref[experts + 1 : experts + 2] += jnp.sum(normed_part * hat, 0, keepdims=True)

    def mix_backs(lo, hi):
        @pl.loop(lo, hi)
        def _(i):
            mix_back(i)

    total[...] = jnp.zeros_like(total)

    def mix_tail():
        @pl.loop(0, experts)
        def _(i):
            mix_relay(i)

        @pl.loop(0, experts)
        def _(i):
            mix_sum(i)

        out_ref[ends.rows, ends.mine] = (mixed_ref[my_rows, side_mine] + total[...]).astype(
            jnp.bfloat16
        )
        ends.start()

    mid = experts // 2
    agenda = {
        0: [lambda: wide.second(0)],
        1: [lambda: wide.third(0), lambda: mix_backs(0, mid)],
        2: [lambda: fold_first(0), lambda: wide.fourth(0), lambda: mix_backs(mid, experts)],
        3: [lambda: piece(0), lambda: fold.second(0)],
        4: [lambda: piece(1), lambda: wide.second(1)],
        5: [lambda: piece(2), lambda: wide.second(2), lambda: fold.third(0)],
    }

    @pl.loop(0, images * heads)
    def _(step):
        attend_back(step // heads, lax.rem(step, heads))
        for at, todo in agenda.items():

            @pl.when(step == at)
            def _():
                for act in todo:
                    act()

    fold_first(1)
    small_move(0).start()
    wide.third(1)
    wide.second(3)
    small_second()
    fold.second(1)
    wide.third(2)
    small_third()
    fold.relay(0)
    mix_tail()
    small_fourth()
    wide.third(3)
    wide.fourth(1)
    fold.third(1)
    wide.fourth(2)
    ends.relay()
    fold.ready(0)

    def input_rows(image):
        @pl.loop(2 * image, 2 * image + 2)
        def _(t):
            part = pl.ds(pl.multiple_of(t * tile, 16), tile)
            _, hat, scaled = normalize(x_ref[part, :].astype(jnp.float32), gain_ref[0:1, :])
            grad = normed_ref[part, :].astype(jnp.float32) * gain_ref[0:1, :]
            inner = (
                grad - jnp.mean(grad, -1, keepdims=True) - hat * jnp.mean(grad * hat, -1, keepdims=True)
            )
            x_grad[part, :] = mixed_grad[part, :] + scaled * inner

    input_rows(0)
    wide.fourth(3)
    fold.relay(1)
    small_last()
    fold.ready(1)
    input_rows(1)
    ends.ready()
    for p in range(pieces):
        wide.ready(p)
    wide.finish()
    fold.finish(images)
    ends.finish()
    for step in range(3):
        small_move(step).wait_send()

    @pl.loop(0, experts)
    def _(i):
        s = place.take(i)
        mix_chip(s).wait_send()
        mix_near(s, mine).wait_send()

        @pl.when(i > 0)
        def _():
            mix_home(s, me).wait_send()
            small_home(s, me).wait_send()


def back(
    counts,
    att_grad,
    mixed_grad,
    head_rows,
    stats,
    attended,
    x,
    gain,
    qkv_w,
    out_w,
    mixed,
    halves,
    keys,
    router_part,
    gain2_part,
):
    rows, width = x.shape
    experts, half = halves.shape[:2]
    cap, side = 2 * half, width // 2
    images = counts.shape[0]
    heads = head_rows.shape[1]
    head_cols = out_w.shape[0]
    pieces = heads + 1
    real = head_cols // 2
    split = max(experts // 2, 1)
    chunk_rows = round_up(-(-real // split), 16)
    padded = chunk_rows * split
    part_rows = rows // images // 2
    small = round_up(experts + 2, 8)
    bf16, f32 = jnp.bfloat16, jnp.float32
    vmem = pl.BlockSpec(memory_space=pltpu.VMEM)
    small_block = pltpu.VMEM((small, width), f32)
    dma = pltpu.SemaphoreType.DMA
    table = max(experts, images, 3)
    return pl.pallas_call(
        functools.partial(back_kernel, experts),
        out_shape=[
            jax.ShapeDtypeStruct((rows, width), bf16),
            jax.ShapeDtypeStruct((rows, width), f32),
            jax.ShapeDtypeStruct((pieces, 2, padded, width), bf16),
            jax.ShapeDtypeStruct((small, width), f32),
        ],
        in_specs=[pl.BlockSpec(memory_space=pltpu.SMEM)] + [vmem] * 14,
        out_specs=[vmem] * 4,
        scratch_shapes=[
            pltpu.VMEM((rows, width), bf16),
            pltpu.VMEM((images, 8, round_up(rows // images, 128)), f32),
            pltpu.VMEM((heads, rows, HEAD_DIM), bf16),
            pltpu.VMEM((3, heads, rows, HEAD_DIM), bf16),
            pltpu.VMEM((experts, half, side), bf16),
            pltpu.VMEM((experts, half, side), bf16),
            pltpu.VMEM((experts, cap, side), bf16),
            pltpu.VMEM((rows // 2, cap), bf16),
            pltpu.VMEM((rows // 2, side), f32),
            pltpu.VMEM((images, part_rows, width), bf16),
            pltpu.VMEM((images, part_rows, width), bf16),
            pltpu.VMEM((images, part_rows, width), f32),
            pltpu.VMEM((images, part_rows, side), bf16),
            pltpu.VMEM((images, part_rows, side), bf16),
            pltpu.VMEM((rows, width), bf16),
            pltpu.VMEM((pieces, padded, width), bf16),
            pltpu.VMEM((pieces, padded, width), bf16),
            pltpu.VMEM((pieces, real, width), f32),
            pltpu.VMEM((pieces, padded, width), bf16),
            pltpu.VMEM((pieces, experts, chunk_rows, side), bf16),
            pltpu.VMEM((chunk_rows, side), f32),
            small_block,
            small_block,
            small_block,
            small_block,
            pltpu.VMEM((experts, small, width), f32),
            pltpu.VMEM((3, small, width), f32),
            dma((B_ROWS, table)),
            dma((B_ROWS, table)),
            dma((2, pieces)),
            dma((2, pieces)),
            dma((2 * pieces, experts)),
            dma((2 * pieces, experts)),
        ],
        compiler_params=pltpu.CompilerParams(
            collective_id=3, has_side_effects=True, vmem_limit_bytes=VMEM_BYTES
        ),
    )(
        counts,
        att_grad,
        mixed_grad,
        head_rows,
        stats,
        attended,
        x,
        gain,
        qkv_w,
        out_w,
        mixed,
        halves,
        keys,
        router_part,
        gain2_part,
    )


def swapped(x, axis, distance):
    return lax.ppermute(x, axis, [(i, i ^ 1 << distance) for i in range(lax.axis_size(axis))])


def body(
    inputs,
    counts,
    routes,
    slot_ids,
    norm_first,
    attn_in,
    attn_out,
    norm_second,
    router,
    expert_in,
    expert_out,
    cotangent,
):
    rows_dev, feat_width = inputs.shape
    experts = router.shape[1]
    half_slots = (105 * rows_dev + 100 * experts - 1) // (100 * experts)
    capacity = 2 * half_slots
    head_cols = attn_out.shape[0]
    local_heads = head_cols // HEAD_DIM
    slot_pad = round_up(capacity, 32)
    slot_keys = jnp.where(slot_ids < capacity, routes * slot_pad + slot_ids, -1)
    gain1, gain2 = norm_first[None], norm_second[None]
    router_pad = jnp.pad(router, ((0, 0), (0, 128 - experts)))
    sent_cots, head_rows, attended, stats, mixed, low_second, prob, gates = front(
        counts,
        inputs,
        cotangent,
        slot_keys.T,
        routes,
        gain1,
        attn_in,
        attn_out,
        gain2,
        router_pad,
        experts,
        slot_pad,
    )
    halves, received, hidden, pre_grad, mixed_grad, att_grad, router_part, gain_part = middle(
        counts,
        low_second,
        cotangent,
        slot_keys,
        gates,
        expert_in[0],
        expert_out[0],
        sent_cots,
        mixed,
        prob,
        routes,
        gain2,
        router_pad,
        experts,
    )
    copy_out_grad = jnp.einsum(
        "scf,scd->fd", hidden, sent_cots, preferred_element_type=jnp.float32
    )[None]
    copy_in_grad = jnp.einsum(
        "scd,scf->df", received, pre_grad, preferred_element_type=jnp.float32
    )[None]
    other_in, other_out = (
        swapped(copy_in_grad.astype(jnp.bfloat16), "wide", 0).astype(copy_in_grad.dtype),
        swapped(copy_out_grad.astype(jnp.bfloat16), "wide", 0).astype(copy_out_grad.dtype),
    )
    output, input_grad, whole, small = back(
        counts,
        att_grad,
        mixed_grad,
        head_rows,
        stats,
        attended,
        inputs,
        gain1,
        attn_in,
        attn_out,
        mixed,
        halves,
        slot_keys,
        router_part,
        gain_part,
    )
    expert_in_grad = copy_in_grad + other_in
    expert_out_grad = copy_out_grad + other_out
    real = head_cols // 2
    pieces = whole[:, :, :real].reshape(-1, head_cols, feat_width).astype(jnp.float32)
    attn_in_grad = (
        pieces[1:]
        .reshape(local_heads, 3, HEAD_DIM, feat_width)
        .transpose(1, 3, 0, 2)
        .reshape(3, feat_width, head_cols)
    )
    return (
        output,
        input_grad,
        small[experts + 1],
        attn_in_grad,
        pieces[0],
        small[experts],
        small[:experts].T,
        expert_in_grad,
        expert_out_grad,
    )


def solution(mesh):
    in_specs = (
        P("wide", None),
        P("wide"),
        P("wide", None),
        P("wide", None),
        P(),
        P(None, None, "narrow"),
        P("narrow", None),
        P(),
        P(),
        P("wide", None, "narrow"),
        P("wide", "narrow", None),
        P("wide", None),
    )
    out_specs = (
        P("wide", None),
        P("wide", None),
        P(),
        P(None, None, "narrow"),
        P("narrow", None),
        P(),
        P(),
        P("wide", None, "narrow"),
        P("wide", "narrow", None),
    )
    return jax.shard_map(body, mesh=mesh, in_specs=in_specs, out_specs=out_specs, check_vma=False)
```

```python
import functools

import jax
import jax.numpy as jnp
from jax import lax
from jax.experimental import pallas as pl
from jax.experimental.pallas import tpu as pltpu
from jax.sharding import PartitionSpec as P

HEAD_DIM = 64
NORM_EPSILON = 1e-06
MASKED_SCORE = -1e30
BY_MESH = pl.DeviceIdType.MESH
VMEM_BYTES = 64 * 1024 * 1024 - 65536


def round_up(value, multiple):
    return -(-value // multiple) * multiple


def dot_rows(left, right):
    return lax.dot_general(left, right, (((1,), (0,)), ((), ())), preferred_element_type=jnp.float32)


def dot_cols(left, right):
    return lax.dot_general(left, right, (((1,), (1,)), ((), ())), preferred_element_type=jnp.float32)


def normal_parts(values):
    t = 1.0 / (1.0 + (0.3275911 * 0.7071067811865476) * jnp.abs(values))
    bell = jnp.exp(-0.5 * values * values)
    poly = t * (
        0.254829592
        + t * (-0.284496736 + t * (1.421413741 + t * (-1.453152027 + t * 1.061405429)))
    )
    tail = 0.5 * poly * bell
    return jnp.where(values >= 0.0, 1.0 - tail, tail), 0.3989422804014327 * values * bell


def normalize(values, gain):
    center = values - jnp.mean(values, -1, keepdims=True)
    scaled = lax.rsqrt(jnp.mean(center * center, -1, keepdims=True) + NORM_EPSILON)
    normed = center * scaled
    return normed * gain, normed, scaled


class Place:
    def __init__(self, experts):
        self.experts = experts
        self.n = lax.axis_index("narrow")
        self.w = lax.axis_index("wide")
        self.core = lax.rem(self.n, 2)
        self.chip = self.n // 2
        self.me = self.w // 2
        self.parity = lax.rem(self.w, 2)
        self.near_n = self.n + 1 - 2 * self.core
        self.across_n = lax.rem(self.n + 2, 4)
        self.near = {"narrow": self.near_n, "wide": self.w}
        self.across = {"narrow": self.across_n, "wide": self.w}

    def home(self, e):
        return {"narrow": self.n, "wide": 2 * e + self.parity}

    def send_to(self, i):
        far_first = jnp.where(2 * self.me >= self.experts, i, self.experts - i)
        return lax.rem(self.me + far_first, self.experts)

    def take(self, i):
        near_first = jnp.where(2 * self.me < self.experts, i, self.experts - i)
        return lax.rem(self.me + near_first, self.experts)

    def part(self, which, size, align):
        return pl.ds(pl.multiple_of(which * size, align), size)

    def greet(self, others=()):
        barrier = pltpu.get_barrier_semaphore()
        for peer in (self.near, self.across, *others):
            pl.semaphore_signal(barrier, inc=1, device_id=peer, device_id_type=BY_MESH)

        @pl.loop(1, self.experts)
        def _(i):
            pl.semaphore_signal(
                barrier, inc=1, device_id=self.home(self.send_to(i)), device_id_type=BY_MESH
            )

        pl.semaphore_wait(barrier, self.experts + 1 + len(others))


def mover(sent, came):
    def move(src, dst, row, sent_at, came_at, where):
        return pltpu.make_async_remote_copy(
            src_ref=src,
            dst_ref=dst,
            send_sem=sent.at[row, sent_at],
            recv_sem=came.at[row, came_at],
            device_id=where,
            device_id_type=BY_MESH,
        )

    return move


class Dispatch:
    def __init__(self, place, move, base, send, landing):
        self.place, self.move, self.base = place, move, base
        self.send, self.landing = send, landing
        cap, width = landing.shape[1:]
        self.cap, self.half, self.side = cap, cap // 2, width // 2
        self.mine = place.part(place.core, self.half, 16)
        self.other = place.part(1 - place.core, self.half, 16)
        self.side_mine = place.part(place.chip, self.side, 128)
        self.side_other = place.part(1 - place.chip, self.side, 128)

    def z_copy(self, e, landed):
        return self.move(
            self.send.at[e],
            self.landing.at[landed, self.mine, self.side_mine],
            self.base,
            e,
            landed,
            self.place.home(e),
        )

    def build(self, i, key_row, source):
        e = self.place.send_to(i)
        hot = self.hot(e, self.place.core, key_row)
        self.send[e] = dot_rows(hot, source[:, self.side_mine]).astype(jnp.bfloat16)
        self.z_copy(e, self.place.me).start()

    def hot(self, e, part, key_row):
        slot = e * self.cap + part * self.half
        slot = slot + lax.broadcasted_iota(jnp.int32, (self.half, key_row.shape[1]), 0)
        hit = (key_row[0:1, :] == slot) | (key_row[1:2, :] == slot)
        return jnp.where(hit, 1.0, 0.0).astype(jnp.bfloat16)

    def build_own(self, key_row, source):
        @pl.loop(0, 2)
        def _(m):
            hot = self.hot(self.place.me, m, key_row)
            part = pl.ds(pl.multiple_of(m * self.half, 16), self.half)
            self.landing[self.place.me, part, :] = dot_rows(hot, source[...]).astype(jnp.bfloat16)

    def spread(self, step, s):
        rows, cols, where = (
            (self.mine, self.side_mine, self.place.across),
            (self.mine, self.side_mine, self.place.near),
            (self.mine, self.side_other, self.place.near),
        )[step]
        ref = self.landing.at[s, rows, cols]
        return self.move(ref, ref, self.base + 1 + step, s, s, where)

    def stage_a(self, i):
        self.landed(i)
        self.relay(i)

    def stage_b(self, i):
        s = self.place.take(i)
        self.spread(0, s).wait_recv()
        self.spread(2, s).start()

    def stage_c(self, i):
        s = self.place.take(i)
        self.spread(1, s).wait_recv()
        self.spread(2, s).wait_recv()

    def landed(self, i):
        s = self.place.take(i)
        self.z_copy(s, s).wait_recv()

    def relay(self, i):
        s = self.place.take(i)
        self.spread(0, s).start()
        self.spread(1, s).start()

    def finish(self, lo, hi, sends=True):
        @pl.loop(lo, hi)
        def _(i):
            s = self.place.take(i)
            for step in range(3):
                self.spread(step, s).wait_send()

        if sends:

            @pl.loop(1, self.place.experts)
            def _(i):
                self.z_copy(self.place.take(i), self.place.me).wait_send()


FRONT_OWN, FRONT_FAR, FRONT_CHIP, FRONT_GATES = 4, 5, 6, 7
FRONT_ROWS = 8
LATE = 1


def front_kernel(
    experts,
    counts,
    x_ref,
    cot_ref,
    key_row,
    key_col,
    routes_col,
    gain1_ref,
    qkv_w,
    out_w,
    gain2_ref,
    router_ref,
    cots_ref,
    heads_hbm,
    attended_hbm,
    stats_hbm,
    mixed_hbm,
    low2_hbm,
    prob_hbm,
    gate_hbm,
    gate_recv,
    heads_ref,
    attended_ref,
    stats_ref,
    mixed_ref,
    low2_ref,
    prob_ref,
    gate_ref,
    cot_send,
    gate_send,
    gather,
    out_all,
    key_wide,
    gate_wide,
    loads,
    sent,
    came,
):
    rows, width = x_ref.shape
    images = counts.shape[0]
    patches = rows // images
    head_cols = out_w.shape[0]
    heads = head_cols // HEAD_DIM
    scale = HEAD_DIM ** (-0.5)
    place = Place(experts)
    move = mover(sent, came)
    cots = Dispatch(place, move, 0, cot_send, cots_ref)
    place.greet()

    def share(ref, at):
        def copy(step):
            piece = ref(place.across_n if step == 2 else place.n)
            where = place.across if step == 0 else place.near
            row = (FRONT_CHIP, FRONT_OWN, FRONT_FAR)[step]
            return move(piece, piece, row, at, at, where)

        return copy

    out_share = share(lambda n: out_all.at[n], images)
    out_all[place.n] = out_w[...]
    out_share(0).start()
    out_share(1).start()

    @pl.loop(1, experts)
    def _(i):
        cots.build(i, key_row, cot_ref)

    tile = patches // 2

    @pl.loop(0, rows // tile)
    def _(t):
        part = pl.ds(pl.multiple_of(t * tile, 16), tile)
        normed, _, _ = normalize(x_ref[part, :].astype(jnp.float32), gain1_ref[0:1, :])
        low = normed.astype(jnp.bfloat16)
        for i in range(3):
            block = dot_rows(low, qkv_w[i]).astype(jnp.bfloat16)
            for h in range(heads):
                heads_ref[i, h, part, :] = block[:, h * HEAD_DIM : (h + 1) * HEAD_DIM]

    outs = [
        pltpu.make_async_copy(src, dst, loads.at[at])
        for at, (src, dst) in enumerate(
            (
                (heads_ref, heads_hbm),
                (attended_ref, attended_hbm),
                (stats_ref, stats_hbm),
                (mixed_ref, mixed_hbm),
                (low2_ref, low2_hbm),
                (prob_ref, prob_hbm),
                (gate_ref, gate_hbm),
            )
        )
    ]
    outs[0].start()
    stats_ref[...] = jnp.zeros_like(stats_ref)

    def attend(image):
        keys_at = pl.ds(image * patches, patches)
        live = lax.broadcasted_iota(jnp.int32, (1, patches), 1) < counts[image]
        for h in range(heads):
            key_rows = heads_ref[1, h, keys_at, :]
            value_rows = heads_ref[2, h, keys_at, :]
            for t in range(patches // tile):
                part = pl.ds(image * patches + t * tile, tile)
                scores = dot_cols(heads_ref[0, h, part, :], key_rows) * scale
                scores = jnp.where(live, scores, MASKED_SCORE)
                top = jnp.max(scores, -1, keepdims=True)
                weights = jnp.exp(scores - top)
                total = jnp.sum(weights, -1, keepdims=True)
                probs = (weights * (1.0 / total)).astype(jnp.bfloat16)
                block = dot_rows(probs, value_rows).astype(jnp.bfloat16)
                at = t * head_cols + h * HEAD_DIM
                gather[place.n, pl.ds(image * tile, tile), at : at + HEAD_DIM] = block
                attended_ref[part, h * HEAD_DIM : (h + 1) * HEAD_DIM] = block
                stats_ref[part, h : h + 1] = top + jnp.log(total)

    shares = [
        share(lambda n, image=image: gather.at[n, pl.ds(image * tile, tile), :], image)
        for image in range(images)
    ]
    for image in range(images):
        attend(image)
        shares[image](0).start()
        shares[image](1).start()
    outs[1].start()
    outs[2].start()
    out_share(0).wait_recv()
    out_share(2).start()
    cots.build_own(key_row, cot_ref)

    @pl.loop(1, experts - LATE)
    def _(i):
        cots.stage_a(i)

    out_share(1).wait_recv()
    out_share(2).wait_recv()

    def finish(image):
        shares[image](0).wait_recv()
        shares[image](2).start()
        shares[image](1).wait_recv()
        shares[image](2).wait_recv()

        for t in range(2):
            part = pl.ds(image * patches + t * tile, tile)
            cols = slice(t * head_cols, (t + 1) * head_cols)
            attention = dot_rows(gather[0, pl.ds(image * tile, tile), cols], out_all[0])
            for n in range(1, 4):
                attention += dot_rows(gather[n, pl.ds(image * tile, tile), cols], out_all[n])
            offset = t * tile + lax.broadcasted_iota(jnp.int32, (tile, 1), 0)
            mixed = x_ref[part, :].astype(jnp.float32) + jnp.where(
                offset < counts[image], attention, 0.0
            )
            mixed_ref[part, :] = mixed
            normed, _, _ = normalize(mixed, gain2_ref[0:1, :])
            low = normed.astype(jnp.bfloat16)
            low2_ref[part, :] = low
            lane = lax.broadcasted_iota(jnp.int32, (tile, 128), 1)
            logits = jnp.where(lane < experts, dot_rows(low, router_ref[...]), MASKED_SCORE)
            powers = jnp.exp(logits - jnp.max(logits, -1, keepdims=True))
            prob = powers / jnp.sum(powers, -1, keepdims=True)
            prob_ref[part, :] = prob
            picked = [
                jnp.sum(jnp.where(lane == routes_col[part, k : k + 1], prob, 0.0), 1, keepdims=True)
                for k in range(2)
            ]
            both = picked[0] + picked[1]
            gate_ref[part, :] = jnp.where(
                lane == 0, picked[0] / both, jnp.where(lane == 1, picked[1] / both, both)
            )

    for image in range(images):
        finish(image)
    for out in outs[3:]:
        out.start()

    wide_cap = gate_send.shape[2]

    def gate_copy(e, landed):
        return move(gate_send.at[e], gate_recv.at[landed], FRONT_GATES, e, landed, place.home(e))

    for k in range(2):
        key_wide[k] = jnp.broadcast_to(key_col[:, k : k + 1], (rows, 128))
        gate_wide[k] = jnp.broadcast_to(gate_ref[:, k : k + 1], (rows, 128))

    @pl.loop(0, experts)
    def _(i):
        e = place.send_to(i + 1)

        @pl.loop(0, wide_cap // 128)
        def _(j):
            lanes = pl.ds(pl.multiple_of(j * 128, 128), 128)
            slot = e * cots.cap + j * 128 + lax.broadcasted_iota(jnp.int32, (rows, 128), 1)
            picked = jnp.where(key_wide[0] == slot, gate_wide[0], 0.0) + jnp.where(
                key_wide[1] == slot, gate_wide[1], 0.0
            )
            gate_send[e, :, lanes] = jnp.broadcast_to(jnp.sum(picked, 0, keepdims=True), (8, 128))

        @pl.when(e == place.me)
        def _():
            gate_recv[place.me] = gate_send[place.me]

        @pl.when(e != place.me)
        def _():
            gate_copy(e, place.me).start()

    @pl.loop(1, experts - LATE)
    def _(i):
        cots.stage_b(i)

    @pl.loop(1, experts - LATE)
    def _(i):
        cots.stage_c(i)

    @pl.loop(1, experts)
    def _(i):
        s = place.take(i)
        gate_copy(s, s).wait_recv()
        gate_copy(s, place.me).wait_send()

    @pl.loop(experts - LATE, experts)
    def _(i):
        cots.landed(i)

    cots.finish(1, experts - LATE)
    for out in outs:
        out.wait()
    for copy in (out_share, *shares):
        for step in range(3):
            copy(step).wait_send()


def front(counts, x, cot, keys, routes, gain1, qkv_w, out_w, gain2, router, experts, cap):
    rows, width = x.shape
    head_cols = out_w.shape[0]
    heads = head_cols // HEAD_DIM
    images = counts.shape[0]
    bf16, f32 = jnp.bfloat16, jnp.float32
    vmem = pl.BlockSpec(memory_space=pltpu.VMEM)
    hbm = pl.BlockSpec(memory_space=pl.ANY)
    slots = max(experts, images + 1)
    wide_cap = round_up(cap, 128)
    return pl.pallas_call(
        functools.partial(front_kernel, experts),
        out_shape=[
            jax.ShapeDtypeStruct((experts, cap, width), bf16),
            jax.ShapeDtypeStruct((3, heads, rows, HEAD_DIM), bf16),
            jax.ShapeDtypeStruct((rows, head_cols), bf16),
            jax.ShapeDtypeStruct((rows, 128), f32),
            jax.ShapeDtypeStruct((rows, width), f32),
            jax.ShapeDtypeStruct((rows, width), bf16),
            jax.ShapeDtypeStruct((rows, 128), f32),
            jax.ShapeDtypeStruct((rows, 128), f32),
            jax.ShapeDtypeStruct((experts, 8, wide_cap), f32),
        ],
        in_specs=[pl.BlockSpec(memory_space=pltpu.SMEM)] + [vmem] * 10,
        out_specs=[vmem] + [hbm] * 7 + [vmem],
        scratch_shapes=[
            pltpu.VMEM((3, heads, rows, HEAD_DIM), bf16),
            pltpu.VMEM((rows, head_cols), bf16),
            pltpu.VMEM((rows, 128), f32),
            pltpu.VMEM((rows, width), f32),
            pltpu.VMEM((rows, width), bf16),
            pltpu.VMEM((rows, 128), f32),
            pltpu.VMEM((rows, 128), f32),
            pltpu.VMEM((experts, cap // 2, width // 2), bf16),
            pltpu.VMEM((experts, 8, wide_cap), f32),
            pltpu.VMEM((4, rows // 2, 2 * head_cols), bf16),
            pltpu.VMEM((4, head_cols, width), bf16),
            pltpu.VMEM((2, rows, 128), jnp.int32),
            pltpu.VMEM((2, rows, 128), f32),
            pltpu.SemaphoreType.DMA((7,)),
            pltpu.SemaphoreType.DMA((FRONT_ROWS, slots)),
            pltpu.SemaphoreType.DMA((FRONT_ROWS, slots)),
        ],
        compiler_params=pltpu.CompilerParams(
            collective_id=2, has_side_effects=True, vmem_limit_bytes=VMEM_BYTES
        ),
    )(counts, x, cot, keys.T, keys, routes, gain1, qkv_w, out_w, gain2, router)


class Return:
    def __init__(self, place, move, base, core_send, core_recv, kept, chip_send, chip_recv, back):
        self.place, self.move, self.base = place, move, base
        self.core_send, self.core_recv, self.kept = core_send, core_recv, kept
        self.chip_send, self.chip_recv, self.back = chip_send, chip_recv, back
        self.half, self.side = chip_send.shape[1:]
        self.mine = place.part(place.core, self.half, 16)
        self.other = place.part(1 - place.core, self.half, 16)
        self.side_mine = place.part(place.chip, self.side, 128)
        self.side_other = place.part(1 - place.chip, self.side, 128)

    def rows(self, s):
        return pl.ds(pl.multiple_of(s * self.half, 16), self.half)

    def core_move(self, s):
        return self.move(
            self.core_send.at[s], self.core_recv.at[s], self.base, s, s, self.place.near
        )

    def chip_move(self, s):
        return self.move(
            self.chip_send.at[s], self.chip_recv.at[s], self.base + 1, s, s, self.place.across
        )

    def home_move(self, s, landed):
        return self.move(
            self.core_send.at[s, :, pl.ds(0, self.side)],
            self.back.at[landed, self.mine, :],
            self.base + 2,
            s,
            landed,
            self.place.home(s),
        )

    def pair_move(self, e, part):
        ref = self.back.at[e, part, :]
        return self.move(ref, ref, self.base + 3, e, e, self.place.near)

    def first(self, s, product):
        self.core_send[s] = product(self.other).astype(jnp.bfloat16)
        self.core_move(s).start()
        self.kept[self.rows(s), :] = product(self.mine)

    def second(self, s):
        self.core_move(s).wait_recv()
        self.chip_send[s] = (
            self.kept[self.rows(s), self.side_other]
            + self.core_recv[s, :, self.side_other].astype(jnp.float32)
        ).astype(jnp.bfloat16)
        self.chip_move(s).start()

    def third(self, s):
        self.chip_move(s).wait_recv()
        self.core_move(s).wait_send()
        piece = (
            self.kept[self.rows(s), self.side_mine]
            + self.core_recv[s, :, self.side_mine].astype(jnp.float32)
            + self.chip_recv[s].astype(jnp.float32)
        ).astype(jnp.bfloat16)

        @pl.when(s == self.place.me)
        def _():
            self.back[self.place.me, self.mine, :] = piece

        @pl.when(s != self.place.me)
        def _():
            self.core_send[s, :, 0 : self.side] = piece
            self.home_move(s, self.place.me).start()

    def fourth(self, i):
        e = self.place.take(i)

        @pl.when(e != self.place.me)
        def _():
            self.home_move(e, e).wait_recv()

        self.pair_move(e, self.mine).start()

    def ready(self, i):
        self.pair_move(self.place.take(i), self.other).wait_recv()

    def finish(self):
        @pl.loop(0, self.place.experts)
        def _(i):
            s = self.place.take(i)
            self.chip_move(s).wait_send()
            self.pair_move(s, self.mine).wait_send()

            @pl.when(i > 0)
            def _():
                self.home_move(s, self.place.me).wait_send()


class Quarters:
    def __init__(self, place, move, base, at, ref):
        self.place, self.move, self.base, self.at, self.ref = place, move, base, at, ref
        rows, width = ref.shape
        self.rows = place.part(place.core, rows // 2, 16)
        self.mine = place.part(place.chip, width // 2, 128)
        self.other = place.part(1 - place.chip, width // 2, 128)

    def copy(self, step):
        ref = self.ref.at[self.rows, self.other if step == 2 else self.mine]
        where = self.place.across if step == 0 else self.place.near
        return self.move(ref, ref, self.base + step, self.at, self.at, where)

    def start(self):
        self.copy(0).start()
        self.copy(1).start()

    def relay(self):
        self.copy(0).wait_recv()
        self.copy(2).start()

    def ready(self):
        self.copy(1).wait_recv()
        self.copy(2).wait_recv()

    def finish(self):
        for step in range(3):
            self.copy(step).wait_send()


M_CORE, M_CHIP, M_HOME, M_BACK, M_MIX, M_END, M_PAIR, M_LATE = 4, 5, 6, 7, 11, 13, 16, 17
M_ROWS = 21


def middle_kernel(
    experts,
    counts,
    low_ref,
    cot_hbm,
    key_row,
    key_col,
    gate_col,
    gate_rows,
    in_hbm,
    out_hbm,
    cots_hbm,
    mixed_hbm,
    prob_ref,
    routes_col,
    gain_ref,
    router_ref,
    half_hbm,
    mixed_grad_hbm,
    att_grad_hbm,
    router_grad,
    gain_grad,
    grad_out,
    grad_in,
    grad_in_low,
    in_ref,
    out_ref,
    cots_ref,
    rows_ref,
    hid_ref,
    pre_ref,
    send_rows,
    gate_tall,
    pair_tall,
    pair_part,
    pair_core,
    pair_sum,
    pair_chip,
    pair_home,
    pair_back,
    core_send,
    core_recv,
    kept,
    chip_send,
    chip_recv,
    back,
    mix_send,
    mix_recv,
    mix_last,
    key_wide,
    hot_ref,
    total,
    pair_ref,
    dis_ref,
    copy_send,
    copy_recv,
    cot_tile,
    loads,
    cot_loads,
    sent,
    came,
):
    rows, width = low_ref.shape
    images = counts.shape[0]
    patches = rows // images
    cap = rows_ref.shape[1]
    half = cap // 2
    units = in_ref.shape[1]
    place = Place(experts)
    move = mover(sent, came)
    me = place.me
    lows = Dispatch(place, move, 0, send_rows, rows_ref)
    late = Dispatch(place, move, M_LATE, send_rows, cots_ref)
    dgrad = Return(
        place, move, M_BACK, core_send, core_recv, kept, chip_send, chip_recv, back
    )
    other_copy = {"narrow": place.n, "wide": place.w + 1 - 2 * place.parity}

    def load(at, src, dst):
        return pltpu.make_async_copy(src, dst, loads.at[at])

    fetched = [
        load(0, in_hbm, in_ref),
        load(1, out_hbm, out_ref),
    ]
    for copy in fetched:
        copy.start()

    def cots_in(i, whole):
        s = place.take(i)
        at = (s,) if whole else (s, late.mine, late.side_mine)
        return pltpu.make_async_copy(cots_hbm.at[at], cots_ref.at[at], cot_loads.at[i])

    @pl.loop(0, experts - LATE)
    def _(i):
        cots_in(i, True).start()

    for i in range(experts - LATE, experts):
        cots_in(i, False).start()
    place.greet((other_copy,))

    @pl.loop(1, experts)
    def _(i):
        lows.build(i, key_row, low_ref)

    for copy in fetched:
        copy.wait()

    @pl.loop(0, experts - LATE)
    def _(i):
        cots_in(i, True).wait()

    for i in range(experts - LATE, experts):
        cots_in(i, False).wait()
        late.relay(i)

    lows.build_own(key_row, low_ref)
    pair_tall[...] = jnp.zeros_like(pair_tall)
    grad_out[...] = jnp.zeros_like(grad_out)
    grad_in[...] = jnp.zeros_like(grad_in)
    for k in range(2):
        key_wide[k] = jnp.broadcast_to(key_col[:, k : k + 1], (rows, 128))

    def pair_move(step, s):
        src, dst, row, where = (
            (pair_part, pair_core, M_CORE, place.near),
            (pair_sum, pair_chip, M_CHIP, place.across),
        )[step]
        return move(src.at[s], dst.at[s], row, s, s, where)

    def pair_return(s, landed):
        return move(pair_home.at[s], pair_back.at[landed], M_HOME, s, landed, place.home(s))

    chunk = 256 if units % 256 == 0 else units

    def compute(s, m):
        part = pl.ds(m * half, half)
        left = rows_ref[s, part, :]
        cots = cots_ref[s, part, :]
        gate = gate_tall[part, 0:1]
        pair = jnp.zeros((half, 1), jnp.float32)
        for j in range(units // chunk):
            cols = slice(j * chunk, (j + 1) * chunk)
            pre = dot_rows(left, in_ref[:, cols])
            free = dot_cols(cots, out_ref[cols, :])
            cdf, slope = normal_parts(pre)
            hidden = pre * cdf
            hid_ref[s, part, cols] = (gate * hidden).astype(jnp.bfloat16)
            pre_ref[s, part, cols] = (gate * free * (cdf + slope)).astype(jnp.bfloat16)
            pair += jnp.sum(hidden * free, 1, keepdims=True)
        pair_tall[part, :] = jnp.broadcast_to(pair, (half, 128))

    def second(s):
        dgrad.second(s)
        pair_move(0, s).wait_recv()
        pair_sum[s] = pair_part[s] + pair_core[s]
        pair_move(1, s).start()

    def third(s):
        dgrad.third(s)
        pair_move(1, s).wait_recv()
        line = pair_sum[s] + pair_chip[s]

        @pl.when(s == me)
        def _():
            pair_back[me] = line

        @pl.when(s != me)
        def _():
            pair_home[s] = line
            pair_return(s, me).start()

    def contract(left, right):
        return lax.dot_general(
            left, right, (((0,), (0,)), ((), ())), preferred_element_type=jnp.float32
        )

    def mix_move(s):
        return move(mix_send.at[s], mix_recv.at[s], M_MIX, s, s, place.near)

    def mix_chip(s):
        src = mix_recv.at[s, :, dgrad.side_other]
        return move(src, mix_last.at[s], M_MIX + 1, s, s, place.across)

    def mix_first(s):
        mix_send[s] = dot_rows(hid_ref[s, dgrad.other, :], out_ref[...]).astype(jnp.bfloat16)
        mix_move(s).start()

    def mix_second(s):
        mix_move(s).wait_recv()
        mix_recv[s] = (
            dot_rows(hid_ref[s, dgrad.mine, :], out_ref[...]) + mix_recv[s].astype(jnp.float32)
        ).astype(jnp.bfloat16)

    def mix_third(s):
        mix_chip(s).wait_recv()
        mix_last[s] = (
            mix_recv[s, :, dgrad.side_mine].astype(jnp.float32) + mix_last[s].astype(jnp.float32)
        ).astype(jnp.bfloat16)

    def work(i, between):
        s = place.take(i)
        gate_tall[...] = jnp.transpose(gate_rows[s])
        compute(s, 0)
        between()
        compute(s, 1)
        pair_part[s] = jnp.transpose(pair_tall[...])[0:8]
        pair_move(0, s).start()
        dgrad.first(s, lambda part: dot_cols(pre_ref[s, part, :], in_ref[...]))

    def gather(i):
        s = place.take(i)
        grad_out[...] += contract(hid_ref[s], cots_ref[s])
        grad_in[...] += contract(rows_ref[s], pre_ref[s])
        mix_first(s)

    work(0, lambda: None)
    lows.stage_a(1)
    gather(0)

    @pl.loop(experts - LATE, experts)
    def _(i):
        late.stage_b(i)

    @pl.loop(1, experts)
    def _(i):
        @pl.when(i + 1 < experts)
        def _():
            lows.stage_a(i + 1)

        lows.stage_b(i)
        lows.stage_c(i)

        @pl.when(i >= experts - LATE)
        def _():
            late.stage_c(i)

        work(i, lambda: second(place.take(i - 1)))

        @pl.when(i > 1)
        def _():
            third(place.take(i - 2))

        gather(i)
        mix_second(place.take(i - 1))

    last = place.take(experts - 1)
    second(last)
    copy_send[...] = grad_out[...].astype(jnp.bfloat16)
    copy_move = move(copy_send, copy_recv, M_PAIR, 0, 0, other_copy)
    copy_move.start()
    third(place.take(experts - 2))
    mix_second(last)
    early = experts // 2

    @pl.loop(0, early)
    def _(i):
        mix_chip(place.take(i)).start()

    third(last)
    pair_ref[...] = jnp.zeros_like(pair_ref)

    def build_hot(e):
        lane = lax.broadcasted_iota(jnp.int32, (rows // 4, 128), 1)

        @pl.loop(0, 4)
        def _(m):
            part = pl.ds(pl.multiple_of(m * (rows // 4), 16), rows // 4)
            keys = [key_wide[k, part, :] - e * cap for k in range(2)]
            for low in range(0, cap, 128):
                size = min(128, cap - low)
                hit = (keys[0] == lane + low) | (keys[1] == lane + low)
                hot_ref[part, low : low + size] = jnp.where(hit, 1.0, 0.0).astype(jnp.bfloat16)[
                    :, 0:size
                ]

    my_rows = place.part(place.core, rows // 2, 16)
    total[...] = jnp.zeros_like(total)

    @pl.loop(0, experts)
    def _(i):
        e = place.take(i)
        build_hot(e)
        dgrad.fourth(i)

        @pl.when(i > 0)
        def _():
            pair_return(e, e).wait_recv()

        tall = jnp.transpose(pair_back[e])[0:cap, 0:1]
        high = tall.astype(jnp.bfloat16).astype(jnp.float32)
        middle = (tall - high).astype(jnp.bfloat16).astype(jnp.float32)
        lane = lax.broadcasted_iota(jnp.int32, (cap, 128), 1)
        spelled = jnp.where(
            lane == 0, high, jnp.where(lane == 1, middle, jnp.where(lane == 2, tall - high - middle, 0.0))
        ).astype(jnp.bfloat16)
        found = jnp.sum(dot_rows(hot_ref[...], spelled), 1, keepdims=True)
        lane_rows = lax.broadcasted_iota(jnp.int32, (rows, 128), 1)
        pair_ref[...] += jnp.where(lane_rows == e, found, 0.0)
        dgrad.ready(i)
        total[...] += dot_rows(hot_ref[my_rows, :], back[e])

    ends = Quarters(place, move, M_END, 0, dis_ref)
    dis_ref[ends.rows, ends.mine] = total[...].astype(jnp.bfloat16)
    ends.start()

    @pl.loop(early, experts)
    def _(i):
        mix_chip(place.take(i)).start()

    mixed_in = load(1, mixed_hbm, kept.at[pl.ds(0, rows), :])
    mixed_in.start()
    grad_in_low[...] = grad_in[...].astype(jnp.bfloat16)

    @pl.loop(0, early)
    def _(i):
        mix_third(place.take(i))

    ends.relay()
    ends.ready()
    ends.finish()
    mixed_in.wait()

    tile = patches // 2
    router_grad[...] = jnp.zeros_like(router_grad)
    gain_grad[...] = jnp.zeros_like(gain_grad)

    def cot_in(t):
        slot = lax.rem(t, 2)
        part = pl.ds(pl.multiple_of(t * tile, 16), tile)
        return pltpu.make_async_copy(
            cot_hbm.at[part, :], cot_tile.at[slot], loads.at[2 + slot]
        )

    def rows_out(t, what):
        part = pl.ds(pl.multiple_of(t * tile, 16), tile)
        src, dst = ((kept, mixed_grad_hbm), (dis_ref, att_grad_hbm))[what]
        return pltpu.make_async_copy(src.at[part, :], dst.at[part, :], loads.at[4 + 2 * t + what])

    cot_in(0).start()

    @pl.loop(0, rows // tile)
    def _(t):
        @pl.when(t + 1 < rows // tile)
        def _():
            cot_in(t + 1).start()

        part = pl.ds(pl.multiple_of(t * tile, 16), tile)
        lane = lax.broadcasted_iota(jnp.int32, (tile, 128), 1)
        by_expert = pair_ref[part, :]
        hots = [lane == routes_col[part, k : k + 1] for k in range(2)]
        pair = [jnp.sum(jnp.where(hot, by_expert, 0.0), 1, keepdims=True) for hot in hots]
        weighted = pair[0] * gate_col[part, 0:1] + pair[1] * gate_col[part, 1:2]
        both = gate_col[part, 2:3]
        prob = prob_ref[part, :]
        prob_grad = jnp.where(hots[0], (pair[0] - weighted) / both, 0.0) + jnp.where(
            hots[1], (pair[1] - weighted) / both, 0.0
        )
        logit_grad = (
            prob * (prob_grad - jnp.sum(prob * prob_grad, 1, keepdims=True))
        ).astype(jnp.bfloat16)
        router_grad[...] += contract(logit_grad, low_ref[part, :])
        normed_grad = dis_ref[part, :].astype(jnp.float32) + dot_cols(logit_grad, router_ref[...])
        _, hat, scaled = normalize(kept[part, :], gain_ref[0:1, :])
        gain_grad[...] += jnp.sum(normed_grad * hat, 0, keepdims=True)
        grad = normed_grad * gain_ref[0:1, :]
        inner = (
            grad - jnp.mean(grad, -1, keepdims=True) - hat * jnp.mean(grad * hat, -1, keepdims=True)
        )
        cot_in(t).wait()
        full = cot_tile[lax.rem(t, 2)].astype(jnp.float32) + scaled * inner
        kept[part, :] = full
        rows_out(t, 0).start()
        row = t * tile + lax.broadcasted_iota(jnp.int32, (tile, 1), 0)
        live = lax.rem(row, patches) < jnp.where(t * tile < patches, counts[0], counts[images - 1])
        dis_ref[part, :] = jnp.where(live, full, 0.0).astype(jnp.bfloat16)
        rows_out(t, 1).start()

    @pl.loop(early, experts)
    def _(i):
        mix_third(place.take(i))

    half_out = load(0, mix_last, half_hbm)
    half_out.start()
    copy_move.wait()
    grad_out[...] += copy_recv[...].astype(jnp.float32)
    half_out.wait()

    @pl.loop(0, rows // tile)
    def _(t):
        rows_out(t, 0).wait()
        rows_out(t, 1).wait()

    dgrad.finish()
    lows.finish(1, experts)
    late.finish(experts - LATE, experts, False)

    @pl.loop(0, experts)
    def _(i):
        s = place.take(i)
        pair_move(0, s).wait_send()
        pair_move(1, s).wait_send()
        mix_move(s).wait_send()
        mix_chip(s).wait_send()

        @pl.when(i > 0)
        def _():
            pair_return(s, me).wait_send()


def middle(
    counts,
    low,
    cot,
    keys,
    gates,
    gate_rows,
    weight_in,
    weight_out,
    cots,
    mixed,
    prob,
    routes,
    gain,
    router,
    experts,
):
    rows, width = low.shape
    units = weight_in.shape[1]
    cap = cots.shape[1]
    half, side, wide_cap = cap // 2, width // 2, round_up(cap, 128)
    bf16, f32 = jnp.bfloat16, jnp.float32
    vmem = pl.BlockSpec(memory_space=pltpu.VMEM)
    hbm = pl.BlockSpec(memory_space=pl.ANY)
    line = pltpu.VMEM((experts, 8, wide_cap), f32)
    halves = pltpu.VMEM((experts, half, width), bf16)
    tile = rows // counts.shape[0] // 2
    return pl.pallas_call(
        functools.partial(middle_kernel, experts),
        out_shape=[
            jax.ShapeDtypeStruct((experts, half, side), bf16),
            jax.ShapeDtypeStruct((rows, width), f32),
            jax.ShapeDtypeStruct((rows, width), bf16),
            jax.ShapeDtypeStruct((128, width), f32),
            jax.ShapeDtypeStruct((1, width), f32),
            jax.ShapeDtypeStruct((units, width), f32),
            jax.ShapeDtypeStruct((width, units), f32),
            jax.ShapeDtypeStruct((width, units), bf16),
        ],
        in_specs=[
            pl.BlockSpec(memory_space=pltpu.SMEM),
            vmem,
            hbm,
            vmem,
            vmem,
            vmem,
            vmem,
            hbm,
            hbm,
            hbm,
            hbm,
            vmem,
            vmem,
            vmem,
            vmem,
        ],
        out_specs=[hbm] * 3 + [vmem] * 5,
        scratch_shapes=[
            pltpu.VMEM((width, units), bf16),
            pltpu.VMEM((units, width), bf16),
            pltpu.VMEM((experts, cap, width), bf16),
            pltpu.VMEM((experts, cap, width), bf16),
            pltpu.VMEM((experts, cap, units), bf16),
            pltpu.VMEM((experts, cap, units), bf16),
            pltpu.VMEM((experts, half, side), bf16),
            pltpu.VMEM((wide_cap, 8), f32),
            pltpu.VMEM((wide_cap, 128), f32),
            line,
            line,
            line,
            line,
            line,
            line,
            halves,
            halves,
            pltpu.VMEM((max(experts * half, rows), width), f32),
            pltpu.VMEM((experts, half, side), bf16),
            pltpu.VMEM((experts, half, side), bf16),
            pltpu.VMEM((experts, cap, side), bf16),
            halves,
            halves,
            pltpu.VMEM((experts, half, side), bf16),
            pltpu.VMEM((2, rows, 128), jnp.int32),
            pltpu.VMEM((rows, cap), bf16),
            pltpu.VMEM((rows // 2, side), f32),
            pltpu.VMEM((rows, 128), f32),
            pltpu.VMEM((rows, width), bf16),
            pltpu.VMEM((units, width), bf16),
            pltpu.VMEM((units, width), bf16),
            pltpu.VMEM((2, tile, width), bf16),
            pltpu.SemaphoreType.DMA((4 + 2 * (rows // tile),)),
            pltpu.SemaphoreType.DMA((experts,)),
            pltpu.SemaphoreType.DMA((M_ROWS, experts)),
            pltpu.SemaphoreType.DMA((M_ROWS, experts)),
        ],
        compiler_params=pltpu.CompilerParams(
            collective_id=1, has_side_effects=True, vmem_limit_bytes=VMEM_BYTES
        ),
    )(
        counts,
        low,
        cot,
        keys.T,
        keys,
        gates,
        gate_rows,
        weight_in,
        weight_out,
        cots,
        mixed,
        prob,
        routes,
        gain,
        router,
    )


class Fold:
    def __init__(self, place, move, base, core_send, core_recv, kept, chip_send, chip_recv, whole):
        self.place, self.move, self.base = place, move, base
        self.core_send, self.core_recv, self.kept = core_send, core_recv, kept
        self.chip_send, self.chip_recv, self.whole = chip_send, chip_recv, whole
        self.half, self.side = chip_send.shape[1:]
        self.side_mine = place.part(place.chip, self.side, 128)
        self.side_other = place.part(1 - place.chip, self.side, 128)

    def rows(self, image, core):
        start = (2 * image + core) * self.half
        return pl.ds(pl.multiple_of(start, 16), self.half)

    def core_move(self, image):
        return self.move(
            self.core_send.at[image],
            self.core_recv.at[image],
            self.base,
            image,
            image,
            self.place.near,
        )

    def chip_move(self, image):
        return self.move(
            self.chip_send.at[image],
            self.chip_recv.at[image],
            self.base + 1,
            image,
            image,
            self.place.across,
        )

    def share(self, image, step):
        cols = self.side_other if step == 2 else self.side_mine
        ref = self.whole.at[self.rows(image, self.place.core), cols]
        where = self.place.across if step == 0 else self.place.near
        return self.move(ref, ref, self.base + 2 + step, image, image, where)

    def second(self, image):
        self.core_move(image).wait_recv()
        self.chip_send[image] = (
            self.kept[image, :, self.side_other]
            + self.core_recv[image, :, self.side_other].astype(jnp.float32)
        ).astype(jnp.bfloat16)
        self.chip_move(image).start()

    def third(self, image):
        self.chip_move(image).wait_recv()
        self.whole[self.rows(image, self.place.core), self.side_mine] = (
            self.kept[image, :, self.side_mine]
            + self.core_recv[image, :, self.side_mine].astype(jnp.float32)
            + self.chip_recv[image].astype(jnp.float32)
        ).astype(jnp.bfloat16)
        self.share(image, 0).start()
        self.share(image, 1).start()

    def relay(self, image):
        self.share(image, 0).wait_recv()
        self.share(image, 2).start()

    def ready(self, image):
        self.share(image, 1).wait_recv()
        self.share(image, 2).wait_recv()

    def finish(self, images):
        for image in range(images):
            self.core_move(image).wait_send()
            self.chip_move(image).wait_send()
            for step in range(3):
                self.share(image, step).wait_send()


class WideSum:
    def __init__(self, place, move, tables, pair_send, pair_recv, kept, group_send, group_recv, whole):
        self.place, self.move = place, move
        self.pair_sems, self.group_out, self.group_in = tables
        self.pair_send, self.pair_recv, self.kept = pair_send, pair_recv, kept
        self.group_send, self.group_recv, self.whole = group_send, group_recv, whole
        self.rows, self.cols = group_recv.shape[2:]
        self.half = pair_send.shape[1]
        self.real = kept.shape[1]
        self.pair = {"narrow": place.n, "wide": place.w + 1 - 2 * place.parity}

    def pair_move(self, p):
        return self.move[0](
            self.pair_send.at[p], self.pair_recv.at[p], 0, p, p, self.pair
        )

    def chunk(self, e):
        return (
            pl.ds(pl.multiple_of((e // 2) * self.rows, 16), self.rows),
            pl.ds(pl.multiple_of(lax.rem(e, 2) * self.cols, 128), self.cols),
        )

    def group_move(self, p, e, landed):
        rows, cols = self.chunk(e)
        return self.move[1](
            self.group_send.at[p, rows, cols],
            self.group_recv.at[p, landed],
            p,
            e,
            landed,
            self.place.home(e),
        )

    def group_share(self, p, owner, at, landed, where):
        rows, cols = self.chunk(owner)
        ref = self.whole.at[p, self.place.parity, rows, cols]
        pieces = self.pair_send.shape[0]
        return self.move[1](ref, ref, pieces + p, at, landed, where)

    def pair_share(self, p, parity):
        ref = self.whole.at[p, parity]
        return self.move[0](ref, ref, 1, p, p, self.pair)

    def first(self, p, halves):
        @pl.when(self.place.parity == 0)
        def _():
            self.kept[p] = halves[0]
            self.pair_send[p, 0 : self.real] = halves[1].astype(jnp.bfloat16)

        @pl.when(self.place.parity == 1)
        def _():
            self.kept[p] = halves[1]
            self.pair_send[p, 0 : self.real] = halves[0].astype(jnp.bfloat16)

        self.pair_move(p).start()

    def second(self, p):
        self.pair_move(p).wait_recv()
        self.group_send[p, 0 : self.real] = (
            self.kept[p] + self.pair_recv[p, 0 : self.real].astype(jnp.float32)
        ).astype(jnp.bfloat16)

        @pl.loop(1, self.place.experts)
        def _(i):
            self.group_move(p, self.place.send_to(i), self.place.me).start()

    def third(self, p):
        rows, cols = self.chunk(self.place.me)
        total = self.group_send[p, rows, cols].astype(jnp.float32)
        self.total[...] = total

        @pl.loop(1, self.place.experts)
        def _(i):
            s = self.place.take(i)
            self.group_move(p, s, s).wait_recv()
            self.total[...] += self.group_recv[p, s].astype(jnp.float32)

        self.whole[p, self.place.parity, rows, cols] = self.total[...].astype(jnp.bfloat16)

        @pl.loop(1, self.place.experts)
        def _(i):
            e = self.place.send_to(i)
            self.group_share(p, self.place.me, e, self.place.me, self.place.home(e)).start()

    def fourth(self, p):
        @pl.loop(1, self.place.experts)
        def _(i):
            s = self.place.take(i)
            self.group_share(p, s, s, s, self.place.home(s)).wait_recv()

        self.pair_share(p, self.place.parity).start()

    def ready(self, p):
        self.pair_share(p, 1 - self.place.parity).wait_recv()

    def finish(self):
        for p in range(self.pair_send.shape[0]):
            self.pair_move(p).wait_send()
            self.pair_share(p, self.place.parity).wait_send()

            @pl.loop(1, self.place.experts)
            def _(i):
                e = self.place.send_to(i)
                self.group_move(p, e, self.place.me).wait_send()
                self.group_share(p, self.place.me, e, self.place.me, self.place.home(e)).wait_send()


B_MIX, B_ENDMIX, B_FOLD, B_SMALL = 0, 3, 6, 11
B_ROWS = 14


def back_kernel(
    experts,
    counts,
    att_grad,
    mixed_grad,
    heads_ref,
    stats_ref,
    attended_ref,
    x_ref,
    gain_ref,
    qkv_w,
    out_w,
    mixed_ref,
    half_ref,
    key_col,
    router_part,
    gain2_part,
    out_ref,
    x_grad,
    whole_ref,
    small_out,
    low_ref,
    lines,
    head_grad,
    proj_grad,
    key_wide,
    back,
    hot_ref,
    total,
    fold_send,
    fold_recv,
    fold_kept,
    fold_chip_send,
    fold_chip_recv,
    normed_ref,
    pair_send,
    pair_recv,
    pair_kept,
    group_send,
    group_recv,
    group_total,
    small_ref,
    small_near,
    small_far,
    small_pair,
    small_group,
    small_steps,
    sent,
    came,
    pair_sent,
    pair_came,
    group_sent,
    group_came,
):
    rows, width = att_grad.shape
    images = counts.shape[0]
    patches = rows // images
    head_cols = attended_ref.shape[1]
    heads = head_cols // HEAD_DIM
    scale = HEAD_DIM ** (-0.5)
    cap = back.shape[1]
    tile = patches // 2
    pieces = heads + 1
    place = Place(experts)
    move = mover(sent, came)
    me = place.me
    wide = WideSum(
        place,
        (mover(pair_sent, pair_came), mover(group_sent, group_came)),
        (None, None, None),
        pair_send,
        pair_recv,
        pair_kept,
        group_send,
        group_recv,
        whole_ref,
    )
    wide.total = group_total
    fold = Fold(
        place,
        move,
        B_FOLD,
        fold_send,
        fold_recv,
        fold_kept,
        fold_chip_send,
        fold_chip_recv,
        normed_ref,
    )
    place.greet((wide.pair,))

    half = half_ref.shape[1]
    mine = place.part(place.core, half, 16)
    other = place.part(1 - place.core, half, 16)
    side_mine = place.part(place.chip, width // 2, 128)

    def mix_home(s, landed):
        return move(half_ref.at[s], back.at[landed, mine, :], B_MIX + 1, s, landed, place.home(s))

    def mix_near(e, part):
        ref = back.at[e, part, :]
        return move(ref, ref, B_MIX + 2, e, e, place.near)

    @pl.loop(1, experts)
    def _(i):
        mix_home(place.send_to(i), me).start()

    back[me, mine, :] = half_ref[me]

    def mix_relay(i):
        e = place.take(i)

        @pl.when(e != me)
        def _():
            mix_home(e, e).wait_recv()

        mix_near(e, mine).start()

    my_rows = place.part(place.core, rows // 2, 16)

    def mix_sum(i):
        e = place.take(i)

        lane = lax.broadcasted_iota(jnp.int32, (rows // 4, 128), 1)

        @pl.loop(0, 2)
        def _(m):
            part = pl.ds(pl.multiple_of(m * (rows // 4), 16), rows // 4)
            keys = [key_wide[k, part, :] - e * cap for k in range(2)]
            for low in range(0, cap, 128):
                size = min(128, cap - low)
                hit = (keys[0] == lane + low) | (keys[1] == lane + low)
                hot_ref[part, low : low + size] = jnp.where(hit, 1.0, 0.0).astype(jnp.bfloat16)[
                    :, 0:size
                ]

        mix_near(e, other).wait_recv()
        total[...] += dot_rows(hot_ref[...], back[e])

    ends = Quarters(place, move, B_ENDMIX, 0, out_ref)

    small_sizes = small_ref.shape
    small_ref[...] = jnp.zeros_like(small_ref)
    small_ref[0:experts] = router_part[0:experts]
    small_ref[experts : experts + 1] = gain2_part[...]

    def small_move(step):
        src, dst, where = (
            (small_ref, small_near, place.near),
            (small_steps.at[0], small_far, place.across),
            (small_steps.at[1], small_pair, wide.pair),
        )[step]
        return move(src, dst, B_SMALL, step, step, where)

    def small_home(e, landed):
        return move(
            small_steps.at[2], small_group.at[landed], B_SMALL + 1, e, landed, place.home(e)
        )

    share_row = lax.broadcasted_iota(jnp.int32, small_sizes, 0) == experts + 1

    def small_second():
        small_move(0).wait_recv()
        small_steps[0] = small_ref[...] + jnp.where(share_row, small_near[...], 0.0)
        small_move(1).start()

    def small_third():
        small_move(1).wait_recv()
        small_steps[1] = small_steps[0] + jnp.where(share_row, small_far[...], 0.0)
        small_move(2).start()

    def small_fourth():
        small_move(2).wait_recv()
        small_steps[2] = small_steps[1] + small_pair[...]
        small_group[me] = small_steps[2]

        @pl.loop(1, experts)
        def _(i):
            small_home(place.send_to(i), me).start()

    def small_last():
        @pl.loop(1, experts)
        def _(i):
            s = place.take(i)
            small_home(s, s).wait_recv()

        small_out[...] = jnp.zeros_like(small_out)

        @pl.loop(0, experts)
        def _(e):
            small_out[...] += small_group[e]

    real = pair_kept.shape[1]

    def contract(left, right):
        return lax.dot_general(
            left, right, (((0,), (0,)), ((), ())), preferred_element_type=jnp.float32
        )

    def zero_pads():
        if pair_send.shape[1] > real:
            pair_send[:, real:] = jnp.zeros_like(pair_send[:, real:])
            group_send[:, real:] = jnp.zeros_like(group_send[:, real:])

    zero_pads()
    product = contract(attended_ref[...], att_grad[...])
    wide.first(0, (product[0:real], product[real:]))

    @pl.loop(0, rows // tile)
    def _(t):
        part = pl.ds(pl.multiple_of(t * tile, 16), tile)
        normed, _, _ = normalize(x_ref[part, :].astype(jnp.float32), gain_ref[0:1, :])
        low_ref[part, :] = normed.astype(jnp.bfloat16)
        block = dot_cols(att_grad[part, :], out_w[...]).astype(jnp.bfloat16)
        for h in range(heads):
            head_grad[h, part, :] = block[:, h * HEAD_DIM : (h + 1) * HEAD_DIM]

    @pl.loop(0, images)
    def _(image):
        part = pl.ds(pl.multiple_of(image * patches, 16), patches)
        padded = round_up(patches, 128)
        column = jnp.concatenate(
            [stats_ref[part, :], jnp.zeros((padded - patches, 128), jnp.float32)], 0
        )
        lines[image] = jnp.transpose(column)[0:8, :]

    def attend_back(image, h):
        part = pl.ds(pl.multiple_of(image * patches, 16), patches)
        query = heads_ref[0, h, part, :]
        key_rows = heads_ref[1, h, part, :]
        out_grad = head_grad[h, part, :]
        live = lax.broadcasted_iota(jnp.int32, (patches, 1), 0) < counts[image]
        line = lines[image, pl.ds(h, 1), 0:patches]
        scores = jnp.where(live, dot_cols(key_rows, query) * scale, MASKED_SCORE)
        probs = jnp.exp(scores - line)
        change = dot_cols(heads_ref[2, h, part, :], out_grad)
        delta = jnp.sum(probs * change, 0, keepdims=True)
        score_grad = (scale * probs * (change - delta)).astype(jnp.bfloat16)
        proj_grad[2, h, part, :] = dot_rows(probs.astype(jnp.bfloat16), out_grad).astype(
            jnp.bfloat16
        )
        proj_grad[1, h, part, :] = dot_rows(score_grad, query).astype(jnp.bfloat16)
        proj_grad[0, h, part, :] = contract(score_grad, key_rows).astype(jnp.bfloat16)

    def piece(h):
        grads = jnp.concatenate([proj_grad[i, h] for i in range(3)], 1)
        product = contract(grads, low_ref[...])
        wide.first(h + 1, (product[0:real], product[real:]))

    def fold_first(image):
        for mine_too in (False, True):
            part = fold.rows(image, place.core if mine_too else 1 - place.core)
            normed_part = jnp.zeros((tile, width), jnp.float32)
            for i in range(3):
                grads = jnp.concatenate([proj_grad[i, h, part, :] for h in range(heads)], 1)
                normed_part += dot_cols(grads, qkv_w[i])
            if mine_too:
                fold_kept[image] = normed_part
            else:
                fold_send[image] = normed_part.astype(jnp.bfloat16)
                fold.core_move(image).start()
            _, hat, _ = normalize(x_ref[part, :].astype(jnp.float32), gain_ref[0:1, :])
            small_ref[experts + 1 : experts + 2] += jnp.sum(normed_part * hat, 0, keepdims=True)

    for k in range(2):
        key_wide[k] = jnp.broadcast_to(key_col[my_rows, k : k + 1], (rows // 2, 128))

    def mix_relays(lo, hi):
        @pl.loop(lo, hi)
        def _(i):
            mix_relay(i)

    def mix_sums(lo, hi):
        @pl.loop(lo, hi)
        def _(i):
            mix_sum(i)

    total[...] = jnp.zeros_like(total)

    def mix_tail():
        out_ref[ends.rows, ends.mine] = (mixed_ref[my_rows, side_mine] + total[...]).astype(
            jnp.bfloat16
        )
        ends.start()

    mid = experts // 2
    agenda = {
        1: [lambda: mix_relays(0, mid)],
        2: [lambda: fold_first(0), lambda: mix_sums(0, mid)],
        3: [lambda: piece(0), lambda: fold.second(0), lambda: mix_relays(mid, experts)],
        4: [lambda: piece(1), lambda: fold.third(0), lambda: mix_sums(mid, experts)],
        5: [lambda: piece(2), lambda: wide.second(0), lambda: fold.relay(0)],
    }

    @pl.loop(0, images * heads)
    def _(step):
        attend_back(step // heads, lax.rem(step, heads))
        for at, todo in agenda.items():

            @pl.when(step == at)
            def _():
                for act in todo:
                    act()

    fold_first(1)
    small_move(0).start()
    wide.second(1)
    fold.second(1)
    small_second()
    mix_tail()
    wide.second(2)
    wide.third(0)
    small_third()
    wide.second(3)
    wide.third(1)
    fold.third(1)
    small_fourth()
    wide.third(2)
    wide.fourth(0)
    wide.third(3)
    wide.fourth(1)
    fold.ready(0)

    def input_rows(image):
        @pl.loop(2 * image, 2 * image + 2)
        def _(t):
            part = pl.ds(pl.multiple_of(t * tile, 16), tile)
            _, hat, scaled = normalize(x_ref[part, :].astype(jnp.float32), gain_ref[0:1, :])
            grad = normed_ref[part, :].astype(jnp.float32) * gain_ref[0:1, :]
            inner = (
                grad - jnp.mean(grad, -1, keepdims=True) - hat * jnp.mean(grad * hat, -1, keepdims=True)
            )
            x_grad[part, :] = mixed_grad[part, :] + scaled * inner

    input_rows(0)
    wide.fourth(2)
    ends.relay()
    fold.relay(1)
    wide.fourth(3)
    small_last()
    fold.ready(1)
    input_rows(1)
    ends.ready()
    for p in range(pieces):
        wide.ready(p)
    wide.finish()
    fold.finish(images)
    ends.finish()
    for step in range(3):
        small_move(step).wait_send()

    @pl.loop(0, experts)
    def _(i):
        s = place.take(i)
        mix_near(s, mine).wait_send()

        @pl.when(i > 0)
        def _():
            mix_home(s, me).wait_send()
            small_home(s, me).wait_send()


def back(
    counts,
    att_grad,
    mixed_grad,
    head_rows,
    stats,
    attended,
    x,
    gain,
    qkv_w,
    out_w,
    mixed,
    halves,
    keys,
    router_part,
    gain2_part,
):
    rows, width = x.shape
    experts, half = halves.shape[:2]
    cap, side = 2 * half, width // 2
    images = counts.shape[0]
    heads = head_rows.shape[1]
    head_cols = out_w.shape[0]
    pieces = heads + 1
    real = head_cols // 2
    split = max(experts // 2, 1)
    chunk_rows = round_up(-(-real // split), 16)
    padded = chunk_rows * split
    part_rows = rows // images // 2
    small = round_up(experts + 2, 8)
    bf16, f32 = jnp.bfloat16, jnp.float32
    vmem = pl.BlockSpec(memory_space=pltpu.VMEM)
    small_block = pltpu.VMEM((small, width), f32)
    dma = pltpu.SemaphoreType.DMA
    table = max(experts, images, 3)
    return pl.pallas_call(
        functools.partial(back_kernel, experts),
        out_shape=[
            jax.ShapeDtypeStruct((rows, width), bf16),
            jax.ShapeDtypeStruct((rows, width), f32),
            jax.ShapeDtypeStruct((pieces, 2, padded, width), bf16),
            jax.ShapeDtypeStruct((small, width), f32),
        ],
        in_specs=[pl.BlockSpec(memory_space=pltpu.SMEM)] + [vmem] * 14,
        out_specs=[vmem] * 4,
        scratch_shapes=[
            pltpu.VMEM((rows, width), bf16),
            pltpu.VMEM((images, 8, round_up(rows // images, 128)), f32),
            pltpu.VMEM((heads, rows, HEAD_DIM), bf16),
            pltpu.VMEM((3, heads, rows, HEAD_DIM), bf16),
            pltpu.VMEM((2, rows // 2, 128), jnp.int32),
            pltpu.VMEM((experts, cap, side), bf16),
            pltpu.VMEM((rows // 2, cap), bf16),
            pltpu.VMEM((rows // 2, side), f32),
            pltpu.VMEM((images, part_rows, width), bf16),
            pltpu.VMEM((images, part_rows, width), bf16),
            pltpu.VMEM((images, part_rows, width), f32),
            pltpu.VMEM((images, part_rows, side), bf16),
            pltpu.VMEM((images, part_rows, side), bf16),
            pltpu.VMEM((rows, width), bf16),
            pltpu.VMEM((pieces, padded, width), bf16),
            pltpu.VMEM((pieces, padded, width), bf16),
            pltpu.VMEM((pieces, real, width), f32),
            pltpu.VMEM((pieces, padded, width), bf16),
            pltpu.VMEM((pieces, experts, chunk_rows, side), bf16),
            pltpu.VMEM((chunk_rows, side), f32),
            small_block,
            small_block,
            small_block,
            small_block,
            pltpu.VMEM((experts, small, width), f32),
            pltpu.VMEM((3, small, width), f32),
            dma((B_ROWS, table)),
            dma((B_ROWS, table)),
            dma((2, pieces)),
            dma((2, pieces)),
            dma((2 * pieces, experts)),
            dma((2 * pieces, experts)),
        ],
        compiler_params=pltpu.CompilerParams(
            collective_id=3, has_side_effects=True, vmem_limit_bytes=VMEM_BYTES
        ),
    )(
        counts,
        att_grad,
        mixed_grad,
        head_rows,
        stats,
        attended,
        x,
        gain,
        qkv_w,
        out_w,
        mixed,
        halves,
        keys,
        router_part,
        gain2_part,
    )


def swapped(x, axis, distance):
    return lax.ppermute(x, axis, [(i, i ^ 1 << distance) for i in range(lax.axis_size(axis))])


def body(
    inputs,
    counts,
    routes,
    slot_ids,
    norm_first,
    attn_in,
    attn_out,
    norm_second,
    router,
    expert_in,
    expert_out,
    cotangent,
):
    rows_dev, feat_width = inputs.shape
    experts = router.shape[1]
    half_slots = (105 * rows_dev + 100 * experts - 1) // (100 * experts)
    capacity = 2 * half_slots
    head_cols = attn_out.shape[0]
    local_heads = head_cols // HEAD_DIM
    slot_pad = round_up(capacity, 32)
    slot_keys = jnp.where(slot_ids < capacity, routes * slot_pad + slot_ids, -1)
    gain1, gain2 = norm_first[None], norm_second[None]
    router_pad = jnp.pad(router, ((0, 0), (0, 128 - experts)))
    sent_cots, head_rows, attended, stats, mixed, low_second, prob, gates, gate_rows = front(
        counts,
        inputs,
        cotangent,
        slot_keys,
        routes,
        gain1,
        attn_in,
        attn_out,
        gain2,
        router_pad,
        experts,
        slot_pad,
    )
    halves, mixed_grad, att_grad, router_part, gain_part, expert_out_grad, in_grad, in_low = middle(
        counts,
        low_second,
        cotangent,
        slot_keys,
        gates,
        gate_rows,
        expert_in[0],
        expert_out[0],
        sent_cots,
        mixed,
        prob,
        routes,
        gain2,
        router_pad,
        experts,
    )
    other_in = swapped(in_low, "wide", 0)
    output, input_grad, whole, small = back(
        counts,
        att_grad,
        mixed_grad,
        head_rows,
        stats,
        attended,
        inputs,
        gain1,
        attn_in,
        attn_out,
        mixed,
        halves,
        slot_keys,
        router_part,
        gain_part,
    )
    expert_in_grad = in_grad + other_in.astype(jnp.float32)
    real = head_cols // 2
    pieces = whole[:, :, :real].reshape(-1, head_cols, feat_width).astype(jnp.float32)
    attn_in_grad = (
        pieces[1:]
        .reshape(local_heads, 3, HEAD_DIM, feat_width)
        .transpose(1, 3, 0, 2)
        .reshape(3, feat_width, head_cols)
    )
    return (
        output,
        input_grad,
        small[experts + 1],
        attn_in_grad,
        pieces[0],
        small[experts],
        small[:experts].T,
        expert_in_grad[None],
        expert_out_grad[None],
    )


def solution(mesh):
    in_specs = (
        P("wide", None),
        P("wide"),
        P("wide", None),
        P("wide", None),
        P(),
        P(None, None, "narrow"),
        P("narrow", None),
        P(),
        P(),
        P("wide", None, "narrow"),
        P("wide", "narrow", None),
        P("wide", None),
    )
    out_specs = (
        P("wide", None),
        P("wide", None),
        P(),
        P(None, None, "narrow"),
        P("narrow", None),
        P(),
        P(),
        P("wide", None, "narrow"),
        P("wide", "narrow", None),
    )
    return jax.shard_map(body, mesh=mesh, in_specs=in_specs, out_specs=out_specs, check_vma=False)
```

```python
import functools

import jax
import jax.numpy as jnp
from jax import lax
from jax.experimental import pallas as pl
from jax.experimental.pallas import tpu as pltpu
from jax.sharding import PartitionSpec as P

HEAD_DIM = 64
NORM_EPSILON = 1e-06
MASKED_SCORE = -1e30
BY_MESH = pl.DeviceIdType.MESH
VMEM_BYTES = 64 * 1024 * 1024 - 65536


def round_up(value, multiple):
    return -(-value // multiple) * multiple


def dot_rows(left, right):
    return lax.dot_general(left, right, (((1,), (0,)), ((), ())), preferred_element_type=jnp.float32)


def dot_cols(left, right):
    return lax.dot_general(left, right, (((1,), (1,)), ((), ())), preferred_element_type=jnp.float32)


def normal_parts(values):
    t = 1.0 / (1.0 + (0.3275911 * 0.7071067811865476) * jnp.abs(values))
    bell = jnp.exp(-0.5 * values * values)
    poly = t * (
        0.254829592
        + t * (-0.284496736 + t * (1.421413741 + t * (-1.453152027 + t * 1.061405429)))
    )
    tail = 0.5 * poly * bell
    return jnp.where(values >= 0.0, 1.0 - tail, tail), 0.3989422804014327 * values * bell


def normalize(values, gain):
    center = values - jnp.mean(values, -1, keepdims=True)
    scaled = lax.rsqrt(jnp.mean(center * center, -1, keepdims=True) + NORM_EPSILON)
    normed = center * scaled
    return normed * gain, normed, scaled


def slot_keys(routes_ref, slots_ref, capacity, cap):
    return jnp.where(slots_ref[...] < capacity, routes_ref[...] * cap + slots_ref[...], -1)


def widen(rows):
    count = rows.shape[1]
    padded = jnp.concatenate([rows.astype(jnp.float32), jnp.zeros((6, count), jnp.float32)], 0)
    tall = jnp.transpose(padded)
    return [jnp.broadcast_to(tall[:, k : k + 1], (count, 128)).astype(jnp.int32) for k in range(2)]


def flat(gain_ref):
    return gain_ref[...].reshape(1, gain_ref.shape[0])


class Place:
    def __init__(self, experts):
        self.experts = experts
        self.n = lax.axis_index("narrow")
        self.w = lax.axis_index("wide")
        self.core = lax.rem(self.n, 2)
        self.chip = self.n // 2
        self.me = self.w // 2
        self.parity = lax.rem(self.w, 2)
        self.near_n = self.n + 1 - 2 * self.core
        self.across_n = lax.rem(self.n + 2, 4)
        self.near = {"narrow": self.near_n, "wide": self.w}
        self.across = {"narrow": self.across_n, "wide": self.w}

    def home(self, e):
        return {"narrow": self.n, "wide": 2 * e + self.parity}

    def take(self, i):
        short = jnp.minimum(self.me, self.experts - 1 - self.me)
        swing = jnp.where(lax.rem(i, 2) == 1, (i + 1) // 2, -(i // 2))
        away = jnp.where(i <= 2 * short, swing, i - short)
        return self.me + jnp.where(2 * self.me < self.experts, away, -away)

    def part(self, which, size, align):
        return pl.ds(pl.multiple_of(which * size, align), size)

    def greet(self, others=()):
        barrier = pltpu.get_barrier_semaphore()
        for peer in (self.near, self.across, *others):
            pl.semaphore_signal(barrier, inc=1, device_id=peer, device_id_type=BY_MESH)

        @pl.loop(1, self.experts)
        def _(i):
            pl.semaphore_signal(
                barrier, inc=1, device_id=self.home(self.take(i)), device_id_type=BY_MESH
            )

        pl.semaphore_wait(barrier, self.experts + 1 + len(others))


def mover(sent, came):
    def move(src, dst, row, sent_at, came_at, where):
        return pltpu.make_async_remote_copy(
            src_ref=src,
            dst_ref=dst,
            send_sem=sent.at[row, sent_at],
            recv_sem=came.at[row, came_at],
            device_id=where,
            device_id_type=BY_MESH,
        )

    return move


class Dispatch:
    def __init__(self, place, move, base, send, landing):
        self.place, self.move, self.base = place, move, base
        self.send, self.landing = send, landing
        cap, width = landing.shape[1:]
        self.cap, self.half, self.side = cap, cap // 2, width // 2
        self.mine = place.part(place.core, self.half, 16)
        self.other = place.part(1 - place.core, self.half, 16)
        self.side_mine = place.part(place.chip, self.side, 128)
        self.side_other = place.part(1 - place.chip, self.side, 128)

    def z_copy(self, e, landed):
        return self.move(
            self.send.at[e],
            self.landing.at[landed, self.mine, self.side_mine],
            self.base,
            e,
            landed,
            self.place.home(e),
        )

    def build(self, i, key_row, source):
        e = self.place.take(i)
        hot = self.hot(e, self.place.core, key_row)
        self.send[e] = dot_rows(hot, source[:, self.side_mine]).astype(jnp.bfloat16)
        self.z_copy(e, self.place.me).start()

    def hot(self, e, part, key_row):
        slot = e * self.cap + part * self.half
        slot = slot + lax.broadcasted_iota(jnp.int32, (self.half, key_row.shape[1]), 0)
        hit = (key_row[0:1, :] == slot) | (key_row[1:2, :] == slot)
        return jnp.where(hit, 1.0, 0.0).astype(jnp.bfloat16)

    def build_own(self, key_row, source):
        @pl.loop(0, 2)
        def _(m):
            hot = self.hot(self.place.me, m, key_row)
            part = pl.ds(pl.multiple_of(m * self.half, 16), self.half)
            self.landing[self.place.me, part, :] = dot_rows(hot, source[...]).astype(jnp.bfloat16)

    def spread(self, step, s):
        rows, cols, where = (
            (self.mine, self.side_mine, self.place.across),
            (self.mine, self.side_mine, self.place.near),
            (self.mine, self.side_other, self.place.near),
        )[step]
        ref = self.landing.at[s, rows, cols]
        return self.move(ref, ref, self.base + 1 + step, s, s, where)

    def stage_a(self, i):
        self.landed(i)
        self.relay(i)

    def stage_b(self, i):
        s = self.place.take(i)
        self.spread(0, s).wait_recv()
        self.spread(2, s).start()

    def stage_c(self, i):
        s = self.place.take(i)
        self.spread(1, s).wait_recv()
        self.spread(2, s).wait_recv()

    def landed(self, i):
        s = self.place.take(i)
        self.z_copy(s, s).wait_recv()

    def relay(self, i):
        s = self.place.take(i)
        self.spread(0, s).start()
        self.spread(1, s).start()

    def finish(self, lo, hi, sends=True):
        @pl.loop(lo, hi)
        def _(i):
            s = self.place.take(i)
            for step in range(3):
                self.spread(step, s).wait_send()

        if sends:

            @pl.loop(1, self.place.experts)
            def _(i):
                self.z_copy(self.place.take(i), self.place.me).wait_send()


FRONT_OWN, FRONT_FAR, FRONT_CHIP = 4, 5, 6
FRONT_ROWS = 7
LATE = 1


def front_kernel(
    experts,
    capacity,
    counts,
    x_ref,
    cot_ref,
    routes_ref,
    slots_ref,
    gain1_ref,
    qkv_w,
    out_w,
    gain2_ref,
    router_ref,
    cots_ref,
    heads_hbm,
    attended_hbm,
    stats_hbm,
    mixed_hbm,
    low2_hbm,
    prob_hbm,
    gate_hbm,
    gate_send,
    heads_ref,
    attended_ref,
    stats_ref,
    mixed_ref,
    low2_ref,
    prob_ref,
    gate_ref,
    cot_send,
    gather,
    out_all,
    key_row,
    key_wide,
    route_wide,
    gate_wide,
    router_pad,
    loads,
    sent,
    came,
):
    rows, width = x_ref.shape
    images = counts.shape[0]
    patches = rows // images
    head_cols = out_w.shape[0]
    heads = head_cols // HEAD_DIM
    scale = HEAD_DIM ** (-0.5)
    place = Place(experts)
    move = mover(sent, came)
    cots = Dispatch(place, move, 0, cot_send, cots_ref)
    place.greet()
    key_row[...] = slot_keys(routes_ref, slots_ref, capacity, cots.cap)

    def share(ref, at):
        def copy(step):
            piece = ref(place.across_n if step == 2 else place.n)
            where = place.across if step == 0 else place.near
            row = (FRONT_CHIP, FRONT_OWN, FRONT_FAR)[step]
            return move(piece, piece, row, at, at, where)

        return copy

    out_share = share(lambda n: out_all.at[n], images)
    out_all[place.n] = out_w[...]
    out_share(0).start()
    out_share(1).start()

    @pl.loop(1, experts)
    def _(i):
        cots.build(i, key_row, cot_ref)

    tile = patches // 2

    @pl.loop(0, rows // tile)
    def _(t):
        part = pl.ds(pl.multiple_of(t * tile, 16), tile)
        normed, _, _ = normalize(x_ref[part, :].astype(jnp.float32), flat(gain1_ref))
        low = normed.astype(jnp.bfloat16)
        for i in range(3):
            block = dot_cols(low, qkv_w[i]).astype(jnp.bfloat16)
            for h in range(heads):
                heads_ref[i, h, part, :] = block[:, h * HEAD_DIM : (h + 1) * HEAD_DIM]

    outs = [
        pltpu.make_async_copy(src, dst, loads.at[at])
        for at, (src, dst) in enumerate(
            (
                (heads_ref, heads_hbm),
                (attended_ref, attended_hbm),
                (stats_ref, stats_hbm),
                (mixed_ref, mixed_hbm),
                (low2_ref, low2_hbm),
                (prob_ref, prob_hbm),
                (gate_ref, gate_hbm),
            )
        )
    ]
    outs[0].start()
    for k, column in enumerate(widen(key_row[...])):
        key_wide[k] = column
    for k, column in enumerate(widen(routes_ref[...])):
        route_wide[k] = column
    router_pad[...] = jnp.zeros_like(router_pad)
    router_pad[0:experts] = router_ref[...]
    stats_ref[...] = jnp.zeros_like(stats_ref)

    def attend(image):
        keys_at = pl.ds(pl.multiple_of(image * patches, 16), patches)
        pack = pl.ds(pl.multiple_of(image * tile, 16), tile)
        live = lax.broadcasted_iota(jnp.int32, (1, patches), 1) < counts[image]
        for h in range(heads):
            key_rows = heads_ref[1, h, keys_at, :]
            value_rows = heads_ref[2, h, keys_at, :]
            for t in range(patches // tile):
                part = pl.ds(pl.multiple_of(image * patches + t * tile, 16), tile)
                scores = dot_cols(heads_ref[0, h, part, :], key_rows) * scale
                scores = jnp.where(live, scores, MASKED_SCORE)
                top = jnp.max(scores, -1, keepdims=True)
                weights = jnp.exp(scores - top)
                total = jnp.sum(weights, -1, keepdims=True)
                probs = (weights * (1.0 / total)).astype(jnp.bfloat16)
                block = dot_rows(probs, value_rows).astype(jnp.bfloat16)
                at = t * head_cols + h * HEAD_DIM
                gather[place.n, pack, at : at + HEAD_DIM] = block
                attended_ref[part, h * HEAD_DIM : (h + 1) * HEAD_DIM] = block
                stats_ref[part, h : h + 1] = top + jnp.log(total)

    def image_share(image):
        pack = pl.ds(pl.multiple_of(image * tile, 16), tile)
        return share(lambda n: gather.at[n, pack, :], image)

    @pl.loop(0, images)
    def _(image):
        attend(image)
        image_share(image)(0).start()
        image_share(image)(1).start()

    outs[1].start()
    outs[2].start()
    out_share(0).wait_recv()
    out_share(2).start()
    cots.build_own(key_row, cot_ref)

    @pl.loop(1, experts - LATE)
    def _(i):
        cots.stage_a(i)

    out_share(1).wait_recv()
    out_share(2).wait_recv()

    def finish(image):
        copy = image_share(image)
        copy(0).wait_recv()
        copy(2).start()
        copy(1).wait_recv()
        copy(2).wait_recv()
        pack = pl.ds(pl.multiple_of(image * tile, 16), tile)

        for t in range(2):
            part = pl.ds(pl.multiple_of(image * patches + t * tile, 16), tile)
            cols = slice(t * head_cols, (t + 1) * head_cols)
            attention = dot_rows(gather[0, pack, cols], out_all[0])
            for n in range(1, 4):
                attention += dot_rows(gather[n, pack, cols], out_all[n])
            offset = t * tile + lax.broadcasted_iota(jnp.int32, (tile, 1), 0)
            mixed = x_ref[part, :].astype(jnp.float32) + jnp.where(
                offset < counts[image], attention, 0.0
            )
            mixed_ref[part, :] = mixed
            normed, _, _ = normalize(mixed, flat(gain2_ref))
            low = normed.astype(jnp.bfloat16)
            low2_ref[part, :] = low
            lane = lax.broadcasted_iota(jnp.int32, (tile, 128), 1)
            logits = jnp.where(lane < experts, dot_cols(low, router_pad[...]), MASKED_SCORE)
            powers = jnp.exp(logits - jnp.max(logits, -1, keepdims=True))
            prob = powers / jnp.sum(powers, -1, keepdims=True)
            prob_ref[part, :] = prob
            picked = [
                jnp.sum(jnp.where(lane == route_wide[k, part, :], prob, 0.0), 1, keepdims=True)
                for k in range(2)
            ]
            both = picked[0] + picked[1]
            gate_ref[part, :] = jnp.where(
                lane == 0, picked[0] / both, jnp.where(lane == 1, picked[1] / both, both)
            )

    @pl.loop(0, images)
    def _(image):
        finish(image)

    for out in outs[3:]:
        out.start()

    wide_cap = gate_send.shape[2]

    for k in range(2):
        gate_wide[k] = jnp.broadcast_to(gate_ref[:, k : k + 1], (rows, 128))

    @pl.loop(0, experts)
    def _(e):
        @pl.loop(0, wide_cap // 128)
        def _(j):
            lanes = pl.ds(pl.multiple_of(j * 128, 128), 128)
            slot = e * cots.cap + j * 128 + lax.broadcasted_iota(jnp.int32, (rows, 128), 1)
            picked = jnp.where(key_wide[0] == slot, gate_wide[0], 0.0) + jnp.where(
                key_wide[1] == slot, gate_wide[1], 0.0
            )
            gate_send[e, :, lanes] = jnp.broadcast_to(jnp.sum(picked, 0, keepdims=True), (8, 128))

    @pl.loop(1, experts - LATE)
    def _(i):
        cots.stage_b(i)

    @pl.loop(1, experts - LATE)
    def _(i):
        cots.stage_c(i)

    @pl.loop(experts - LATE, experts)
    def _(i):
        cots.landed(i)

    cots.finish(1, experts - LATE)
    for out in outs:
        out.wait()
    for step in range(3):
        out_share(step).wait_send()
        for image in range(images):
            image_share(image)(step).wait_send()


def front(
    counts, x, cot, routes, slots, gain1, qkv_w, out_w, gain2, router, experts, capacity, cap
):
    rows, width = x.shape
    head_cols = out_w.shape[0]
    heads = head_cols // HEAD_DIM
    images = counts.shape[0]
    bf16, f32 = jnp.bfloat16, jnp.float32
    vmem = pl.BlockSpec(memory_space=pltpu.VMEM)
    hbm = pl.BlockSpec(memory_space=pl.ANY)
    table = max(experts, images + 1)
    wide_cap = round_up(cap, 128)
    return pl.pallas_call(
        functools.partial(front_kernel, experts, capacity),
        out_shape=[
            jax.ShapeDtypeStruct((experts, cap, width), bf16),
            jax.ShapeDtypeStruct((3, heads, rows, HEAD_DIM), bf16),
            jax.ShapeDtypeStruct((rows, head_cols), bf16),
            jax.ShapeDtypeStruct((rows, 128), f32),
            jax.ShapeDtypeStruct((rows, width), f32),
            jax.ShapeDtypeStruct((rows, width), bf16),
            jax.ShapeDtypeStruct((rows, 128), f32),
            jax.ShapeDtypeStruct((rows, 128), f32),
            jax.ShapeDtypeStruct((experts, 8, wide_cap), f32),
        ],
        in_specs=[pl.BlockSpec(memory_space=pltpu.SMEM)] + [vmem] * 9,
        out_specs=[vmem] + [hbm] * 7 + [vmem],
        scratch_shapes=[
            pltpu.VMEM((3, heads, rows, HEAD_DIM), bf16),
            pltpu.VMEM((rows, head_cols), bf16),
            pltpu.VMEM((rows, 128), f32),
            pltpu.VMEM((rows, width), f32),
            pltpu.VMEM((rows, width), bf16),
            pltpu.VMEM((rows, 128), f32),
            pltpu.VMEM((rows, 128), f32),
            pltpu.VMEM((experts, cap // 2, width // 2), bf16),
            pltpu.VMEM((4, rows // 2, 2 * head_cols), bf16),
            pltpu.VMEM((4, head_cols, width), bf16),
            pltpu.VMEM((2, rows), jnp.int32),
            pltpu.VMEM((2, rows, 128), jnp.int32),
            pltpu.VMEM((2, rows, 128), jnp.int32),
            pltpu.VMEM((2, rows, 128), f32),
            pltpu.VMEM((128, width), bf16),
            pltpu.SemaphoreType.DMA((7,)),
            pltpu.SemaphoreType.DMA((FRONT_ROWS, table)),
            pltpu.SemaphoreType.DMA((FRONT_ROWS, table)),
        ],
        compiler_params=pltpu.CompilerParams(
            collective_id=2, has_side_effects=True, vmem_limit_bytes=VMEM_BYTES
        ),
    )(counts, x, cot, routes, slots, gain1, qkv_w, out_w, gain2, router)


class Return:
    def __init__(self, place, move, base, core_send, core_recv, kept, chip_send, chip_recv, back):
        self.place, self.move, self.base = place, move, base
        self.core_send, self.core_recv, self.kept = core_send, core_recv, kept
        self.chip_send, self.chip_recv, self.back = chip_send, chip_recv, back
        self.half, self.side = chip_send.shape[1:]
        self.mine = place.part(place.core, self.half, 16)
        self.other = place.part(1 - place.core, self.half, 16)
        self.side_mine = place.part(place.chip, self.side, 128)
        self.side_other = place.part(1 - place.chip, self.side, 128)

    def rows(self, s):
        return pl.ds(pl.multiple_of(s * self.half, 16), self.half)

    def core_move(self, s):
        return self.move(
            self.core_send.at[s], self.core_recv.at[s], self.base, s, s, self.place.near
        )

    def chip_move(self, s):
        return self.move(
            self.chip_send.at[s], self.chip_recv.at[s], self.base + 1, s, s, self.place.across
        )

    def home_move(self, s, landed):
        return self.move(
            self.core_send.at[s, :, pl.ds(0, self.side)],
            self.back.at[landed, self.mine, :],
            self.base + 2,
            s,
            landed,
            self.place.home(s),
        )

    def pair_move(self, e, part):
        ref = self.back.at[e, part, :]
        return self.move(ref, ref, self.base + 3, e, e, self.place.near)

    def first(self, s, product):
        self.core_send[s] = product(self.other).astype(jnp.bfloat16)
        self.core_move(s).start()
        self.kept[self.rows(s), :] = product(self.mine)

    def second(self, s):
        self.core_move(s).wait_recv()
        self.chip_send[s] = (
            self.kept[self.rows(s), self.side_other]
            + self.core_recv[s, :, self.side_other].astype(jnp.float32)
        ).astype(jnp.bfloat16)
        self.chip_move(s).start()

    def third(self, s):
        self.chip_move(s).wait_recv()
        self.core_move(s).wait_send()
        piece = (
            self.kept[self.rows(s), self.side_mine]
            + self.core_recv[s, :, self.side_mine].astype(jnp.float32)
            + self.chip_recv[s].astype(jnp.float32)
        ).astype(jnp.bfloat16)

        @pl.when(s == self.place.me)
        def _():
            self.back[self.place.me, self.mine, :] = piece

        @pl.when(s != self.place.me)
        def _():
            self.core_send[s, :, 0 : self.side] = piece
            self.home_move(s, self.place.me).start()

    def fourth(self, i):
        e = self.place.take(i)

        @pl.when(e != self.place.me)
        def _():
            self.home_move(e, e).wait_recv()

        self.pair_move(e, self.mine).start()

    def ready(self, i):
        self.pair_move(self.place.take(i), self.other).wait_recv()

    def finish(self):
        @pl.loop(0, self.place.experts)
        def _(i):
            s = self.place.take(i)
            self.chip_move(s).wait_send()
            self.pair_move(s, self.mine).wait_send()

            @pl.when(i > 0)
            def _():
                self.home_move(s, self.place.me).wait_send()


class Quarters:
    def __init__(self, place, move, base, at, ref):
        self.place, self.move, self.base, self.at, self.ref = place, move, base, at, ref
        rows, width = ref.shape
        self.rows = place.part(place.core, rows // 2, 16)
        self.mine = place.part(place.chip, width // 2, 128)
        self.other = place.part(1 - place.chip, width // 2, 128)

    def copy(self, step):
        ref = self.ref.at[self.rows, self.other if step == 2 else self.mine]
        where = self.place.across if step == 0 else self.place.near
        return self.move(ref, ref, self.base + step, self.at, self.at, where)

    def start(self):
        self.copy(0).start()
        self.copy(1).start()

    def relay(self):
        self.copy(0).wait_recv()
        self.copy(2).start()

    def ready(self):
        self.copy(1).wait_recv()
        self.copy(2).wait_recv()

    def finish(self):
        for step in range(3):
            self.copy(step).wait_send()


M_CORE, M_CHIP, M_HOME, M_BACK, M_MIX, M_END, M_PAIR, M_LATE, M_GATES = 4, 5, 6, 7, 11, 13, 16, 17, 21
M_ROWS = 22
GRAD_PARTS, GRAD_EARLY = 4, 2


def middle_kernel(
    experts,
    capacity,
    counts,
    low_ref,
    cot_hbm,
    routes_ref,
    slots_ref,
    gate_col,
    gate_send,
    in_hbm,
    out_hbm,
    cots_hbm,
    mixed_hbm,
    prob_ref,
    gain_ref,
    router_ref,
    half_hbm,
    mixed_grad_hbm,
    att_grad_hbm,
    router_grad,
    gain_grad,
    grad_out,
    grad_in,
    in_ref,
    out_ref,
    cots_ref,
    rows_ref,
    hid_ref,
    pre_ref,
    send_rows,
    gate_rows,
    gate_tall,
    pair_tall,
    pair_part,
    pair_core,
    pair_sum,
    pair_chip,
    pair_home,
    pair_back,
    core_send,
    core_recv,
    kept,
    chip_send,
    chip_recv,
    back,
    mix_send,
    mix_recv,
    mix_last,
    key_row,
    key_wide,
    route_wide,
    router_pad,
    hot_ref,
    total,
    pair_ref,
    dis_ref,
    copy_send,
    copy_recv,
    in_send,
    in_recv,
    cot_tile,
    scale_wide,
    loads,
    cot_loads,
    sent,
    came,
):
    rows, width = low_ref.shape
    images = counts.shape[0]
    patches = rows // images
    cap = rows_ref.shape[1]
    half = cap // 2
    units = in_ref.shape[1]
    place = Place(experts)
    move = mover(sent, came)
    me = place.me
    lows = Dispatch(place, move, 0, send_rows, rows_ref)
    late = Dispatch(place, move, M_LATE, send_rows, cots_ref)
    dgrad = Return(
        place, move, M_BACK, core_send, core_recv, kept, chip_send, chip_recv, back
    )
    other_copy = {"narrow": place.n, "wide": place.w + 1 - 2 * place.parity}

    def load(at, src, dst):
        return pltpu.make_async_copy(src, dst, loads.at[at])

    fetched = [
        load(0, in_hbm, in_ref),
        load(1, out_hbm, out_ref),
    ]
    for copy in fetched:
        copy.start()

    def cots_in(i, whole):
        s = place.take(i)
        at = (s,) if whole else (s, late.mine, late.side_mine)
        return pltpu.make_async_copy(cots_hbm.at[at], cots_ref.at[at], cot_loads.at[i])

    @pl.loop(0, experts - LATE)
    def _(i):
        cots_in(i, True).start()

    for i in range(experts - LATE, experts):
        cots_in(i, False).start()
    place.greet((other_copy,))
    key_row[...] = slot_keys(routes_ref, slots_ref, capacity, cap)

    def gate_copy(e, landed):
        return move(gate_send.at[e], gate_rows.at[landed], M_GATES, e, landed, place.home(e))

    @pl.loop(1, experts)
    def _(i):
        lows.build(i, key_row, low_ref)
        gate_copy(place.take(i), me).start()

    gate_rows[me] = gate_send[me]

    for copy in fetched:
        copy.wait()

    @pl.loop(0, experts - LATE)
    def _(i):
        cots_in(i, True).wait()

    for i in range(experts - LATE, experts):
        cots_in(i, False).wait()
        late.relay(i)

    lows.build_own(key_row, low_ref)
    pair_tall[...] = jnp.zeros_like(pair_tall)
    grad_out[...] = jnp.zeros_like(grad_out)
    grad_in[...] = jnp.zeros_like(grad_in)
    for k, column in enumerate(widen(key_row[...])):
        key_wide[k] = column
    for k, column in enumerate(widen(routes_ref[...])):
        route_wide[k] = column
    router_pad[...] = jnp.zeros_like(router_pad)
    router_pad[0:experts] = router_ref[...]

    def pair_move(step, s):
        src, dst, row, where = (
            (pair_part, pair_core, M_CORE, place.near),
            (pair_sum, pair_chip, M_CHIP, place.across),
        )[step]
        return move(src.at[s], dst.at[s], row, s, s, where)

    def pair_return(s, landed):
        return move(pair_home.at[s], pair_back.at[landed], M_HOME, s, landed, place.home(s))

    chunk = 256 if units % 256 == 0 else units

    def compute(s, m):
        part = pl.ds(m * half, half)
        left = rows_ref[s, part, :]
        cots = cots_ref[s, part, :]
        gate = gate_tall[part, 0:1]
        pair = jnp.zeros((half, 1), jnp.float32)
        for j in range(units // chunk):
            cols = slice(j * chunk, (j + 1) * chunk)
            pre = dot_rows(left, in_ref[:, cols])
            free = dot_cols(cots, out_ref[cols, :])
            cdf, slope = normal_parts(pre)
            hidden = pre * cdf
            hid_ref[s, part, cols] = (gate * hidden).astype(jnp.bfloat16)
            pre_ref[s, part, cols] = (gate * free * (cdf + slope)).astype(jnp.bfloat16)
            pair += jnp.sum(hidden * free, 1, keepdims=True)
        pair_tall[part, :] = jnp.broadcast_to(pair, (half, 128))

    def second(s):
        dgrad.second(s)
        pair_move(0, s).wait_recv()
        pair_sum[s] = pair_part[s] + pair_core[s]
        pair_move(1, s).start()

    def third(s):
        dgrad.third(s)
        pair_move(1, s).wait_recv()
        line = pair_sum[s] + pair_chip[s]

        @pl.when(s == me)
        def _():
            pair_back[me] = line

        @pl.when(s != me)
        def _():
            pair_home[s] = line
            pair_return(s, me).start()

    def contract(left, right):
        return lax.dot_general(
            left, right, (((0,), (0,)), ((), ())), preferred_element_type=jnp.float32
        )

    def mix_move(s):
        return move(mix_send.at[s], mix_recv.at[s], M_MIX, s, s, place.near)

    def mix_chip(s):
        src = mix_recv.at[s, :, dgrad.side_other]
        return move(src, mix_last.at[s], M_MIX + 1, s, s, place.across)

    def mix_first(s):
        mix_send[s] = dot_rows(hid_ref[s, dgrad.other, :], out_ref[...]).astype(jnp.bfloat16)
        mix_move(s).start()

    def mix_second(s):
        mix_move(s).wait_recv()
        mix_recv[s] = (
            dot_rows(hid_ref[s, dgrad.mine, :], out_ref[...]) + mix_recv[s].astype(jnp.float32)
        ).astype(jnp.bfloat16)

    def mix_third(s):
        mix_chip(s).wait_recv()
        mix_last[s] = (
            mix_recv[s, :, dgrad.side_mine].astype(jnp.float32) + mix_last[s].astype(jnp.float32)
        ).astype(jnp.bfloat16)

    def work(i, between):
        s = place.take(i)
        gate_tall[...] = jnp.transpose(gate_rows[s])
        compute(s, 0)
        between()
        compute(s, 1)
        pair_part[s] = jnp.transpose(pair_tall[...])[0:8]
        pair_move(0, s).start()
        dgrad.first(s, lambda part: dot_cols(pre_ref[s, part, :], in_ref[...]))

    def add_out(lo, hi):
        @pl.loop(lo, hi)
        def _(i):
            s = place.take(i)
            grad_out[...] += contract(hid_ref[s], cots_ref[s])

    def add_in(lo, hi):
        @pl.loop(lo, hi)
        def _(i):
            s = place.take(i)
            grad_in[...] += contract(rows_ref[s], pre_ref[s])

    def pass_on(i):
        @pl.when(i + 1 < experts)
        def _():
            lows.stage_a(i + 1)

    work(0, lambda: None)
    lows.stage_a(1)
    second(place.take(0))
    mix_first(place.take(0))
    add_out(0, 1)
    add_in(0, 1)

    @pl.loop(experts - LATE, experts)
    def _(i):
        late.stage_b(i)

    @pl.loop(1, experts)
    def _(i):
        lows.stage_b(i)
        lows.stage_c(i)

        @pl.when(i >= experts - LATE)
        def _():
            late.stage_c(i)

        s = place.take(i)
        gate_copy(s, s).wait_recv()
        work(i, lambda: pass_on(i))

        @pl.when(i == 1)
        def _():
            mix_second(place.take(0))

        second(s)

        @pl.when(i > 1)
        def _():
            third(place.take(i - 2))

    last = place.take(experts - 1)
    mix_chip(place.take(0)).start()
    mix_first(place.take(1))
    third(place.take(experts - 2))
    add_out(1, experts)
    mix_second(place.take(1))
    copy_send[...] = grad_out[...].astype(jnp.bfloat16)
    copy_move = move(copy_send, copy_recv, M_PAIR, 0, 0, other_copy)
    copy_move.start()
    third(last)
    early = 2
    mix_chip(place.take(1)).start()

    @pl.loop(early, experts)
    def _(i):
        mix_first(place.take(i))

    pair_ref[...] = jnp.zeros_like(pair_ref)

    def build_hot(e):
        lane = lax.broadcasted_iota(jnp.int32, (rows // 4, 128), 1)

        @pl.loop(0, 4)
        def _(m):
            part = pl.ds(pl.multiple_of(m * (rows // 4), 16), rows // 4)
            keys = [key_wide[k, part, :] - e * cap for k in range(2)]
            for low in range(0, cap, 128):
                size = min(128, cap - low)
                hit = (keys[0] == lane + low) | (keys[1] == lane + low)
                hot_ref[part, low : low + size] = jnp.where(hit, 1.0, 0.0).astype(jnp.bfloat16)[
                    :, 0:size
                ]

    my_rows = place.part(place.core, rows // 2, 16)
    total[...] = jnp.zeros_like(total)

    @pl.loop(0, experts)
    def _(i):
        e = place.take(i)
        build_hot(e)
        dgrad.fourth(i)

        @pl.when(i > 0)
        def _():
            pair_return(e, e).wait_recv()

        tall = jnp.transpose(pair_back[e])[0:cap, 0:1]
        high = tall.astype(jnp.bfloat16).astype(jnp.float32)
        middle = (tall - high).astype(jnp.bfloat16).astype(jnp.float32)
        lane = lax.broadcasted_iota(jnp.int32, (cap, 128), 1)
        spelled = jnp.where(
            lane == 0, high, jnp.where(lane == 1, middle, jnp.where(lane == 2, tall - high - middle, 0.0))
        ).astype(jnp.bfloat16)
        found = jnp.sum(dot_rows(hot_ref[...], spelled), 1, keepdims=True)
        lane_rows = lax.broadcasted_iota(jnp.int32, (rows, 128), 1)
        pair_ref[...] += jnp.where(lane_rows == e, found, 0.0)
        dgrad.ready(i)
        total[...] += dot_rows(hot_ref[my_rows, :], back[e])

    ends = Quarters(place, move, M_END, 0, dis_ref)
    dis_ref[ends.rows, ends.mine] = total[...].astype(jnp.bfloat16)
    ends.start()

    @pl.loop(early, experts)
    def _(i):
        s = place.take(i)
        mix_second(s)
        mix_chip(s).start()

    add_in(1, experts)
    early_rows = in_send.shape[0]
    in_send[...] = grad_in[0:early_rows].astype(jnp.bfloat16)
    in_move = move(in_send, in_recv, M_PAIR, 1, 1, other_copy)
    in_move.start()
    mixed_in = load(1, mixed_hbm, kept.at[pl.ds(0, rows), :])
    mixed_in.start()
    tile = patches // 2
    router_grad[...] = jnp.zeros_like(router_grad)
    gain_grad[...] = jnp.zeros_like(gain_grad)

    def cot_in(t):
        slot = lax.rem(t, 2)
        part = pl.ds(pl.multiple_of(t * tile, 16), tile)
        return pltpu.make_async_copy(cot_hbm.at[part, :], cot_tile.at[slot], loads.at[2 + slot])

    def rows_out(t, what):
        part = pl.ds(pl.multiple_of(t * tile, 16), tile)
        src, dst = ((kept, mixed_grad_hbm), (dis_ref, att_grad_hbm))[what]
        return pltpu.make_async_copy(src.at[part, :], dst.at[part, :], loads.at[4 + 2 * t + what])

    cot_in(0).start()
    mixed_in.wait()

    def before(t):
        part = pl.ds(pl.multiple_of(t * tile, 16), tile)
        lane = lax.broadcasted_iota(jnp.int32, (tile, 128), 1)
        by_expert = pair_ref[part, :]
        hots = [lane == route_wide[k, part, :] for k in range(2)]
        pair = [jnp.sum(jnp.where(hot, by_expert, 0.0), 1, keepdims=True) for hot in hots]
        weighted = pair[0] * gate_col[part, 0:1] + pair[1] * gate_col[part, 1:2]
        both = gate_col[part, 2:3]
        prob = prob_ref[part, :]
        prob_grad = jnp.where(hots[0], (pair[0] - weighted) / both, 0.0) + jnp.where(
            hots[1], (pair[1] - weighted) / both, 0.0
        )
        logit_grad = prob * (prob_grad - jnp.sum(prob * prob_grad, 1, keepdims=True))
        pair_ref[part, :] = logit_grad
        router_grad[...] += contract(logit_grad.astype(jnp.bfloat16), low_ref[part, :])
        _, hat, scaled = normalize(kept[part, :], flat(gain_ref))
        kept[part, :] = hat
        scale_wide[part, :] = jnp.broadcast_to(scaled, (tile, 128))

    @pl.loop(0, 2)
    def _(t):
        before(t)

    ends.relay()

    @pl.loop(2, rows // tile)
    def _(t):
        before(t)

    @pl.loop(0, early)
    def _(i):
        mix_third(place.take(i))

    ends.ready()
    ends.finish()

    @pl.loop(0, rows // tile)
    def _(t):
        @pl.when(t + 1 < rows // tile)
        def _():
            cot_in(t + 1).start()

        part = pl.ds(pl.multiple_of(t * tile, 16), tile)
        normed_grad = dis_ref[part, :].astype(jnp.float32) + dot_rows(
            pair_ref[part, :].astype(jnp.bfloat16), router_pad[...]
        )
        hat = kept[part, :]
        gain_grad[...] += jnp.sum(normed_grad * hat, 0, keepdims=True)
        grad = normed_grad * flat(gain_ref)
        inner = (
            grad - jnp.mean(grad, -1, keepdims=True) - hat * jnp.mean(grad * hat, -1, keepdims=True)
        )
        cot_in(t).wait()
        full = cot_tile[lax.rem(t, 2)].astype(jnp.float32) + scale_wide[part, 0:1] * inner
        kept[part, :] = full
        rows_out(t, 0).start()
        row = t * tile + lax.broadcasted_iota(jnp.int32, (tile, 1), 0)
        live = lax.rem(row, patches) < jnp.where(t * tile < patches, counts[0], counts[images - 1])
        dis_ref[part, :] = jnp.where(live, full, 0.0).astype(jnp.bfloat16)
        rows_out(t, 1).start()

    @pl.loop(early, experts)
    def _(i):
        mix_third(place.take(i))

    half_out = load(0, mix_last, half_hbm)
    half_out.start()
    copy_move.wait()
    grad_out[...] += copy_recv[...].astype(jnp.float32)
    in_move.wait()
    grad_in[0:early_rows] += in_recv[...].astype(jnp.float32)
    half_out.wait()

    @pl.loop(0, rows // tile)
    def _(t):
        rows_out(t, 0).wait()
        rows_out(t, 1).wait()

    dgrad.finish()
    lows.finish(1, experts)
    late.finish(experts - LATE, experts, False)

    @pl.loop(0, experts)
    def _(i):
        s = place.take(i)
        pair_move(0, s).wait_send()
        pair_move(1, s).wait_send()
        mix_move(s).wait_send()
        mix_chip(s).wait_send()

        @pl.when(i > 0)
        def _():
            pair_return(s, me).wait_send()
            gate_copy(s, me).wait_send()


def middle(
    counts,
    low,
    cot,
    routes,
    slots,
    gates,
    gate_rows,
    weight_in,
    weight_out,
    cots,
    mixed,
    prob,
    gain,
    router,
    experts,
    capacity,
):
    rows, width = low.shape
    units = weight_in.shape[1]
    cap = cots.shape[1]
    half, side, wide_cap = cap // 2, width // 2, round_up(cap, 128)
    bf16, f32 = jnp.bfloat16, jnp.float32
    vmem = pl.BlockSpec(memory_space=pltpu.VMEM)
    hbm = pl.BlockSpec(memory_space=pl.ANY)
    line = pltpu.VMEM((experts, 8, wide_cap), f32)
    halves = pltpu.VMEM((experts, half, width), bf16)
    tile = rows // counts.shape[0] // 2
    return pl.pallas_call(
        functools.partial(middle_kernel, experts, capacity),
        out_shape=[
            jax.ShapeDtypeStruct((experts, half, side), bf16),
            jax.ShapeDtypeStruct((rows, width), f32),
            jax.ShapeDtypeStruct((rows, width), bf16),
            jax.ShapeDtypeStruct((128, width), f32),
            jax.ShapeDtypeStruct((1, width), f32),
            jax.ShapeDtypeStruct((units, width), f32),
            jax.ShapeDtypeStruct((width, units), f32),
        ],
        in_specs=[
            pl.BlockSpec(memory_space=pltpu.SMEM),
            vmem,
            hbm,
            vmem,
            vmem,
            vmem,
            vmem,
            hbm,
            hbm,
            hbm,
            hbm,
            vmem,
            vmem,
            vmem,
        ],
        out_specs=[hbm] * 3 + [vmem] * 4,
        scratch_shapes=[
            pltpu.VMEM((width, units), bf16),
            pltpu.VMEM((units, width), bf16),
            pltpu.VMEM((experts, cap, width), bf16),
            pltpu.VMEM((experts, cap, width), bf16),
            pltpu.VMEM((experts, cap, units), bf16),
            pltpu.VMEM((experts, cap, units), bf16),
            pltpu.VMEM((experts, half, side), bf16),
            line,
            pltpu.VMEM((wide_cap, 8), f32),
            pltpu.VMEM((wide_cap, 128), f32),
            line,
            line,
            line,
            line,
            line,
            line,
            halves,
            halves,
            pltpu.VMEM((max(experts * half, rows), width), f32),
            pltpu.VMEM((experts, half, side), bf16),
            pltpu.VMEM((experts, half, side), bf16),
            pltpu.VMEM((experts, cap, side), bf16),
            halves,
            halves,
            pltpu.VMEM((experts, half, side), bf16),
            pltpu.VMEM((2, rows), jnp.int32),
            pltpu.VMEM((2, rows, 128), jnp.int32),
            pltpu.VMEM((2, rows, 128), jnp.int32),
            pltpu.VMEM((128, width), bf16),
            pltpu.VMEM((rows, cap), bf16),
            pltpu.VMEM((rows // 2, side), f32),
            pltpu.VMEM((rows, 128), f32),
            pltpu.VMEM((rows, width), bf16),
            pltpu.VMEM((units, width), bf16),
            pltpu.VMEM((units, width), bf16),
            pltpu.VMEM((width * GRAD_EARLY // GRAD_PARTS, units), bf16),
            pltpu.VMEM((width * GRAD_EARLY // GRAD_PARTS, units), bf16),
            pltpu.VMEM((2, tile, width), bf16),
            pltpu.VMEM((rows, 128), f32),
            pltpu.SemaphoreType.DMA((4 + 2 * (rows // tile),)),
            pltpu.SemaphoreType.DMA((experts,)),
            pltpu.SemaphoreType.DMA((M_ROWS, experts)),
            pltpu.SemaphoreType.DMA((M_ROWS, experts)),
        ],
        compiler_params=pltpu.CompilerParams(
            collective_id=1, has_side_effects=True, vmem_limit_bytes=VMEM_BYTES
        ),
    )(
        counts,
        low,
        cot,
        routes,
        slots,
        gates,
        gate_rows,
        weight_in,
        weight_out,
        cots,
        mixed,
        prob,
        gain,
        router,
    )


class Fold:
    def __init__(self, place, move, base, core_send, core_recv, kept, chip_send, chip_recv, whole):
        self.place, self.move, self.base = place, move, base
        self.core_send, self.core_recv, self.kept = core_send, core_recv, kept
        self.chip_send, self.chip_recv, self.whole = chip_send, chip_recv, whole
        self.half, self.side = chip_send.shape[1:]
        self.side_mine = place.part(place.chip, self.side, 128)
        self.side_other = place.part(1 - place.chip, self.side, 128)

    def rows(self, image, core):
        start = (2 * image + core) * self.half
        return pl.ds(pl.multiple_of(start, 16), self.half)

    def core_move(self, image):
        return self.move(
            self.core_send.at[image],
            self.core_recv.at[image],
            self.base,
            image,
            image,
            self.place.near,
        )

    def chip_move(self, image):
        return self.move(
            self.chip_send.at[image],
            self.chip_recv.at[image],
            self.base + 1,
            image,
            image,
            self.place.across,
        )

    def share(self, image, step):
        cols = self.side_other if step == 2 else self.side_mine
        ref = self.whole.at[self.rows(image, self.place.core), cols]
        where = self.place.across if step == 0 else self.place.near
        return self.move(ref, ref, self.base + 2 + step, image, image, where)

    def second(self, image):
        self.core_move(image).wait_recv()
        self.chip_send[image] = (
            self.kept[image, :, self.side_other]
            + self.core_recv[image, :, self.side_other].astype(jnp.float32)
        ).astype(jnp.bfloat16)
        self.chip_move(image).start()

    def third(self, image):
        self.chip_move(image).wait_recv()
        self.whole[self.rows(image, self.place.core), self.side_mine] = (
            self.kept[image, :, self.side_mine]
            + self.core_recv[image, :, self.side_mine].astype(jnp.float32)
            + self.chip_recv[image].astype(jnp.float32)
        ).astype(jnp.bfloat16)
        self.share(image, 0).start()
        self.share(image, 1).start()

    def relay(self, image):
        self.share(image, 0).wait_recv()
        self.share(image, 2).start()

    def ready(self, image):
        self.share(image, 1).wait_recv()
        self.share(image, 2).wait_recv()

    def finish(self, images):
        for image in range(images):
            self.core_move(image).wait_send()
            self.chip_move(image).wait_send()
            for step in range(3):
                self.share(image, step).wait_send()


class WideSum:
    def __init__(self, place, move, tables, pair_send, pair_recv, kept, group_send, group_recv, whole):
        self.place, self.move = place, move
        self.pair_sems, self.group_out, self.group_in = tables
        self.pair_send, self.pair_recv, self.kept = pair_send, pair_recv, kept
        self.group_send, self.group_recv, self.whole = group_send, group_recv, whole
        self.rows, self.cols = group_recv.shape[2:]
        self.half = pair_send.shape[1]
        self.real = kept.shape[1]
        self.pair = {"narrow": place.n, "wide": place.w + 1 - 2 * place.parity}

    def pair_move(self, p):
        return self.move[0](
            self.pair_send.at[p], self.pair_recv.at[p], 0, p, p, self.pair
        )

    def chunk(self, e):
        return (
            pl.ds(pl.multiple_of((e // 2) * self.rows, 16), self.rows),
            pl.ds(pl.multiple_of(lax.rem(e, 2) * self.cols, 128), self.cols),
        )

    def group_move(self, p, e, landed):
        rows, cols = self.chunk(e)
        return self.move[1](
            self.group_send.at[p, rows, cols],
            self.group_recv.at[p, landed],
            p,
            e,
            landed,
            self.place.home(e),
        )

    def group_share(self, p, owner, at, landed, where):
        rows, cols = self.chunk(owner)
        ref = self.whole.at[p, self.place.parity, rows, cols]
        pieces = self.pair_send.shape[0]
        return self.move[1](ref, ref, pieces + p, at, landed, where)

    def pair_share(self, p, parity):
        ref = self.whole.at[p, parity]
        return self.move[0](ref, ref, 1, p, p, self.pair)

    def first(self, p, halves):
        @pl.when(self.place.parity == 0)
        def _():
            self.kept[p] = halves[0]
            self.pair_send[p, 0 : self.real] = halves[1].astype(jnp.bfloat16)

        @pl.when(self.place.parity == 1)
        def _():
            self.kept[p] = halves[1]
            self.pair_send[p, 0 : self.real] = halves[0].astype(jnp.bfloat16)

        self.pair_move(p).start()

    def second(self, p):
        self.pair_move(p).wait_recv()
        self.group_send[p, 0 : self.real] = (
            self.kept[p] + self.pair_recv[p, 0 : self.real].astype(jnp.float32)
        ).astype(jnp.bfloat16)

        @pl.loop(1, self.place.experts)
        def _(i):
            self.group_move(p, self.place.take(i), self.place.me).start()

    def third(self, p):
        rows, cols = self.chunk(self.place.me)
        total = self.group_send[p, rows, cols].astype(jnp.float32)
        self.total[...] = total

        @pl.loop(1, self.place.experts)
        def _(i):
            s = self.place.take(i)
            self.group_move(p, s, s).wait_recv()
            self.total[...] += self.group_recv[p, s].astype(jnp.float32)

        self.whole[p, self.place.parity, rows, cols] = self.total[...].astype(jnp.bfloat16)

        @pl.loop(1, self.place.experts)
        def _(i):
            e = self.place.take(i)
            self.group_share(p, self.place.me, e, self.place.me, self.place.home(e)).start()

    def fourth(self, p):
        @pl.loop(1, self.place.experts)
        def _(i):
            s = self.place.take(i)
            self.group_share(p, s, s, s, self.place.home(s)).wait_recv()

        self.pair_share(p, self.place.parity).start()

    def ready(self, p):
        self.pair_share(p, 1 - self.place.parity).wait_recv()

    def finish(self):
        for p in range(self.pair_send.shape[0]):
            self.pair_move(p).wait_send()
            self.pair_share(p, self.place.parity).wait_send()

            @pl.loop(1, self.place.experts)
            def _(i):
                e = self.place.take(i)
                self.group_move(p, e, self.place.me).wait_send()
                self.group_share(p, self.place.me, e, self.place.me, self.place.home(e)).wait_send()


B_MIX, B_ENDMIX, B_FOLD, B_SMALL, B_GRAD = 0, 3, 6, 11, 13
B_ROWS = 14


def back_kernel(
    experts,
    capacity,
    counts,
    att_grad,
    mixed_grad_hbm,
    heads_ref,
    stats_ref,
    attended_ref,
    x_ref,
    gain_ref,
    qkv_w,
    out_w,
    mixed_hbm,
    half_ref,
    routes_ref,
    slots_ref,
    router_part,
    gain2_part,
    grad_hbm,
    out_ref,
    x_grad_hbm,
    in_grad,
    out_grad,
    small_out,
    grad_sum_hbm,
    grad_sum,
    mixed_part,
    x_grad,
    grad_send,
    grad_recv,
    whole_ref,
    loads,
    low_ref,
    lines,
    head_grad,
    proj_grad,
    key_wide,
    back,
    hot_ref,
    total,
    fold_send,
    fold_recv,
    fold_kept,
    fold_chip_send,
    fold_chip_recv,
    normed_ref,
    pair_send,
    pair_recv,
    pair_kept,
    group_send,
    group_recv,
    group_total,
    small_ref,
    small_near,
    small_far,
    small_pair,
    small_group,
    small_steps,
    sent,
    came,
    pair_sent,
    pair_came,
    group_sent,
    group_came,
):
    rows, width = att_grad.shape
    images = counts.shape[0]
    patches = rows // images
    head_cols = attended_ref.shape[1]
    heads = head_cols // HEAD_DIM
    scale = HEAD_DIM ** (-0.5)
    cap = back.shape[1]
    tile = patches // 2
    pieces = heads + 1
    place = Place(experts)
    move = mover(sent, came)
    me = place.me
    wide = WideSum(
        place,
        (mover(pair_sent, pair_came), mover(group_sent, group_came)),
        (None, None, None),
        pair_send,
        pair_recv,
        pair_kept,
        group_send,
        group_recv,
        whole_ref,
    )
    wide.total = group_total
    fold = Fold(
        place,
        move,
        B_FOLD,
        fold_send,
        fold_recv,
        fold_kept,
        fold_chip_send,
        fold_chip_recv,
        normed_ref,
    )
    my_rows = place.part(place.core, rows // 2, 16)
    side_mine = place.part(place.chip, width // 2, 128)

    def load(at, src, dst):
        return pltpu.make_async_copy(src, dst, loads.at[at])

    grad_in = load(0, grad_hbm, grad_sum)
    mixed_in = load(1, mixed_hbm.at[my_rows, side_mine], mixed_part)
    mixed_grad_in = load(2, mixed_grad_hbm, x_grad)
    grad_in.start()
    mixed_in.start()
    mixed_grad_in.start()
    place.greet((wide.pair,))

    def grad_part(k):
        size = grad_sum.shape[0] // GRAD_PARTS
        return pl.ds(k * size, size)

    def grad_move(k):
        part = grad_part(k)
        return move(grad_send.at[part, :], grad_recv.at[part, :], B_GRAD, k, k, wide.pair)

    def grad_go(k):
        part = grad_part(k)
        grad_send[part, :] = grad_sum[part, :].astype(jnp.bfloat16)
        grad_move(k).start()

    def grad_out(k):
        part = grad_part(k)
        return load(3 + 2 * images + k, grad_sum.at[part, :], grad_sum_hbm.at[part, :])

    def grad_end(k):
        part = grad_part(k)
        grad_move(k).wait()
        grad_sum[part, :] += grad_recv[part, :].astype(jnp.float32)
        grad_out(k).start()

    half = half_ref.shape[1]
    mine = place.part(place.core, half, 16)
    other = place.part(1 - place.core, half, 16)

    def mix_home(s, landed):
        return move(half_ref.at[s], back.at[landed, mine, :], B_MIX + 1, s, landed, place.home(s))

    def mix_near(e, part):
        ref = back.at[e, part, :]
        return move(ref, ref, B_MIX + 2, e, e, place.near)

    @pl.loop(1, experts)
    def _(i):
        mix_home(place.take(i), me).start()

    back[me, mine, :] = half_ref[me]
    grad_in.wait()
    for k in range(GRAD_EARLY):
        grad_out(k).start()
    grad_go(2)

    def mix_relay(i):
        e = place.take(i)

        @pl.when(e != me)
        def _():
            mix_home(e, e).wait_recv()

        mix_near(e, mine).start()

    def mix_sum(i):
        e = place.take(i)

        lane = lax.broadcasted_iota(jnp.int32, (rows // 4, 128), 1)

        @pl.loop(0, 2)
        def _(m):
            part = pl.ds(pl.multiple_of(m * (rows // 4), 16), rows // 4)
            full = pl.ds(pl.multiple_of((2 * place.core + m) * (rows // 4), 16), rows // 4)
            keys = [key_wide[k, full, :] - e * cap for k in range(2)]
            for low in range(0, cap, 128):
                size = min(128, cap - low)
                hit = (keys[0] == lane + low) | (keys[1] == lane + low)
                hot_ref[part, low : low + size] = jnp.where(hit, 1.0, 0.0).astype(jnp.bfloat16)[
                    :, 0:size
                ]

        mix_near(e, other).wait_recv()
        total[...] += dot_rows(hot_ref[...], back[e])

    ends = Quarters(place, move, B_ENDMIX, 0, out_ref)

    small_sizes = small_ref.shape
    small_ref[...] = jnp.zeros_like(small_ref)
    small_ref[0:experts] = router_part[0:experts]
    small_ref[experts : experts + 1] = gain2_part[...]

    def small_move(step):
        src, dst, where = (
            (small_ref, small_near, place.near),
            (small_steps.at[0], small_far, place.across),
            (small_steps.at[1], small_pair, wide.pair),
        )[step]
        return move(src, dst, B_SMALL, step, step, where)

    def small_home(e, landed):
        return move(
            small_steps.at[2], small_group.at[landed], B_SMALL + 1, e, landed, place.home(e)
        )

    share_row = lax.broadcasted_iota(jnp.int32, small_sizes, 0) == experts + 1

    def small_second():
        small_move(0).wait_recv()
        small_steps[0] = small_ref[...] + jnp.where(share_row, small_near[...], 0.0)
        small_move(1).start()

    def small_third():
        small_move(1).wait_recv()
        small_steps[1] = small_steps[0] + jnp.where(share_row, small_far[...], 0.0)
        small_move(2).start()

    def small_fourth():
        small_move(2).wait_recv()
        small_steps[2] = small_steps[1] + small_pair[...]
        small_group[me] = small_steps[2]

        @pl.loop(1, experts)
        def _(i):
            small_home(place.take(i), me).start()

    def small_last():
        @pl.loop(1, experts)
        def _(i):
            s = place.take(i)
            small_home(s, s).wait_recv()

        small_out[...] = jnp.zeros_like(small_out)

        @pl.loop(0, experts)
        def _(e):
            small_out[...] += small_group[e]

    real = pair_kept.shape[1]

    def contract(left, right):
        return lax.dot_general(
            left, right, (((0,), (0,)), ((), ())), preferred_element_type=jnp.float32
        )

    def zero_pads():
        if pair_send.shape[1] > real:
            pair_send[:, real:] = jnp.zeros_like(pair_send[:, real:])
            group_send[:, real:] = jnp.zeros_like(group_send[:, real:])

    zero_pads()
    product = contract(attended_ref[...], att_grad[...])
    wide.first(0, (product[0:real], product[real:]))

    @pl.loop(0, rows // tile)
    def _(t):
        part = pl.ds(pl.multiple_of(t * tile, 16), tile)
        normed, _, _ = normalize(x_ref[part, :].astype(jnp.float32), flat(gain_ref))
        low_ref[part, :] = normed.astype(jnp.bfloat16)
        block = dot_cols(att_grad[part, :], out_w[...]).astype(jnp.bfloat16)
        for h in range(heads):
            head_grad[h, part, :] = block[:, h * HEAD_DIM : (h + 1) * HEAD_DIM]

    @pl.loop(0, images)
    def _(image):
        part = pl.ds(pl.multiple_of(image * patches, 16), patches)
        padded = round_up(patches, 128)
        column = jnp.concatenate(
            [stats_ref[part, :], jnp.zeros((padded - patches, 128), jnp.float32)], 0
        )
        lines[image] = jnp.transpose(column)[0:8, :]

    def attend_back(image, h):
        part = pl.ds(pl.multiple_of(image * patches, 16), patches)
        query = heads_ref[0, h, part, :]
        key_rows = heads_ref[1, h, part, :]
        out_grad = head_grad[h, part, :]
        live = lax.broadcasted_iota(jnp.int32, (patches, 1), 0) < counts[image]
        line = lines[image, pl.ds(h, 1), 0:patches]
        scores = jnp.where(live, dot_cols(key_rows, query) * scale, MASKED_SCORE)
        probs = jnp.exp(scores - line)
        change = dot_cols(heads_ref[2, h, part, :], out_grad)
        delta = jnp.sum(probs * change, 0, keepdims=True)
        score_grad = (scale * probs * (change - delta)).astype(jnp.bfloat16)
        proj_grad[2, h, part, :] = dot_rows(probs.astype(jnp.bfloat16), out_grad).astype(
            jnp.bfloat16
        )
        proj_grad[1, h, part, :] = dot_rows(score_grad, query).astype(jnp.bfloat16)
        proj_grad[0, h, part, :] = contract(score_grad, key_rows).astype(jnp.bfloat16)

    def piece(h):
        grads = jnp.concatenate([proj_grad[i, h] for i in range(3)], 1)
        product = contract(grads, low_ref[...])
        wide.first(h + 1, (product[0:real], product[real:]))

    def fold_first(image):
        for mine_too in (False, True):
            part = fold.rows(image, place.core if mine_too else 1 - place.core)
            normed_part = jnp.zeros((tile, width), jnp.float32)
            for i in range(3):
                grads = jnp.concatenate([proj_grad[i, h, part, :] for h in range(heads)], 1)
                normed_part += dot_rows(grads, qkv_w[i])
            if mine_too:
                fold_kept[image] = normed_part
            else:
                fold_send[image] = normed_part.astype(jnp.bfloat16)
                fold.core_move(image).start()
            _, hat, _ = normalize(x_ref[part, :].astype(jnp.float32), flat(gain_ref))
            small_ref[experts + 1 : experts + 2] += jnp.sum(normed_part * hat, 0, keepdims=True)

    for k, column in enumerate(widen(slot_keys(routes_ref, slots_ref, capacity, cap))):
        key_wide[k] = column

    def mix_relays(lo, hi):
        @pl.loop(lo, hi)
        def _(i):
            mix_relay(i)

    def mix_sums(lo, hi):
        @pl.loop(lo, hi)
        def _(i):
            mix_sum(i)

    total[...] = jnp.zeros_like(total)

    def mix_tail():
        mixed_in.wait()
        out_ref[ends.rows, ends.mine] = (mixed_part[...] + total[...]).astype(
            jnp.bfloat16
        )
        ends.start()

    mid = experts // 2
    agenda = {
        1: [lambda: mix_relays(0, mid)],
        2: [lambda: fold_first(0), lambda: mix_sums(0, mid)],
        3: [lambda: piece(0), lambda: fold.second(0)],
        4: [lambda: piece(1), lambda: wide.second(0)],
        5: [
            lambda: piece(2),
            lambda: fold.third(0),
            lambda: wide.second(1),
        ],
    }

    @pl.loop(0, images * heads)
    def _(step):
        attend_back(step // heads, lax.rem(step, heads))
        for at, todo in agenda.items():

            @pl.when(step == at)
            def _():
                for act in todo:
                    act()

    fold_first(1)
    small_move(0).start()
    grad_go(3)
    wide.second(2)
    fold.second(1)
    small_second()
    wide.third(0)
    mix_relays(mid, experts)
    fold.relay(0)
    wide.third(1)
    wide.second(3)
    small_third()
    mix_sums(mid, experts)
    fold.third(1)
    mix_tail()
    wide.third(2)
    wide.fourth(0)
    small_fourth()
    fold.ready(0)
    mixed_grad_in.wait()

    def rows_out(t):
        part = pl.ds(pl.multiple_of(t * tile, 16), tile)
        return load(3 + t, x_grad.at[part, :], x_grad_hbm.at[part, :])

    def input_rows(image):
        @pl.loop(2 * image, 2 * image + 2)
        def _(t):
            part = pl.ds(pl.multiple_of(t * tile, 16), tile)
            _, hat, scaled = normalize(x_ref[part, :].astype(jnp.float32), flat(gain_ref))
            grad = normed_ref[part, :].astype(jnp.float32) * flat(gain_ref)
            inner = (
                grad - jnp.mean(grad, -1, keepdims=True) - hat * jnp.mean(grad * hat, -1, keepdims=True)
            )
            x_grad[part, :] += scaled * inner
            rows_out(t).start()

    input_rows(0)
    wide.fourth(1)
    wide.third(3)
    fold.relay(1)
    wide.fourth(2)
    small_last()
    fold.ready(1)
    input_rows(1)
    wide.fourth(3)
    for k in range(GRAD_EARLY, GRAD_PARTS):
        grad_end(k)
    ends.relay()

    def settle(p):
        wide.ready(p)
        if p == 0:
            for side in range(2):
                out_grad[side * real : (side + 1) * real] = whole_ref[0, side, 0:real].astype(
                    jnp.float32
                )
            return
        lanes = (p - 1) * HEAD_DIM
        for i in range(3):
            row = i * HEAD_DIM
            while row < (i + 1) * HEAD_DIM:
                side, at = row // real, row % real
                size = min((i + 1) * HEAD_DIM - row, real - at)
                put = lanes + row - i * HEAD_DIM
                in_grad[i, put : put + size] = whole_ref[p, side, at : at + size].astype(jnp.float32)
                row += size

    for p in range(pieces):
        settle(p)
    ends.ready()

    @pl.loop(0, rows // tile)
    def _(t):
        rows_out(t).wait()

    for k in range(GRAD_PARTS):
        grad_out(k).wait()
    wide.finish()
    fold.finish(images)
    ends.finish()
    for step in range(3):
        small_move(step).wait_send()

    @pl.loop(0, experts)
    def _(i):
        s = place.take(i)
        mix_near(s, mine).wait_send()

        @pl.when(i > 0)
        def _():
            mix_home(s, me).wait_send()
            small_home(s, me).wait_send()


def back(
    counts,
    att_grad,
    mixed_grad,
    head_rows,
    stats,
    attended,
    x,
    gain,
    qkv_w,
    out_w,
    mixed,
    halves,
    routes,
    slots,
    router_part,
    gain2_part,
    grad_in,
    capacity,
):
    rows, width = x.shape
    experts, half = halves.shape[:2]
    cap, side = 2 * half, width // 2
    images = counts.shape[0]
    heads = head_rows.shape[1]
    head_cols = out_w.shape[0]
    pieces = heads + 1
    real = head_cols // 2
    split = max(experts // 2, 1)
    chunk_rows = round_up(-(-real // split), 16)
    padded = chunk_rows * split
    part_rows = rows // images // 2
    small = round_up(experts + 2, 8)
    bf16, f32 = jnp.bfloat16, jnp.float32
    vmem = pl.BlockSpec(memory_space=pltpu.VMEM)
    hbm = pl.BlockSpec(memory_space=pl.ANY)
    small_block = pltpu.VMEM((small, width), f32)
    dma = pltpu.SemaphoreType.DMA
    table = max(experts, images, 3, GRAD_PARTS)
    return pl.pallas_call(
        functools.partial(back_kernel, experts, capacity),
        out_shape=[
            jax.ShapeDtypeStruct((rows, width), bf16),
            jax.ShapeDtypeStruct((rows, width), f32),
            jax.ShapeDtypeStruct((3, head_cols, width), f32),
            jax.ShapeDtypeStruct((head_cols, width), f32),
            jax.ShapeDtypeStruct((small, width), f32),
            jax.ShapeDtypeStruct(grad_in.shape, f32),
        ],
        in_specs=[pl.BlockSpec(memory_space=pltpu.SMEM), vmem, hbm]
        + [vmem] * 7
        + [hbm]
        + [vmem] * 5
        + [hbm],
        out_specs=[vmem, hbm] + [vmem] * 3 + [hbm],
        scratch_shapes=[
            pltpu.VMEM(grad_in.shape, f32),
            pltpu.VMEM((rows // 2, side), f32),
            pltpu.VMEM((rows, width), f32),
            pltpu.VMEM(grad_in.shape, bf16),
            pltpu.VMEM(grad_in.shape, bf16),
            pltpu.VMEM((pieces, 2, padded, width), bf16),
            dma((3 + 2 * images + GRAD_PARTS,)),
            pltpu.VMEM((rows, width), bf16),
            pltpu.VMEM((images, 8, round_up(rows // images, 128)), f32),
            pltpu.VMEM((heads, rows, HEAD_DIM), bf16),
            pltpu.VMEM((3, heads, rows, HEAD_DIM), bf16),
            pltpu.VMEM((2, rows, 128), jnp.int32),
            pltpu.VMEM((experts, cap, side), bf16),
            pltpu.VMEM((rows // 2, cap), bf16),
            pltpu.VMEM((rows // 2, side), f32),
            pltpu.VMEM((images, part_rows, width), bf16),
            pltpu.VMEM((images, part_rows, width), bf16),
            pltpu.VMEM((images, part_rows, width), f32),
            pltpu.VMEM((images, part_rows, side), bf16),
            pltpu.VMEM((images, part_rows, side), bf16),
            pltpu.VMEM((rows, width), bf16),
            pltpu.VMEM((pieces, padded, width), bf16),
            pltpu.VMEM((pieces, padded, width), bf16),
            pltpu.VMEM((pieces, real, width), f32),
            pltpu.VMEM((pieces, padded, width), bf16),
            pltpu.VMEM((pieces, experts, chunk_rows, side), bf16),
            pltpu.VMEM((chunk_rows, side), f32),
            small_block,
            small_block,
            small_block,
            small_block,
            pltpu.VMEM((experts, small, width), f32),
            pltpu.VMEM((3, small, width), f32),
            dma((B_ROWS, table)),
            dma((B_ROWS, table)),
            dma((2, pieces)),
            dma((2, pieces)),
            dma((2 * pieces, experts)),
            dma((2 * pieces, experts)),
        ],
        compiler_params=pltpu.CompilerParams(
            collective_id=3, has_side_effects=True, vmem_limit_bytes=VMEM_BYTES
        ),
    )(
        counts,
        att_grad,
        mixed_grad,
        head_rows,
        stats,
        attended,
        x,
        gain,
        qkv_w,
        out_w,
        mixed,
        halves,
        routes,
        slots,
        router_part,
        gain2_part,
        grad_in,
    )


def body(
    inputs,
    counts,
    routes,
    slot_ids,
    norm_first,
    attn_in,
    attn_out,
    norm_second,
    router,
    expert_in,
    expert_out,
    cotangent,
):
    rows_dev = inputs.shape[0]
    experts = router.shape[1]
    half_slots = (105 * rows_dev + 100 * experts - 1) // (100 * experts)
    capacity = 2 * half_slots
    slot_pad = round_up(capacity, 32)
    routes, slots = routes.T, slot_ids.T
    router_rows, qkv = router.T, attn_in.transpose(0, 2, 1)
    sent_cots, head_rows, attended, stats, mixed, low_second, prob, gates, gate_rows = front(
        counts,
        inputs,
        cotangent,
        routes,
        slots,
        norm_first,
        qkv,
        attn_out,
        norm_second,
        router_rows,
        experts,
        capacity,
        slot_pad,
    )
    halves, mixed_grad, att_grad, router_part, gain_part, expert_out_grad, in_part = middle(
        counts,
        low_second,
        cotangent,
        routes,
        slots,
        gates,
        gate_rows,
        expert_in[0],
        expert_out[0],
        sent_cots,
        mixed,
        prob,
        norm_second,
        router_rows,
        experts,
        capacity,
    )
    output, input_grad, in_grad, attn_out_grad, small, expert_in_grad = back(
        counts,
        att_grad,
        mixed_grad,
        head_rows,
        stats,
        attended,
        inputs,
        norm_first,
        qkv,
        attn_out,
        mixed,
        halves,
        routes,
        slots,
        router_part,
        gain_part,
        in_part,
        capacity,
    )
    return (
        output,
        input_grad,
        small[experts + 1],
        in_grad.transpose(0, 2, 1),
        attn_out_grad,
        small[experts],
        small[:experts].T,
        expert_in_grad[None],
        expert_out_grad[None],
    )


def solution(mesh):
    in_specs = (
        P("wide", None),
        P("wide"),
        P("wide", None),
        P("wide", None),
        P(),
        P(None, None, "narrow"),
        P("narrow", None),
        P(),
        P(),
        P("wide", None, "narrow"),
        P("wide", "narrow", None),
        P("wide", None),
    )
    out_specs = (
        P("wide", None),
        P("wide", None),
        P(),
        P(None, None, "narrow"),
        P("narrow", None),
        P(),
        P(),
        P("wide", None, "narrow"),
        P("wide", "narrow", None),
    )
    return jax.shard_map(body, mesh=mesh, in_specs=in_specs, out_specs=out_specs, check_vma=False)
```

```python
import functools

import jax
import jax.numpy as jnp
from jax import lax
from jax.experimental import pallas as pl
from jax.experimental.pallas import tpu as pltpu
from jax.sharding import PartitionSpec as P

HEAD_DIM = 64
NORM_EPSILON = 1e-06
MASKED_SCORE = -1e30
BY_MESH = pl.DeviceIdType.MESH
VMEM_BYTES = 64 * 1024 * 1024 - 65536


def round_up(value, multiple):
    return -(-value // multiple) * multiple


def dot_rows(left, right):
    return lax.dot_general(left, right, (((1,), (0,)), ((), ())), preferred_element_type=jnp.float32)


def dot_cols(left, right):
    return lax.dot_general(left, right, (((1,), (1,)), ((), ())), preferred_element_type=jnp.float32)


def normal_parts(values):
    t = 1.0 / (1.0 + (0.3275911 * 0.7071067811865476) * jnp.abs(values))
    bell = jnp.exp(-0.5 * values * values)
    poly = t * (
        0.254829592
        + t * (-0.284496736 + t * (1.421413741 + t * (-1.453152027 + t * 1.061405429)))
    )
    tail = 0.5 * poly * bell
    return jnp.where(values >= 0.0, 1.0 - tail, tail), 0.3989422804014327 * values * bell


def normalize(values, gain):
    center = values - jnp.mean(values, -1, keepdims=True)
    scaled = lax.rsqrt(jnp.mean(center * center, -1, keepdims=True) + NORM_EPSILON)
    normed = center * scaled
    return normed * gain, normed, scaled


def slot_keys(routes_ref, slots_ref, capacity, cap):
    return jnp.where(slots_ref[...] < capacity, routes_ref[...] * cap + slots_ref[...], -1)


def widen(rows):
    count = rows.shape[1]
    padded = jnp.concatenate([rows.astype(jnp.float32), jnp.zeros((6, count), jnp.float32)], 0)
    tall = jnp.transpose(padded)
    return [jnp.broadcast_to(tall[:, k : k + 1], (count, 128)).astype(jnp.int32) for k in range(2)]


def flat(gain_ref):
    return gain_ref[...].reshape(1, gain_ref.shape[0])


class Place:
    def __init__(self, experts):
        self.experts = experts
        self.n = lax.axis_index("narrow")
        self.w = lax.axis_index("wide")
        self.core = lax.rem(self.n, 2)
        self.chip = self.n // 2
        self.me = self.w // 2
        self.parity = lax.rem(self.w, 2)
        self.near_n = self.n + 1 - 2 * self.core
        self.across_n = lax.rem(self.n + 2, 4)
        self.near = {"narrow": self.near_n, "wide": self.w}
        self.across = {"narrow": self.across_n, "wide": self.w}

    def home(self, e):
        return {"narrow": self.n, "wide": 2 * e + self.parity}

    def take(self, i):
        short = jnp.minimum(self.me, self.experts - 1 - self.me)
        swing = jnp.where(lax.rem(i, 2) == 1, (i + 1) // 2, -(i // 2))
        away = jnp.where(i <= 2 * short, swing, i - short)
        return self.me + jnp.where(2 * self.me < self.experts, away, -away)

    def part(self, which, size, align):
        return pl.ds(pl.multiple_of(which * size, align), size)

    def greet(self, others=()):
        barrier = pltpu.get_barrier_semaphore()
        for peer in (self.near, self.across, *others):
            pl.semaphore_signal(barrier, inc=1, device_id=peer, device_id_type=BY_MESH)

        @pl.loop(1, self.experts)
        def _(i):
            pl.semaphore_signal(
                barrier, inc=1, device_id=self.home(self.take(i)), device_id_type=BY_MESH
            )

        pl.semaphore_wait(barrier, self.experts + 1 + len(others))


def mover(sent, came):
    def move(src, dst, row, sent_at, came_at, where):
        return pltpu.make_async_remote_copy(
            src_ref=src,
            dst_ref=dst,
            send_sem=sent.at[row, sent_at],
            recv_sem=came.at[row, came_at],
            device_id=where,
            device_id_type=BY_MESH,
        )

    return move


class Dispatch:
    def __init__(self, place, move, base, send, landing):
        self.place, self.move, self.base = place, move, base
        self.send, self.landing = send, landing
        cap, width = landing.shape[1:]
        self.cap, self.half, self.side = cap, cap // 2, width // 2
        self.mine = place.part(place.core, self.half, 16)
        self.other = place.part(1 - place.core, self.half, 16)
        self.side_mine = place.part(place.chip, self.side, 128)
        self.side_other = place.part(1 - place.chip, self.side, 128)

    def z_copy(self, e, landed):
        return self.move(
            self.send.at[e],
            self.landing.at[landed, self.mine, self.side_mine],
            self.base,
            e,
            landed,
            self.place.home(e),
        )

    def build(self, i, key_row, source):
        e = self.place.take(i)
        hot = self.hot(e, self.place.core, key_row)
        self.send[e] = dot_rows(hot, source[:, self.side_mine]).astype(jnp.bfloat16)
        self.z_copy(e, self.place.me).start()

    def hot(self, e, part, key_row):
        slot = e * self.cap + part * self.half
        slot = slot + lax.broadcasted_iota(jnp.int32, (self.half, key_row.shape[1]), 0)
        hit = (key_row[0:1, :] == slot) | (key_row[1:2, :] == slot)
        return jnp.where(hit, 1.0, 0.0).astype(jnp.bfloat16)

    def build_own(self, key_row, source):
        @pl.loop(0, 2)
        def _(m):
            hot = self.hot(self.place.me, m, key_row)
            part = pl.ds(pl.multiple_of(m * self.half, 16), self.half)
            self.landing[self.place.me, part, :] = dot_rows(hot, source[...]).astype(jnp.bfloat16)

    def spread(self, step, s):
        rows, cols, where = (
            (self.mine, self.side_mine, self.place.across),
            (self.mine, self.side_mine, self.place.near),
            (self.mine, self.side_other, self.place.near),
        )[step]
        ref = self.landing.at[s, rows, cols]
        return self.move(ref, ref, self.base + 1 + step, s, s, where)

    def stage_a(self, i):
        self.landed(i)
        self.relay(i)

    def stage_b(self, i):
        s = self.place.take(i)
        self.spread(0, s).wait_recv()
        self.spread(2, s).start()

    def stage_c(self, i):
        s = self.place.take(i)
        self.spread(1, s).wait_recv()
        self.spread(2, s).wait_recv()

    def landed(self, i):
        s = self.place.take(i)
        self.z_copy(s, s).wait_recv()

    def relay(self, i):
        s = self.place.take(i)
        self.spread(0, s).start()
        self.spread(1, s).start()

    def finish(self, lo, hi, sends=True):
        @pl.loop(lo, hi)
        def _(i):
            s = self.place.take(i)
            for step in range(3):
                self.spread(step, s).wait_send()

        if sends:

            @pl.loop(1, self.place.experts)
            def _(i):
                self.z_copy(self.place.take(i), self.place.me).wait_send()


FRONT_OWN, FRONT_FAR, FRONT_CHIP = 4, 5, 6
FRONT_ROWS = 7
LATE = 1


def front_kernel(
    experts,
    capacity,
    counts,
    x_ref,
    cot_ref,
    routes_ref,
    slots_ref,
    gain1_ref,
    qkv_w,
    out_w,
    gain2_ref,
    router_ref,
    cots_ref,
    heads_hbm,
    attended_hbm,
    stats_hbm,
    mixed_hbm,
    low2_hbm,
    prob_hbm,
    gate_hbm,
    gate_send,
    heads_ref,
    attended_ref,
    stats_ref,
    mixed_ref,
    low2_ref,
    prob_ref,
    gate_ref,
    cot_send,
    gather,
    out_all,
    key_row,
    key_wide,
    route_wide,
    gate_wide,
    router_pad,
    loads,
    sent,
    came,
):
    rows, width = x_ref.shape
    images = counts.shape[0]
    patches = rows // images
    head_cols = out_w.shape[0]
    heads = head_cols // HEAD_DIM
    scale = HEAD_DIM ** (-0.5)
    place = Place(experts)
    move = mover(sent, came)
    cots = Dispatch(place, move, 0, cot_send, cots_ref)
    place.greet()
    key_row[...] = slot_keys(routes_ref, slots_ref, capacity, cots.cap)

    def share(ref, at):
        def copy(step):
            piece = ref(place.across_n if step == 2 else place.n)
            where = place.across if step == 0 else place.near
            row = (FRONT_CHIP, FRONT_OWN, FRONT_FAR)[step]
            return move(piece, piece, row, at, at, where)

        return copy

    out_share = share(lambda n: out_all.at[n], images)
    out_all[place.n] = out_w[...]
    out_share(0).start()
    out_share(1).start()

    @pl.loop(1, experts)
    def _(i):
        cots.build(i, key_row, cot_ref)

    tile = patches // 2

    @pl.loop(0, rows // tile)
    def _(t):
        part = pl.ds(pl.multiple_of(t * tile, 16), tile)
        normed, _, _ = normalize(x_ref[part, :].astype(jnp.float32), flat(gain1_ref))
        low = normed.astype(jnp.bfloat16)
        for i in range(3):
            block = dot_cols(low, qkv_w[i]).astype(jnp.bfloat16)
            for h in range(heads):
                heads_ref[i, h, part, :] = block[:, h * HEAD_DIM : (h + 1) * HEAD_DIM]

    outs = [
        pltpu.make_async_copy(src, dst, loads.at[at])
        for at, (src, dst) in enumerate(
            (
                (heads_ref, heads_hbm),
                (attended_ref, attended_hbm),
                (stats_ref, stats_hbm),
                (mixed_ref, mixed_hbm),
                (low2_ref, low2_hbm),
                (prob_ref, prob_hbm),
                (gate_ref, gate_hbm),
            )
        )
    ]
    outs[0].start()
    for k, column in enumerate(widen(key_row[...])):
        key_wide[k] = column
    for k, column in enumerate(widen(routes_ref[...])):
        route_wide[k] = column
    router_pad[...] = jnp.zeros_like(router_pad)
    router_pad[0:experts] = router_ref[...]
    stats_ref[...] = jnp.zeros_like(stats_ref)

    def attend(image):
        keys_at = pl.ds(pl.multiple_of(image * patches, 16), patches)
        pack = pl.ds(pl.multiple_of(image * tile, 16), tile)
        live = lax.broadcasted_iota(jnp.int32, (1, patches), 1) < counts[image]
        for h in range(heads):
            key_rows = heads_ref[1, h, keys_at, :]
            value_rows = heads_ref[2, h, keys_at, :]
            for t in range(patches // tile):
                part = pl.ds(pl.multiple_of(image * patches + t * tile, 16), tile)
                scores = dot_cols(heads_ref[0, h, part, :], key_rows) * scale
                scores = jnp.where(live, scores, MASKED_SCORE)
                top = jnp.max(scores, -1, keepdims=True)
                weights = jnp.exp(scores - top)
                total = jnp.sum(weights, -1, keepdims=True)
                probs = (weights * (1.0 / total)).astype(jnp.bfloat16)
                block = dot_rows(probs, value_rows).astype(jnp.bfloat16)
                at = t * head_cols + h * HEAD_DIM
                gather[place.n, pack, at : at + HEAD_DIM] = block
                attended_ref[part, h * HEAD_DIM : (h + 1) * HEAD_DIM] = block
                stats_ref[part, h : h + 1] = top + jnp.log(total)

    def image_share(image):
        pack = pl.ds(pl.multiple_of(image * tile, 16), tile)
        return share(lambda n: gather.at[n, pack, :], image)

    @pl.loop(0, images)
    def _(image):
        attend(image)
        image_share(image)(0).start()
        image_share(image)(1).start()

    outs[1].start()
    outs[2].start()
    out_share(0).wait_recv()
    out_share(2).start()
    cots.build_own(key_row, cot_ref)

    @pl.loop(1, experts - LATE)
    def _(i):
        cots.stage_a(i)

    out_share(1).wait_recv()
    out_share(2).wait_recv()

    def finish(image):
        copy = image_share(image)
        copy(0).wait_recv()
        copy(2).start()
        copy(1).wait_recv()
        copy(2).wait_recv()
        pack = pl.ds(pl.multiple_of(image * tile, 16), tile)

        for t in range(2):
            part = pl.ds(pl.multiple_of(image * patches + t * tile, 16), tile)
            cols = slice(t * head_cols, (t + 1) * head_cols)
            attention = dot_rows(gather[0, pack, cols], out_all[0])
            for n in range(1, 4):
                attention += dot_rows(gather[n, pack, cols], out_all[n])
            offset = t * tile + lax.broadcasted_iota(jnp.int32, (tile, 1), 0)
            mixed = x_ref[part, :].astype(jnp.float32) + jnp.where(
                offset < counts[image], attention, 0.0
            )
            mixed_ref[part, :] = mixed
            normed, _, _ = normalize(mixed, flat(gain2_ref))
            low = normed.astype(jnp.bfloat16)
            low2_ref[part, :] = low
            lane = lax.broadcasted_iota(jnp.int32, (tile, 128), 1)
            logits = jnp.where(lane < experts, dot_cols(low, router_pad[...]), MASKED_SCORE)
            powers = jnp.exp(logits - jnp.max(logits, -1, keepdims=True))
            prob = powers / jnp.sum(powers, -1, keepdims=True)
            prob_ref[part, :] = prob
            picked = [
                jnp.sum(jnp.where(lane == route_wide[k, part, :], prob, 0.0), 1, keepdims=True)
                for k in range(2)
            ]
            both = picked[0] + picked[1]
            gate_ref[part, :] = jnp.where(
                lane == 0, picked[0] / both, jnp.where(lane == 1, picked[1] / both, both)
            )

    @pl.loop(0, images)
    def _(image):
        finish(image)

    for out in outs[3:]:
        out.start()

    wide_cap = gate_send.shape[2]

    for k in range(2):
        gate_wide[k] = jnp.broadcast_to(gate_ref[:, k : k + 1], (rows, 128))

    @pl.loop(0, experts)
    def _(e):
        @pl.loop(0, wide_cap // 128)
        def _(j):
            lanes = pl.ds(pl.multiple_of(j * 128, 128), 128)
            slot = e * cots.cap + j * 128 + lax.broadcasted_iota(jnp.int32, (rows, 128), 1)
            picked = jnp.where(key_wide[0] == slot, gate_wide[0], 0.0) + jnp.where(
                key_wide[1] == slot, gate_wide[1], 0.0
            )
            gate_send[e, :, lanes] = jnp.broadcast_to(jnp.sum(picked, 0, keepdims=True), (8, 128))

    @pl.loop(1, experts - LATE)
    def _(i):
        cots.stage_b(i)

    @pl.loop(1, experts - LATE)
    def _(i):
        cots.stage_c(i)

    @pl.loop(experts - LATE, experts)
    def _(i):
        cots.landed(i)

    cots.finish(1, experts - LATE)
    for out in outs:
        out.wait()
    for step in range(3):
        out_share(step).wait_send()
        for image in range(images):
            image_share(image)(step).wait_send()


def front(
    counts, x, cot, routes, slots, gain1, qkv_w, out_w, gain2, router, experts, capacity, cap
):
    rows, width = x.shape
    head_cols = out_w.shape[0]
    heads = head_cols // HEAD_DIM
    images = counts.shape[0]
    bf16, f32 = jnp.bfloat16, jnp.float32
    vmem = pl.BlockSpec(memory_space=pltpu.VMEM)
    hbm = pl.BlockSpec(memory_space=pl.ANY)
    table = max(experts, images + 1)
    wide_cap = round_up(cap, 128)
    return pl.pallas_call(
        functools.partial(front_kernel, experts, capacity),
        out_shape=[
            jax.ShapeDtypeStruct((experts, cap, width), bf16),
            jax.ShapeDtypeStruct((3, heads, rows, HEAD_DIM), bf16),
            jax.ShapeDtypeStruct((rows, head_cols), bf16),
            jax.ShapeDtypeStruct((rows, 128), f32),
            jax.ShapeDtypeStruct((rows, width), f32),
            jax.ShapeDtypeStruct((rows, width), bf16),
            jax.ShapeDtypeStruct((rows, 128), f32),
            jax.ShapeDtypeStruct((rows, 128), f32),
            jax.ShapeDtypeStruct((experts, 8, wide_cap), f32),
        ],
        in_specs=[pl.BlockSpec(memory_space=pltpu.SMEM)] + [vmem] * 9,
        out_specs=[vmem] + [hbm] * 7 + [vmem],
        scratch_shapes=[
            pltpu.VMEM((3, heads, rows, HEAD_DIM), bf16),
            pltpu.VMEM((rows, head_cols), bf16),
            pltpu.VMEM((rows, 128), f32),
            pltpu.VMEM((rows, width), f32),
            pltpu.VMEM((rows, width), bf16),
            pltpu.VMEM((rows, 128), f32),
            pltpu.VMEM((rows, 128), f32),
            pltpu.VMEM((experts, cap // 2, width // 2), bf16),
            pltpu.VMEM((4, rows // 2, 2 * head_cols), bf16),
            pltpu.VMEM((4, head_cols, width), bf16),
            pltpu.VMEM((2, rows), jnp.int32),
            pltpu.VMEM((2, rows, 128), jnp.int32),
            pltpu.VMEM((2, rows, 128), jnp.int32),
            pltpu.VMEM((2, rows, 128), f32),
            pltpu.VMEM((128, width), bf16),
            pltpu.SemaphoreType.DMA((7,)),
            pltpu.SemaphoreType.DMA((FRONT_ROWS, table)),
            pltpu.SemaphoreType.DMA((FRONT_ROWS, table)),
        ],
        compiler_params=pltpu.CompilerParams(
            collective_id=2, has_side_effects=True, vmem_limit_bytes=VMEM_BYTES
        ),
    )(counts, x, cot, routes, slots, gain1, qkv_w, out_w, gain2, router)


class Return:
    def __init__(self, place, move, base, core_send, core_recv, kept, chip_send, chip_recv, back):
        self.place, self.move, self.base = place, move, base
        self.core_send, self.core_recv, self.kept = core_send, core_recv, kept
        self.chip_send, self.chip_recv, self.back = chip_send, chip_recv, back
        self.half, self.side = chip_send.shape[1:]
        self.mine = place.part(place.core, self.half, 16)
        self.other = place.part(1 - place.core, self.half, 16)
        self.side_mine = place.part(place.chip, self.side, 128)
        self.side_other = place.part(1 - place.chip, self.side, 128)

    def rows(self, s):
        return pl.ds(pl.multiple_of(s * self.half, 16), self.half)

    def core_move(self, s):
        return self.move(
            self.core_send.at[s], self.core_recv.at[s], self.base, s, s, self.place.near
        )

    def chip_move(self, s):
        return self.move(
            self.chip_send.at[s], self.chip_recv.at[s], self.base + 1, s, s, self.place.across
        )

    def home_move(self, s, landed):
        return self.move(
            self.core_send.at[s, :, pl.ds(0, self.side)],
            self.back.at[landed, self.mine, :],
            self.base + 2,
            s,
            landed,
            self.place.home(s),
        )

    def pair_move(self, e, part):
        ref = self.back.at[e, part, :]
        return self.move(ref, ref, self.base + 3, e, e, self.place.near)

    def first(self, s, product):
        self.core_send[s] = product(self.other).astype(jnp.bfloat16)
        self.core_move(s).start()
        self.kept[self.rows(s), :] = product(self.mine)

    def second(self, s):
        self.core_move(s).wait_recv()
        self.chip_send[s] = (
            self.kept[self.rows(s), self.side_other]
            + self.core_recv[s, :, self.side_other].astype(jnp.float32)
        ).astype(jnp.bfloat16)
        self.chip_move(s).start()

    def third(self, s):
        self.chip_move(s).wait_recv()
        self.core_move(s).wait_send()
        piece = (
            self.kept[self.rows(s), self.side_mine]
            + self.core_recv[s, :, self.side_mine].astype(jnp.float32)
            + self.chip_recv[s].astype(jnp.float32)
        ).astype(jnp.bfloat16)

        @pl.when(s == self.place.me)
        def _():
            self.back[self.place.me, self.mine, :] = piece

        @pl.when(s != self.place.me)
        def _():
            self.core_send[s, :, 0 : self.side] = piece
            self.home_move(s, self.place.me).start()

    def fourth(self, i):
        e = self.place.take(i)

        @pl.when(e != self.place.me)
        def _():
            self.home_move(e, e).wait_recv()

        self.pair_move(e, self.mine).start()

    def ready(self, i):
        self.pair_move(self.place.take(i), self.other).wait_recv()

    def finish(self):
        @pl.loop(0, self.place.experts)
        def _(i):
            s = self.place.take(i)
            self.chip_move(s).wait_send()
            self.pair_move(s, self.mine).wait_send()

            @pl.when(i > 0)
            def _():
                self.home_move(s, self.place.me).wait_send()


class Quarters:
    def __init__(self, place, move, base, at, ref):
        self.place, self.move, self.base, self.at, self.ref = place, move, base, at, ref
        rows, width = ref.shape
        self.rows = place.part(place.core, rows // 2, 16)
        self.mine = place.part(place.chip, width // 2, 128)
        self.other = place.part(1 - place.chip, width // 2, 128)

    def copy(self, step):
        ref = self.ref.at[self.rows, self.other if step == 2 else self.mine]
        where = self.place.across if step == 0 else self.place.near
        return self.move(ref, ref, self.base + step, self.at, self.at, where)

    def start(self):
        self.copy(0).start()
        self.copy(1).start()

    def relay(self):
        self.copy(0).wait_recv()
        self.copy(2).start()

    def ready(self):
        self.copy(1).wait_recv()
        self.copy(2).wait_recv()

    def finish(self):
        for step in range(3):
            self.copy(step).wait_send()


M_CORE, M_CHIP, M_HOME, M_BACK, M_MIX, M_END, M_PAIR, M_LATE, M_GATES = 4, 5, 6, 7, 11, 13, 16, 17, 21
M_ROWS = 22
MIX_EARLY = 2
GRAD_PARTS, GRAD_EARLY = 4, 2


def middle_kernel(
    experts,
    capacity,
    counts,
    low_ref,
    cot_hbm,
    routes_ref,
    slots_ref,
    gate_col,
    gate_send,
    in_hbm,
    out_hbm,
    cots_hbm,
    mixed_hbm,
    prob_ref,
    gain_ref,
    router_ref,
    half_hbm,
    mixed_grad_hbm,
    att_grad_hbm,
    router_grad,
    gain_grad,
    grad_out,
    grad_in,
    in_ref,
    out_ref,
    cots_ref,
    rows_ref,
    hid_ref,
    pre_ref,
    send_rows,
    gate_rows,
    gate_tall,
    pair_tall,
    pair_part,
    pair_core,
    pair_sum,
    pair_chip,
    pair_home,
    pair_back,
    core_send,
    core_recv,
    kept,
    chip_send,
    chip_recv,
    back,
    mix_send,
    mix_recv,
    mix_last,
    key_row,
    key_wide,
    route_wide,
    router_pad,
    hot_ref,
    total,
    pair_ref,
    dis_ref,
    copy_send,
    copy_recv,
    in_send,
    in_recv,
    cot_tile,
    scale_wide,
    loads,
    cot_loads,
    sent,
    came,
):
    rows, width = low_ref.shape
    images = counts.shape[0]
    patches = rows // images
    cap = rows_ref.shape[1]
    half = cap // 2
    units = in_ref.shape[1]
    place = Place(experts)
    move = mover(sent, came)
    me = place.me
    lows = Dispatch(place, move, 0, send_rows, rows_ref)
    late = Dispatch(place, move, M_LATE, send_rows, cots_ref)
    dgrad = Return(
        place, move, M_BACK, core_send, core_recv, kept, chip_send, chip_recv, back
    )
    other_copy = {"narrow": place.n, "wide": place.w + 1 - 2 * place.parity}

    def load(at, src, dst):
        return pltpu.make_async_copy(src, dst, loads.at[at])

    fetched = [
        load(0, in_hbm, in_ref),
        load(1, out_hbm, out_ref),
    ]
    for copy in fetched:
        copy.start()

    def cots_in(i, whole):
        s = place.take(i)
        at = (s,) if whole else (s, late.mine, late.side_mine)
        return pltpu.make_async_copy(cots_hbm.at[at], cots_ref.at[at], cot_loads.at[i])

    @pl.loop(0, experts - LATE)
    def _(i):
        cots_in(i, True).start()

    for i in range(experts - LATE, experts):
        cots_in(i, False).start()
    place.greet((other_copy,))
    key_row[...] = slot_keys(routes_ref, slots_ref, capacity, cap)

    def gate_copy(e, landed):
        return move(gate_send.at[e], gate_rows.at[landed], M_GATES, e, landed, place.home(e))

    @pl.loop(1, experts)
    def _(i):
        lows.build(i, key_row, low_ref)
        gate_copy(place.take(i), me).start()

    gate_rows[me] = gate_send[me]

    for copy in fetched:
        copy.wait()

    @pl.loop(0, experts - LATE)
    def _(i):
        cots_in(i, True).wait()

    for i in range(experts - LATE, experts):
        cots_in(i, False).wait()
        late.relay(i)

    lows.build_own(key_row, low_ref)
    pair_tall[...] = jnp.zeros_like(pair_tall)
    grad_out[...] = jnp.zeros_like(grad_out)
    grad_in[...] = jnp.zeros_like(grad_in)
    for k, column in enumerate(widen(key_row[...])):
        key_wide[k] = column
    for k, column in enumerate(widen(routes_ref[...])):
        route_wide[k] = column
    router_pad[...] = jnp.zeros_like(router_pad)
    router_pad[0:experts] = router_ref[...]

    def pair_move(step, s):
        src, dst, row, where = (
            (pair_part, pair_core, M_CORE, place.near),
            (pair_sum, pair_chip, M_CHIP, place.across),
        )[step]
        return move(src.at[s], dst.at[s], row, s, s, where)

    def pair_return(s, landed):
        return move(pair_home.at[s], pair_back.at[landed], M_HOME, s, landed, place.home(s))

    chunk = 256 if units % 256 == 0 else units

    def compute(s, m):
        part = pl.ds(pl.multiple_of(m * half, 16), half)
        left = rows_ref[s, part, :]
        cots = cots_ref[s, part, :]
        gate = gate_tall[part, 0:1]
        pair = jnp.zeros((half, 1), jnp.float32)
        for j in range(units // chunk):
            cols = slice(j * chunk, (j + 1) * chunk)
            pre = dot_rows(left, in_ref[:, cols])
            free = dot_cols(cots, out_ref[cols, :])
            cdf, slope = normal_parts(pre)
            hidden = pre * cdf
            hid_ref[s, part, cols] = (gate * hidden).astype(jnp.bfloat16)
            pre_ref[s, part, cols] = (gate * free * (cdf + slope)).astype(jnp.bfloat16)
            pair += jnp.sum(hidden * free, 1, keepdims=True)
        pair_tall[part, :] = jnp.broadcast_to(pair, (half, 128))

    def second(s):
        dgrad.second(s)
        pair_move(0, s).wait_recv()
        pair_sum[s] = pair_part[s] + pair_core[s]
        pair_move(1, s).start()

    def third(s):
        dgrad.third(s)
        pair_move(1, s).wait_recv()
        line = pair_sum[s] + pair_chip[s]

        @pl.when(s == me)
        def _():
            pair_back[me] = line

        @pl.when(s != me)
        def _():
            pair_home[s] = line
            pair_return(s, me).start()

    def contract(left, right):
        return lax.dot_general(
            left, right, (((0,), (0,)), ((), ())), preferred_element_type=jnp.float32
        )

    def mix_move(s):
        return move(mix_send.at[s], mix_recv.at[s], M_MIX, s, s, place.near)

    def mix_chip(s):
        src = mix_recv.at[s, :, dgrad.side_other]
        return move(src, mix_last.at[s], M_MIX + 1, s, s, place.across)

    def mix_first(s):
        mix_send[s] = dot_rows(hid_ref[s, dgrad.other, :], out_ref[...]).astype(jnp.bfloat16)
        mix_move(s).start()

    def mix_second(s):
        mix_move(s).wait_recv()
        mix_recv[s] = (
            dot_rows(hid_ref[s, dgrad.mine, :], out_ref[...]) + mix_recv[s].astype(jnp.float32)
        ).astype(jnp.bfloat16)

    def mix_third(s):
        mix_chip(s).wait()
        total_part = mix_recv[s, :, dgrad.side_mine].astype(jnp.float32)
        mix_recv[s, :, 0 : dgrad.side] = (total_part + mix_last[s].astype(jnp.float32)).astype(
            jnp.bfloat16
        )

    def work(i, between):
        s = place.take(i)
        gate_tall[...] = jnp.transpose(gate_rows[s])

        @pl.loop(0, 2)
        def _(m):
            compute(s, m)

            @pl.when(m == 0)
            def _():
                between()

        pair_part[s] = jnp.transpose(pair_tall[...])[0:8]
        pair_move(0, s).start()
        dgrad.first(s, lambda part: dot_cols(pre_ref[s, part, :], in_ref[...]))

    def add_out(lo, hi):
        @pl.loop(lo, hi)
        def _(i):
            s = place.take(i)
            grad_out[...] += contract(hid_ref[s], cots_ref[s])

    def add_in(lo, hi):
        @pl.loop(lo, hi)
        def _(i):
            s = place.take(i)
            grad_in[...] += contract(rows_ref[s], pre_ref[s])

    def pass_on(i):
        @pl.when((i > 0) & (i + 1 < experts))
        def _():
            lows.stage_a(i + 1)

    @pl.loop(0, experts)
    def _(i):
        s = place.take(i)

        @pl.when(i > 0)
        def _():
            lows.stage_b(i)
            lows.stage_c(i)
            gate_copy(s, s).wait_recv()

        @pl.when(i >= experts - LATE)
        def _():
            late.stage_c(i)

        work(i, lambda: pass_on(i))

        @pl.when(i == 0)
        def _():
            lows.stage_a(1)

        second(s)

        @pl.when(i == 0)
        def _():
            mix_first(s)
            add_out(0, 1)
            add_in(0, 1)
            for j in range(experts - LATE, experts):
                late.stage_b(j)

        @pl.when(i > 1)
        def _():
            third(place.take(i - 2))

    last = place.take(experts - 1)

    @pl.loop(1, experts)
    def _(i):
        mix_first(place.take(i))

    third(place.take(experts - 2))

    @pl.loop(0, MIX_EARLY)
    def _(i):
        s = place.take(i)
        mix_second(s)
        mix_chip(s).start()

    add_out(1, experts)
    copy_send[...] = grad_out[...].astype(jnp.bfloat16)
    copy_move = move(copy_send, copy_recv, M_PAIR, 0, 0, other_copy)
    copy_move.start()
    third(last)

    pair_ref[...] = jnp.zeros_like(pair_ref)

    def build_hot(e):
        lane = lax.broadcasted_iota(jnp.int32, (rows // 4, 128), 1)

        @pl.loop(0, 4)
        def _(m):
            part = pl.ds(pl.multiple_of(m * (rows // 4), 16), rows // 4)
            keys = [key_wide[k, part, :] - e * cap for k in range(2)]
            for low in range(0, cap, 128):
                size = min(128, cap - low)
                hit = (keys[0] == lane + low) | (keys[1] == lane + low)
                hot_ref[part, low : low + size] = jnp.where(hit, 1.0, 0.0).astype(jnp.bfloat16)[
                    :, 0:size
                ]

    my_rows = place.part(place.core, rows // 2, 16)
    total[...] = jnp.zeros_like(total)

    @pl.loop(0, experts)
    def _(i):
        e = place.take(i)
        build_hot(e)
        dgrad.fourth(i)

        @pl.when(i > 0)
        def _():
            pair_return(e, e).wait_recv()

        tall = jnp.transpose(pair_back[e])[0:cap, 0:1]
        high = tall.astype(jnp.bfloat16).astype(jnp.float32)
        middle = (tall - high).astype(jnp.bfloat16).astype(jnp.float32)
        lane = lax.broadcasted_iota(jnp.int32, (cap, 128), 1)
        spelled = jnp.where(
            lane == 0, high, jnp.where(lane == 1, middle, jnp.where(lane == 2, tall - high - middle, 0.0))
        ).astype(jnp.bfloat16)
        found = jnp.sum(dot_rows(hot_ref[...], spelled), 1, keepdims=True)
        lane_rows = lax.broadcasted_iota(jnp.int32, (rows, 128), 1)
        pair_ref[...] += jnp.where(lane_rows == e, found, 0.0)
        dgrad.ready(i)
        total[...] += dot_rows(hot_ref[my_rows, :], back[e])

    ends = Quarters(place, move, M_END, 0, dis_ref)
    dis_ref[ends.rows, ends.mine] = total[...].astype(jnp.bfloat16)
    ends.start()

    @pl.loop(MIX_EARLY, experts)
    def _(i):
        mix_second(place.take(i))

    add_in(1, experts)
    early_rows = in_send.shape[0]
    in_send[...] = grad_in[0:early_rows].astype(jnp.bfloat16)
    in_move = move(in_send, in_recv, M_PAIR, 1, 1, other_copy)
    in_move.start()
    mixed_in = load(1, mixed_hbm, kept.at[pl.ds(0, rows), :])
    mixed_in.start()
    tile = patches // 2
    router_grad[...] = jnp.zeros_like(router_grad)
    gain_grad[...] = jnp.zeros_like(gain_grad)

    def cot_in(t):
        slot = lax.rem(t, 2)
        part = pl.ds(pl.multiple_of(t * tile, 16), tile)
        return pltpu.make_async_copy(cot_hbm.at[part, :], cot_tile.at[slot], loads.at[2 + slot])

    def rows_out(t, what):
        part = pl.ds(pl.multiple_of(t * tile, 16), tile)
        src, dst = ((kept, mixed_grad_hbm), (dis_ref, att_grad_hbm))[what]
        return pltpu.make_async_copy(src.at[part, :], dst.at[part, :], loads.at[4 + 2 * t + what])

    cot_in(0).start()
    mixed_in.wait()

    def before(t):
        part = pl.ds(pl.multiple_of(t * tile, 16), tile)
        lane = lax.broadcasted_iota(jnp.int32, (tile, 128), 1)
        by_expert = pair_ref[part, :]
        hots = [lane == route_wide[k, part, :] for k in range(2)]
        pair = [jnp.sum(jnp.where(hot, by_expert, 0.0), 1, keepdims=True) for hot in hots]
        weighted = pair[0] * gate_col[part, 0:1] + pair[1] * gate_col[part, 1:2]
        both = gate_col[part, 2:3]
        prob = prob_ref[part, :]
        prob_grad = jnp.where(hots[0], (pair[0] - weighted) / both, 0.0) + jnp.where(
            hots[1], (pair[1] - weighted) / both, 0.0
        )
        logit_grad = prob * (prob_grad - jnp.sum(prob * prob_grad, 1, keepdims=True))
        pair_ref[part, :] = logit_grad
        router_grad[...] += contract(logit_grad.astype(jnp.bfloat16), low_ref[part, :])
        _, hat, scaled = normalize(kept[part, :], flat(gain_ref))
        kept[part, :] = hat
        scale_wide[part, :] = jnp.broadcast_to(scaled, (tile, 128))

    @pl.loop(0, rows // tile)
    def _(t):
        @pl.when(t == 2)
        def _():
            ends.relay()

        before(t)

    @pl.loop(0, MIX_EARLY)
    def _(i):
        mix_third(place.take(i))

    half_out = load(0, mix_recv, half_hbm)
    half_out.start()
    ends.ready()
    ends.finish()

    @pl.loop(0, rows // tile)
    def _(t):
        @pl.when(t + 1 < rows // tile)
        def _():
            cot_in(t + 1).start()

        part = pl.ds(pl.multiple_of(t * tile, 16), tile)
        normed_grad = dis_ref[part, :].astype(jnp.float32) + dot_rows(
            pair_ref[part, :].astype(jnp.bfloat16), router_pad[...]
        )
        hat = kept[part, :]
        gain_grad[...] += jnp.sum(normed_grad * hat, 0, keepdims=True)
        grad = normed_grad * flat(gain_ref)
        inner = (
            grad - jnp.mean(grad, -1, keepdims=True) - hat * jnp.mean(grad * hat, -1, keepdims=True)
        )
        cot_in(t).wait()
        full = cot_tile[lax.rem(t, 2)].astype(jnp.float32) + scale_wide[part, 0:1] * inner
        kept[part, :] = full
        rows_out(t, 0).start()
        row = t * tile + lax.broadcasted_iota(jnp.int32, (tile, 1), 0)
        live = lax.rem(row, patches) < jnp.where(t * tile < patches, counts[0], counts[images - 1])
        dis_ref[part, :] = jnp.where(live, full, 0.0).astype(jnp.bfloat16)
        rows_out(t, 1).start()

    copy_move.wait()
    grad_out[...] += copy_recv[...].astype(jnp.float32)
    in_move.wait()
    grad_in[0:early_rows] += in_recv[...].astype(jnp.float32)
    half_out.wait()

    @pl.loop(0, rows // tile)
    def _(t):
        rows_out(t, 0).wait()
        rows_out(t, 1).wait()

    dgrad.finish()
    lows.finish(1, experts)
    late.finish(experts - LATE, experts, False)

    @pl.loop(0, experts)
    def _(i):
        s = place.take(i)
        pair_move(0, s).wait_send()
        pair_move(1, s).wait_send()
        mix_move(s).wait_send()

        @pl.when(i > 0)
        def _():
            pair_return(s, me).wait_send()
            gate_copy(s, me).wait_send()


def middle(
    counts,
    low,
    cot,
    routes,
    slots,
    gates,
    gate_rows,
    weight_in,
    weight_out,
    cots,
    mixed,
    prob,
    gain,
    router,
    experts,
    capacity,
):
    rows, width = low.shape
    units = weight_in.shape[1]
    cap = cots.shape[1]
    half, side, wide_cap = cap // 2, width // 2, round_up(cap, 128)
    bf16, f32 = jnp.bfloat16, jnp.float32
    vmem = pl.BlockSpec(memory_space=pltpu.VMEM)
    hbm = pl.BlockSpec(memory_space=pl.ANY)
    line = pltpu.VMEM((experts, 8, wide_cap), f32)
    halves = pltpu.VMEM((experts, half, width), bf16)
    tile = rows // counts.shape[0] // 2
    return pl.pallas_call(
        functools.partial(middle_kernel, experts, capacity),
        out_shape=[
            jax.ShapeDtypeStruct((experts, half, width), bf16),
            jax.ShapeDtypeStruct((rows, width), f32),
            jax.ShapeDtypeStruct((rows, width), bf16),
            jax.ShapeDtypeStruct((128, width), f32),
            jax.ShapeDtypeStruct((1, width), f32),
            jax.ShapeDtypeStruct((units, width), f32),
            jax.ShapeDtypeStruct((width, units), f32),
        ],
        in_specs=[
            pl.BlockSpec(memory_space=pltpu.SMEM),
            vmem,
            hbm,
            vmem,
            vmem,
            vmem,
            vmem,
            hbm,
            hbm,
            hbm,
            hbm,
            vmem,
            vmem,
            vmem,
        ],
        out_specs=[hbm] * 3 + [vmem] * 4,
        scratch_shapes=[
            pltpu.VMEM((width, units), bf16),
            pltpu.VMEM((units, width), bf16),
            pltpu.VMEM((experts, cap, width), bf16),
            pltpu.VMEM((experts, cap, width), bf16),
            pltpu.VMEM((experts, cap, units), bf16),
            pltpu.VMEM((experts, cap, units), bf16),
            pltpu.VMEM((experts, half, side), bf16),
            line,
            pltpu.VMEM((wide_cap, 8), f32),
            pltpu.VMEM((wide_cap, 128), f32),
            line,
            line,
            line,
            line,
            line,
            line,
            halves,
            halves,
            pltpu.VMEM((max(experts * half, rows), width), f32),
            pltpu.VMEM((experts, half, side), bf16),
            pltpu.VMEM((experts, half, side), bf16),
            pltpu.VMEM((experts, cap, side), bf16),
            halves,
            halves,
            pltpu.VMEM((experts, half, side), bf16),
            pltpu.VMEM((2, rows), jnp.int32),
            pltpu.VMEM((2, rows, 128), jnp.int32),
            pltpu.VMEM((2, rows, 128), jnp.int32),
            pltpu.VMEM((128, width), bf16),
            pltpu.VMEM((rows, cap), bf16),
            pltpu.VMEM((rows // 2, side), f32),
            pltpu.VMEM((rows, 128), f32),
            pltpu.VMEM((rows, width), bf16),
            pltpu.VMEM((units, width), bf16),
            pltpu.VMEM((units, width), bf16),
            pltpu.VMEM((width * GRAD_EARLY // GRAD_PARTS, units), bf16),
            pltpu.VMEM((width * GRAD_EARLY // GRAD_PARTS, units), bf16),
            pltpu.VMEM((2, tile, width), bf16),
            pltpu.VMEM((rows, 128), f32),
            pltpu.SemaphoreType.DMA((4 + 2 * (rows // tile),)),
            pltpu.SemaphoreType.DMA((experts,)),
            pltpu.SemaphoreType.DMA((M_ROWS, experts)),
            pltpu.SemaphoreType.DMA((M_ROWS, experts)),
        ],
        compiler_params=pltpu.CompilerParams(
            collective_id=1, has_side_effects=True, vmem_limit_bytes=VMEM_BYTES
        ),
    )(
        counts,
        low,
        cot,
        routes,
        slots,
        gates,
        gate_rows,
        weight_in,
        weight_out,
        cots,
        mixed,
        prob,
        gain,
        router,
    )


class Fold:
    def __init__(self, place, move, base, core_send, core_recv, kept, chip_send, chip_recv, whole):
        self.place, self.move, self.base = place, move, base
        self.core_send, self.core_recv, self.kept = core_send, core_recv, kept
        self.chip_send, self.chip_recv, self.whole = chip_send, chip_recv, whole
        self.half, self.side = chip_send.shape[1:]
        self.side_mine = place.part(place.chip, self.side, 128)
        self.side_other = place.part(1 - place.chip, self.side, 128)

    def rows(self, image, core):
        start = (2 * image + core) * self.half
        return pl.ds(pl.multiple_of(start, 16), self.half)

    def core_move(self, image):
        return self.move(
            self.core_send.at[image],
            self.core_recv.at[image],
            self.base,
            image,
            image,
            self.place.near,
        )

    def chip_move(self, image):
        return self.move(
            self.chip_send.at[image],
            self.chip_recv.at[image],
            self.base + 1,
            image,
            image,
            self.place.across,
        )

    def share(self, image, step):
        cols = self.side_other if step == 2 else self.side_mine
        ref = self.whole.at[self.rows(image, self.place.core), cols]
        where = self.place.across if step == 0 else self.place.near
        return self.move(ref, ref, self.base + 2 + step, image, image, where)

    def second(self, image):
        self.core_move(image).wait_recv()
        self.chip_send[image] = (
            self.kept[image, :, self.side_other]
            + self.core_recv[image, :, self.side_other].astype(jnp.float32)
        ).astype(jnp.bfloat16)
        self.chip_move(image).start()

    def third(self, image):
        self.chip_move(image).wait_recv()
        self.whole[self.rows(image, self.place.core), self.side_mine] = (
            self.kept[image, :, self.side_mine]
            + self.core_recv[image, :, self.side_mine].astype(jnp.float32)
            + self.chip_recv[image].astype(jnp.float32)
        ).astype(jnp.bfloat16)
        self.share(image, 0).start()
        self.share(image, 1).start()

    def relay(self, image):
        self.share(image, 0).wait_recv()
        self.share(image, 2).start()

    def ready(self, image):
        self.share(image, 1).wait_recv()
        self.share(image, 2).wait_recv()

    def finish(self, images):
        for image in range(images):
            self.core_move(image).wait_send()
            self.chip_move(image).wait_send()
            for step in range(3):
                self.share(image, step).wait_send()


class WideSum:
    def __init__(self, place, move, tables, pair_send, pair_recv, kept, group_send, group_recv, whole):
        self.place, self.move = place, move
        self.pair_sems, self.group_out, self.group_in = tables
        self.pair_send, self.pair_recv, self.kept = pair_send, pair_recv, kept
        self.group_send, self.group_recv, self.whole = group_send, group_recv, whole
        self.rows, self.cols = group_recv.shape[2:]
        self.half = pair_send.shape[1]
        self.real = kept.shape[1]
        self.pair = {"narrow": place.n, "wide": place.w + 1 - 2 * place.parity}

    def pair_move(self, p):
        return self.move[0](
            self.pair_send.at[p], self.pair_recv.at[p], 0, p, p, self.pair
        )

    def chunk(self, e):
        return (
            pl.ds(pl.multiple_of((e // 2) * self.rows, 16), self.rows),
            pl.ds(pl.multiple_of(lax.rem(e, 2) * self.cols, 128), self.cols),
        )

    def group_move(self, p, e, landed):
        rows, cols = self.chunk(e)
        return self.move[1](
            self.group_send.at[p, rows, cols],
            self.group_recv.at[p, landed],
            p,
            e,
            landed,
            self.place.home(e),
        )

    def group_share(self, p, owner, at, landed, where):
        rows, cols = self.chunk(owner)
        ref = self.whole.at[p, self.place.parity, rows, cols]
        pieces = self.pair_send.shape[0]
        return self.move[1](ref, ref, pieces + p, at, landed, where)

    def pair_share(self, p, parity):
        ref = self.whole.at[p, parity]
        return self.move[0](ref, ref, 1, p, p, self.pair)

    def first(self, p, halves):
        @pl.when(self.place.parity == 0)
        def _():
            self.kept[p] = halves[0]
            self.pair_send[p, 0 : self.real] = halves[1].astype(jnp.bfloat16)

        @pl.when(self.place.parity == 1)
        def _():
            self.kept[p] = halves[1]
            self.pair_send[p, 0 : self.real] = halves[0].astype(jnp.bfloat16)

        self.pair_move(p).start()

    def second(self, p):
        self.pair_move(p).wait_recv()
        self.group_send[p, 0 : self.real] = (
            self.kept[p] + self.pair_recv[p, 0 : self.real].astype(jnp.float32)
        ).astype(jnp.bfloat16)

        @pl.loop(1, self.place.experts)
        def _(i):
            self.group_move(p, self.place.take(i), self.place.me).start()

    def third(self, p):
        rows, cols = self.chunk(self.place.me)
        total = self.group_send[p, rows, cols].astype(jnp.float32)
        self.total[...] = total

        @pl.loop(1, self.place.experts)
        def _(i):
            s = self.place.take(i)
            self.group_move(p, s, s).wait_recv()
            self.total[...] += self.group_recv[p, s].astype(jnp.float32)

        self.whole[p, self.place.parity, rows, cols] = self.total[...].astype(jnp.bfloat16)

        @pl.loop(1, self.place.experts)
        def _(i):
            e = self.place.take(i)
            self.group_share(p, self.place.me, e, self.place.me, self.place.home(e)).start()

    def fourth(self, p):
        @pl.loop(1, self.place.experts)
        def _(i):
            s = self.place.take(i)
            self.group_share(p, s, s, s, self.place.home(s)).wait_recv()

        self.pair_share(p, self.place.parity).start()

    def ready(self, p):
        self.pair_share(p, 1 - self.place.parity).wait_recv()

    def finish(self):
        for p in range(self.pair_send.shape[0]):
            self.pair_move(p).wait_send()
            self.pair_share(p, self.place.parity).wait_send()

            @pl.loop(1, self.place.experts)
            def _(i):
                e = self.place.take(i)
                self.group_move(p, e, self.place.me).wait_send()
                self.group_share(p, self.place.me, e, self.place.me, self.place.home(e)).wait_send()


B_MIX, B_ENDMIX, B_FOLD, B_SMALL, B_GRAD = 0, 3, 6, 11, 13
B_ROWS = 14


def back_kernel(
    experts,
    capacity,
    counts,
    att_grad,
    mixed_grad_hbm,
    heads_ref,
    stats_ref,
    attended_ref,
    x_ref,
    gain_ref,
    qkv_w,
    out_w,
    mixed_hbm,
    half_ref,
    routes_ref,
    slots_ref,
    router_part,
    gain2_part,
    grad_hbm,
    out_ref,
    x_grad_hbm,
    in_grad,
    out_grad,
    small_out,
    grad_sum_hbm,
    grad_sum,
    mixed_part,
    x_grad,
    grad_send,
    grad_recv,
    whole_ref,
    loads,
    low_ref,
    lines,
    head_grad,
    proj_grad,
    key_wide,
    chip_recv,
    back,
    hot_ref,
    total,
    fold_send,
    fold_recv,
    fold_kept,
    fold_chip_send,
    fold_chip_recv,
    normed_ref,
    pair_send,
    pair_recv,
    pair_kept,
    group_send,
    group_recv,
    group_total,
    small_ref,
    small_near,
    small_far,
    small_pair,
    small_group,
    small_steps,
    sent,
    came,
    pair_sent,
    pair_came,
    group_sent,
    group_came,
):
    rows, width = att_grad.shape
    images = counts.shape[0]
    patches = rows // images
    head_cols = attended_ref.shape[1]
    heads = head_cols // HEAD_DIM
    scale = HEAD_DIM ** (-0.5)
    cap = back.shape[1]
    tile = patches // 2
    pieces = heads + 1
    place = Place(experts)
    move = mover(sent, came)
    me = place.me
    wide = WideSum(
        place,
        (mover(pair_sent, pair_came), mover(group_sent, group_came)),
        (None, None, None),
        pair_send,
        pair_recv,
        pair_kept,
        group_send,
        group_recv,
        whole_ref,
    )
    wide.total = group_total
    fold = Fold(
        place,
        move,
        B_FOLD,
        fold_send,
        fold_recv,
        fold_kept,
        fold_chip_send,
        fold_chip_recv,
        normed_ref,
    )
    my_rows = place.part(place.core, rows // 2, 16)
    side_mine = place.part(place.chip, width // 2, 128)

    def load(at, src, dst):
        return pltpu.make_async_copy(src, dst, loads.at[at])

    grad_in = load(0, grad_hbm, grad_sum)
    mixed_in = load(1, mixed_hbm.at[my_rows, side_mine], mixed_part)
    mixed_grad_in = load(2, mixed_grad_hbm, x_grad)
    grad_in.start()
    mixed_in.start()
    mixed_grad_in.start()
    place.greet((wide.pair,))

    def grad_part(k):
        size = grad_sum.shape[0] // GRAD_PARTS
        return pl.ds(k * size, size)

    def grad_move(k):
        part = grad_part(k)
        return move(grad_send.at[part, :], grad_recv.at[part, :], B_GRAD, k, k, wide.pair)

    def grad_go(k):
        part = grad_part(k)
        grad_send[part, :] = grad_sum[part, :].astype(jnp.bfloat16)
        grad_move(k).start()

    def grad_out(k):
        part = grad_part(k)
        return load(3 + 2 * images + k, grad_sum.at[part, :], grad_sum_hbm.at[part, :])

    def grad_end(k):
        part = grad_part(k)
        grad_move(k).wait()
        grad_sum[part, :] += grad_recv[part, :].astype(jnp.float32)
        grad_out(k).start()

    half = half_ref.shape[1]
    side = width // 2
    mine = place.part(place.core, half, 16)
    other = place.part(1 - place.core, half, 16)
    side_other = place.part(1 - place.chip, side, 128)

    def mix_chip(s):
        return move(half_ref.at[s, :, side_other], chip_recv.at[s], B_MIX, s, s, place.across)

    def mix_home(i, landed):
        s = place.take(i)
        early = isinstance(i, int) and i < MIX_EARLY
        src = half_ref.at[s, :, pl.ds(0, side)] if early else chip_recv.at[s]
        return move(src, back.at[landed, mine, :], B_MIX + 1, s, landed, place.home(s))

    def mix_near(e, part):
        ref = back.at[e, part, :]
        return move(ref, ref, B_MIX + 2, e, e, place.near)

    for i in range(1, MIX_EARLY):
        mix_home(i, me).start()

    @pl.loop(MIX_EARLY, experts)
    def _(i):
        mix_chip(place.take(i)).start()

    back[me, mine, :] = half_ref[me, :, 0:side]
    grad_in.wait()
    for k in range(GRAD_EARLY):
        grad_out(k).start()
    grad_go(2)

    def mix_backs():
        @pl.loop(MIX_EARLY, experts)
        def _(i):
            s = place.take(i)
            mix_chip(s).wait_recv()
            chip_recv[s] = (
                half_ref[s, :, side_mine].astype(jnp.float32) + chip_recv[s].astype(jnp.float32)
            ).astype(jnp.bfloat16)
            mix_home(i, me).start()

    def mix_relay(i):
        e = place.take(i)

        @pl.when(e != me)
        def _():
            mix_home(i, e).wait_recv()

        mix_near(e, mine).start()

    def mix_sum(i):
        e = place.take(i)

        lane = lax.broadcasted_iota(jnp.int32, (rows // 4, 128), 1)

        @pl.loop(0, 2)
        def _(m):
            part = pl.ds(pl.multiple_of(m * (rows // 4), 16), rows // 4)
            full = pl.ds(pl.multiple_of((2 * place.core + m) * (rows // 4), 16), rows // 4)
            keys = [key_wide[k, full, :] - e * cap for k in range(2)]
            for low in range(0, cap, 128):
                size = min(128, cap - low)
                hit = (keys[0] == lane + low) | (keys[1] == lane + low)
                hot_ref[part, low : low + size] = jnp.where(hit, 1.0, 0.0).astype(jnp.bfloat16)[
                    :, 0:size
                ]

        mix_near(e, other).wait_recv()
        total[...] += dot_rows(hot_ref[...], back[e])

    ends = Quarters(place, move, B_ENDMIX, 0, out_ref)

    small_sizes = small_ref.shape
    small_ref[...] = jnp.zeros_like(small_ref)
    small_ref[0:experts] = router_part[0:experts]
    small_ref[experts : experts + 1] = gain2_part[...]

    def small_move(step):
        src, dst, where = (
            (small_ref, small_near, place.near),
            (small_steps.at[0], small_far, place.across),
            (small_steps.at[1], small_pair, wide.pair),
        )[step]
        return move(src, dst, B_SMALL, step, step, where)

    def small_home(e, landed):
        return move(
            small_steps.at[2], small_group.at[landed], B_SMALL + 1, e, landed, place.home(e)
        )

    share_row = lax.broadcasted_iota(jnp.int32, small_sizes, 0) == experts + 1

    def small_second():
        small_move(0).wait_recv()
        small_steps[0] = small_ref[...] + jnp.where(share_row, small_near[...], 0.0)
        small_move(1).start()

    def small_third():
        small_move(1).wait_recv()
        small_steps[1] = small_steps[0] + jnp.where(share_row, small_far[...], 0.0)
        small_move(2).start()

    def small_fourth():
        small_move(2).wait_recv()
        small_steps[2] = small_steps[1] + small_pair[...]
        small_group[me] = small_steps[2]

        @pl.loop(1, experts)
        def _(i):
            small_home(place.take(i), me).start()

    def small_last():
        @pl.loop(1, experts)
        def _(i):
            s = place.take(i)
            small_home(s, s).wait_recv()

        small_out[...] = jnp.zeros_like(small_out)

        @pl.loop(0, experts)
        def _(e):
            small_out[...] += small_group[e]

    real = pair_kept.shape[1]

    def contract(left, right):
        return lax.dot_general(
            left, right, (((0,), (0,)), ((), ())), preferred_element_type=jnp.float32
        )

    def zero_pads():
        if pair_send.shape[1] > real:
            pair_send[:, real:] = jnp.zeros_like(pair_send[:, real:])
            group_send[:, real:] = jnp.zeros_like(group_send[:, real:])

    zero_pads()
    product = contract(attended_ref[...], att_grad[...])
    wide.first(0, (product[0:real], product[real:]))

    @pl.loop(0, rows // tile)
    def _(t):
        part = pl.ds(pl.multiple_of(t * tile, 16), tile)
        normed, _, _ = normalize(x_ref[part, :].astype(jnp.float32), flat(gain_ref))
        low_ref[part, :] = normed.astype(jnp.bfloat16)
        block = dot_cols(att_grad[part, :], out_w[...]).astype(jnp.bfloat16)
        for h in range(heads):
            head_grad[h, part, :] = block[:, h * HEAD_DIM : (h + 1) * HEAD_DIM]

    @pl.loop(0, images)
    def _(image):
        part = pl.ds(pl.multiple_of(image * patches, 16), patches)
        padded = round_up(patches, 128)
        column = jnp.concatenate(
            [stats_ref[part, :], jnp.zeros((padded - patches, 128), jnp.float32)], 0
        )
        lines[image] = jnp.transpose(column)[0:8, :]

    def attend_back(image, h):
        part = pl.ds(pl.multiple_of(image * patches, 16), patches)
        query = heads_ref[0, h, part, :]
        key_rows = heads_ref[1, h, part, :]
        out_grad = head_grad[h, part, :]
        live = lax.broadcasted_iota(jnp.int32, (patches, 1), 0) < counts[image]
        line = lines[image, pl.ds(h, 1), 0:patches]
        scores = jnp.where(live, dot_cols(key_rows, query) * scale, MASKED_SCORE)
        probs = jnp.exp(scores - line)
        change = dot_cols(heads_ref[2, h, part, :], out_grad)
        delta = jnp.sum(probs * change, 0, keepdims=True)
        score_grad = (scale * probs * (change - delta)).astype(jnp.bfloat16)
        proj_grad[2, h, part, :] = dot_rows(probs.astype(jnp.bfloat16), out_grad).astype(
            jnp.bfloat16
        )
        proj_grad[1, h, part, :] = dot_rows(score_grad, query).astype(jnp.bfloat16)
        proj_grad[0, h, part, :] = contract(score_grad, key_rows).astype(jnp.bfloat16)

    def piece(h):
        grads = jnp.concatenate([proj_grad[i, h] for i in range(3)], 1)
        product = contract(grads, low_ref[...])
        wide.first(h + 1, (product[0:real], product[real:]))

    def fold_first(image):
        @pl.loop(0, 2)
        def _(turn):
            part = fold.rows(image, jnp.where(turn == 0, 1 - place.core, place.core))
            normed_part = jnp.zeros((tile, width), jnp.float32)
            for i in range(3):
                grads = jnp.concatenate([proj_grad[i, h, part, :] for h in range(heads)], 1)
                normed_part += dot_rows(grads, qkv_w[i])

            @pl.when(turn == 0)
            def _():
                fold_send[image] = normed_part.astype(jnp.bfloat16)
                fold.core_move(image).start()

            @pl.when(turn == 1)
            def _():
                fold_kept[image] = normed_part

            _, hat, _ = normalize(x_ref[part, :].astype(jnp.float32), flat(gain_ref))
            small_ref[experts + 1 : experts + 2] += jnp.sum(normed_part * hat, 0, keepdims=True)

    for k, column in enumerate(widen(slot_keys(routes_ref, slots_ref, capacity, cap))):
        key_wide[k] = column

    def mix_relays(lo, hi):
        @pl.loop(lo, hi)
        def _(i):
            mix_relay(i)

    def mix_sums(lo, hi):
        @pl.loop(lo, hi)
        def _(i):
            mix_sum(i)

    total[...] = jnp.zeros_like(total)

    def mix_tail():
        mixed_in.wait()
        out_ref[ends.rows, ends.mine] = (mixed_part[...] + total[...]).astype(
            jnp.bfloat16
        )
        ends.start()

    agenda = {
        2: [lambda: mix_backs()],
        3: [lambda: fold.second(0)],
        4: [lambda: wide.second(0)],
        5: [lambda: fold.third(0), lambda: wide.second(1)],
    }

    @pl.loop(0, images * heads)
    def _(step):
        attend_back(step // heads, lax.rem(step, heads))

        @pl.when((step == heads - 1) | (step == 2 * heads - 1))
        def _():
            fold_first(step // heads)

        @pl.when(step >= heads)
        def _():
            piece(step - heads)

        for at, todo in agenda.items():

            @pl.when(step == at)
            def _():
                for act in todo:
                    act()

    small_move(0).start()
    grad_go(3)
    wide.second(2)
    fold.second(1)
    small_second()
    wide.third(0)
    fold.relay(0)
    mix_relays(0, experts)
    wide.third(1)
    wide.second(3)
    small_third()
    mix_sums(0, experts)
    fold.third(1)
    mix_tail()
    wide.third(2)
    wide.fourth(0)
    small_fourth()
    fold.ready(0)
    mixed_grad_in.wait()

    def rows_out(t):
        part = pl.ds(pl.multiple_of(t * tile, 16), tile)
        return load(3 + t, x_grad.at[part, :], x_grad_hbm.at[part, :])

    def input_rows(image):
        @pl.loop(2 * image, 2 * image + 2)
        def _(t):
            part = pl.ds(pl.multiple_of(t * tile, 16), tile)
            _, hat, scaled = normalize(x_ref[part, :].astype(jnp.float32), flat(gain_ref))
            grad = normed_ref[part, :].astype(jnp.float32) * flat(gain_ref)
            inner = (
                grad - jnp.mean(grad, -1, keepdims=True) - hat * jnp.mean(grad * hat, -1, keepdims=True)
            )
            x_grad[part, :] += scaled * inner
            rows_out(t).start()

    input_rows(0)
    wide.fourth(1)
    wide.third(3)
    fold.relay(1)
    wide.fourth(2)
    small_last()
    fold.ready(1)
    input_rows(1)
    wide.fourth(3)
    for k in range(GRAD_EARLY, GRAD_PARTS):
        grad_end(k)
    ends.relay()

    def settle(p):
        wide.ready(p)
        if p == 0:
            for side in range(2):
                out_grad[side * real : (side + 1) * real] = whole_ref[0, side, 0:real].astype(
                    jnp.float32
                )
            return
        lanes = (p - 1) * HEAD_DIM
        for i in range(3):
            row = i * HEAD_DIM
            while row < (i + 1) * HEAD_DIM:
                side, at = row // real, row % real
                size = min((i + 1) * HEAD_DIM - row, real - at)
                put = lanes + row - i * HEAD_DIM
                in_grad[i, put : put + size] = whole_ref[p, side, at : at + size].astype(jnp.float32)
                row += size

    for p in range(pieces):
        settle(p)
    ends.ready()

    @pl.loop(0, rows // tile)
    def _(t):
        rows_out(t).wait()

    for k in range(GRAD_PARTS):
        grad_out(k).wait()
    wide.finish()
    fold.finish(images)
    ends.finish()
    for step in range(3):
        small_move(step).wait_send()

    @pl.loop(0, experts)
    def _(i):
        s = place.take(i)
        mix_near(s, mine).wait_send()

        @pl.when(i > 0)
        def _():
            mix_home(i, me).wait_send()
            small_home(s, me).wait_send()

        @pl.when(i >= MIX_EARLY)
        def _():
            mix_chip(s).wait_send()


def back(
    counts,
    att_grad,
    mixed_grad,
    head_rows,
    stats,
    attended,
    x,
    gain,
    qkv_w,
    out_w,
    mixed,
    halves,
    routes,
    slots,
    router_part,
    gain2_part,
    grad_in,
    capacity,
):
    rows, width = x.shape
    experts, half = halves.shape[:2]
    cap, side = 2 * half, width // 2
    images = counts.shape[0]
    heads = head_rows.shape[1]
    head_cols = out_w.shape[0]
    pieces = heads + 1
    real = head_cols // 2
    split = max(experts // 2, 1)
    chunk_rows = round_up(-(-real // split), 16)
    padded = chunk_rows * split
    part_rows = rows // images // 2
    small = round_up(experts + 2, 8)
    bf16, f32 = jnp.bfloat16, jnp.float32
    vmem = pl.BlockSpec(memory_space=pltpu.VMEM)
    hbm = pl.BlockSpec(memory_space=pl.ANY)
    small_block = pltpu.VMEM((small, width), f32)
    dma = pltpu.SemaphoreType.DMA
    table = max(experts, images, 3, GRAD_PARTS)
    return pl.pallas_call(
        functools.partial(back_kernel, experts, capacity),
        out_shape=[
            jax.ShapeDtypeStruct((rows, width), bf16),
            jax.ShapeDtypeStruct((rows, width), f32),
            jax.ShapeDtypeStruct((3, head_cols, width), f32),
            jax.ShapeDtypeStruct((head_cols, width), f32),
            jax.ShapeDtypeStruct((small, width), f32),
            jax.ShapeDtypeStruct(grad_in.shape, f32),
        ],
        in_specs=[pl.BlockSpec(memory_space=pltpu.SMEM), vmem, hbm]
        + [vmem] * 7
        + [hbm]
        + [vmem] * 5
        + [hbm],
        out_specs=[vmem, hbm] + [vmem] * 3 + [hbm],
        scratch_shapes=[
            pltpu.VMEM(grad_in.shape, f32),
            pltpu.VMEM((rows // 2, side), f32),
            pltpu.VMEM((rows, width), f32),
            pltpu.VMEM(grad_in.shape, bf16),
            pltpu.VMEM(grad_in.shape, bf16),
            pltpu.VMEM((pieces, 2, padded, width), bf16),
            dma((3 + 2 * images + GRAD_PARTS,)),
            pltpu.VMEM((rows, width), bf16),
            pltpu.VMEM((images, 8, round_up(rows // images, 128)), f32),
            pltpu.VMEM((heads, rows, HEAD_DIM), bf16),
            pltpu.VMEM((3, heads, rows, HEAD_DIM), bf16),
            pltpu.VMEM((2, rows, 128), jnp.int32),
            pltpu.VMEM((experts, half, side), bf16),
            pltpu.VMEM((experts, cap, side), bf16),
            pltpu.VMEM((rows // 2, cap), bf16),
            pltpu.VMEM((rows // 2, side), f32),
            pltpu.VMEM((images, part_rows, width), bf16),
            pltpu.VMEM((images, part_rows, width), bf16),
            pltpu.VMEM((images, part_rows, width), f32),
            pltpu.VMEM((images, part_rows, side), bf16),
            pltpu.VMEM((images, part_rows, side), bf16),
            pltpu.VMEM((rows, width), bf16),
            pltpu.VMEM((pieces, padded, width), bf16),
            pltpu.VMEM((pieces, padded, width), bf16),
            pltpu.VMEM((pieces, real, width), f32),
            pltpu.VMEM((pieces, padded, width), bf16),
            pltpu.VMEM((pieces, experts, chunk_rows, side), bf16),
            pltpu.VMEM((chunk_rows, side), f32),
            small_block,
            small_block,
            small_block,
            small_block,
            pltpu.VMEM((experts, small, width), f32),
            pltpu.VMEM((3, small, width), f32),
            dma((B_ROWS, table)),
            dma((B_ROWS, table)),
            dma((2, pieces)),
            dma((2, pieces)),
            dma((2 * pieces, experts)),
            dma((2 * pieces, experts)),
        ],
        compiler_params=pltpu.CompilerParams(
            collective_id=3, has_side_effects=True, vmem_limit_bytes=VMEM_BYTES
        ),
    )(
        counts,
        att_grad,
        mixed_grad,
        head_rows,
        stats,
        attended,
        x,
        gain,
        qkv_w,
        out_w,
        mixed,
        halves,
        routes,
        slots,
        router_part,
        gain2_part,
        grad_in,
    )


def body(
    inputs,
    counts,
    routes,
    slot_ids,
    norm_first,
    attn_in,
    attn_out,
    norm_second,
    router,
    expert_in,
    expert_out,
    cotangent,
):
    rows_dev = inputs.shape[0]
    experts = router.shape[1]
    half_slots = (105 * rows_dev + 100 * experts - 1) // (100 * experts)
    capacity = 2 * half_slots
    slot_pad = round_up(capacity, 32)
    routes, slots = routes.T, slot_ids.T
    router_rows, qkv = router.T, attn_in.transpose(0, 2, 1)
    sent_cots, head_rows, attended, stats, mixed, low_second, prob, gates, gate_rows = front(
        counts,
        inputs,
        cotangent,
        routes,
        slots,
        norm_first,
        qkv,
        attn_out,
        norm_second,
        router_rows,
        experts,
        capacity,
        slot_pad,
    )
    halves, mixed_grad, att_grad, router_part, gain_part, expert_out_grad, in_part = middle(
        counts,
        low_second,
        cotangent,
        routes,
        slots,
        gates,
        gate_rows,
        expert_in[0],
        expert_out[0],
        sent_cots,
        mixed,
        prob,
        norm_second,
        router_rows,
        experts,
        capacity,
    )
    output, input_grad, in_grad, attn_out_grad, small, expert_in_grad = back(
        counts,
        att_grad,
        mixed_grad,
        head_rows,
        stats,
        attended,
        inputs,
        norm_first,
        qkv,
        attn_out,
        mixed,
        halves,
        routes,
        slots,
        router_part,
        gain_part,
        in_part,
        capacity,
    )
    return (
        output,
        input_grad,
        small[experts + 1],
        in_grad.transpose(0, 2, 1),
        attn_out_grad,
        small[experts],
        small[:experts].T,
        expert_in_grad[None],
        expert_out_grad[None],
    )


def solution(mesh):
    in_specs = (
        P("wide", None),
        P("wide"),
        P("wide", None),
        P("wide", None),
        P(),
        P(None, None, "narrow"),
        P("narrow", None),
        P(),
        P(),
        P("wide", None, "narrow"),
        P("wide", "narrow", None),
        P("wide", None),
    )
    out_specs = (
        P("wide", None),
        P("wide", None),
        P(),
        P(None, None, "narrow"),
        P("narrow", None),
        P(),
        P(),
        P("wide", None, "narrow"),
        P("wide", "narrow", None),
    )
    return jax.shard_map(body, mesh=mesh, in_specs=in_specs, out_specs=out_specs, check_vma=False)
```

```python
import functools

import jax
import jax.numpy as jnp
from jax import lax
from jax.experimental import pallas as pl
from jax.experimental.pallas import tpu as pltpu
from jax.sharding import PartitionSpec as P

HEAD_DIM = 64
NORM_EPSILON = 1e-06
MASKED_SCORE = -1e30
BY_MESH = pl.DeviceIdType.MESH
VMEM_BYTES = 64 * 1024 * 1024 - 65536


def round_up(value, multiple):
    return -(-value // multiple) * multiple


def dot_rows(left, right):
    return lax.dot_general(left, right, (((1,), (0,)), ((), ())), preferred_element_type=jnp.float32)


def dot_cols(left, right):
    return lax.dot_general(left, right, (((1,), (1,)), ((), ())), preferred_element_type=jnp.float32)


def normal_parts(values):
    t = 1.0 / (1.0 + (0.3275911 * 0.7071067811865476) * jnp.abs(values))
    bell = jnp.exp(-0.5 * values * values)
    poly = t * (
        0.254829592
        + t * (-0.284496736 + t * (1.421413741 + t * (-1.453152027 + t * 1.061405429)))
    )
    tail = 0.5 * poly * bell
    return jnp.where(values >= 0.0, 1.0 - tail, tail), 0.3989422804014327 * values * bell


def normalize(values, gain):
    center = values - jnp.mean(values, -1, keepdims=True)
    scaled = lax.rsqrt(jnp.mean(center * center, -1, keepdims=True) + NORM_EPSILON)
    normed = center * scaled
    return normed * gain, normed, scaled


def slot_keys(routes_ref, slots_ref, capacity, cap):
    return jnp.where(slots_ref[...] < capacity, routes_ref[...] * cap + slots_ref[...], -1)


def widen(rows):
    count = rows.shape[1]
    padded = jnp.concatenate([rows.astype(jnp.float32), jnp.zeros((6, count), jnp.float32)], 0)
    tall = jnp.transpose(padded)
    return [jnp.broadcast_to(tall[:, k : k + 1], (count, 128)).astype(jnp.int32) for k in range(2)]


def flat(gain_ref):
    return gain_ref[...].reshape(1, gain_ref.shape[0])


class Place:
    def __init__(self, experts):
        self.experts = experts
        self.n = lax.axis_index("narrow")
        self.w = lax.axis_index("wide")
        self.core = lax.rem(self.n, 2)
        self.chip = self.n // 2
        self.me = self.w // 2
        self.parity = lax.rem(self.w, 2)
        self.near_n = self.n + 1 - 2 * self.core
        self.across_n = lax.rem(self.n + 2, 4)
        self.near = {"narrow": self.near_n, "wide": self.w}
        self.across = {"narrow": self.across_n, "wide": self.w}

    def home(self, e):
        return {"narrow": self.n, "wide": 2 * e + self.parity}

    def take(self, i):
        short = jnp.minimum(self.me, self.experts - 1 - self.me)
        swing = jnp.where(lax.rem(i, 2) == 1, (i + 1) // 2, -(i // 2))
        away = jnp.where(i <= 2 * short, swing, i - short)
        return self.me + jnp.where(2 * self.me < self.experts, away, -away)

    def part(self, which, size, align):
        return pl.ds(pl.multiple_of(which * size, align), size)

    def greet(self, others=()):
        barrier = pltpu.get_barrier_semaphore()
        for peer in (self.near, self.across, *others):
            pl.semaphore_signal(barrier, inc=1, device_id=peer, device_id_type=BY_MESH)

        @pl.loop(1, self.experts)
        def _(i):
            pl.semaphore_signal(
                barrier, inc=1, device_id=self.home(self.take(i)), device_id_type=BY_MESH
            )

        pl.semaphore_wait(barrier, self.experts + 1 + len(others))


def mover(sent, came):
    def move(src, dst, row, sent_at, came_at, where):
        return pltpu.make_async_remote_copy(
            src_ref=src,
            dst_ref=dst,
            send_sem=sent.at[row, sent_at],
            recv_sem=came.at[row, came_at],
            device_id=where,
            device_id_type=BY_MESH,
        )

    return move


class Dispatch:
    def __init__(self, place, move, base, send, landing):
        self.place, self.move, self.base = place, move, base
        self.send, self.landing = send, landing
        cap, width = landing.shape[1:]
        self.cap, self.half, self.side = cap, cap // 2, width // 2
        self.mine = place.part(place.core, self.half, 16)
        self.other = place.part(1 - place.core, self.half, 16)
        self.side_mine = place.part(place.chip, self.side, 128)
        self.side_other = place.part(1 - place.chip, self.side, 128)

    def z_copy(self, e, landed):
        return self.move(
            self.send.at[e],
            self.landing.at[landed, self.mine, self.side_mine],
            self.base,
            e,
            landed,
            self.place.home(e),
        )

    def build(self, i, key_row, source):
        e = self.place.take(i)
        hot = self.hot(e, self.place.core, key_row)
        self.send[e] = dot_rows(hot, source[:, self.side_mine]).astype(jnp.bfloat16)
        self.z_copy(e, self.place.me).start()

    def hot(self, e, part, key_row):
        slot = e * self.cap + part * self.half
        slot = slot + lax.broadcasted_iota(jnp.int32, (self.half, key_row.shape[1]), 0)
        hit = (key_row[0:1, :] == slot) | (key_row[1:2, :] == slot)
        return jnp.where(hit, 1.0, 0.0).astype(jnp.bfloat16)

    def build_own(self, key_row, source):
        @pl.loop(0, 2)
        def _(m):
            hot = self.hot(self.place.me, m, key_row)
            part = pl.ds(pl.multiple_of(m * self.half, 16), self.half)
            self.landing[self.place.me, part, :] = dot_rows(hot, source[...]).astype(jnp.bfloat16)

    def spread(self, step, s):
        rows, cols, where = (
            (self.mine, self.side_mine, self.place.across),
            (self.mine, self.side_mine, self.place.near),
            (self.mine, self.side_other, self.place.near),
        )[step]
        ref = self.landing.at[s, rows, cols]
        return self.move(ref, ref, self.base + 1 + step, s, s, where)

    def stage_a(self, i):
        self.landed(i)
        self.relay(i)

    def stage_b(self, i):
        s = self.place.take(i)
        self.spread(0, s).wait_recv()
        self.spread(2, s).start()

    def stage_c(self, i):
        s = self.place.take(i)
        self.spread(1, s).wait_recv()
        self.spread(2, s).wait_recv()

    def landed(self, i):
        s = self.place.take(i)
        self.z_copy(s, s).wait_recv()

    def relay(self, i):
        s = self.place.take(i)
        self.spread(0, s).start()
        self.spread(1, s).start()

    def finish(self, lo, hi, sends=True):
        @pl.loop(lo, hi)
        def _(i):
            s = self.place.take(i)
            for step in range(3):
                self.spread(step, s).wait_send()

        if sends:

            @pl.loop(1, self.place.experts)
            def _(i):
                self.z_copy(self.place.take(i), self.place.me).wait_send()


FRONT_OWN, FRONT_FAR, FRONT_CHIP = 4, 5, 6
FRONT_ROWS = 7
LATE = 2


def front_kernel(
    experts,
    capacity,
    counts,
    x_ref,
    cot_ref,
    routes_ref,
    slots_ref,
    gain1_ref,
    qkv_w,
    out_w,
    gain2_ref,
    router_ref,
    cots_ref,
    heads_hbm,
    attended_hbm,
    stats_hbm,
    mixed_hbm,
    low2_hbm,
    prob_hbm,
    gate_hbm,
    gate_send,
    heads_ref,
    attended_ref,
    stats_ref,
    mixed_ref,
    low2_ref,
    prob_ref,
    gate_ref,
    cot_send,
    gather,
    out_all,
    key_row,
    key_wide,
    route_wide,
    gate_wide,
    router_pad,
    loads,
    sent,
    came,
):
    rows, width = x_ref.shape
    images = counts.shape[0]
    patches = rows // images
    head_cols = out_w.shape[0]
    heads = head_cols // HEAD_DIM
    scale = HEAD_DIM ** (-0.5)
    place = Place(experts)
    move = mover(sent, came)
    cots = Dispatch(place, move, 0, cot_send, cots_ref)
    place.greet()
    key_row[...] = slot_keys(routes_ref, slots_ref, capacity, cots.cap)

    def share(ref, at):
        def copy(step):
            piece = ref(place.across_n if step == 2 else place.n)
            where = place.across if step == 0 else place.near
            row = (FRONT_CHIP, FRONT_OWN, FRONT_FAR)[step]
            return move(piece, piece, row, at, at, where)

        return copy

    out_share = share(lambda n: out_all.at[n], images)
    out_all[place.n] = out_w[...]
    out_share(0).start()
    out_share(1).start()

    @pl.loop(1, experts)
    def _(i):
        cots.build(i, key_row, cot_ref)

    tile = patches // 2

    @pl.loop(0, rows // tile)
    def _(t):
        part = pl.ds(pl.multiple_of(t * tile, 16), tile)
        normed, _, _ = normalize(x_ref[part, :].astype(jnp.float32), flat(gain1_ref))
        low = normed.astype(jnp.bfloat16)
        for i in range(3):
            block = dot_cols(low, qkv_w[i]).astype(jnp.bfloat16)
            for h in range(heads):
                heads_ref[i, h, part, :] = block[:, h * HEAD_DIM : (h + 1) * HEAD_DIM]

    outs = [
        pltpu.make_async_copy(src, dst, loads.at[at])
        for at, (src, dst) in enumerate(
            (
                (heads_ref, heads_hbm),
                (attended_ref, attended_hbm),
                (stats_ref, stats_hbm),
                (mixed_ref, mixed_hbm),
                (low2_ref, low2_hbm),
                (prob_ref, prob_hbm),
                (gate_ref, gate_hbm),
            )
        )
    ]
    outs[0].start()
    for k, column in enumerate(widen(key_row[...])):
        key_wide[k] = column
    for k, column in enumerate(widen(routes_ref[...])):
        route_wide[k] = column
    router_pad[...] = jnp.zeros_like(router_pad)
    router_pad[0:experts] = router_ref[...]
    stats_ref[...] = jnp.zeros_like(stats_ref)

    def attend(image):
        keys_at = pl.ds(pl.multiple_of(image * patches, 16), patches)
        pack = pl.ds(pl.multiple_of(image * tile, 16), tile)
        live = lax.broadcasted_iota(jnp.int32, (1, patches), 1) < counts[image]
        for h in range(heads):
            key_rows = heads_ref[1, h, keys_at, :]
            value_rows = heads_ref[2, h, keys_at, :]
            for t in range(patches // tile):
                part = pl.ds(pl.multiple_of(image * patches + t * tile, 16), tile)
                scores = dot_cols(heads_ref[0, h, part, :], key_rows) * scale
                scores = jnp.where(live, scores, MASKED_SCORE)
                top = jnp.max(scores, -1, keepdims=True)
                weights = jnp.exp(scores - top)
                total = jnp.sum(weights, -1, keepdims=True)
                probs = (weights * (1.0 / total)).astype(jnp.bfloat16)
                block = dot_rows(probs, value_rows).astype(jnp.bfloat16)
                at = t * head_cols + h * HEAD_DIM
                gather[place.n, pack, at : at + HEAD_DIM] = block
                attended_ref[part, h * HEAD_DIM : (h + 1) * HEAD_DIM] = block
                stats_ref[part, h : h + 1] = top + jnp.log(total)

    def image_share(image):
        pack = pl.ds(pl.multiple_of(image * tile, 16), tile)
        return share(lambda n: gather.at[n, pack, :], image)

    @pl.loop(0, images)
    def _(image):
        attend(image)
        image_share(image)(0).start()
        image_share(image)(1).start()

    outs[1].start()
    outs[2].start()
    out_share(0).wait_recv()
    out_share(2).start()
    cots.build_own(key_row, cot_ref)

    @pl.loop(1, experts - LATE)
    def _(i):
        cots.stage_a(i)

    out_share(1).wait_recv()
    out_share(2).wait_recv()

    def finish(image):
        copy = image_share(image)
        copy(0).wait_recv()
        copy(2).start()
        copy(1).wait_recv()
        copy(2).wait_recv()
        pack = pl.ds(pl.multiple_of(image * tile, 16), tile)

        for t in range(2):
            part = pl.ds(pl.multiple_of(image * patches + t * tile, 16), tile)
            cols = slice(t * head_cols, (t + 1) * head_cols)
            attention = dot_rows(gather[0, pack, cols], out_all[0])
            for n in range(1, 4):
                attention += dot_rows(gather[n, pack, cols], out_all[n])
            offset = t * tile + lax.broadcasted_iota(jnp.int32, (tile, 1), 0)
            mixed = x_ref[part, :].astype(jnp.float32) + jnp.where(
                offset < counts[image], attention, 0.0
            )
            mixed_ref[part, :] = mixed
            normed, _, _ = normalize(mixed, flat(gain2_ref))
            low = normed.astype(jnp.bfloat16)
            low2_ref[part, :] = low
            lane = lax.broadcasted_iota(jnp.int32, (tile, 128), 1)
            logits = jnp.where(lane < experts, dot_cols(low, router_pad[...]), MASKED_SCORE)
            powers = jnp.exp(logits - jnp.max(logits, -1, keepdims=True))
            prob = powers / jnp.sum(powers, -1, keepdims=True)
            prob_ref[part, :] = prob
            picked = [
                jnp.sum(jnp.where(lane == route_wide[k, part, :], prob, 0.0), 1, keepdims=True)
                for k in range(2)
            ]
            both = picked[0] + picked[1]
            gate_ref[part, :] = jnp.where(
                lane == 0, picked[0] / both, jnp.where(lane == 1, picked[1] / both, both)
            )

    @pl.loop(0, images)
    def _(image):
        finish(image)

    for out in outs[3:]:
        out.start()

    wide_cap = gate_send.shape[2]

    for k in range(2):
        gate_wide[k] = jnp.broadcast_to(gate_ref[:, k : k + 1], (rows, 128))

    @pl.loop(0, experts)
    def _(e):
        @pl.loop(0, wide_cap // 128)
        def _(j):
            lanes = pl.ds(pl.multiple_of(j * 128, 128), 128)
            slot = e * cots.cap + j * 128 + lax.broadcasted_iota(jnp.int32, (rows, 128), 1)
            picked = jnp.where(key_wide[0] == slot, gate_wide[0], 0.0) + jnp.where(
                key_wide[1] == slot, gate_wide[1], 0.0
            )
            gate_send[e, :, lanes] = jnp.broadcast_to(jnp.sum(picked, 0, keepdims=True), (8, 128))

    @pl.loop(1, experts - LATE)
    def _(i):
        cots.stage_b(i)

    @pl.loop(1, experts - LATE)
    def _(i):
        cots.stage_c(i)

    @pl.loop(experts - LATE, experts)
    def _(i):
        cots.landed(i)

    cots.finish(1, experts - LATE)
    for out in outs:
        out.wait()
    for step in range(3):
        out_share(step).wait_send()
        for image in range(images):
            image_share(image)(step).wait_send()


def front(
    counts, x, cot, routes, slots, gain1, qkv_w, out_w, gain2, router, experts, capacity, cap
):
    rows, width = x.shape
    head_cols = out_w.shape[0]
    heads = head_cols // HEAD_DIM
    images = counts.shape[0]
    bf16, f32 = jnp.bfloat16, jnp.float32
    vmem = pl.BlockSpec(memory_space=pltpu.VMEM)
    hbm = pl.BlockSpec(memory_space=pl.ANY)
    table = max(experts, images + 1)
    wide_cap = round_up(cap, 128)
    return pl.pallas_call(
        functools.partial(front_kernel, experts, capacity),
        out_shape=[
            jax.ShapeDtypeStruct((experts, cap, width), bf16),
            jax.ShapeDtypeStruct((3, heads, rows, HEAD_DIM), bf16),
            jax.ShapeDtypeStruct((rows, head_cols), bf16),
            jax.ShapeDtypeStruct((rows, 128), f32),
            jax.ShapeDtypeStruct((rows, width), f32),
            jax.ShapeDtypeStruct((rows, width), bf16),
            jax.ShapeDtypeStruct((rows, 128), f32),
            jax.ShapeDtypeStruct((rows, 128), f32),
            jax.ShapeDtypeStruct((experts, 8, wide_cap), f32),
        ],
        in_specs=[pl.BlockSpec(memory_space=pltpu.SMEM)] + [vmem] * 9,
        out_specs=[vmem] + [hbm] * 7 + [vmem],
        scratch_shapes=[
            pltpu.VMEM((3, heads, rows, HEAD_DIM), bf16),
            pltpu.VMEM((rows, head_cols), bf16),
            pltpu.VMEM((rows, 128), f32),
            pltpu.VMEM((rows, width), f32),
            pltpu.VMEM((rows, width), bf16),
            pltpu.VMEM((rows, 128), f32),
            pltpu.VMEM((rows, 128), f32),
            pltpu.VMEM((experts, cap // 2, width // 2), bf16),
            pltpu.VMEM((4, rows // 2, 2 * head_cols), bf16),
            pltpu.VMEM((4, head_cols, width), bf16),
            pltpu.VMEM((2, rows), jnp.int32),
            pltpu.VMEM((2, rows, 128), jnp.int32),
            pltpu.VMEM((2, rows, 128), jnp.int32),
            pltpu.VMEM((2, rows, 128), f32),
            pltpu.VMEM((128, width), bf16),
            pltpu.SemaphoreType.DMA((7,)),
            pltpu.SemaphoreType.DMA((FRONT_ROWS, table)),
            pltpu.SemaphoreType.DMA((FRONT_ROWS, table)),
        ],
        compiler_params=pltpu.CompilerParams(
            collective_id=2, has_side_effects=True, vmem_limit_bytes=VMEM_BYTES
        ),
    )(counts, x, cot, routes, slots, gain1, qkv_w, out_w, gain2, router)


class Return:
    def __init__(self, place, move, base, core_send, core_recv, kept, chip_send, chip_recv, back):
        self.place, self.move, self.base = place, move, base
        self.core_send, self.core_recv, self.kept = core_send, core_recv, kept
        self.chip_send, self.chip_recv, self.back = chip_send, chip_recv, back
        self.half, self.side = chip_send.shape[1:]
        self.mine = place.part(place.core, self.half, 16)
        self.other = place.part(1 - place.core, self.half, 16)
        self.side_mine = place.part(place.chip, self.side, 128)
        self.side_other = place.part(1 - place.chip, self.side, 128)

    def rows(self, s):
        return pl.ds(pl.multiple_of(s * self.half, 16), self.half)

    def core_move(self, s):
        return self.move(
            self.core_send.at[s], self.core_recv.at[s], self.base, s, s, self.place.near
        )

    def chip_move(self, s):
        return self.move(
            self.chip_send.at[s], self.chip_recv.at[s], self.base + 1, s, s, self.place.across
        )

    def home_move(self, s, landed):
        return self.move(
            self.core_send.at[s, :, pl.ds(0, self.side)],
            self.back.at[landed, self.mine, :],
            self.base + 2,
            s,
            landed,
            self.place.home(s),
        )

    def pair_move(self, e, part):
        ref = self.back.at[e, part, :]
        return self.move(ref, ref, self.base + 3, e, e, self.place.near)

    def first(self, s, product):
        self.core_send[s] = product(self.other).astype(jnp.bfloat16)
        self.core_move(s).start()
        self.kept[self.rows(s), :] = product(self.mine)

    def second(self, s):
        self.core_move(s).wait_recv()
        self.chip_send[s] = (
            self.kept[self.rows(s), self.side_other]
            + self.core_recv[s, :, self.side_other].astype(jnp.float32)
        ).astype(jnp.bfloat16)
        self.chip_move(s).start()

    def third(self, s):
        self.chip_move(s).wait_recv()
        self.core_move(s).wait_send()
        piece = (
            self.kept[self.rows(s), self.side_mine]
            + self.core_recv[s, :, self.side_mine].astype(jnp.float32)
            + self.chip_recv[s].astype(jnp.float32)
        ).astype(jnp.bfloat16)

        @pl.when(s == self.place.me)
        def _():
            self.back[self.place.me, self.mine, :] = piece

        @pl.when(s != self.place.me)
        def _():
            self.core_send[s, :, 0 : self.side] = piece
            self.home_move(s, self.place.me).start()

    def fourth(self, i):
        e = self.place.take(i)

        @pl.when(e != self.place.me)
        def _():
            self.home_move(e, e).wait_recv()

        self.pair_move(e, self.mine).start()

    def ready(self, i):
        self.pair_move(self.place.take(i), self.other).wait_recv()

    def finish(self):
        @pl.loop(0, self.place.experts)
        def _(i):
            s = self.place.take(i)
            self.chip_move(s).wait_send()
            self.pair_move(s, self.mine).wait_send()

            @pl.when(i > 0)
            def _():
                self.home_move(s, self.place.me).wait_send()


class Quarters:
    def __init__(self, place, move, base, at, ref):
        self.place, self.move, self.base, self.at, self.ref = place, move, base, at, ref
        rows, width = ref.shape
        self.rows = place.part(place.core, rows // 2, 16)
        self.mine = place.part(place.chip, width // 2, 128)
        self.other = place.part(1 - place.chip, width // 2, 128)

    def copy(self, step):
        ref = self.ref.at[self.rows, self.other if step == 2 else self.mine]
        where = self.place.across if step == 0 else self.place.near
        return self.move(ref, ref, self.base + step, self.at, self.at, where)

    def start(self):
        self.copy(0).start()
        self.copy(1).start()

    def relay(self):
        self.copy(0).wait_recv()
        self.copy(2).start()

    def ready(self):
        self.copy(1).wait_recv()
        self.copy(2).wait_recv()

    def finish(self):
        for step in range(3):
            self.copy(step).wait_send()


M_CORE, M_CHIP, M_HOME, M_BACK, M_MIX, M_END, M_PAIR, M_LATE, M_GATES = 4, 5, 6, 7, 11, 13, 16, 17, 21
M_ROWS = 22
MIX_EARLY = 4
GRAD_PARTS, GRAD_EARLY = 4, 2


def middle_kernel(
    experts,
    capacity,
    counts,
    low_ref,
    cot_hbm,
    routes_ref,
    slots_ref,
    gate_col,
    gate_send,
    in_hbm,
    out_hbm,
    cots_hbm,
    mixed_hbm,
    prob_ref,
    gain_ref,
    router_ref,
    half_hbm,
    mixed_grad_hbm,
    att_grad_hbm,
    router_grad,
    gain_grad,
    grad_out,
    grad_in,
    in_ref,
    out_ref,
    cots_ref,
    rows_ref,
    hid_ref,
    pre_ref,
    send_rows,
    gate_rows,
    gate_tall,
    pair_tall,
    pair_part,
    pair_core,
    pair_sum,
    pair_chip,
    pair_home,
    pair_back,
    core_send,
    core_recv,
    kept,
    chip_send,
    chip_recv,
    back,
    mix_send,
    mix_recv,
    mix_last,
    key_row,
    key_wide,
    route_wide,
    router_pad,
    hot_ref,
    total,
    pair_ref,
    dis_ref,
    copy_send,
    copy_recv,
    in_send,
    in_recv,
    cot_tile,
    scale_wide,
    loads,
    cot_loads,
    sent,
    came,
):
    rows, width = low_ref.shape
    images = counts.shape[0]
    patches = rows // images
    cap = rows_ref.shape[1]
    half = cap // 2
    units = in_ref.shape[1]
    place = Place(experts)
    move = mover(sent, came)
    me = place.me
    lows = Dispatch(place, move, 0, send_rows, rows_ref)
    late = Dispatch(place, move, M_LATE, send_rows, cots_ref)
    dgrad = Return(
        place, move, M_BACK, core_send, core_recv, kept, chip_send, chip_recv, back
    )
    other_copy = {"narrow": place.n, "wide": place.w + 1 - 2 * place.parity}

    def load(at, src, dst):
        return pltpu.make_async_copy(src, dst, loads.at[at])

    fetched = [
        load(0, in_hbm, in_ref),
        load(1, out_hbm, out_ref),
    ]
    for copy in fetched:
        copy.start()

    def cots_in(i, whole):
        s = place.take(i)
        at = (s,) if whole else (s, late.mine, late.side_mine)
        return pltpu.make_async_copy(cots_hbm.at[at], cots_ref.at[at], cot_loads.at[i])

    @pl.loop(0, experts - LATE)
    def _(i):
        cots_in(i, True).start()

    for i in range(experts - LATE, experts):
        cots_in(i, False).start()
    place.greet((other_copy,))
    key_row[...] = slot_keys(routes_ref, slots_ref, capacity, cap)

    def gate_copy(e, landed):
        return move(gate_send.at[e], gate_rows.at[landed], M_GATES, e, landed, place.home(e))

    @pl.loop(1, experts)
    def _(i):
        lows.build(i, key_row, low_ref)
        gate_copy(place.take(i), me).start()

    gate_rows[me] = gate_send[me]

    for copy in fetched:
        copy.wait()

    @pl.loop(0, experts - LATE)
    def _(i):
        cots_in(i, True).wait()

    for i in range(experts - LATE, experts):
        cots_in(i, False).wait()
        late.relay(i)

    lows.build_own(key_row, low_ref)
    pair_tall[...] = jnp.zeros_like(pair_tall)
    grad_out[...] = jnp.zeros_like(grad_out)
    grad_in[...] = jnp.zeros_like(grad_in)
    for k, column in enumerate(widen(key_row[...])):
        key_wide[k] = column
    for k, column in enumerate(widen(routes_ref[...])):
        route_wide[k] = column
    router_pad[...] = jnp.zeros_like(router_pad)
    router_pad[0:experts] = router_ref[...]

    def pair_move(step, s):
        src, dst, row, where = (
            (pair_part, pair_core, M_CORE, place.near),
            (pair_sum, pair_chip, M_CHIP, place.across),
        )[step]
        return move(src.at[s], dst.at[s], row, s, s, where)

    def pair_return(s, landed):
        return move(pair_home.at[s], pair_back.at[landed], M_HOME, s, landed, place.home(s))

    chunk = 256 if units % 256 == 0 else units

    def compute(s, m):
        part = pl.ds(pl.multiple_of(m * half, 16), half)
        left = rows_ref[s, part, :]
        cots = cots_ref[s, part, :]
        gate = gate_tall[part, 0:1]
        pair = jnp.zeros((half, 1), jnp.float32)
        for j in range(units // chunk):
            cols = slice(j * chunk, (j + 1) * chunk)
            pre = dot_rows(left, in_ref[:, cols])
            free = dot_cols(cots, out_ref[cols, :])
            cdf, slope = normal_parts(pre)
            hidden = pre * cdf
            hid_ref[s, part, cols] = (gate * hidden).astype(jnp.bfloat16)
            pre_ref[s, part, cols] = (gate * free * (cdf + slope)).astype(jnp.bfloat16)
            pair += jnp.sum(hidden * free, 1, keepdims=True)
        pair_tall[part, :] = jnp.broadcast_to(pair, (half, 128))

    def second(s):
        dgrad.second(s)
        pair_move(0, s).wait_recv()
        pair_sum[s] = pair_part[s] + pair_core[s]
        pair_move(1, s).start()

    def third(s):
        dgrad.third(s)
        pair_move(1, s).wait_recv()
        line = pair_sum[s] + pair_chip[s]

        @pl.when(s == me)
        def _():
            pair_back[me] = line

        @pl.when(s != me)
        def _():
            pair_home[s] = line
            pair_return(s, me).start()

    def contract(left, right):
        return lax.dot_general(
            left, right, (((0,), (0,)), ((), ())), preferred_element_type=jnp.float32
        )

    def mix_move(s):
        return move(mix_send.at[s], mix_recv.at[s], M_MIX, s, s, place.near)

    def mix_chip(s):
        src = mix_recv.at[s, :, dgrad.side_other]
        return move(src, mix_last.at[s], M_MIX + 1, s, s, place.across)

    def mix_first(s):
        mix_send[s] = dot_rows(hid_ref[s, dgrad.other, :], out_ref[...]).astype(jnp.bfloat16)
        mix_move(s).start()

    def mix_second(s):
        mix_move(s).wait_recv()
        mix_recv[s] = (
            dot_rows(hid_ref[s, dgrad.mine, :], out_ref[...]) + mix_recv[s].astype(jnp.float32)
        ).astype(jnp.bfloat16)

    def mix_third(s):
        mix_chip(s).wait()
        total_part = mix_recv[s, :, dgrad.side_mine].astype(jnp.float32)
        mix_recv[s, :, 0 : dgrad.side] = (total_part + mix_last[s].astype(jnp.float32)).astype(
            jnp.bfloat16
        )

    def work(i, between):
        s = place.take(i)
        gate_tall[...] = jnp.transpose(gate_rows[s])

        @pl.loop(0, 2)
        def _(m):
            compute(s, m)

            @pl.when(m == 0)
            def _():
                between()

        pair_part[s] = jnp.transpose(pair_tall[...])[0:8]
        pair_move(0, s).start()
        dgrad.first(s, lambda part: dot_cols(pre_ref[s, part, :], in_ref[...]))

    def add_out(s):
        grad_out[...] += contract(hid_ref[s], cots_ref[s])

    def add_in(lo, hi):
        @pl.loop(lo, hi)
        def _(i):
            s = place.take(i)
            grad_in[...] += contract(rows_ref[s], pre_ref[s])

    def pass_on(i):
        @pl.when((i > 0) & (i + 1 < experts))
        def _():
            lows.stage_a(i + 1)

    @pl.loop(0, experts)
    def _(i):
        s = place.take(i)

        @pl.when(i > 0)
        def _():
            lows.stage_b(i)
            lows.stage_c(i)
            gate_copy(s, s).wait_recv()

        @pl.when(i >= experts - LATE)
        def _():
            late.stage_c(i)

        work(i, lambda: pass_on(i))

        @pl.when(i == 0)
        def _():
            lows.stage_a(1)

        second(s)

        @pl.when(i == 0)
        def _():
            mix_first(s)
            add_in(0, 1)
            for j in range(experts - LATE, experts):
                late.stage_b(j)

        add_out(s)

        @pl.when(i > 1)
        def _():
            third(place.take(i - 2))

    last = place.take(experts - 1)
    copy_send[...] = grad_out[...].astype(jnp.bfloat16)
    copy_move = move(copy_send, copy_recv, M_PAIR, 0, 0, other_copy)
    copy_move.start()

    @pl.loop(1, experts)
    def _(i):
        mix_first(place.take(i))

    third(place.take(experts - 2))

    @pl.loop(0, MIX_EARLY)
    def _(i):
        s = place.take(i)
        mix_second(s)
        mix_chip(s).start()

    third(last)
    add_in(1, experts)
    early_rows = in_send.shape[0]
    in_send[...] = grad_in[0:early_rows].astype(jnp.bfloat16)
    in_move = move(in_send, in_recv, M_PAIR, 1, 1, other_copy)
    in_move.start()
    pair_ref[...] = jnp.zeros_like(pair_ref)

    def build_hot(e):
        lane = lax.broadcasted_iota(jnp.int32, (rows // 4, 128), 1)

        @pl.loop(0, 4)
        def _(m):
            part = pl.ds(pl.multiple_of(m * (rows // 4), 16), rows // 4)
            keys = [key_wide[k, part, :] - e * cap for k in range(2)]
            for low in range(0, cap, 128):
                size = min(128, cap - low)
                hit = (keys[0] == lane + low) | (keys[1] == lane + low)
                hot_ref[part, low : low + size] = jnp.where(hit, 1.0, 0.0).astype(jnp.bfloat16)[
                    :, 0:size
                ]

    my_rows = place.part(place.core, rows // 2, 16)
    total[...] = jnp.zeros_like(total)

    @pl.loop(0, experts)
    def _(i):
        e = place.take(i)
        build_hot(e)
        dgrad.fourth(i)

        @pl.when(i > 0)
        def _():
            pair_return(e, e).wait_recv()

        tall = jnp.transpose(pair_back[e])[0:cap, 0:1]
        high = tall.astype(jnp.bfloat16).astype(jnp.float32)
        middle = (tall - high).astype(jnp.bfloat16).astype(jnp.float32)
        lane = lax.broadcasted_iota(jnp.int32, (cap, 128), 1)
        spelled = jnp.where(
            lane == 0, high, jnp.where(lane == 1, middle, jnp.where(lane == 2, tall - high - middle, 0.0))
        ).astype(jnp.bfloat16)
        found = jnp.sum(dot_rows(hot_ref[...], spelled), 1, keepdims=True)
        lane_rows = lax.broadcasted_iota(jnp.int32, (rows, 128), 1)
        pair_ref[...] += jnp.where(lane_rows == e, found, 0.0)
        dgrad.ready(i)
        total[...] += dot_rows(hot_ref[my_rows, :], back[e])

    ends = Quarters(place, move, M_END, 0, dis_ref)
    dis_ref[ends.rows, ends.mine] = total[...].astype(jnp.bfloat16)
    ends.start()

    @pl.loop(MIX_EARLY, experts)
    def _(i):
        mix_second(place.take(i))

    mixed_in = load(1, mixed_hbm, kept.at[pl.ds(0, rows), :])
    mixed_in.start()
    tile = patches // 2
    router_grad[...] = jnp.zeros_like(router_grad)
    gain_grad[...] = jnp.zeros_like(gain_grad)

    def cot_in(t):
        slot = lax.rem(t, 2)
        part = pl.ds(pl.multiple_of(t * tile, 16), tile)
        return pltpu.make_async_copy(cot_hbm.at[part, :], cot_tile.at[slot], loads.at[2 + slot])

    def rows_out(t, what):
        part = pl.ds(pl.multiple_of(t * tile, 16), tile)
        src, dst = ((kept, mixed_grad_hbm), (dis_ref, att_grad_hbm))[what]
        return pltpu.make_async_copy(src.at[part, :], dst.at[part, :], loads.at[4 + 2 * t + what])

    cot_in(0).start()
    mixed_in.wait()

    def before(t):
        part = pl.ds(pl.multiple_of(t * tile, 16), tile)
        lane = lax.broadcasted_iota(jnp.int32, (tile, 128), 1)
        by_expert = pair_ref[part, :]
        hots = [lane == route_wide[k, part, :] for k in range(2)]
        pair = [jnp.sum(jnp.where(hot, by_expert, 0.0), 1, keepdims=True) for hot in hots]
        weighted = pair[0] * gate_col[part, 0:1] + pair[1] * gate_col[part, 1:2]
        both = gate_col[part, 2:3]
        prob = prob_ref[part, :]
        prob_grad = jnp.where(hots[0], (pair[0] - weighted) / both, 0.0) + jnp.where(
            hots[1], (pair[1] - weighted) / both, 0.0
        )
        logit_grad = prob * (prob_grad - jnp.sum(prob * prob_grad, 1, keepdims=True))
        pair_ref[part, :] = logit_grad
        router_grad[...] += contract(logit_grad.astype(jnp.bfloat16), low_ref[part, :])
        _, hat, scaled = normalize(kept[part, :], flat(gain_ref))
        kept[part, :] = hat
        scale_wide[part, :] = jnp.broadcast_to(scaled, (tile, 128))

    @pl.loop(0, rows // tile)
    def _(t):
        @pl.when(t == 2)
        def _():
            ends.relay()

        before(t)

    ends.ready()
    ends.finish()

    @pl.loop(0, rows // tile)
    def _(t):
        @pl.when(t + 1 < rows // tile)
        def _():
            cot_in(t + 1).start()

        part = pl.ds(pl.multiple_of(t * tile, 16), tile)
        normed_grad = dis_ref[part, :].astype(jnp.float32) + dot_rows(
            pair_ref[part, :].astype(jnp.bfloat16), router_pad[...]
        )
        hat = kept[part, :]
        gain_grad[...] += jnp.sum(normed_grad * hat, 0, keepdims=True)
        grad = normed_grad * flat(gain_ref)
        inner = (
            grad - jnp.mean(grad, -1, keepdims=True) - hat * jnp.mean(grad * hat, -1, keepdims=True)
        )
        cot_in(t).wait()
        full = cot_tile[lax.rem(t, 2)].astype(jnp.float32) + scale_wide[part, 0:1] * inner
        kept[part, :] = full
        rows_out(t, 0).start()
        row = t * tile + lax.broadcasted_iota(jnp.int32, (tile, 1), 0)
        live = lax.rem(row, patches) < jnp.where(t * tile < patches, counts[0], counts[images - 1])
        dis_ref[part, :] = jnp.where(live, full, 0.0).astype(jnp.bfloat16)
        rows_out(t, 1).start()

    @pl.loop(0, MIX_EARLY)
    def _(i):
        mix_third(place.take(i))

    half_out = load(0, mix_recv, half_hbm)
    half_out.start()
    copy_move.wait()
    grad_out[...] += copy_recv[...].astype(jnp.float32)
    in_move.wait()
    grad_in[0:early_rows] += in_recv[...].astype(jnp.float32)
    half_out.wait()

    @pl.loop(0, rows // tile)
    def _(t):
        rows_out(t, 0).wait()
        rows_out(t, 1).wait()

    dgrad.finish()
    lows.finish(1, experts)
    late.finish(experts - LATE, experts, False)

    @pl.loop(0, experts)
    def _(i):
        s = place.take(i)
        pair_move(0, s).wait_send()
        pair_move(1, s).wait_send()
        mix_move(s).wait_send()

        @pl.when(i > 0)
        def _():
            pair_return(s, me).wait_send()
            gate_copy(s, me).wait_send()


def middle(
    counts,
    low,
    cot,
    routes,
    slots,
    gates,
    gate_rows,
    weight_in,
    weight_out,
    cots,
    mixed,
    prob,
    gain,
    router,
    experts,
    capacity,
):
    rows, width = low.shape
    units = weight_in.shape[1]
    cap = cots.shape[1]
    half, side, wide_cap = cap // 2, width // 2, round_up(cap, 128)
    bf16, f32 = jnp.bfloat16, jnp.float32
    vmem = pl.BlockSpec(memory_space=pltpu.VMEM)
    hbm = pl.BlockSpec(memory_space=pl.ANY)
    line = pltpu.VMEM((experts, 8, wide_cap), f32)
    halves = pltpu.VMEM((experts, half, width), bf16)
    tile = rows // counts.shape[0] // 2
    return pl.pallas_call(
        functools.partial(middle_kernel, experts, capacity),
        out_shape=[
            jax.ShapeDtypeStruct((experts, half, width), bf16),
            jax.ShapeDtypeStruct((rows, width), f32),
            jax.ShapeDtypeStruct((rows, width), bf16),
            jax.ShapeDtypeStruct((128, width), f32),
            jax.ShapeDtypeStruct((1, width), f32),
            jax.ShapeDtypeStruct((units, width), f32),
            jax.ShapeDtypeStruct((width, units), f32),
        ],
        in_specs=[
            pl.BlockSpec(memory_space=pltpu.SMEM),
            vmem,
            hbm,
            vmem,
            vmem,
            vmem,
            vmem,
            hbm,
            hbm,
            hbm,
            hbm,
            vmem,
            vmem,
            vmem,
        ],
        out_specs=[hbm] * 3 + [vmem] * 4,
        scratch_shapes=[
            pltpu.VMEM((width, units), bf16),
            pltpu.VMEM((units, width), bf16),
            pltpu.VMEM((experts, cap, width), bf16),
            pltpu.VMEM((experts, cap, width), bf16),
            pltpu.VMEM((experts, cap, units), bf16),
            pltpu.VMEM((experts, cap, units), bf16),
            pltpu.VMEM((experts, half, side), bf16),
            line,
            pltpu.VMEM((wide_cap, 8), f32),
            pltpu.VMEM((wide_cap, 128), f32),
            line,
            line,
            line,
            line,
            line,
            line,
            halves,
            halves,
            pltpu.VMEM((max(experts * half, rows), width), f32),
            pltpu.VMEM((experts, half, side), bf16),
            pltpu.VMEM((experts, half, side), bf16),
            pltpu.VMEM((experts, cap, side), bf16),
            halves,
            halves,
            pltpu.VMEM((experts, half, side), bf16),
            pltpu.VMEM((2, rows), jnp.int32),
            pltpu.VMEM((2, rows, 128), jnp.int32),
            pltpu.VMEM((2, rows, 128), jnp.int32),
            pltpu.VMEM((128, width), bf16),
            pltpu.VMEM((rows, cap), bf16),
            pltpu.VMEM((rows // 2, side), f32),
            pltpu.VMEM((rows, 128), f32),
            pltpu.VMEM((rows, width), bf16),
            pltpu.VMEM((units, width), bf16),
            pltpu.VMEM((units, width), bf16),
            pltpu.VMEM((width * GRAD_EARLY // GRAD_PARTS, units), bf16),
            pltpu.VMEM((width * GRAD_EARLY // GRAD_PARTS, units), bf16),
            pltpu.VMEM((2, tile, width), bf16),
            pltpu.VMEM((rows, 128), f32),
            pltpu.SemaphoreType.DMA((4 + 2 * (rows // tile),)),
            pltpu.SemaphoreType.DMA((experts,)),
            pltpu.SemaphoreType.DMA((M_ROWS, experts)),
            pltpu.SemaphoreType.DMA((M_ROWS, experts)),
        ],
        compiler_params=pltpu.CompilerParams(
            collective_id=1, has_side_effects=True, vmem_limit_bytes=VMEM_BYTES
        ),
    )(
        counts,
        low,
        cot,
        routes,
        slots,
        gates,
        gate_rows,
        weight_in,
        weight_out,
        cots,
        mixed,
        prob,
        gain,
        router,
    )


class Fold:
    def __init__(self, place, move, base, core_send, core_recv, kept, chip_send, chip_recv, whole):
        self.place, self.move, self.base = place, move, base
        self.core_send, self.core_recv, self.kept = core_send, core_recv, kept
        self.chip_send, self.chip_recv, self.whole = chip_send, chip_recv, whole
        self.half, self.side = chip_send.shape[1:]
        self.side_mine = place.part(place.chip, self.side, 128)
        self.side_other = place.part(1 - place.chip, self.side, 128)

    def rows(self, image, core):
        start = (2 * image + core) * self.half
        return pl.ds(pl.multiple_of(start, 16), self.half)

    def core_move(self, image):
        return self.move(
            self.core_send.at[image],
            self.core_recv.at[image],
            self.base,
            image,
            image,
            self.place.near,
        )

    def chip_move(self, image):
        return self.move(
            self.chip_send.at[image],
            self.chip_recv.at[image],
            self.base + 1,
            image,
            image,
            self.place.across,
        )

    def share(self, image, step):
        cols = self.side_other if step == 2 else self.side_mine
        ref = self.whole.at[self.rows(image, self.place.core), cols]
        where = self.place.across if step == 0 else self.place.near
        return self.move(ref, ref, self.base + 2 + step, image, image, where)

    def second(self, image):
        self.core_move(image).wait_recv()
        self.chip_send[image] = (
            self.kept[image, :, self.side_other]
            + self.core_recv[image, :, self.side_other].astype(jnp.float32)
        ).astype(jnp.bfloat16)
        self.chip_move(image).start()

    def third(self, image):
        self.chip_move(image).wait_recv()
        self.whole[self.rows(image, self.place.core), self.side_mine] = (
            self.kept[image, :, self.side_mine]
            + self.core_recv[image, :, self.side_mine].astype(jnp.float32)
            + self.chip_recv[image].astype(jnp.float32)
        ).astype(jnp.bfloat16)
        self.share(image, 0).start()
        self.share(image, 1).start()

    def relay(self, image):
        self.share(image, 0).wait_recv()
        self.share(image, 2).start()

    def ready(self, image):
        self.share(image, 1).wait_recv()
        self.share(image, 2).wait_recv()

    def finish(self, images):
        for image in range(images):
            self.core_move(image).wait_send()
            self.chip_move(image).wait_send()
            for step in range(3):
                self.share(image, step).wait_send()


class WideSum:
    def __init__(self, place, move, tables, pair_send, pair_recv, kept, group_send, group_recv, whole):
        self.place, self.move = place, move
        self.pair_sems, self.group_out, self.group_in = tables
        self.pair_send, self.pair_recv, self.kept = pair_send, pair_recv, kept
        self.group_send, self.group_recv, self.whole = group_send, group_recv, whole
        self.rows, self.cols = group_recv.shape[2:]
        self.half = pair_send.shape[1]
        self.real = kept.shape[1]
        self.pair = {"narrow": place.n, "wide": place.w + 1 - 2 * place.parity}

    def pair_move(self, p):
        return self.move[0](
            self.pair_send.at[p], self.pair_recv.at[p], 0, p, p, self.pair
        )

    def chunk(self, e):
        return (
            pl.ds(pl.multiple_of((e // 2) * self.rows, 16), self.rows),
            pl.ds(pl.multiple_of(lax.rem(e, 2) * self.cols, 128), self.cols),
        )

    def group_move(self, p, e, landed):
        rows, cols = self.chunk(e)
        return self.move[1](
            self.group_send.at[p, rows, cols],
            self.group_recv.at[p, landed],
            p,
            e,
            landed,
            self.place.home(e),
        )

    def group_share(self, p, owner, at, landed, where):
        rows, cols = self.chunk(owner)
        ref = self.whole.at[p, self.place.parity, rows, cols]
        pieces = self.pair_send.shape[0]
        return self.move[1](ref, ref, pieces + p, at, landed, where)

    def pair_share(self, p, parity):
        ref = self.whole.at[p, parity]
        return self.move[0](ref, ref, 1, p, p, self.pair)

    def first(self, p, halves):
        @pl.when(self.place.parity == 0)
        def _():
            self.kept[p] = halves[0]
            self.pair_send[p, 0 : self.real] = halves[1].astype(jnp.bfloat16)

        @pl.when(self.place.parity == 1)
        def _():
            self.kept[p] = halves[1]
            self.pair_send[p, 0 : self.real] = halves[0].astype(jnp.bfloat16)

        self.pair_move(p).start()

    def second(self, p):
        self.pair_move(p).wait_recv()
        self.group_send[p, 0 : self.real] = (
            self.kept[p] + self.pair_recv[p, 0 : self.real].astype(jnp.float32)
        ).astype(jnp.bfloat16)

        @pl.loop(1, self.place.experts)
        def _(i):
            self.group_move(p, self.place.take(i), self.place.me).start()

    def third(self, p):
        rows, cols = self.chunk(self.place.me)
        total = self.group_send[p, rows, cols].astype(jnp.float32)
        self.total[...] = total

        @pl.loop(1, self.place.experts)
        def _(i):
            s = self.place.take(i)
            self.group_move(p, s, s).wait_recv()
            self.total[...] += self.group_recv[p, s].astype(jnp.float32)

        self.whole[p, self.place.parity, rows, cols] = self.total[...].astype(jnp.bfloat16)

        @pl.loop(1, self.place.experts)
        def _(i):
            e = self.place.take(i)
            self.group_share(p, self.place.me, e, self.place.me, self.place.home(e)).start()

    def fourth(self, p):
        @pl.loop(1, self.place.experts)
        def _(i):
            s = self.place.take(i)
            self.group_share(p, s, s, s, self.place.home(s)).wait_recv()

        self.pair_share(p, self.place.parity).start()

    def ready(self, p):
        self.pair_share(p, 1 - self.place.parity).wait_recv()

    def finish(self):
        for p in range(self.pair_send.shape[0]):
            self.pair_move(p).wait_send()
            self.pair_share(p, self.place.parity).wait_send()

            @pl.loop(1, self.place.experts)
            def _(i):
                e = self.place.take(i)
                self.group_move(p, e, self.place.me).wait_send()
                self.group_share(p, self.place.me, e, self.place.me, self.place.home(e)).wait_send()


B_MIX, B_ENDMIX, B_FOLD, B_SMALL, B_GRAD = 0, 3, 6, 11, 13
B_ROWS = 14


def back_kernel(
    experts,
    capacity,
    counts,
    att_grad,
    mixed_grad_hbm,
    heads_ref,
    stats_ref,
    attended_ref,
    x_ref,
    gain_ref,
    qkv_w,
    out_w,
    mixed_hbm,
    half_ref,
    routes_ref,
    slots_ref,
    router_part,
    gain2_part,
    grad_hbm,
    out_ref,
    x_grad_hbm,
    in_grad,
    out_grad,
    small_out,
    grad_sum_hbm,
    grad_sum,
    mixed_part,
    x_grad,
    grad_send,
    grad_recv,
    whole_ref,
    loads,
    low_ref,
    lines,
    head_grad,
    proj_grad,
    key_wide,
    chip_recv,
    back,
    hot_ref,
    total,
    fold_send,
    fold_recv,
    fold_kept,
    fold_chip_send,
    fold_chip_recv,
    normed_ref,
    pair_send,
    pair_recv,
    pair_kept,
    group_send,
    group_recv,
    group_total,
    small_ref,
    small_near,
    small_far,
    small_pair,
    small_group,
    small_steps,
    sent,
    came,
    pair_sent,
    pair_came,
    group_sent,
    group_came,
):
    rows, width = att_grad.shape
    images = counts.shape[0]
    patches = rows // images
    head_cols = attended_ref.shape[1]
    heads = head_cols // HEAD_DIM
    scale = HEAD_DIM ** (-0.5)
    cap = back.shape[1]
    tile = patches // 2
    pieces = heads + 1
    place = Place(experts)
    move = mover(sent, came)
    me = place.me
    wide = WideSum(
        place,
        (mover(pair_sent, pair_came), mover(group_sent, group_came)),
        (None, None, None),
        pair_send,
        pair_recv,
        pair_kept,
        group_send,
        group_recv,
        whole_ref,
    )
    wide.total = group_total
    fold = Fold(
        place,
        move,
        B_FOLD,
        fold_send,
        fold_recv,
        fold_kept,
        fold_chip_send,
        fold_chip_recv,
        normed_ref,
    )
    my_rows = place.part(place.core, rows // 2, 16)
    side_mine = place.part(place.chip, width // 2, 128)

    def load(at, src, dst):
        return pltpu.make_async_copy(src, dst, loads.at[at])

    grad_in = load(0, grad_hbm, grad_sum)
    mixed_in = load(1, mixed_hbm.at[my_rows, side_mine], mixed_part)
    mixed_grad_in = load(2, mixed_grad_hbm, x_grad)
    grad_in.start()
    mixed_in.start()
    mixed_grad_in.start()
    place.greet((wide.pair,))

    def grad_part(k):
        size = grad_sum.shape[0] // GRAD_PARTS
        return pl.ds(k * size, size)

    def grad_move(k):
        part = grad_part(k)
        return move(grad_send.at[part, :], grad_recv.at[part, :], B_GRAD, k, k, wide.pair)

    def grad_go(k):
        part = grad_part(k)
        grad_send[part, :] = grad_sum[part, :].astype(jnp.bfloat16)
        grad_move(k).start()

    def grad_out(k):
        part = grad_part(k)
        return load(3 + 2 * images + k, grad_sum.at[part, :], grad_sum_hbm.at[part, :])

    def grad_end(k):
        part = grad_part(k)
        grad_move(k).wait()
        grad_sum[part, :] += grad_recv[part, :].astype(jnp.float32)
        grad_out(k).start()

    half = half_ref.shape[1]
    side = width // 2
    mine = place.part(place.core, half, 16)
    other = place.part(1 - place.core, half, 16)
    side_other = place.part(1 - place.chip, side, 128)

    def mix_chip(s):
        return move(half_ref.at[s, :, side_other], chip_recv.at[s], B_MIX, s, s, place.across)

    def mix_home(i, landed):
        s = place.take(i)
        early = isinstance(i, int) and i < MIX_EARLY
        src = half_ref.at[s, :, pl.ds(0, side)] if early else chip_recv.at[s]
        return move(src, back.at[landed, mine, :], B_MIX + 1, s, landed, place.home(s))

    def mix_near(e, part):
        ref = back.at[e, part, :]
        return move(ref, ref, B_MIX + 2, e, e, place.near)

    for i in range(1, MIX_EARLY):
        mix_home(i, me).start()

    @pl.loop(MIX_EARLY, experts)
    def _(i):
        mix_chip(place.take(i)).start()

    back[me, mine, :] = half_ref[me, :, 0:side]
    grad_in.wait()
    for k in range(GRAD_EARLY):
        grad_out(k).start()
    grad_go(2)

    def mix_backs():
        @pl.loop(MIX_EARLY, experts)
        def _(i):
            s = place.take(i)
            mix_chip(s).wait_recv()
            chip_recv[s] = (
                half_ref[s, :, side_mine].astype(jnp.float32) + chip_recv[s].astype(jnp.float32)
            ).astype(jnp.bfloat16)
            mix_home(i, me).start()

    def mix_relay(i):
        e = place.take(i)

        @pl.when(e != me)
        def _():
            mix_home(i, e).wait_recv()

        mix_near(e, mine).start()

    def mix_sum(i):
        e = place.take(i)

        lane = lax.broadcasted_iota(jnp.int32, (rows // 4, 128), 1)

        @pl.loop(0, 2)
        def _(m):
            part = pl.ds(pl.multiple_of(m * (rows // 4), 16), rows // 4)
            full = pl.ds(pl.multiple_of((2 * place.core + m) * (rows // 4), 16), rows // 4)
            keys = [key_wide[k, full, :] - e * cap for k in range(2)]
            for low in range(0, cap, 128):
                size = min(128, cap - low)
                hit = (keys[0] == lane + low) | (keys[1] == lane + low)
                hot_ref[part, low : low + size] = jnp.where(hit, 1.0, 0.0).astype(jnp.bfloat16)[
                    :, 0:size
                ]

        mix_near(e, other).wait_recv()
        total[...] += dot_rows(hot_ref[...], back[e])

    ends = Quarters(place, move, B_ENDMIX, 0, out_ref)

    small_sizes = small_ref.shape
    small_ref[...] = jnp.zeros_like(small_ref)
    small_ref[0:experts] = router_part[0:experts]
    small_ref[experts : experts + 1] = gain2_part[...]

    def small_move(step):
        src, dst, where = (
            (small_ref, small_near, place.near),
            (small_steps.at[0], small_far, place.across),
            (small_steps.at[1], small_pair, wide.pair),
        )[step]
        return move(src, dst, B_SMALL, step, step, where)

    def small_home(e, landed):
        return move(
            small_steps.at[2], small_group.at[landed], B_SMALL + 1, e, landed, place.home(e)
        )

    share_row = lax.broadcasted_iota(jnp.int32, small_sizes, 0) == experts + 1

    def small_second():
        small_move(0).wait_recv()
        small_steps[0] = small_ref[...] + jnp.where(share_row, small_near[...], 0.0)
        small_move(1).start()

    def small_third():
        small_move(1).wait_recv()
        small_steps[1] = small_steps[0] + jnp.where(share_row, small_far[...], 0.0)
        small_move(2).start()

    def small_fourth():
        small_move(2).wait_recv()
        small_steps[2] = small_steps[1] + small_pair[...]
        small_group[me] = small_steps[2]

        @pl.loop(1, experts)
        def _(i):
            small_home(place.take(i), me).start()

    def small_last():
        @pl.loop(1, experts)
        def _(i):
            s = place.take(i)
            small_home(s, s).wait_recv()

        small_out[...] = jnp.zeros_like(small_out)

        @pl.loop(0, experts)
        def _(e):
            small_out[...] += small_group[e]

    real = pair_kept.shape[1]

    def contract(left, right):
        return lax.dot_general(
            left, right, (((0,), (0,)), ((), ())), preferred_element_type=jnp.float32
        )

    def zero_pads():
        if pair_send.shape[1] > real:
            pair_send[:, real:] = jnp.zeros_like(pair_send[:, real:])
            group_send[:, real:] = jnp.zeros_like(group_send[:, real:])

    zero_pads()
    product = contract(attended_ref[...], att_grad[...])
    wide.first(0, (product[0:real], product[real:]))

    @pl.loop(0, rows // tile)
    def _(t):
        part = pl.ds(pl.multiple_of(t * tile, 16), tile)
        normed, _, _ = normalize(x_ref[part, :].astype(jnp.float32), flat(gain_ref))
        low_ref[part, :] = normed.astype(jnp.bfloat16)
        block = dot_cols(att_grad[part, :], out_w[...]).astype(jnp.bfloat16)
        for h in range(heads):
            head_grad[h, part, :] = block[:, h * HEAD_DIM : (h + 1) * HEAD_DIM]

    @pl.loop(0, images)
    def _(image):
        part = pl.ds(pl.multiple_of(image * patches, 16), patches)
        padded = round_up(patches, 128)
        column = jnp.concatenate(
            [stats_ref[part, :], jnp.zeros((padded - patches, 128), jnp.float32)], 0
        )
        lines[image] = jnp.transpose(column)[0:8, :]

    def attend_back(image, h):
        part = pl.ds(pl.multiple_of(image * patches, 16), patches)
        query = heads_ref[0, h, part, :]
        key_rows = heads_ref[1, h, part, :]
        out_grad = head_grad[h, part, :]
        live = lax.broadcasted_iota(jnp.int32, (patches, 1), 0) < counts[image]
        line = lines[image, pl.ds(h, 1), 0:patches]
        scores = jnp.where(live, dot_cols(key_rows, query) * scale, MASKED_SCORE)
        probs = jnp.exp(scores - line)
        change = dot_cols(heads_ref[2, h, part, :], out_grad)
        delta = jnp.sum(probs * change, 0, keepdims=True)
        score_grad = (scale * probs * (change - delta)).astype(jnp.bfloat16)
        proj_grad[2, h, part, :] = dot_rows(probs.astype(jnp.bfloat16), out_grad).astype(
            jnp.bfloat16
        )
        proj_grad[1, h, part, :] = dot_rows(score_grad, query).astype(jnp.bfloat16)
        proj_grad[0, h, part, :] = contract(score_grad, key_rows).astype(jnp.bfloat16)

    def piece(h):
        grads = jnp.concatenate([proj_grad[i, h] for i in range(3)], 1)
        product = contract(grads, low_ref[...])
        wide.first(h + 1, (product[0:real], product[real:]))

    def fold_first(image):
        @pl.loop(0, 2)
        def _(turn):
            part = fold.rows(image, jnp.where(turn == 0, 1 - place.core, place.core))
            normed_part = jnp.zeros((tile, width), jnp.float32)
            for i in range(3):
                grads = jnp.concatenate([proj_grad[i, h, part, :] for h in range(heads)], 1)
                normed_part += dot_rows(grads, qkv_w[i])

            @pl.when(turn == 0)
            def _():
                fold_send[image] = normed_part.astype(jnp.bfloat16)
                fold.core_move(image).start()

            @pl.when(turn == 1)
            def _():
                fold_kept[image] = normed_part

            _, hat, _ = normalize(x_ref[part, :].astype(jnp.float32), flat(gain_ref))
            small_ref[experts + 1 : experts + 2] += jnp.sum(normed_part * hat, 0, keepdims=True)

    for k, column in enumerate(widen(slot_keys(routes_ref, slots_ref, capacity, cap))):
        key_wide[k] = column

    def mix_relays(lo, hi):
        @pl.loop(lo, hi)
        def _(i):
            mix_relay(i)

    def mix_sums(lo, hi):
        @pl.loop(lo, hi)
        def _(i):
            mix_sum(i)

    total[...] = jnp.zeros_like(total)

    def mix_tail():
        mixed_in.wait()
        out_ref[ends.rows, ends.mine] = (mixed_part[...] + total[...]).astype(
            jnp.bfloat16
        )
        ends.start()

    agenda = {
        2: [lambda: mix_backs()],
        3: [lambda: fold.second(0)],
        4: [lambda: wide.second(0)],
        5: [lambda: fold.third(0), lambda: wide.second(1)],
    }

    @pl.loop(0, images * heads)
    def _(step):
        attend_back(step // heads, lax.rem(step, heads))

        @pl.when((step == heads - 1) | (step == 2 * heads - 1))
        def _():
            fold_first(step // heads)

        @pl.when(step >= heads)
        def _():
            piece(step - heads)

        for at, todo in agenda.items():

            @pl.when(step == at)
            def _():
                for act in todo:
                    act()

    small_move(0).start()
    grad_go(3)
    wide.second(2)
    fold.second(1)
    small_second()
    wide.third(0)
    fold.relay(0)
    mix_relays(0, experts)
    wide.third(1)
    wide.second(3)
    small_third()
    mix_sums(0, experts)
    fold.third(1)
    mix_tail()
    wide.third(2)
    wide.fourth(0)
    small_fourth()
    fold.ready(0)
    mixed_grad_in.wait()

    def rows_out(t):
        part = pl.ds(pl.multiple_of(t * tile, 16), tile)
        return load(3 + t, x_grad.at[part, :], x_grad_hbm.at[part, :])

    def input_rows(image):
        @pl.loop(2 * image, 2 * image + 2)
        def _(t):
            part = pl.ds(pl.multiple_of(t * tile, 16), tile)
            _, hat, scaled = normalize(x_ref[part, :].astype(jnp.float32), flat(gain_ref))
            grad = normed_ref[part, :].astype(jnp.float32) * flat(gain_ref)
            inner = (
                grad - jnp.mean(grad, -1, keepdims=True) - hat * jnp.mean(grad * hat, -1, keepdims=True)
            )
            x_grad[part, :] += scaled * inner
            rows_out(t).start()

    input_rows(0)
    wide.fourth(1)
    wide.third(3)
    fold.relay(1)
    wide.fourth(2)
    small_last()
    fold.ready(1)
    input_rows(1)
    wide.fourth(3)
    for k in range(GRAD_EARLY, GRAD_PARTS):
        grad_end(k)
    ends.relay()

    def settle(p):
        wide.ready(p)
        if p == 0:
            for side in range(2):
                out_grad[side * real : (side + 1) * real] = whole_ref[0, side, 0:real].astype(
                    jnp.float32
                )
            return
        lanes = (p - 1) * HEAD_DIM
        for i in range(3):
            row = i * HEAD_DIM
            while row < (i + 1) * HEAD_DIM:
                side, at = row // real, row % real
                size = min((i + 1) * HEAD_DIM - row, real - at)
                put = lanes + row - i * HEAD_DIM
                in_grad[i, put : put + size] = whole_ref[p, side, at : at + size].astype(jnp.float32)
                row += size

    for p in range(pieces):
        settle(p)
    ends.ready()

    @pl.loop(0, rows // tile)
    def _(t):
        rows_out(t).wait()

    for k in range(GRAD_PARTS):
        grad_out(k).wait()
    wide.finish()
    fold.finish(images)
    ends.finish()
    for step in range(3):
        small_move(step).wait_send()

    @pl.loop(0, experts)
    def _(i):
        s = place.take(i)
        mix_near(s, mine).wait_send()

        @pl.when(i > 0)
        def _():
            mix_home(i, me).wait_send()
            small_home(s, me).wait_send()

        @pl.when(i >= MIX_EARLY)
        def _():
            mix_chip(s).wait_send()


def back(
    counts,
    att_grad,
    mixed_grad,
    head_rows,
    stats,
    attended,
    x,
    gain,
    qkv_w,
    out_w,
    mixed,
    halves,
    routes,
    slots,
    router_part,
    gain2_part,
    grad_in,
    capacity,
):
    rows, width = x.shape
    experts, half = halves.shape[:2]
    cap, side = 2 * half, width // 2
    images = counts.shape[0]
    heads = head_rows.shape[1]
    head_cols = out_w.shape[0]
    pieces = heads + 1
    real = head_cols // 2
    split = max(experts // 2, 1)
    chunk_rows = round_up(-(-real // split), 16)
    padded = chunk_rows * split
    part_rows = rows // images // 2
    small = round_up(experts + 2, 8)
    bf16, f32 = jnp.bfloat16, jnp.float32
    vmem = pl.BlockSpec(memory_space=pltpu.VMEM)
    hbm = pl.BlockSpec(memory_space=pl.ANY)
    small_block = pltpu.VMEM((small, width), f32)
    dma = pltpu.SemaphoreType.DMA
    table = max(experts, images, 3, GRAD_PARTS)
    return pl.pallas_call(
        functools.partial(back_kernel, experts, capacity),
        out_shape=[
            jax.ShapeDtypeStruct((rows, width), bf16),
            jax.ShapeDtypeStruct((rows, width), f32),
            jax.ShapeDtypeStruct((3, head_cols, width), f32),
            jax.ShapeDtypeStruct((head_cols, width), f32),
            jax.ShapeDtypeStruct((small, width), f32),
            jax.ShapeDtypeStruct(grad_in.shape, f32),
        ],
        in_specs=[pl.BlockSpec(memory_space=pltpu.SMEM), vmem, hbm]
        + [vmem] * 7
        + [hbm]
        + [vmem] * 5
        + [hbm],
        out_specs=[vmem, hbm] + [vmem] * 3 + [hbm],
        scratch_shapes=[
            pltpu.VMEM(grad_in.shape, f32),
            pltpu.VMEM((rows // 2, side), f32),
            pltpu.VMEM((rows, width), f32),
            pltpu.VMEM(grad_in.shape, bf16),
            pltpu.VMEM(grad_in.shape, bf16),
            pltpu.VMEM((pieces, 2, padded, width), bf16),
            dma((3 + 2 * images + GRAD_PARTS,)),
            pltpu.VMEM((rows, width), bf16),
            pltpu.VMEM((images, 8, round_up(rows // images, 128)), f32),
            pltpu.VMEM((heads, rows, HEAD_DIM), bf16),
            pltpu.VMEM((3, heads, rows, HEAD_DIM), bf16),
            pltpu.VMEM((2, rows, 128), jnp.int32),
            pltpu.VMEM((experts, half, side), bf16),
            pltpu.VMEM((experts, cap, side), bf16),
            pltpu.VMEM((rows // 2, cap), bf16),
            pltpu.VMEM((rows // 2, side), f32),
            pltpu.VMEM((images, part_rows, width), bf16),
            pltpu.VMEM((images, part_rows, width), bf16),
            pltpu.VMEM((images, part_rows, width), f32),
            pltpu.VMEM((images, part_rows, side), bf16),
            pltpu.VMEM((images, part_rows, side), bf16),
            pltpu.VMEM((rows, width), bf16),
            pltpu.VMEM((pieces, padded, width), bf16),
            pltpu.VMEM((pieces, padded, width), bf16),
            pltpu.VMEM((pieces, real, width), f32),
            pltpu.VMEM((pieces, padded, width), bf16),
            pltpu.VMEM((pieces, experts, chunk_rows, side), bf16),
            pltpu.VMEM((chunk_rows, side), f32),
            small_block,
            small_block,
            small_block,
            small_block,
            pltpu.VMEM((experts, small, width), f32),
            pltpu.VMEM((3, small, width), f32),
            dma((B_ROWS, table)),
            dma((B_ROWS, table)),
            dma((2, pieces)),
            dma((2, pieces)),
            dma((2 * pieces, experts)),
            dma((2 * pieces, experts)),
        ],
        compiler_params=pltpu.CompilerParams(
            collective_id=3, has_side_effects=True, vmem_limit_bytes=VMEM_BYTES
        ),
    )(
        counts,
        att_grad,
        mixed_grad,
        head_rows,
        stats,
        attended,
        x,
        gain,
        qkv_w,
        out_w,
        mixed,
        halves,
        routes,
        slots,
        router_part,
        gain2_part,
        grad_in,
    )


def body(
    inputs,
    counts,
    routes,
    slot_ids,
    norm_first,
    attn_in,
    attn_out,
    norm_second,
    router,
    expert_in,
    expert_out,
    cotangent,
):
    rows_dev = inputs.shape[0]
    experts = router.shape[1]
    half_slots = (105 * rows_dev + 100 * experts - 1) // (100 * experts)
    capacity = 2 * half_slots
    slot_pad = round_up(capacity, 32)
    routes, slots = routes.T, slot_ids.T
    router_rows, qkv = router.T, attn_in.transpose(0, 2, 1)
    sent_cots, head_rows, attended, stats, mixed, low_second, prob, gates, gate_rows = front(
        counts,
        inputs,
        cotangent,
        routes,
        slots,
        norm_first,
        qkv,
        attn_out,
        norm_second,
        router_rows,
        experts,
        capacity,
        slot_pad,
    )
    halves, mixed_grad, att_grad, router_part, gain_part, expert_out_grad, in_part = middle(
        counts,
        low_second,
        cotangent,
        routes,
        slots,
        gates,
        gate_rows,
        expert_in[0],
        expert_out[0],
        sent_cots,
        mixed,
        prob,
        norm_second,
        router_rows,
        experts,
        capacity,
    )
    output, input_grad, in_grad, attn_out_grad, small, expert_in_grad = back(
        counts,
        att_grad,
        mixed_grad,
        head_rows,
        stats,
        attended,
        inputs,
        norm_first,
        qkv,
        attn_out,
        mixed,
        halves,
        routes,
        slots,
        router_part,
        gain_part,
        in_part,
        capacity,
    )
    return (
        output,
        input_grad,
        small[experts + 1],
        in_grad.transpose(0, 2, 1),
        attn_out_grad,
        small[experts],
        small[:experts].T,
        expert_in_grad[None],
        expert_out_grad[None],
    )


def solution(mesh):
    in_specs = (
        P("wide", None),
        P("wide"),
        P("wide", None),
        P("wide", None),
        P(),
        P(None, None, "narrow"),
        P("narrow", None),
        P(),
        P(),
        P("wide", None, "narrow"),
        P("wide", "narrow", None),
        P("wide", None),
    )
    out_specs = (
        P("wide", None),
        P("wide", None),
        P(),
        P(None, None, "narrow"),
        P("narrow", None),
        P(),
        P(),
        P("wide", None, "narrow"),
        P("wide", "narrow", None),
    )
    return jax.shard_map(body, mesh=mesh, in_specs=in_specs, out_specs=out_specs, check_vma=False)
```

```python
import functools

import jax
import jax.numpy as jnp
from jax import lax
from jax.experimental import pallas as pl
from jax.experimental.pallas import tpu as pltpu
from jax.sharding import PartitionSpec as P

HEAD_DIM = 64
NORM_EPSILON = 1e-06
MASKED_SCORE = -1e30
BY_MESH = pl.DeviceIdType.MESH
VMEM_BYTES = 64 * 1024 * 1024 - 65536


def round_up(value, multiple):
    return -(-value // multiple) * multiple


def dot_rows(left, right):
    return lax.dot_general(left, right, (((1,), (0,)), ((), ())), preferred_element_type=jnp.float32)


def dot_cols(left, right):
    return lax.dot_general(left, right, (((1,), (1,)), ((), ())), preferred_element_type=jnp.float32)


def normal_parts(values):
    t = 1.0 / (1.0 + (0.3275911 * 0.7071067811865476) * jnp.abs(values))
    bell = jnp.exp(-0.5 * values * values)
    poly = t * (
        0.254829592
        + t * (-0.284496736 + t * (1.421413741 + t * (-1.453152027 + t * 1.061405429)))
    )
    tail = 0.5 * poly * bell
    return jnp.where(values >= 0.0, 1.0 - tail, tail), 0.3989422804014327 * values * bell


def normalize(values, gain):
    center = values - jnp.mean(values, -1, keepdims=True)
    scaled = lax.rsqrt(jnp.mean(center * center, -1, keepdims=True) + NORM_EPSILON)
    normed = center * scaled
    return normed * gain, normed, scaled


def slot_keys(routes_ref, slots_ref, capacity, cap):
    return jnp.where(slots_ref[...] < capacity, routes_ref[...] * cap + slots_ref[...], -1)


def widen(rows):
    count = rows.shape[1]
    padded = jnp.concatenate([rows.astype(jnp.float32), jnp.zeros((6, count), jnp.float32)], 0)
    tall = jnp.transpose(padded)
    return [jnp.broadcast_to(tall[:, k : k + 1], (count, 128)).astype(jnp.int32) for k in range(2)]


def flat(gain_ref):
    return gain_ref[...].reshape(1, gain_ref.shape[0])


class Place:
    def __init__(self, experts):
        self.experts = experts
        self.n = lax.axis_index("narrow")
        self.w = lax.axis_index("wide")
        self.core = lax.rem(self.n, 2)
        self.chip = self.n // 2
        self.me = self.w // 2
        self.parity = lax.rem(self.w, 2)
        self.near_n = self.n + 1 - 2 * self.core
        self.across_n = lax.rem(self.n + 2, 4)
        self.near = {"narrow": self.near_n, "wide": self.w}
        self.across = {"narrow": self.across_n, "wide": self.w}

    def home(self, e):
        return {"narrow": self.n, "wide": 2 * e + self.parity}

    def take(self, i):
        short = jnp.minimum(self.me, self.experts - 1 - self.me)
        swing = jnp.where(lax.rem(i, 2) == 1, (i + 1) // 2, -(i // 2))
        away = jnp.where(i <= 2 * short, swing, i - short)
        return self.me + jnp.where(2 * self.me < self.experts, away, -away)

    def part(self, which, size, align):
        return pl.ds(pl.multiple_of(which * size, align), size)

    def greet(self, others=()):
        barrier = pltpu.get_barrier_semaphore()
        for peer in (self.near, self.across, *others):
            pl.semaphore_signal(barrier, inc=1, device_id=peer, device_id_type=BY_MESH)

        @pl.loop(1, self.experts)
        def _(i):
            pl.semaphore_signal(
                barrier, inc=1, device_id=self.home(self.take(i)), device_id_type=BY_MESH
            )

        pl.semaphore_wait(barrier, self.experts + 1 + len(others))


def mover(sent, came):
    def move(src, dst, row, sent_at, came_at, where):
        return pltpu.make_async_remote_copy(
            src_ref=src,
            dst_ref=dst,
            send_sem=sent.at[row, sent_at],
            recv_sem=came.at[row, came_at],
            device_id=where,
            device_id_type=BY_MESH,
        )

    return move


class Dispatch:
    def __init__(self, place, move, base, send, landing):
        self.place, self.move, self.base = place, move, base
        self.send, self.landing = send, landing
        cap, width = landing.shape[1:]
        self.cap, self.half, self.side = cap, cap // 2, width // 2
        self.mine = place.part(place.core, self.half, 16)
        self.other = place.part(1 - place.core, self.half, 16)
        self.side_mine = place.part(place.chip, self.side, 128)
        self.side_other = place.part(1 - place.chip, self.side, 128)

    def z_copy(self, e, landed):
        return self.move(
            self.send.at[e],
            self.landing.at[landed, self.mine, self.side_mine],
            self.base,
            e,
            landed,
            self.place.home(e),
        )

    def build(self, i, key_row, source):
        e = self.place.take(i)
        hot = self.hot(e, self.place.core, key_row)
        self.send[e] = dot_rows(hot, source[:, self.side_mine]).astype(jnp.bfloat16)
        self.z_copy(e, self.place.me).start()

    def hot(self, e, part, key_row):
        slot = e * self.cap + part * self.half
        slot = slot + lax.broadcasted_iota(jnp.int32, (self.half, key_row.shape[1]), 0)
        hit = (key_row[0:1, :] == slot) | (key_row[1:2, :] == slot)
        return jnp.where(hit, 1.0, 0.0).astype(jnp.bfloat16)

    def build_own(self, key_row, source):
        @pl.loop(0, 2)
        def _(m):
            hot = self.hot(self.place.me, m, key_row)
            part = pl.ds(pl.multiple_of(m * self.half, 16), self.half)
            self.landing[self.place.me, part, :] = dot_rows(hot, source[...]).astype(jnp.bfloat16)

    def spread(self, step, s):
        rows, cols, where = (
            (self.mine, self.side_mine, self.place.across),
            (self.mine, self.side_mine, self.place.near),
            (self.mine, self.side_other, self.place.near),
        )[step]
        ref = self.landing.at[s, rows, cols]
        return self.move(ref, ref, self.base + 1 + step, s, s, where)

    def stage_a(self, i):
        self.landed(i)
        self.relay(i)

    def stage_b(self, i):
        s = self.place.take(i)
        self.spread(0, s).wait_recv()
        self.spread(2, s).start()

    def stage_c(self, i):
        s = self.place.take(i)
        self.spread(1, s).wait_recv()
        self.spread(2, s).wait_recv()

    def landed(self, i):
        s = self.place.take(i)
        self.z_copy(s, s).wait_recv()

    def relay(self, i):
        s = self.place.take(i)
        self.spread(0, s).start()
        self.spread(1, s).start()

    def finish(self, lo, hi, sends=True):
        @pl.loop(lo, hi)
        def _(i):
            s = self.place.take(i)
            for step in range(3):
                self.spread(step, s).wait_send()

        if sends:

            @pl.loop(1, self.place.experts)
            def _(i):
                self.z_copy(self.place.take(i), self.place.me).wait_send()


FRONT_OWN, FRONT_FAR, FRONT_CHIP = 4, 5, 6
FRONT_ROWS = 7
LATE = 2


def front_kernel(
    experts,
    capacity,
    counts,
    x_ref,
    cot_ref,
    routes_ref,
    slots_ref,
    gain1_ref,
    qkv_w,
    out_w,
    gain2_ref,
    router_ref,
    cots_ref,
    heads_hbm,
    attended_hbm,
    stats_hbm,
    mixed_hbm,
    low2_hbm,
    prob_hbm,
    gate_hbm,
    gate_send,
    heads_ref,
    attended_ref,
    stats_ref,
    mixed_ref,
    low2_ref,
    prob_ref,
    gate_ref,
    cot_send,
    gather,
    out_all,
    key_row,
    key_wide,
    route_wide,
    gate_wide,
    router_pad,
    loads,
    sent,
    came,
):
    rows, width = x_ref.shape
    images = counts.shape[0]
    patches = rows // images
    head_cols = out_w.shape[0]
    heads = head_cols // HEAD_DIM
    scale = HEAD_DIM ** (-0.5)
    place = Place(experts)
    move = mover(sent, came)
    cots = Dispatch(place, move, 0, cot_send, cots_ref)
    place.greet()
    key_row[...] = slot_keys(routes_ref, slots_ref, capacity, cots.cap)

    def share(ref, at):
        def copy(step):
            piece = ref(place.across_n if step == 2 else place.n)
            where = place.across if step == 0 else place.near
            row = (FRONT_CHIP, FRONT_OWN, FRONT_FAR)[step]
            return move(piece, piece, row, at, at, where)

        return copy

    out_share = share(lambda n: out_all.at[n], images)
    out_all[place.n] = out_w[...]
    out_share(0).start()
    out_share(1).start()

    @pl.loop(1, experts)
    def _(i):
        cots.build(i, key_row, cot_ref)

    tile = patches // 2

    @pl.loop(0, rows // tile)
    def _(t):
        part = pl.ds(pl.multiple_of(t * tile, 16), tile)
        normed, _, _ = normalize(x_ref[part, :].astype(jnp.float32), flat(gain1_ref))
        low = normed.astype(jnp.bfloat16)
        for i in range(3):
            block = dot_cols(low, qkv_w[i]).astype(jnp.bfloat16)
            for h in range(heads):
                heads_ref[i, h, part, :] = block[:, h * HEAD_DIM : (h + 1) * HEAD_DIM]

    outs = [
        pltpu.make_async_copy(src, dst, loads.at[at])
        for at, (src, dst) in enumerate(
            (
                (heads_ref, heads_hbm),
                (attended_ref, attended_hbm),
                (stats_ref, stats_hbm),
                (mixed_ref, mixed_hbm),
                (low2_ref, low2_hbm),
                (prob_ref, prob_hbm),
                (gate_ref, gate_hbm),
            )
        )
    ]
    outs[0].start()
    for k, column in enumerate(widen(key_row[...])):
        key_wide[k] = column
    for k, column in enumerate(widen(routes_ref[...])):
        route_wide[k] = column
    router_pad[...] = jnp.zeros_like(router_pad)
    router_pad[0:experts] = router_ref[...]
    stats_ref[...] = jnp.zeros_like(stats_ref)

    def attend(image):
        keys_at = pl.ds(pl.multiple_of(image * patches, 16), patches)
        pack = pl.ds(pl.multiple_of(image * tile, 16), tile)
        live = lax.broadcasted_iota(jnp.int32, (1, patches), 1) < counts[image]
        for h in range(heads):
            key_rows = heads_ref[1, h, keys_at, :]
            value_rows = heads_ref[2, h, keys_at, :]
            for t in range(patches // tile):
                part = pl.ds(pl.multiple_of(image * patches + t * tile, 16), tile)
                scores = dot_cols(heads_ref[0, h, part, :], key_rows) * scale
                scores = jnp.where(live, scores, MASKED_SCORE)
                top = jnp.max(scores, -1, keepdims=True)
                weights = jnp.exp(scores - top)
                total = jnp.sum(weights, -1, keepdims=True)
                probs = (weights * (1.0 / total)).astype(jnp.bfloat16)
                block = dot_rows(probs, value_rows).astype(jnp.bfloat16)
                at = t * head_cols + h * HEAD_DIM
                gather[place.n, pack, at : at + HEAD_DIM] = block
                attended_ref[part, h * HEAD_DIM : (h + 1) * HEAD_DIM] = block
                stats_ref[part, h : h + 1] = top + jnp.log(total)

    def image_share(image):
        pack = pl.ds(pl.multiple_of(image * tile, 16), tile)
        return share(lambda n: gather.at[n, pack, :], image)

    @pl.loop(0, images)
    def _(image):
        attend(image)
        image_share(image)(0).start()
        image_share(image)(1).start()

    outs[1].start()
    outs[2].start()
    out_share(0).wait_recv()
    out_share(2).start()
    cots.build_own(key_row, cot_ref)

    @pl.loop(1, experts - LATE)
    def _(i):
        cots.stage_a(i)

    out_share(1).wait_recv()
    out_share(2).wait_recv()

    def finish(image):
        copy = image_share(image)
        copy(0).wait_recv()
        copy(2).start()
        copy(1).wait_recv()
        copy(2).wait_recv()
        pack = pl.ds(pl.multiple_of(image * tile, 16), tile)

        for t in range(2):
            part = pl.ds(pl.multiple_of(image * patches + t * tile, 16), tile)
            cols = slice(t * head_cols, (t + 1) * head_cols)
            attention = dot_rows(gather[0, pack, cols], out_all[0])
            for n in range(1, 4):
                attention += dot_rows(gather[n, pack, cols], out_all[n])
            offset = t * tile + lax.broadcasted_iota(jnp.int32, (tile, 1), 0)
            mixed = x_ref[part, :].astype(jnp.float32) + jnp.where(
                offset < counts[image], attention, 0.0
            )
            mixed_ref[part, :] = mixed
            normed, _, _ = normalize(mixed, flat(gain2_ref))
            low = normed.astype(jnp.bfloat16)
            low2_ref[part, :] = low
            lane = lax.broadcasted_iota(jnp.int32, (tile, 128), 1)
            logits = jnp.where(lane < experts, dot_cols(low, router_pad[...]), MASKED_SCORE)
            powers = jnp.exp(logits - jnp.max(logits, -1, keepdims=True))
            prob = powers / jnp.sum(powers, -1, keepdims=True)
            prob_ref[part, :] = prob
            picked = [
                jnp.sum(jnp.where(lane == route_wide[k, part, :], prob, 0.0), 1, keepdims=True)
                for k in range(2)
            ]
            both = picked[0] + picked[1]
            gate_ref[part, :] = jnp.where(
                lane == 0, picked[0] / both, jnp.where(lane == 1, picked[1] / both, both)
            )

    @pl.loop(0, images)
    def _(image):
        finish(image)

    for out in outs[3:]:
        out.start()

    wide_cap = gate_send.shape[2]

    for k in range(2):
        gate_wide[k] = jnp.broadcast_to(gate_ref[:, k : k + 1], (rows, 128))

    @pl.loop(0, experts)
    def _(e):
        @pl.loop(0, wide_cap // 128)
        def _(j):
            lanes = pl.ds(pl.multiple_of(j * 128, 128), 128)
            slot = e * cots.cap + j * 128 + lax.broadcasted_iota(jnp.int32, (rows, 128), 1)
            picked = jnp.where(key_wide[0] == slot, gate_wide[0], 0.0) + jnp.where(
                key_wide[1] == slot, gate_wide[1], 0.0
            )
            gate_send[e, :, lanes] = jnp.broadcast_to(jnp.sum(picked, 0, keepdims=True), (8, 128))

    @pl.loop(1, experts - LATE)
    def _(i):
        cots.stage_b(i)

    @pl.loop(1, experts - LATE)
    def _(i):
        cots.stage_c(i)

    @pl.loop(experts - LATE, experts)
    def _(i):
        cots.landed(i)

    cots.finish(1, experts - LATE)
    for out in outs:
        out.wait()
    for step in range(3):
        out_share(step).wait_send()
        for image in range(images):
            image_share(image)(step).wait_send()


def front(
    counts, x, cot, routes, slots, gain1, qkv_w, out_w, gain2, router, experts, capacity, cap
):
    rows, width = x.shape
    head_cols = out_w.shape[0]
    heads = head_cols // HEAD_DIM
    images = counts.shape[0]
    bf16, f32 = jnp.bfloat16, jnp.float32
    vmem = pl.BlockSpec(memory_space=pltpu.VMEM)
    hbm = pl.BlockSpec(memory_space=pl.ANY)
    table = max(experts, images + 1)
    wide_cap = round_up(cap, 128)
    return pl.pallas_call(
        functools.partial(front_kernel, experts, capacity),
        out_shape=[
            jax.ShapeDtypeStruct((experts, cap, width), bf16),
            jax.ShapeDtypeStruct((3, heads, rows, HEAD_DIM), bf16),
            jax.ShapeDtypeStruct((rows, head_cols), bf16),
            jax.ShapeDtypeStruct((rows, 128), f32),
            jax.ShapeDtypeStruct((rows, width), f32),
            jax.ShapeDtypeStruct((rows, width), bf16),
            jax.ShapeDtypeStruct((rows, 128), f32),
            jax.ShapeDtypeStruct((rows, 128), f32),
            jax.ShapeDtypeStruct((experts, 8, wide_cap), f32),
        ],
        in_specs=[pl.BlockSpec(memory_space=pltpu.SMEM)] + [vmem] * 9,
        out_specs=[vmem] + [hbm] * 7 + [vmem],
        scratch_shapes=[
            pltpu.VMEM((3, heads, rows, HEAD_DIM), bf16),
            pltpu.VMEM((rows, head_cols), bf16),
            pltpu.VMEM((rows, 128), f32),
            pltpu.VMEM((rows, width), f32),
            pltpu.VMEM((rows, width), bf16),
            pltpu.VMEM((rows, 128), f32),
            pltpu.VMEM((rows, 128), f32),
            pltpu.VMEM((experts, cap // 2, width // 2), bf16),
            pltpu.VMEM((4, rows // 2, 2 * head_cols), bf16),
            pltpu.VMEM((4, head_cols, width), bf16),
            pltpu.VMEM((2, rows), jnp.int32),
            pltpu.VMEM((2, rows, 128), jnp.int32),
            pltpu.VMEM((2, rows, 128), jnp.int32),
            pltpu.VMEM((2, rows, 128), f32),
            pltpu.VMEM((128, width), bf16),
            pltpu.SemaphoreType.DMA((7,)),
            pltpu.SemaphoreType.DMA((FRONT_ROWS, table)),
            pltpu.SemaphoreType.DMA((FRONT_ROWS, table)),
        ],
        compiler_params=pltpu.CompilerParams(
            collective_id=2, has_side_effects=True, vmem_limit_bytes=VMEM_BYTES
        ),
    )(counts, x, cot, routes, slots, gain1, qkv_w, out_w, gain2, router)


class Return:
    def __init__(self, place, move, base, core_send, core_recv, kept, chip_send, chip_recv, back):
        self.place, self.move, self.base = place, move, base
        self.core_send, self.core_recv, self.kept = core_send, core_recv, kept
        self.chip_send, self.chip_recv, self.back = chip_send, chip_recv, back
        self.half, self.side = chip_send.shape[1:]
        self.mine = place.part(place.core, self.half, 16)
        self.other = place.part(1 - place.core, self.half, 16)
        self.side_mine = place.part(place.chip, self.side, 128)
        self.side_other = place.part(1 - place.chip, self.side, 128)

    def rows(self, s):
        return pl.ds(pl.multiple_of(s * self.half, 16), self.half)

    def core_move(self, s):
        return self.move(
            self.core_send.at[s], self.core_recv.at[s], self.base, s, s, self.place.near
        )

    def chip_move(self, s):
        return self.move(
            self.chip_send.at[s], self.chip_recv.at[s], self.base + 1, s, s, self.place.across
        )

    def home_move(self, s, landed):
        return self.move(
            self.core_send.at[s, :, pl.ds(0, self.side)],
            self.back.at[landed, self.mine, :],
            self.base + 2,
            s,
            landed,
            self.place.home(s),
        )

    def pair_move(self, e, part):
        ref = self.back.at[e, part, :]
        return self.move(ref, ref, self.base + 3, e, e, self.place.near)

    def first(self, s, product):
        self.core_send[s] = product(self.other).astype(jnp.bfloat16)
        self.core_move(s).start()
        self.kept[self.rows(s), :] = product(self.mine)

    def second(self, s):
        self.core_move(s).wait_recv()
        self.chip_send[s] = (
            self.kept[self.rows(s), self.side_other]
            + self.core_recv[s, :, self.side_other].astype(jnp.float32)
        ).astype(jnp.bfloat16)
        self.chip_move(s).start()

    def third(self, s):
        self.chip_move(s).wait_recv()
        self.core_move(s).wait_send()
        piece = (
            self.kept[self.rows(s), self.side_mine]
            + self.core_recv[s, :, self.side_mine].astype(jnp.float32)
            + self.chip_recv[s].astype(jnp.float32)
        ).astype(jnp.bfloat16)

        @pl.when(s == self.place.me)
        def _():
            self.back[self.place.me, self.mine, :] = piece

        @pl.when(s != self.place.me)
        def _():
            self.core_send[s, :, 0 : self.side] = piece
            self.home_move(s, self.place.me).start()

    def fourth(self, i):
        e = self.place.take(i)

        @pl.when(e != self.place.me)
        def _():
            self.home_move(e, e).wait_recv()

        self.pair_move(e, self.mine).start()

    def ready(self, i):
        self.pair_move(self.place.take(i), self.other).wait_recv()

    def finish(self):
        @pl.loop(0, self.place.experts)
        def _(i):
            s = self.place.take(i)
            self.chip_move(s).wait_send()
            self.pair_move(s, self.mine).wait_send()

            @pl.when(i > 0)
            def _():
                self.home_move(s, self.place.me).wait_send()


class Quarters:
    def __init__(self, place, move, base, at, ref):
        self.place, self.move, self.base, self.at, self.ref = place, move, base, at, ref
        rows, width = ref.shape
        self.rows = place.part(place.core, rows // 2, 16)
        self.mine = place.part(place.chip, width // 2, 128)
        self.other = place.part(1 - place.chip, width // 2, 128)

    def copy(self, step):
        ref = self.ref.at[self.rows, self.other if step == 2 else self.mine]
        where = self.place.across if step == 0 else self.place.near
        return self.move(ref, ref, self.base + step, self.at, self.at, where)

    def start(self):
        self.copy(0).start()
        self.copy(1).start()

    def relay(self):
        self.copy(0).wait_recv()
        self.copy(2).start()

    def ready(self):
        self.copy(1).wait_recv()
        self.copy(2).wait_recv()

    def finish(self):
        for step in range(3):
            self.copy(step).wait_send()


M_CORE, M_CHIP, M_HOME, M_BACK, M_MIX, M_END, M_PAIR, M_LATE, M_GATES = 4, 5, 6, 7, 11, 13, 16, 17, 21
M_ROWS = 22
MIX_EARLY = 4
GRAD_PARTS, GRAD_EARLY = 4, 2


def middle_kernel(
    experts,
    capacity,
    counts,
    low_ref,
    cot_hbm,
    routes_ref,
    slots_ref,
    gate_col,
    gate_send,
    in_hbm,
    out_hbm,
    cots_hbm,
    mixed_hbm,
    prob_ref,
    gain_ref,
    router_ref,
    half_hbm,
    mixed_grad_hbm,
    att_grad_hbm,
    router_grad,
    gain_grad,
    grad_out,
    grad_in,
    in_ref,
    out_ref,
    cots_ref,
    rows_ref,
    hid_ref,
    pre_ref,
    send_rows,
    gate_rows,
    gate_tall,
    pair_tall,
    pair_part,
    pair_core,
    pair_sum,
    pair_chip,
    pair_home,
    pair_back,
    core_send,
    core_recv,
    kept,
    chip_send,
    chip_recv,
    back,
    mix_send,
    mix_recv,
    mix_last,
    key_row,
    key_wide,
    route_wide,
    router_pad,
    hot_ref,
    total,
    pair_ref,
    dis_ref,
    copy_send,
    copy_recv,
    in_send,
    in_recv,
    cot_tile,
    scale_wide,
    loads,
    cot_loads,
    sent,
    came,
):
    rows, width = low_ref.shape
    images = counts.shape[0]
    patches = rows // images
    cap = rows_ref.shape[1]
    half = cap // 2
    units = in_ref.shape[1]
    place = Place(experts)
    move = mover(sent, came)
    me = place.me
    lows = Dispatch(place, move, 0, send_rows, rows_ref)
    late = Dispatch(place, move, M_LATE, send_rows, cots_ref)
    dgrad = Return(
        place, move, M_BACK, core_send, core_recv, kept, chip_send, chip_recv, back
    )
    other_copy = {"narrow": place.n, "wide": place.w + 1 - 2 * place.parity}

    def load(at, src, dst):
        return pltpu.make_async_copy(src, dst, loads.at[at])

    fetched = [
        load(0, in_hbm, in_ref),
        load(1, out_hbm, out_ref),
    ]
    for copy in fetched:
        copy.start()

    def cots_in(i, whole):
        s = place.take(i)
        at = (s,) if whole else (s, late.mine, late.side_mine)
        return pltpu.make_async_copy(cots_hbm.at[at], cots_ref.at[at], cot_loads.at[i])

    @pl.loop(0, experts - LATE)
    def _(i):
        cots_in(i, True).start()

    for i in range(experts - LATE, experts):
        cots_in(i, False).start()
    place.greet((other_copy,))
    key_row[...] = slot_keys(routes_ref, slots_ref, capacity, cap)

    def gate_copy(e, landed):
        return move(gate_send.at[e], gate_rows.at[landed], M_GATES, e, landed, place.home(e))

    @pl.loop(1, experts)
    def _(i):
        lows.build(i, key_row, low_ref)
        gate_copy(place.take(i), me).start()

    gate_rows[me] = gate_send[me]

    for copy in fetched:
        copy.wait()

    @pl.loop(0, experts - LATE)
    def _(i):
        cots_in(i, True).wait()

    for i in range(experts - LATE, experts):
        cots_in(i, False).wait()
        late.relay(i)

    lows.build_own(key_row, low_ref)
    pair_tall[...] = jnp.zeros_like(pair_tall)
    grad_out[...] = jnp.zeros_like(grad_out)
    grad_in[...] = jnp.zeros_like(grad_in)
    for k, column in enumerate(widen(key_row[...])):
        key_wide[k] = column
    for k, column in enumerate(widen(routes_ref[...])):
        route_wide[k] = column
    router_pad[...] = jnp.zeros_like(router_pad)
    router_pad[0:experts] = router_ref[...]

    def pair_move(step, s):
        src, dst, row, where = (
            (pair_part, pair_core, M_CORE, place.near),
            (pair_sum, pair_chip, M_CHIP, place.across),
        )[step]
        return move(src.at[s], dst.at[s], row, s, s, where)

    def pair_return(s, landed):
        return move(pair_home.at[s], pair_back.at[landed], M_HOME, s, landed, place.home(s))

    chunk = 256 if units % 256 == 0 else units

    def compute(s, m):
        part = pl.ds(pl.multiple_of(m * half, 16), half)
        left = rows_ref[s, part, :]
        cots = cots_ref[s, part, :]
        gate = gate_tall[part, 0:1]
        pair = jnp.zeros((half, 1), jnp.float32)
        for j in range(units // chunk):
            cols = slice(j * chunk, (j + 1) * chunk)
            pre = dot_rows(left, in_ref[:, cols])
            free = dot_cols(cots, out_ref[cols, :])
            cdf, slope = normal_parts(pre)
            hidden = pre * cdf
            hid_ref[s, part, cols] = (gate * hidden).astype(jnp.bfloat16)
            pre_ref[s, part, cols] = (gate * free * (cdf + slope)).astype(jnp.bfloat16)
            pair += jnp.sum(hidden * free, 1, keepdims=True)
        pair_tall[part, :] = jnp.broadcast_to(pair, (half, 128))

    def second(s):
        dgrad.second(s)
        pair_move(0, s).wait_recv()
        pair_sum[s] = pair_part[s] + pair_core[s]
        pair_move(1, s).start()

    def third(s):
        dgrad.third(s)
        pair_move(1, s).wait_recv()
        line = pair_sum[s] + pair_chip[s]

        @pl.when(s == me)
        def _():
            pair_back[me] = line

        @pl.when(s != me)
        def _():
            pair_home[s] = line
            pair_return(s, me).start()

    def contract(left, right):
        return lax.dot_general(
            left, right, (((0,), (0,)), ((), ())), preferred_element_type=jnp.float32
        )

    def mix_move(s):
        return move(mix_send.at[s], mix_recv.at[s], M_MIX, s, s, place.near)

    def mix_chip(s):
        src = mix_recv.at[s, :, dgrad.side_other]
        return move(src, mix_last.at[s], M_MIX + 1, s, s, place.across)

    def mix_first(s):
        mix_send[s] = dot_rows(hid_ref[s, dgrad.other, :], out_ref[...]).astype(jnp.bfloat16)
        mix_move(s).start()

    def mix_second(s):
        mix_move(s).wait_recv()
        mix_recv[s] = (
            dot_rows(hid_ref[s, dgrad.mine, :], out_ref[...]) + mix_recv[s].astype(jnp.float32)
        ).astype(jnp.bfloat16)

    def mix_third(s):
        mix_chip(s).wait()
        total_part = mix_recv[s, :, dgrad.side_mine].astype(jnp.float32)
        mix_recv[s, :, 0 : dgrad.side] = (total_part + mix_last[s].astype(jnp.float32)).astype(
            jnp.bfloat16
        )

    def work(i, between):
        s = place.take(i)
        gate_tall[...] = jnp.transpose(gate_rows[s])

        @pl.loop(0, 2)
        def _(m):
            compute(s, m)

            @pl.when(m == 0)
            def _():
                between()

        pair_part[s] = jnp.transpose(pair_tall[...])[0:8]
        pair_move(0, s).start()
        dgrad.first(s, lambda part: dot_cols(pre_ref[s, part, :], in_ref[...]))

    def add_out(s):
        grad_out[...] += contract(hid_ref[s], cots_ref[s])

    def add_in(lo, hi):
        @pl.loop(lo, hi)
        def _(i):
            s = place.take(i)
            grad_in[...] += contract(rows_ref[s], pre_ref[s])

    def pass_on(i):
        @pl.when((i > 0) & (i + 1 < experts))
        def _():
            lows.stage_a(i + 1)

    @pl.loop(0, experts)
    def _(i):
        s = place.take(i)

        @pl.when(i > 0)
        def _():
            lows.stage_b(i)
            lows.stage_c(i)
            gate_copy(s, s).wait_recv()

        @pl.when(i >= experts - LATE)
        def _():
            late.stage_c(i)

        work(i, lambda: pass_on(i))

        @pl.when(i == 0)
        def _():
            lows.stage_a(1)

        second(s)

        @pl.when(i == 0)
        def _():
            mix_first(s)
            add_in(0, 1)
            for j in range(experts - LATE, experts):
                late.stage_b(j)

        add_out(s)

        @pl.when(i > 1)
        def _():
            third(place.take(i - 2))

    last = place.take(experts - 1)
    copy_send[...] = grad_out[...].astype(jnp.bfloat16)
    copy_move = move(copy_send, copy_recv, M_PAIR, 0, 0, other_copy)
    copy_move.start()

    @pl.loop(1, experts)
    def _(i):
        mix_first(place.take(i))

    third(place.take(experts - 2))

    @pl.loop(0, MIX_EARLY)
    def _(i):
        s = place.take(i)
        mix_second(s)
        mix_chip(s).start()

    third(last)
    add_in(1, experts)
    early_rows = in_send.shape[0]
    in_send[...] = grad_in[0:early_rows].astype(jnp.bfloat16)
    in_move = move(in_send, in_recv, M_PAIR, 1, 1, other_copy)
    in_move.start()
    pair_ref[...] = jnp.zeros_like(pair_ref)

    def build_hot(e):
        lane = lax.broadcasted_iota(jnp.int32, (rows // 4, 128), 1)

        @pl.loop(0, 4)
        def _(m):
            part = pl.ds(pl.multiple_of(m * (rows // 4), 16), rows // 4)
            keys = [key_wide[k, part, :] - e * cap for k in range(2)]
            for low in range(0, cap, 128):
                size = min(128, cap - low)
                hit = (keys[0] == lane + low) | (keys[1] == lane + low)
                hot_ref[part, low : low + size] = jnp.where(hit, 1.0, 0.0).astype(jnp.bfloat16)[
                    :, 0:size
                ]

    my_rows = place.part(place.core, rows // 2, 16)
    total[...] = jnp.zeros_like(total)

    @pl.loop(0, experts)
    def _(i):
        e = place.take(i)
        build_hot(e)
        dgrad.fourth(i)

        @pl.when(i > 0)
        def _():
            pair_return(e, e).wait_recv()

        tall = jnp.transpose(pair_back[e])[0:cap, 0:1]
        high = tall.astype(jnp.bfloat16).astype(jnp.float32)
        middle = (tall - high).astype(jnp.bfloat16).astype(jnp.float32)
        lane = lax.broadcasted_iota(jnp.int32, (cap, 128), 1)
        spelled = jnp.where(
            lane == 0, high, jnp.where(lane == 1, middle, jnp.where(lane == 2, tall - high - middle, 0.0))
        ).astype(jnp.bfloat16)
        found = jnp.sum(dot_rows(hot_ref[...], spelled), 1, keepdims=True)
        lane_rows = lax.broadcasted_iota(jnp.int32, (rows, 128), 1)
        pair_ref[...] += jnp.where(lane_rows == e, found, 0.0)
        dgrad.ready(i)
        total[...] += dot_rows(hot_ref[my_rows, :], back[e])

    ends = Quarters(place, move, M_END, 0, dis_ref)
    dis_ref[ends.rows, ends.mine] = total[...].astype(jnp.bfloat16)
    ends.start()

    @pl.loop(MIX_EARLY, experts)
    def _(i):
        mix_second(place.take(i))

    mixed_in = load(1, mixed_hbm, kept.at[pl.ds(0, rows), :])
    mixed_in.start()
    tile = patches // 2
    router_grad[...] = jnp.zeros_like(router_grad)
    gain_grad[...] = jnp.zeros_like(gain_grad)

    def cot_in(t):
        slot = lax.rem(t, 2)
        part = pl.ds(pl.multiple_of(t * tile, 16), tile)
        return pltpu.make_async_copy(cot_hbm.at[part, :], cot_tile.at[slot], loads.at[2 + slot])

    def rows_out(t, what):
        part = pl.ds(pl.multiple_of(t * tile, 16), tile)
        src, dst = ((kept, mixed_grad_hbm), (dis_ref, att_grad_hbm))[what]
        return pltpu.make_async_copy(src.at[part, :], dst.at[part, :], loads.at[4 + 2 * t + what])

    cot_in(0).start()
    mixed_in.wait()

    def before(t):
        part = pl.ds(pl.multiple_of(t * tile, 16), tile)
        lane = lax.broadcasted_iota(jnp.int32, (tile, 128), 1)
        by_expert = pair_ref[part, :]
        hots = [lane == route_wide[k, part, :] for k in range(2)]
        pair = [jnp.sum(jnp.where(hot, by_expert, 0.0), 1, keepdims=True) for hot in hots]
        weighted = pair[0] * gate_col[part, 0:1] + pair[1] * gate_col[part, 1:2]
        both = gate_col[part, 2:3]
        prob = prob_ref[part, :]
        prob_grad = jnp.where(hots[0], (pair[0] - weighted) / both, 0.0) + jnp.where(
            hots[1], (pair[1] - weighted) / both, 0.0
        )
        logit_grad = prob * (prob_grad - jnp.sum(prob * prob_grad, 1, keepdims=True))
        pair_ref[part, :] = logit_grad
        router_grad[...] += contract(logit_grad.astype(jnp.bfloat16), low_ref[part, :])
        _, hat, scaled = normalize(kept[part, :], flat(gain_ref))
        kept[part, :] = hat
        scale_wide[part, :] = jnp.broadcast_to(scaled, (tile, 128))

    @pl.loop(0, rows // tile)
    def _(t):
        @pl.when(t == 2)
        def _():
            ends.relay()

        before(t)

    ends.ready()
    ends.finish()

    @pl.loop(0, rows // tile)
    def _(t):
        @pl.when(t + 1 < rows // tile)
        def _():
            cot_in(t + 1).start()

        part = pl.ds(pl.multiple_of(t * tile, 16), tile)
        normed_grad = dis_ref[part, :].astype(jnp.float32) + dot_rows(
            pair_ref[part, :].astype(jnp.bfloat16), router_pad[...]
        )
        hat = kept[part, :]
        gain_grad[...] += jnp.sum(normed_grad * hat, 0, keepdims=True)
        grad = normed_grad * flat(gain_ref)
        inner = (
            grad - jnp.mean(grad, -1, keepdims=True) - hat * jnp.mean(grad * hat, -1, keepdims=True)
        )
        cot_in(t).wait()
        full = cot_tile[lax.rem(t, 2)].astype(jnp.float32) + scale_wide[part, 0:1] * inner
        kept[part, :] = full
        rows_out(t, 0).start()
        row = t * tile + lax.broadcasted_iota(jnp.int32, (tile, 1), 0)
        live = lax.rem(row, patches) < jnp.where(t * tile < patches, counts[0], counts[images - 1])
        dis_ref[part, :] = jnp.where(live, full, 0.0).astype(jnp.bfloat16)
        rows_out(t, 1).start()

    @pl.loop(0, MIX_EARLY)
    def _(i):
        mix_third(place.take(i))

    half_out = load(0, mix_recv, half_hbm)
    half_out.start()
    copy_move.wait()
    grad_out[...] += copy_recv[...].astype(jnp.float32)
    in_move.wait()
    grad_in[0:early_rows] += in_recv[...].astype(jnp.float32)
    half_out.wait()

    @pl.loop(0, rows // tile)
    def _(t):
        rows_out(t, 0).wait()
        rows_out(t, 1).wait()

    dgrad.finish()
    lows.finish(1, experts)
    late.finish(experts - LATE, experts, False)

    @pl.loop(0, experts)
    def _(i):
        s = place.take(i)
        pair_move(0, s).wait_send()
        pair_move(1, s).wait_send()
        mix_move(s).wait_send()

        @pl.when(i > 0)
        def _():
            pair_return(s, me).wait_send()
            gate_copy(s, me).wait_send()


def middle(
    counts,
    low,
    cot,
    routes,
    slots,
    gates,
    gate_rows,
    weight_in,
    weight_out,
    cots,
    mixed,
    prob,
    gain,
    router,
    experts,
    capacity,
):
    rows, width = low.shape
    units = weight_in.shape[1]
    cap = cots.shape[1]
    half, side, wide_cap = cap // 2, width // 2, round_up(cap, 128)
    bf16, f32 = jnp.bfloat16, jnp.float32
    vmem = pl.BlockSpec(memory_space=pltpu.VMEM)
    hbm = pl.BlockSpec(memory_space=pl.ANY)
    line = pltpu.VMEM((experts, 8, wide_cap), f32)
    halves = pltpu.VMEM((experts, half, width), bf16)
    tile = rows // counts.shape[0] // 2
    return pl.pallas_call(
        functools.partial(middle_kernel, experts, capacity),
        out_shape=[
            jax.ShapeDtypeStruct((experts, half, width), bf16),
            jax.ShapeDtypeStruct((rows, width), f32),
            jax.ShapeDtypeStruct((rows, width), bf16),
            jax.ShapeDtypeStruct((128, width), f32),
            jax.ShapeDtypeStruct((1, width), f32),
            jax.ShapeDtypeStruct((units, width), f32),
            jax.ShapeDtypeStruct((width, units), f32),
        ],
        in_specs=[
            pl.BlockSpec(memory_space=pltpu.SMEM),
            vmem,
            hbm,
            vmem,
            vmem,
            vmem,
            vmem,
            hbm,
            hbm,
            hbm,
            hbm,
            vmem,
            vmem,
            vmem,
        ],
        out_specs=[hbm] * 3 + [vmem] * 4,
        scratch_shapes=[
            pltpu.VMEM((width, units), bf16),
            pltpu.VMEM((units, width), bf16),
            pltpu.VMEM((experts, cap, width), bf16),
            pltpu.VMEM((experts, cap, width), bf16),
            pltpu.VMEM((experts, cap, units), bf16),
            pltpu.VMEM((experts, cap, units), bf16),
            pltpu.VMEM((experts, half, side), bf16),
            line,
            pltpu.VMEM((wide_cap, 8), f32),
            pltpu.VMEM((wide_cap, 128), f32),
            line,
            line,
            line,
            line,
            line,
            line,
            halves,
            halves,
            pltpu.VMEM((max(experts * half, rows), width), f32),
            pltpu.VMEM((experts, half, side), bf16),
            pltpu.VMEM((experts, half, side), bf16),
            pltpu.VMEM((experts, cap, side), bf16),
            halves,
            halves,
            pltpu.VMEM((experts, half, side), bf16),
            pltpu.VMEM((2, rows), jnp.int32),
            pltpu.VMEM((2, rows, 128), jnp.int32),
            pltpu.VMEM((2, rows, 128), jnp.int32),
            pltpu.VMEM((128, width), bf16),
            pltpu.VMEM((rows, cap), bf16),
            pltpu.VMEM((rows // 2, side), f32),
            pltpu.VMEM((rows, 128), f32),
            pltpu.VMEM((rows, width), bf16),
            pltpu.VMEM((units, width), bf16),
            pltpu.VMEM((units, width), bf16),
            pltpu.VMEM((width * GRAD_EARLY // GRAD_PARTS, units), bf16),
            pltpu.VMEM((width * GRAD_EARLY // GRAD_PARTS, units), bf16),
            pltpu.VMEM((2, tile, width), bf16),
            pltpu.VMEM((rows, 128), f32),
            pltpu.SemaphoreType.DMA((4 + 2 * (rows // tile),)),
            pltpu.SemaphoreType.DMA((experts,)),
            pltpu.SemaphoreType.DMA((M_ROWS, experts)),
            pltpu.SemaphoreType.DMA((M_ROWS, experts)),
        ],
        compiler_params=pltpu.CompilerParams(
            collective_id=1, has_side_effects=True, vmem_limit_bytes=VMEM_BYTES
        ),
    )(
        counts,
        low,
        cot,
        routes,
        slots,
        gates,
        gate_rows,
        weight_in,
        weight_out,
        cots,
        mixed,
        prob,
        gain,
        router,
    )


class Fold:
    def __init__(self, place, move, base, core_send, core_recv, kept, chip_send, chip_recv, whole):
        self.place, self.move, self.base = place, move, base
        self.core_send, self.core_recv, self.kept = core_send, core_recv, kept
        self.chip_send, self.chip_recv, self.whole = chip_send, chip_recv, whole
        self.half, self.side = chip_send.shape[1:]
        self.side_mine = place.part(place.chip, self.side, 128)
        self.side_other = place.part(1 - place.chip, self.side, 128)

    def rows(self, image, core):
        start = (2 * image + core) * self.half
        return pl.ds(pl.multiple_of(start, 16), self.half)

    def core_move(self, image):
        return self.move(
            self.core_send.at[image],
            self.core_recv.at[image],
            self.base,
            image,
            image,
            self.place.near,
        )

    def chip_move(self, image):
        return self.move(
            self.chip_send.at[image],
            self.chip_recv.at[image],
            self.base + 1,
            image,
            image,
            self.place.across,
        )

    def share(self, image, step):
        cols = self.side_other if step == 2 else self.side_mine
        ref = self.whole.at[self.rows(image, self.place.core), cols]
        where = self.place.across if step == 0 else self.place.near
        return self.move(ref, ref, self.base + 2 + step, image, image, where)

    def second(self, image):
        self.core_move(image).wait_recv()
        self.chip_send[image] = (
            self.kept[image, :, self.side_other]
            + self.core_recv[image, :, self.side_other].astype(jnp.float32)
        ).astype(jnp.bfloat16)
        self.chip_move(image).start()

    def third(self, image):
        self.chip_move(image).wait_recv()
        self.whole[self.rows(image, self.place.core), self.side_mine] = (
            self.kept[image, :, self.side_mine]
            + self.core_recv[image, :, self.side_mine].astype(jnp.float32)
            + self.chip_recv[image].astype(jnp.float32)
        ).astype(jnp.bfloat16)
        self.share(image, 0).start()
        self.share(image, 1).start()

    def relay(self, image):
        self.share(image, 0).wait_recv()
        self.share(image, 2).start()

    def ready(self, image):
        self.share(image, 1).wait_recv()
        self.share(image, 2).wait_recv()

    def finish(self, images):
        for image in range(images):
            self.core_move(image).wait_send()
            self.chip_move(image).wait_send()
            for step in range(3):
                self.share(image, step).wait_send()


class WideSum:
    def __init__(self, place, move, tables, pair_send, pair_recv, kept, group_send, group_recv, whole):
        self.place, self.move = place, move
        self.pair_sems, self.group_out, self.group_in = tables
        self.pair_send, self.pair_recv, self.kept = pair_send, pair_recv, kept
        self.group_send, self.group_recv, self.whole = group_send, group_recv, whole
        self.rows, self.cols = group_recv.shape[2:]
        self.half = pair_send.shape[1]
        self.real = kept.shape[1]
        self.pair = {"narrow": place.n, "wide": place.w + 1 - 2 * place.parity}

    def pair_move(self, p):
        return self.move[0](
            self.pair_send.at[p], self.pair_recv.at[p], 0, p, p, self.pair
        )

    def chunk(self, e):
        return (
            pl.ds(pl.multiple_of((e // 2) * self.rows, 16), self.rows),
            pl.ds(pl.multiple_of(lax.rem(e, 2) * self.cols, 128), self.cols),
        )

    def group_move(self, p, e, landed):
        rows, cols = self.chunk(e)
        return self.move[1](
            self.group_send.at[p, rows, cols],
            self.group_recv.at[p, landed],
            p,
            e,
            landed,
            self.place.home(e),
        )

    def group_share(self, p, owner, at, landed, where):
        rows, cols = self.chunk(owner)
        ref = self.whole.at[p, self.place.parity, rows, cols]
        pieces = self.pair_send.shape[0]
        return self.move[1](ref, ref, pieces + p, at, landed, where)

    def pair_share(self, p, parity):
        ref = self.whole.at[p, parity]
        return self.move[0](ref, ref, 1, p, p, self.pair)

    def first(self, p, halves):
        @pl.when(self.place.parity == 0)
        def _():
            self.kept[p] = halves[0]
            self.pair_send[p, 0 : self.real] = halves[1].astype(jnp.bfloat16)

        @pl.when(self.place.parity == 1)
        def _():
            self.kept[p] = halves[1]
            self.pair_send[p, 0 : self.real] = halves[0].astype(jnp.bfloat16)

        self.pair_move(p).start()

    def second(self, p):
        self.pair_move(p).wait_recv()
        self.group_send[p, 0 : self.real] = (
            self.kept[p] + self.pair_recv[p, 0 : self.real].astype(jnp.float32)
        ).astype(jnp.bfloat16)

        @pl.loop(1, self.place.experts)
        def _(i):
            self.group_move(p, self.place.take(i), self.place.me).start()

    def third(self, p):
        rows, cols = self.chunk(self.place.me)
        total = self.group_send[p, rows, cols].astype(jnp.float32)
        self.total[...] = total

        @pl.loop(1, self.place.experts)
        def _(i):
            s = self.place.take(i)
            self.group_move(p, s, s).wait_recv()
            self.total[...] += self.group_recv[p, s].astype(jnp.float32)

        self.whole[p, self.place.parity, rows, cols] = self.total[...].astype(jnp.bfloat16)

        @pl.loop(1, self.place.experts)
        def _(i):
            e = self.place.take(i)
            self.group_share(p, self.place.me, e, self.place.me, self.place.home(e)).start()

    def fourth(self, p):
        @pl.loop(1, self.place.experts)
        def _(i):
            s = self.place.take(i)
            self.group_share(p, s, s, s, self.place.home(s)).wait_recv()

        self.pair_share(p, self.place.parity).start()

    def ready(self, p):
        self.pair_share(p, 1 - self.place.parity).wait_recv()

    def finish(self):
        for p in range(self.pair_send.shape[0]):
            self.pair_move(p).wait_send()
            self.pair_share(p, self.place.parity).wait_send()

            @pl.loop(1, self.place.experts)
            def _(i):
                e = self.place.take(i)
                self.group_move(p, e, self.place.me).wait_send()
                self.group_share(p, self.place.me, e, self.place.me, self.place.home(e)).wait_send()


B_MIX, B_ENDMIX, B_FOLD, B_SMALL, B_GRAD = 0, 3, 6, 11, 13
B_ROWS = 14


def back_kernel(
    experts,
    capacity,
    counts,
    att_grad,
    mixed_grad_hbm,
    heads_ref,
    stats_ref,
    attended_ref,
    x_ref,
    gain_ref,
    qkv_w,
    out_w,
    mixed_hbm,
    half_ref,
    routes_ref,
    slots_ref,
    router_part,
    gain2_part,
    grad_hbm,
    out_ref,
    x_grad_hbm,
    in_grad,
    out_grad,
    gain1_out,
    gain2_out,
    router_out,
    grad_sum_hbm,
    small_out,
    grad_sum,
    mixed_part,
    x_grad,
    grad_send,
    grad_recv,
    whole_ref,
    loads,
    low_ref,
    lines,
    head_grad,
    proj_grad,
    key_wide,
    chip_recv,
    back,
    hot_ref,
    total,
    fold_send,
    fold_recv,
    fold_kept,
    fold_chip_send,
    fold_chip_recv,
    normed_ref,
    pair_send,
    pair_recv,
    pair_kept,
    group_send,
    group_recv,
    group_total,
    small_ref,
    small_near,
    small_far,
    small_pair,
    small_group,
    small_steps,
    sent,
    came,
    pair_sent,
    pair_came,
    group_sent,
    group_came,
):
    rows, width = att_grad.shape
    images = counts.shape[0]
    patches = rows // images
    head_cols = attended_ref.shape[1]
    heads = head_cols // HEAD_DIM
    scale = HEAD_DIM ** (-0.5)
    cap = back.shape[1]
    tile = patches // 2
    pieces = heads + 1
    place = Place(experts)
    move = mover(sent, came)
    me = place.me
    wide = WideSum(
        place,
        (mover(pair_sent, pair_came), mover(group_sent, group_came)),
        (None, None, None),
        pair_send,
        pair_recv,
        pair_kept,
        group_send,
        group_recv,
        whole_ref,
    )
    wide.total = group_total
    fold = Fold(
        place,
        move,
        B_FOLD,
        fold_send,
        fold_recv,
        fold_kept,
        fold_chip_send,
        fold_chip_recv,
        normed_ref,
    )
    my_rows = place.part(place.core, rows // 2, 16)
    side_mine = place.part(place.chip, width // 2, 128)

    def load(at, src, dst):
        return pltpu.make_async_copy(src, dst, loads.at[at])

    grad_in = load(0, grad_hbm, grad_sum)
    mixed_in = load(1, mixed_hbm.at[my_rows, side_mine], mixed_part)
    mixed_grad_in = load(2, mixed_grad_hbm, x_grad)
    grad_in.start()
    mixed_in.start()
    mixed_grad_in.start()
    place.greet((wide.pair,))

    def grad_part(k):
        size = grad_sum.shape[0] // GRAD_PARTS
        return pl.ds(k * size, size)

    def grad_move(k):
        part = grad_part(k)
        return move(grad_send.at[part, :], grad_recv.at[part, :], B_GRAD, k, k, wide.pair)

    def grad_go(k):
        part = grad_part(k)
        grad_send[part, :] = grad_sum[part, :].astype(jnp.bfloat16)
        grad_move(k).start()

    def grad_out(k):
        part = grad_part(k)
        return load(3 + 2 * images + k, grad_sum.at[part, :], grad_sum_hbm.at[part, :])

    def grad_end(k):
        part = grad_part(k)
        grad_move(k).wait()
        grad_sum[part, :] += grad_recv[part, :].astype(jnp.float32)
        grad_out(k).start()

    half = half_ref.shape[1]
    side = width // 2
    mine = place.part(place.core, half, 16)
    other = place.part(1 - place.core, half, 16)
    side_other = place.part(1 - place.chip, side, 128)

    def mix_chip(s):
        return move(half_ref.at[s, :, side_other], chip_recv.at[s], B_MIX, s, s, place.across)

    def mix_home(i, landed):
        s = place.take(i)
        early = isinstance(i, int) and i < MIX_EARLY
        src = half_ref.at[s, :, pl.ds(0, side)] if early else chip_recv.at[s]
        return move(src, back.at[landed, mine, :], B_MIX + 1, s, landed, place.home(s))

    def mix_near(e, part):
        ref = back.at[e, part, :]
        return move(ref, ref, B_MIX + 2, e, e, place.near)

    for i in range(1, MIX_EARLY):
        mix_home(i, me).start()

    @pl.loop(MIX_EARLY, experts)
    def _(i):
        mix_chip(place.take(i)).start()

    back[me, mine, :] = half_ref[me, :, 0:side]
    grad_in.wait()
    for k in range(GRAD_EARLY):
        grad_out(k).start()
    grad_go(2)

    def mix_backs():
        @pl.loop(MIX_EARLY, experts)
        def _(i):
            s = place.take(i)
            mix_chip(s).wait_recv()
            chip_recv[s] = (
                half_ref[s, :, side_mine].astype(jnp.float32) + chip_recv[s].astype(jnp.float32)
            ).astype(jnp.bfloat16)
            mix_home(i, me).start()

    def mix_relay(i):
        e = place.take(i)

        @pl.when(e != me)
        def _():
            mix_home(i, e).wait_recv()

        mix_near(e, mine).start()

    def mix_sum(i):
        e = place.take(i)

        lane = lax.broadcasted_iota(jnp.int32, (rows // 4, 128), 1)

        @pl.loop(0, 2)
        def _(m):
            part = pl.ds(pl.multiple_of(m * (rows // 4), 16), rows // 4)
            full = pl.ds(pl.multiple_of((2 * place.core + m) * (rows // 4), 16), rows // 4)
            keys = [key_wide[k, full, :] - e * cap for k in range(2)]
            for low in range(0, cap, 128):
                size = min(128, cap - low)
                hit = (keys[0] == lane + low) | (keys[1] == lane + low)
                hot_ref[part, low : low + size] = jnp.where(hit, 1.0, 0.0).astype(jnp.bfloat16)[
                    :, 0:size
                ]

        mix_near(e, other).wait_recv()
        total[...] += dot_rows(hot_ref[...], back[e])

    ends = Quarters(place, move, B_ENDMIX, 0, out_ref)

    small_sizes = small_ref.shape
    small_ref[...] = jnp.zeros_like(small_ref)
    small_ref[0:experts] = router_part[0:experts]
    small_ref[experts : experts + 1] = gain2_part[...]

    def small_move(step):
        src, dst, where = (
            (small_ref, small_near, place.near),
            (small_steps.at[0], small_far, place.across),
            (small_steps.at[1], small_pair, wide.pair),
        )[step]
        return move(src, dst, B_SMALL, step, step, where)

    def small_home(e, landed):
        return move(
            small_steps.at[2], small_group.at[landed], B_SMALL + 1, e, landed, place.home(e)
        )

    share_row = lax.broadcasted_iota(jnp.int32, small_sizes, 0) == experts + 1

    def small_second():
        small_move(0).wait_recv()
        small_steps[0] = small_ref[...] + jnp.where(share_row, small_near[...], 0.0)
        small_move(1).start()

    def small_third():
        small_move(1).wait_recv()
        small_steps[1] = small_steps[0] + jnp.where(share_row, small_far[...], 0.0)
        small_move(2).start()

    def small_fourth():
        small_move(2).wait_recv()
        small_steps[2] = small_steps[1] + small_pair[...]
        small_group[me] = small_steps[2]

        @pl.loop(1, experts)
        def _(i):
            small_home(place.take(i), me).start()

    def small_last():
        @pl.loop(1, experts)
        def _(i):
            s = place.take(i)
            small_home(s, s).wait_recv()

        small_out[...] = jnp.zeros_like(small_out)

        @pl.loop(0, experts)
        def _(e):
            small_out[...] += small_group[e]

        router_out[...] = small_out[0:experts]
        gain2_out[...] = small_out[experts : experts + 1].reshape(width)
        gain1_out[...] = small_out[experts + 1 : experts + 2].reshape(width)

    real = pair_kept.shape[1]

    def contract(left, right):
        return lax.dot_general(
            left, right, (((0,), (0,)), ((), ())), preferred_element_type=jnp.float32
        )

    def zero_pads():
        if pair_send.shape[1] > real:
            pair_send[:, real:] = jnp.zeros_like(pair_send[:, real:])
            group_send[:, real:] = jnp.zeros_like(group_send[:, real:])

    zero_pads()
    product = contract(attended_ref[...], att_grad[...])
    wide.first(0, (product[0:real], product[real:]))

    @pl.loop(0, rows // tile)
    def _(t):
        part = pl.ds(pl.multiple_of(t * tile, 16), tile)
        normed, _, _ = normalize(x_ref[part, :].astype(jnp.float32), flat(gain_ref))
        low_ref[part, :] = normed.astype(jnp.bfloat16)
        block = dot_cols(att_grad[part, :], out_w[...]).astype(jnp.bfloat16)
        for h in range(heads):
            head_grad[h, part, :] = block[:, h * HEAD_DIM : (h + 1) * HEAD_DIM]

    @pl.loop(0, images)
    def _(image):
        part = pl.ds(pl.multiple_of(image * patches, 16), patches)
        padded = round_up(patches, 128)
        column = jnp.concatenate(
            [stats_ref[part, :], jnp.zeros((padded - patches, 128), jnp.float32)], 0
        )
        lines[image] = jnp.transpose(column)[0:8, :]

    def attend_back(image, h):
        part = pl.ds(pl.multiple_of(image * patches, 16), patches)
        query = heads_ref[0, h, part, :]
        key_rows = heads_ref[1, h, part, :]
        out_grad = head_grad[h, part, :]
        live = lax.broadcasted_iota(jnp.int32, (patches, 1), 0) < counts[image]
        line = lines[image, pl.ds(h, 1), 0:patches]
        scores = jnp.where(live, dot_cols(key_rows, query) * scale, MASKED_SCORE)
        probs = jnp.exp(scores - line)
        change = dot_cols(heads_ref[2, h, part, :], out_grad)
        delta = jnp.sum(probs * change, 0, keepdims=True)
        score_grad = (scale * probs * (change - delta)).astype(jnp.bfloat16)
        proj_grad[2, h, part, :] = dot_rows(probs.astype(jnp.bfloat16), out_grad).astype(
            jnp.bfloat16
        )
        proj_grad[1, h, part, :] = dot_rows(score_grad, query).astype(jnp.bfloat16)
        proj_grad[0, h, part, :] = contract(score_grad, key_rows).astype(jnp.bfloat16)

    def piece(h):
        grads = jnp.concatenate([proj_grad[i, h] for i in range(3)], 1)
        product = contract(grads, low_ref[...])
        wide.first(h + 1, (product[0:real], product[real:]))

    def fold_first(image):
        @pl.loop(0, 2)
        def _(turn):
            part = fold.rows(image, jnp.where(turn == 0, 1 - place.core, place.core))
            normed_part = jnp.zeros((tile, width), jnp.float32)
            for i in range(3):
                grads = jnp.concatenate([proj_grad[i, h, part, :] for h in range(heads)], 1)
                normed_part += dot_rows(grads, qkv_w[i])

            @pl.when(turn == 0)
            def _():
                fold_send[image] = normed_part.astype(jnp.bfloat16)
                fold.core_move(image).start()

            @pl.when(turn == 1)
            def _():
                fold_kept[image] = normed_part

            _, hat, _ = normalize(x_ref[part, :].astype(jnp.float32), flat(gain_ref))
            small_ref[experts + 1 : experts + 2] += jnp.sum(normed_part * hat, 0, keepdims=True)

    for k, column in enumerate(widen(slot_keys(routes_ref, slots_ref, capacity, cap))):
        key_wide[k] = column

    def mix_relays(lo, hi):
        @pl.loop(lo, hi)
        def _(i):
            mix_relay(i)

    def mix_sums(lo, hi):
        @pl.loop(lo, hi)
        def _(i):
            mix_sum(i)

    total[...] = jnp.zeros_like(total)

    def mix_tail():
        mixed_in.wait()
        out_ref[ends.rows, ends.mine] = (mixed_part[...] + total[...]).astype(
            jnp.bfloat16
        )
        ends.start()

    agenda = {
        2: [lambda: mix_backs()],
        3: [lambda: fold.second(0)],
        4: [lambda: wide.second(0)],
        5: [lambda: fold.third(0), lambda: wide.second(1)],
    }

    @pl.loop(0, images * heads)
    def _(step):
        attend_back(step // heads, lax.rem(step, heads))

        @pl.when((step == heads - 1) | (step == 2 * heads - 1))
        def _():
            fold_first(step // heads)

        @pl.when(step >= heads)
        def _():
            piece(step - heads)

        for at, todo in agenda.items():

            @pl.when(step == at)
            def _():
                for act in todo:
                    act()

    small_move(0).start()
    grad_go(3)
    wide.second(2)
    fold.second(1)
    small_second()
    wide.third(0)
    fold.relay(0)
    mix_relays(0, experts)
    wide.third(1)
    wide.second(3)
    small_third()
    mix_sums(0, experts)
    fold.third(1)
    mix_tail()
    wide.third(2)
    wide.fourth(0)
    small_fourth()
    fold.ready(0)
    mixed_grad_in.wait()

    def rows_out(t):
        part = pl.ds(pl.multiple_of(t * tile, 16), tile)
        return load(3 + t, x_grad.at[part, :], x_grad_hbm.at[part, :])

    def input_rows(image):
        @pl.loop(2 * image, 2 * image + 2)
        def _(t):
            part = pl.ds(pl.multiple_of(t * tile, 16), tile)
            _, hat, scaled = normalize(x_ref[part, :].astype(jnp.float32), flat(gain_ref))
            grad = normed_ref[part, :].astype(jnp.float32) * flat(gain_ref)
            inner = (
                grad - jnp.mean(grad, -1, keepdims=True) - hat * jnp.mean(grad * hat, -1, keepdims=True)
            )
            x_grad[part, :] += scaled * inner
            rows_out(t).start()

    input_rows(0)
    wide.fourth(1)
    wide.third(3)
    fold.relay(1)
    wide.fourth(2)
    small_last()
    fold.ready(1)
    input_rows(1)
    wide.fourth(3)
    for k in range(GRAD_EARLY, GRAD_PARTS):
        grad_end(k)
    ends.relay()

    def settle(p):
        wide.ready(p)
        if p == 0:
            for side in range(2):
                out_grad[side * real : (side + 1) * real] = whole_ref[0, side, 0:real].astype(
                    jnp.float32
                )
            return
        lanes = (p - 1) * HEAD_DIM
        for i in range(3):
            row = i * HEAD_DIM
            while row < (i + 1) * HEAD_DIM:
                side, at = row // real, row % real
                size = min((i + 1) * HEAD_DIM - row, real - at)
                put = lanes + row - i * HEAD_DIM
                in_grad[i, put : put + size] = whole_ref[p, side, at : at + size].astype(jnp.float32)
                row += size

    for p in range(pieces):
        settle(p)
    ends.ready()

    @pl.loop(0, rows // tile)
    def _(t):
        rows_out(t).wait()

    for k in range(GRAD_PARTS):
        grad_out(k).wait()
    wide.finish()
    fold.finish(images)
    ends.finish()
    for step in range(3):
        small_move(step).wait_send()

    @pl.loop(0, experts)
    def _(i):
        s = place.take(i)
        mix_near(s, mine).wait_send()

        @pl.when(i > 0)
        def _():
            mix_home(i, me).wait_send()
            small_home(s, me).wait_send()

        @pl.when(i >= MIX_EARLY)
        def _():
            mix_chip(s).wait_send()


def back(
    counts,
    att_grad,
    mixed_grad,
    head_rows,
    stats,
    attended,
    x,
    gain,
    qkv_w,
    out_w,
    mixed,
    halves,
    routes,
    slots,
    router_part,
    gain2_part,
    grad_in,
    capacity,
):
    rows, width = x.shape
    experts, half = halves.shape[:2]
    cap, side = 2 * half, width // 2
    images = counts.shape[0]
    heads = head_rows.shape[1]
    head_cols = out_w.shape[0]
    pieces = heads + 1
    real = head_cols // 2
    split = max(experts // 2, 1)
    chunk_rows = round_up(-(-real // split), 16)
    padded = chunk_rows * split
    part_rows = rows // images // 2
    small = round_up(experts + 2, 8)
    bf16, f32 = jnp.bfloat16, jnp.float32
    vmem = pl.BlockSpec(memory_space=pltpu.VMEM)
    hbm = pl.BlockSpec(memory_space=pl.ANY)
    small_block = pltpu.VMEM((small, width), f32)
    dma = pltpu.SemaphoreType.DMA
    table = max(experts, images, 3, GRAD_PARTS)
    return pl.pallas_call(
        functools.partial(back_kernel, experts, capacity),
        out_shape=[
            jax.ShapeDtypeStruct((rows, width), bf16),
            jax.ShapeDtypeStruct((rows, width), f32),
            jax.ShapeDtypeStruct((3, head_cols, width), f32),
            jax.ShapeDtypeStruct((head_cols, width), f32),
            jax.ShapeDtypeStruct((width,), f32),
            jax.ShapeDtypeStruct((width,), f32),
            jax.ShapeDtypeStruct((experts, width), f32),
            jax.ShapeDtypeStruct(grad_in.shape, f32),
        ],
        in_specs=[pl.BlockSpec(memory_space=pltpu.SMEM), vmem, hbm]
        + [vmem] * 7
        + [hbm]
        + [vmem] * 5
        + [hbm],
        out_specs=[vmem, hbm] + [vmem] * 5 + [hbm],
        scratch_shapes=[
            small_block,
            pltpu.VMEM(grad_in.shape, f32),
            pltpu.VMEM((rows // 2, side), f32),
            pltpu.VMEM((rows, width), f32),
            pltpu.VMEM(grad_in.shape, bf16),
            pltpu.VMEM(grad_in.shape, bf16),
            pltpu.VMEM((pieces, 2, padded, width), bf16),
            dma((3 + 2 * images + GRAD_PARTS,)),
            pltpu.VMEM((rows, width), bf16),
            pltpu.VMEM((images, 8, round_up(rows // images, 128)), f32),
            pltpu.VMEM((heads, rows, HEAD_DIM), bf16),
            pltpu.VMEM((3, heads, rows, HEAD_DIM), bf16),
            pltpu.VMEM((2, rows, 128), jnp.int32),
            pltpu.VMEM((experts, half, side), bf16),
            pltpu.VMEM((experts, cap, side), bf16),
            pltpu.VMEM((rows // 2, cap), bf16),
            pltpu.VMEM((rows // 2, side), f32),
            pltpu.VMEM((images, part_rows, width), bf16),
            pltpu.VMEM((images, part_rows, width), bf16),
            pltpu.VMEM((images, part_rows, width), f32),
            pltpu.VMEM((images, part_rows, side), bf16),
            pltpu.VMEM((images, part_rows, side), bf16),
            pltpu.VMEM((rows, width), bf16),
            pltpu.VMEM((pieces, padded, width), bf16),
            pltpu.VMEM((pieces, padded, width), bf16),
            pltpu.VMEM((pieces, real, width), f32),
            pltpu.VMEM((pieces, padded, width), bf16),
            pltpu.VMEM((pieces, experts, chunk_rows, side), bf16),
            pltpu.VMEM((chunk_rows, side), f32),
            small_block,
            small_block,
            small_block,
            small_block,
            pltpu.VMEM((experts, small, width), f32),
            pltpu.VMEM((3, small, width), f32),
            dma((B_ROWS, table)),
            dma((B_ROWS, table)),
            dma((2, pieces)),
            dma((2, pieces)),
            dma((2 * pieces, experts)),
            dma((2 * pieces, experts)),
        ],
        compiler_params=pltpu.CompilerParams(
            collective_id=3, has_side_effects=True, vmem_limit_bytes=VMEM_BYTES
        ),
    )(
        counts,
        att_grad,
        mixed_grad,
        head_rows,
        stats,
        attended,
        x,
        gain,
        qkv_w,
        out_w,
        mixed,
        halves,
        routes,
        slots,
        router_part,
        gain2_part,
        grad_in,
    )


def body(
    inputs,
    counts,
    routes,
    slot_ids,
    norm_first,
    attn_in,
    attn_out,
    norm_second,
    router,
    expert_in,
    expert_out,
    cotangent,
):
    rows_dev = inputs.shape[0]
    experts = router.shape[1]
    half_slots = (105 * rows_dev + 100 * experts - 1) // (100 * experts)
    capacity = 2 * half_slots
    slot_pad = round_up(capacity, 32)
    routes, slots = routes.T, slot_ids.T
    router_rows, qkv = router.T, attn_in.transpose(0, 2, 1)
    sent_cots, head_rows, attended, stats, mixed, low_second, prob, gates, gate_rows = front(
        counts,
        inputs,
        cotangent,
        routes,
        slots,
        norm_first,
        qkv,
        attn_out,
        norm_second,
        router_rows,
        experts,
        capacity,
        slot_pad,
    )
    halves, mixed_grad, att_grad, router_part, gain_part, expert_out_grad, in_part = middle(
        counts,
        low_second,
        cotangent,
        routes,
        slots,
        gates,
        gate_rows,
        expert_in[0],
        expert_out[0],
        sent_cots,
        mixed,
        prob,
        norm_second,
        router_rows,
        experts,
        capacity,
    )
    output, input_grad, in_grad, attn_out_grad, gain1_grad, gain2_grad, router_grad, expert_in_grad = back(
        counts,
        att_grad,
        mixed_grad,
        head_rows,
        stats,
        attended,
        inputs,
        norm_first,
        qkv,
        attn_out,
        mixed,
        halves,
        routes,
        slots,
        router_part,
        gain_part,
        in_part,
        capacity,
    )
    return (
        output,
        input_grad,
        gain1_grad,
        in_grad.transpose(0, 2, 1),
        attn_out_grad,
        gain2_grad,
        router_grad.T,
        expert_in_grad[None],
        expert_out_grad[None],
    )


def solution(mesh):
    in_specs = (
        P("wide", None),
        P("wide"),
        P("wide", None),
        P("wide", None),
        P(),
        P(None, None, "narrow"),
        P("narrow", None),
        P(),
        P(),
        P("wide", None, "narrow"),
        P("wide", "narrow", None),
        P("wide", None),
    )
    out_specs = (
        P("wide", None),
        P("wide", None),
        P(),
        P(None, None, "narrow"),
        P("narrow", None),
        P(),
        P(),
        P("wide", None, "narrow"),
        P("wide", "narrow", None),
    )
    return jax.shard_map(body, mesh=mesh, in_specs=in_specs, out_specs=out_specs, check_vma=False)
```

```python
import functools

import jax
import jax.numpy as jnp
from jax import lax
from jax.experimental import pallas as pl
from jax.experimental.pallas import tpu as pltpu
from jax.sharding import PartitionSpec as P

HEAD_DIM = 64
NORM_EPSILON = 1e-06
MASKED_SCORE = -1e30
BY_MESH = pl.DeviceIdType.MESH
VMEM_BYTES = 64 * 1024 * 1024 - 65536


def round_up(value, multiple):
    return -(-value // multiple) * multiple


def dot_rows(left, right):
    return lax.dot_general(left, right, (((1,), (0,)), ((), ())), preferred_element_type=jnp.float32)


def dot_cols(left, right):
    return lax.dot_general(left, right, (((1,), (1,)), ((), ())), preferred_element_type=jnp.float32)


def normal_parts(values):
    t = 1.0 / (1.0 + (0.3275911 * 0.7071067811865476) * jnp.abs(values))
    bell = jnp.exp(-0.5 * values * values)
    poly = t * (
        0.254829592
        + t * (-0.284496736 + t * (1.421413741 + t * (-1.453152027 + t * 1.061405429)))
    )
    tail = 0.5 * poly * bell
    return jnp.where(values >= 0.0, 1.0 - tail, tail), 0.3989422804014327 * values * bell


def normalize(values, gain):
    center = values - jnp.mean(values, -1, keepdims=True)
    scaled = lax.rsqrt(jnp.mean(center * center, -1, keepdims=True) + NORM_EPSILON)
    normed = center * scaled
    return normed * gain, normed, scaled


def slot_keys(routes_ref, slots_ref, capacity, cap):
    return jnp.where(slots_ref[...] < capacity, routes_ref[...] * cap + slots_ref[...], -1)


def widen(rows):
    count = rows.shape[1]
    padded = jnp.concatenate([rows.astype(jnp.float32), jnp.zeros((6, count), jnp.float32)], 0)
    tall = jnp.transpose(padded)
    return [jnp.broadcast_to(tall[:, k : k + 1], (count, 128)).astype(jnp.int32) for k in range(2)]


def flat(gain_ref):
    return gain_ref[...].reshape(1, gain_ref.shape[0])


class Place:
    def __init__(self, experts):
        self.experts = experts
        self.n = lax.axis_index("narrow")
        self.w = lax.axis_index("wide")
        self.core = lax.rem(self.n, 2)
        self.chip = self.n // 2
        self.me = self.w // 2
        self.parity = lax.rem(self.w, 2)
        self.near_n = self.n + 1 - 2 * self.core
        self.across_n = lax.rem(self.n + 2, 4)
        self.near = {"narrow": self.near_n, "wide": self.w}
        self.across = {"narrow": self.across_n, "wide": self.w}

    def home(self, e):
        return {"narrow": self.n, "wide": 2 * e + self.parity}

    def take(self, i):
        short = jnp.minimum(self.me, self.experts - 1 - self.me)
        swing = jnp.where(lax.rem(i, 2) == 1, (i + 1) // 2, -(i // 2))
        away = jnp.where(i <= 2 * short, swing, i - short)
        return self.me + jnp.where(2 * self.me < self.experts, away, -away)

    def part(self, which, size, align):
        return pl.ds(pl.multiple_of(which * size, align), size)

    def greet(self, others=()):
        barrier = pltpu.get_barrier_semaphore()
        for peer in (self.near, self.across, *others):
            pl.semaphore_signal(barrier, inc=1, device_id=peer, device_id_type=BY_MESH)

        @pl.loop(1, self.experts)
        def _(i):
            pl.semaphore_signal(
                barrier, inc=1, device_id=self.home(self.take(i)), device_id_type=BY_MESH
            )

        pl.semaphore_wait(barrier, self.experts + 1 + len(others))


def mover(sent, came):
    def move(src, dst, row, sent_at, came_at, where):
        return pltpu.make_async_remote_copy(
            src_ref=src,
            dst_ref=dst,
            send_sem=sent.at[row, sent_at],
            recv_sem=came.at[row, came_at],
            device_id=where,
            device_id_type=BY_MESH,
        )

    return move


class Dispatch:
    def __init__(self, place, move, base, send, landing):
        self.place, self.move, self.base = place, move, base
        self.send, self.landing = send, landing
        cap, width = landing.shape[1:]
        self.cap, self.half, self.side = cap, cap // 2, width // 2
        self.mine = place.part(place.core, self.half, 16)
        self.other = place.part(1 - place.core, self.half, 16)
        self.side_mine = place.part(place.chip, self.side, 128)
        self.side_other = place.part(1 - place.chip, self.side, 128)

    def z_copy(self, e, landed):
        return self.move(
            self.send.at[e],
            self.landing.at[landed, self.mine, self.side_mine],
            self.base,
            e,
            landed,
            self.place.home(e),
        )

    def build(self, i, key_row, source):
        e = self.place.take(i)
        hot = self.hot(e, self.place.core, key_row)
        self.send[e] = dot_rows(hot, source[:, self.side_mine]).astype(jnp.bfloat16)
        self.z_copy(e, self.place.me).start()

    def hot(self, e, part, key_row):
        slot = e * self.cap + part * self.half
        slot = slot + lax.broadcasted_iota(jnp.int32, (self.half, key_row.shape[1]), 0)
        hit = (key_row[0:1, :] == slot) | (key_row[1:2, :] == slot)
        return jnp.where(hit, 1.0, 0.0).astype(jnp.bfloat16)

    def build_own(self, key_row, source):
        @pl.loop(0, 2)
        def _(m):
            hot = self.hot(self.place.me, m, key_row)
            part = pl.ds(pl.multiple_of(m * self.half, 16), self.half)
            self.landing[self.place.me, part, :] = dot_rows(hot, source[...]).astype(jnp.bfloat16)

    def spread(self, step, s):
        rows, cols, where = (
            (self.mine, self.side_mine, self.place.across),
            (self.mine, self.side_mine, self.place.near),
            (self.mine, self.side_other, self.place.near),
        )[step]
        ref = self.landing.at[s, rows, cols]
        return self.move(ref, ref, self.base + 1 + step, s, s, where)

    def stage_a(self, i):
        self.landed(i)
        self.relay(i)

    def stage_b(self, i):
        s = self.place.take(i)
        self.spread(0, s).wait_recv()
        self.spread(2, s).start()

    def stage_c(self, i):
        s = self.place.take(i)
        self.spread(1, s).wait_recv()
        self.spread(2, s).wait_recv()

    def landed(self, i):
        s = self.place.take(i)
        self.z_copy(s, s).wait_recv()

    def relay(self, i):
        s = self.place.take(i)
        self.spread(0, s).start()
        self.spread(1, s).start()

    def finish(self, lo, hi, sends=True):
        @pl.loop(lo, hi)
        def _(i):
            s = self.place.take(i)
            for step in range(3):
                self.spread(step, s).wait_send()

        if sends:

            @pl.loop(1, self.place.experts)
            def _(i):
                self.z_copy(self.place.take(i), self.place.me).wait_send()


FRONT_OWN, FRONT_FAR, FRONT_CHIP = 4, 5, 6
FRONT_ROWS = 7
LATE = 2


def front_kernel(
    experts,
    capacity,
    counts,
    x_ref,
    cot_ref,
    routes_ref,
    slots_ref,
    gain1_ref,
    qkv_w,
    out_w,
    gain2_ref,
    router_ref,
    cots_ref,
    heads_hbm,
    attended_hbm,
    stats_hbm,
    mixed_hbm,
    low2_hbm,
    prob_hbm,
    gate_hbm,
    gate_send,
    heads_ref,
    attended_ref,
    stats_ref,
    mixed_ref,
    low2_ref,
    prob_ref,
    gate_ref,
    cot_send,
    gather,
    out_all,
    key_row,
    key_wide,
    route_wide,
    gate_wide,
    router_pad,
    loads,
    sent,
    came,
):
    rows, width = x_ref.shape
    images = counts.shape[0]
    patches = rows // images
    head_cols = out_w.shape[0]
    heads = head_cols // HEAD_DIM
    scale = HEAD_DIM ** (-0.5)
    place = Place(experts)
    move = mover(sent, came)
    cots = Dispatch(place, move, 0, cot_send, cots_ref)
    place.greet()
    key_row[...] = slot_keys(routes_ref, slots_ref, capacity, cots.cap)

    def share(ref, at):
        def copy(step):
            piece = ref(place.across_n if step == 2 else place.n)
            where = place.across if step == 0 else place.near
            row = (FRONT_CHIP, FRONT_OWN, FRONT_FAR)[step]
            return move(piece, piece, row, at, at, where)

        return copy

    out_share = share(lambda n: out_all.at[n], images)
    out_all[place.n] = out_w[...]
    out_share(0).start()
    out_share(1).start()

    @pl.loop(1, experts)
    def _(i):
        cots.build(i, key_row, cot_ref)

    tile = patches // 2

    @pl.loop(0, rows // tile)
    def _(t):
        part = pl.ds(pl.multiple_of(t * tile, 16), tile)
        normed, _, _ = normalize(x_ref[part, :].astype(jnp.float32), flat(gain1_ref))
        low = normed.astype(jnp.bfloat16)
        for i in range(3):
            block = dot_cols(low, qkv_w[i]).astype(jnp.bfloat16)
            for h in range(heads):
                heads_ref[i, h, part, :] = block[:, h * HEAD_DIM : (h + 1) * HEAD_DIM]

    outs = [
        pltpu.make_async_copy(src, dst, loads.at[at])
        for at, (src, dst) in enumerate(
            (
                (heads_ref, heads_hbm),
                (attended_ref, attended_hbm),
                (stats_ref, stats_hbm),
                (mixed_ref, mixed_hbm),
                (low2_ref, low2_hbm),
                (prob_ref, prob_hbm),
                (gate_ref, gate_hbm),
            )
        )
    ]
    outs[0].start()
    for k, column in enumerate(widen(key_row[...])):
        key_wide[k] = column
    for k, column in enumerate(widen(routes_ref[...])):
        route_wide[k] = column
    router_pad[...] = jnp.zeros_like(router_pad)
    router_pad[0:experts] = router_ref[...]
    stats_ref[...] = jnp.zeros_like(stats_ref)

    def attend(image):
        keys_at = pl.ds(pl.multiple_of(image * patches, 16), patches)
        pack = pl.ds(pl.multiple_of(image * tile, 16), tile)
        live = lax.broadcasted_iota(jnp.int32, (1, patches), 1) < counts[image]
        for h in range(heads):
            key_rows = heads_ref[1, h, keys_at, :]
            value_rows = heads_ref[2, h, keys_at, :]
            for t in range(patches // tile):
                part = pl.ds(pl.multiple_of(image * patches + t * tile, 16), tile)
                scores = dot_cols(heads_ref[0, h, part, :], key_rows) * scale
                scores = jnp.where(live, scores, MASKED_SCORE)
                top = jnp.max(scores, -1, keepdims=True)
                weights = jnp.exp(scores - top)
                total = jnp.sum(weights, -1, keepdims=True)
                probs = (weights * (1.0 / total)).astype(jnp.bfloat16)
                block = dot_rows(probs, value_rows).astype(jnp.bfloat16)
                at = t * head_cols + h * HEAD_DIM
                gather[place.n, pack, at : at + HEAD_DIM] = block
                attended_ref[part, h * HEAD_DIM : (h + 1) * HEAD_DIM] = block
                stats_ref[part, h : h + 1] = top + jnp.log(total)

    def image_share(image):
        pack = pl.ds(pl.multiple_of(image * tile, 16), tile)
        return share(lambda n: gather.at[n, pack, :], image)

    @pl.loop(0, images)
    def _(image):
        attend(image)
        image_share(image)(0).start()
        image_share(image)(1).start()

    outs[1].start()
    outs[2].start()
    out_share(0).wait_recv()
    out_share(2).start()
    cots.build_own(key_row, cot_ref)

    @pl.loop(1, experts - LATE)
    def _(i):
        cots.stage_a(i)

    out_share(1).wait_recv()
    out_share(2).wait_recv()

    def finish(image):
        copy = image_share(image)
        copy(0).wait_recv()
        copy(2).start()
        copy(1).wait_recv()
        copy(2).wait_recv()
        pack = pl.ds(pl.multiple_of(image * tile, 16), tile)

        for t in range(2):
            part = pl.ds(pl.multiple_of(image * patches + t * tile, 16), tile)
            cols = slice(t * head_cols, (t + 1) * head_cols)
            attention = dot_rows(gather[0, pack, cols], out_all[0])
            for n in range(1, 4):
                attention += dot_rows(gather[n, pack, cols], out_all[n])
            offset = t * tile + lax.broadcasted_iota(jnp.int32, (tile, 1), 0)
            mixed = x_ref[part, :].astype(jnp.float32) + jnp.where(
                offset < counts[image], attention, 0.0
            )
            mixed_ref[part, :] = mixed
            normed, _, _ = normalize(mixed, flat(gain2_ref))
            low = normed.astype(jnp.bfloat16)
            low2_ref[part, :] = low
            lane = lax.broadcasted_iota(jnp.int32, (tile, 128), 1)
            logits = jnp.where(lane < experts, dot_cols(low, router_pad[...]), MASKED_SCORE)
            powers = jnp.exp(logits - jnp.max(logits, -1, keepdims=True))
            prob = powers / jnp.sum(powers, -1, keepdims=True)
            prob_ref[part, :] = prob
            picked = [
                jnp.sum(jnp.where(lane == route_wide[k, part, :], prob, 0.0), 1, keepdims=True)
                for k in range(2)
            ]
            both = picked[0] + picked[1]
            gate_ref[part, :] = jnp.where(
                lane == 0, picked[0] / both, jnp.where(lane == 1, picked[1] / both, both)
            )

    @pl.loop(0, images)
    def _(image):
        finish(image)

    for out in outs[3:]:
        out.start()

    wide_cap = gate_send.shape[2]

    for k in range(2):
        gate_wide[k] = jnp.broadcast_to(gate_ref[:, k : k + 1], (rows, 128))

    @pl.loop(0, experts)
    def _(e):
        @pl.loop(0, wide_cap // 128)
        def _(j):
            lanes = pl.ds(pl.multiple_of(j * 128, 128), 128)
            slot = e * cots.cap + j * 128 + lax.broadcasted_iota(jnp.int32, (rows, 128), 1)
            picked = jnp.where(key_wide[0] == slot, gate_wide[0], 0.0) + jnp.where(
                key_wide[1] == slot, gate_wide[1], 0.0
            )
            gate_send[e, :, lanes] = jnp.broadcast_to(jnp.sum(picked, 0, keepdims=True), (8, 128))

    @pl.loop(1, experts - LATE)
    def _(i):
        cots.stage_b(i)

    @pl.loop(1, experts - LATE)
    def _(i):
        cots.stage_c(i)

    @pl.loop(experts - LATE, experts)
    def _(i):
        cots.landed(i)

    cots.finish(1, experts - LATE)
    for out in outs:
        out.wait()
    for step in range(3):
        out_share(step).wait_send()
        for image in range(images):
            image_share(image)(step).wait_send()


def front(
    counts, x, cot, routes, slots, gain1, qkv_w, out_w, gain2, router, experts, capacity, cap
):
    rows, width = x.shape
    head_cols = out_w.shape[0]
    heads = head_cols // HEAD_DIM
    images = counts.shape[0]
    bf16, f32 = jnp.bfloat16, jnp.float32
    vmem = pl.BlockSpec(memory_space=pltpu.VMEM)
    hbm = pl.BlockSpec(memory_space=pl.ANY)
    table = max(experts, images + 1)
    wide_cap = round_up(cap, 128)
    return pl.pallas_call(
        functools.partial(front_kernel, experts, capacity),
        out_shape=[
            jax.ShapeDtypeStruct((experts, cap, width), bf16),
            jax.ShapeDtypeStruct((3, heads, rows, HEAD_DIM), bf16),
            jax.ShapeDtypeStruct((rows, head_cols), bf16),
            jax.ShapeDtypeStruct((rows, 128), f32),
            jax.ShapeDtypeStruct((rows, width), f32),
            jax.ShapeDtypeStruct((rows, width), bf16),
            jax.ShapeDtypeStruct((rows, 128), f32),
            jax.ShapeDtypeStruct((rows, 128), f32),
            jax.ShapeDtypeStruct((experts, 8, wide_cap), f32),
        ],
        in_specs=[pl.BlockSpec(memory_space=pltpu.SMEM)] + [vmem] * 9,
        out_specs=[vmem] + [hbm] * 7 + [vmem],
        scratch_shapes=[
            pltpu.VMEM((3, heads, rows, HEAD_DIM), bf16),
            pltpu.VMEM((rows, head_cols), bf16),
            pltpu.VMEM((rows, 128), f32),
            pltpu.VMEM((rows, width), f32),
            pltpu.VMEM((rows, width), bf16),
            pltpu.VMEM((rows, 128), f32),
            pltpu.VMEM((rows, 128), f32),
            pltpu.VMEM((experts, cap // 2, width // 2), bf16),
            pltpu.VMEM((4, rows // 2, 2 * head_cols), bf16),
            pltpu.VMEM((4, head_cols, width), bf16),
            pltpu.VMEM((2, rows), jnp.int32),
            pltpu.VMEM((2, rows, 128), jnp.int32),
            pltpu.VMEM((2, rows, 128), jnp.int32),
            pltpu.VMEM((2, rows, 128), f32),
            pltpu.VMEM((128, width), bf16),
            pltpu.SemaphoreType.DMA((7,)),
            pltpu.SemaphoreType.DMA((FRONT_ROWS, table)),
            pltpu.SemaphoreType.DMA((FRONT_ROWS, table)),
        ],
        compiler_params=pltpu.CompilerParams(
            collective_id=2, has_side_effects=True, vmem_limit_bytes=VMEM_BYTES
        ),
    )(counts, x, cot, routes, slots, gain1, qkv_w, out_w, gain2, router)


class Return:
    def __init__(self, place, move, base, core_send, core_recv, kept, chip_send, chip_recv, back):
        self.place, self.move, self.base = place, move, base
        self.core_send, self.core_recv, self.kept = core_send, core_recv, kept
        self.chip_send, self.chip_recv, self.back = chip_send, chip_recv, back
        self.half, self.side = chip_send.shape[1:]
        self.mine = place.part(place.core, self.half, 16)
        self.other = place.part(1 - place.core, self.half, 16)
        self.side_mine = place.part(place.chip, self.side, 128)
        self.side_other = place.part(1 - place.chip, self.side, 128)

    def rows(self, s):
        return pl.ds(pl.multiple_of(s * self.half, 16), self.half)

    def core_move(self, s):
        return self.move(
            self.core_send.at[s], self.core_recv.at[s], self.base, s, s, self.place.near
        )

    def chip_move(self, s):
        return self.move(
            self.chip_send.at[s], self.chip_recv.at[s], self.base + 1, s, s, self.place.across
        )

    def home_move(self, s, landed):
        return self.move(
            self.core_send.at[s, :, pl.ds(0, self.side)],
            self.back.at[landed, self.mine, :],
            self.base + 2,
            s,
            landed,
            self.place.home(s),
        )

    def pair_move(self, e, part):
        ref = self.back.at[e, part, :]
        return self.move(ref, ref, self.base + 3, e, e, self.place.near)

    def first(self, s, product):
        self.core_send[s] = product(self.other).astype(jnp.bfloat16)
        self.core_move(s).start()
        self.kept[self.rows(s), :] = product(self.mine)

    def second(self, s):
        self.core_move(s).wait_recv()
        self.chip_send[s] = (
            self.kept[self.rows(s), self.side_other]
            + self.core_recv[s, :, self.side_other].astype(jnp.float32)
        ).astype(jnp.bfloat16)
        self.chip_move(s).start()

    def third(self, s):
        self.chip_move(s).wait_recv()
        self.core_move(s).wait_send()
        piece = (
            self.kept[self.rows(s), self.side_mine]
            + self.core_recv[s, :, self.side_mine].astype(jnp.float32)
            + self.chip_recv[s].astype(jnp.float32)
        ).astype(jnp.bfloat16)

        @pl.when(s == self.place.me)
        def _():
            self.back[self.place.me, self.mine, :] = piece

        @pl.when(s != self.place.me)
        def _():
            self.core_send[s, :, 0 : self.side] = piece
            self.home_move(s, self.place.me).start()

    def fourth(self, i):
        e = self.place.take(i)

        @pl.when(e != self.place.me)
        def _():
            self.home_move(e, e).wait_recv()

        self.pair_move(e, self.mine).start()

    def ready(self, i):
        self.pair_move(self.place.take(i), self.other).wait_recv()

    def finish(self):
        @pl.loop(0, self.place.experts)
        def _(i):
            s = self.place.take(i)
            self.chip_move(s).wait_send()
            self.pair_move(s, self.mine).wait_send()

            @pl.when(i > 0)
            def _():
                self.home_move(s, self.place.me).wait_send()


class Quarters:
    def __init__(self, place, move, base, at, ref):
        self.place, self.move, self.base, self.at, self.ref = place, move, base, at, ref
        rows, width = ref.shape
        self.rows = place.part(place.core, rows // 2, 16)
        self.mine = place.part(place.chip, width // 2, 128)
        self.other = place.part(1 - place.chip, width // 2, 128)

    def copy(self, step):
        ref = self.ref.at[self.rows, self.other if step == 2 else self.mine]
        where = self.place.across if step == 0 else self.place.near
        return self.move(ref, ref, self.base + step, self.at, self.at, where)

    def start(self):
        self.copy(0).start()
        self.copy(1).start()

    def relay(self):
        self.copy(0).wait_recv()
        self.copy(2).start()

    def ready(self):
        self.copy(1).wait_recv()
        self.copy(2).wait_recv()

    def finish(self):
        for step in range(3):
            self.copy(step).wait_send()


M_CORE, M_CHIP, M_HOME, M_BACK, M_MIX, M_END, M_PAIR, M_LATE, M_GATES = 4, 5, 6, 7, 11, 13, 16, 17, 21
M_ROWS = 22
MIX_EARLY = 4
GRAD_PARTS, GRAD_EARLY = 4, 2


def middle_kernel(
    experts,
    capacity,
    counts,
    low_ref,
    cot_hbm,
    routes_ref,
    slots_ref,
    gate_col,
    gate_send,
    in_hbm,
    out_hbm,
    cots_hbm,
    mixed_hbm,
    prob_ref,
    gain_ref,
    router_ref,
    half_hbm,
    mixed_grad_hbm,
    att_grad_hbm,
    router_grad,
    gain_grad,
    grad_out_hbm,
    grad_in_hbm,
    grad_out,
    grad_in,
    in_ref,
    out_ref,
    cots_ref,
    rows_ref,
    hid_ref,
    pre_ref,
    send_rows,
    gate_rows,
    gate_tall,
    pair_tall,
    pair_part,
    pair_core,
    pair_sum,
    pair_chip,
    pair_home,
    pair_back,
    core_send,
    core_recv,
    kept,
    chip_send,
    chip_recv,
    back,
    mix_send,
    mix_recv,
    mix_last,
    key_row,
    key_wide,
    route_wide,
    router_pad,
    hot_ref,
    total,
    pair_ref,
    dis_ref,
    copy_send,
    copy_recv,
    in_send,
    in_recv,
    cot_tile,
    scale_wide,
    loads,
    cot_loads,
    sent,
    came,
):
    rows, width = low_ref.shape
    images = counts.shape[0]
    patches = rows // images
    cap = rows_ref.shape[1]
    half = cap // 2
    units = in_ref.shape[1]
    place = Place(experts)
    move = mover(sent, came)
    me = place.me
    lows = Dispatch(place, move, 0, send_rows, rows_ref)
    late = Dispatch(place, move, M_LATE, send_rows, cots_ref)
    dgrad = Return(
        place, move, M_BACK, core_send, core_recv, kept, chip_send, chip_recv, back
    )
    other_copy = {"narrow": place.n, "wide": place.w + 1 - 2 * place.parity}

    def load(at, src, dst):
        return pltpu.make_async_copy(src, dst, loads.at[at])

    fetched = [
        load(0, in_hbm, in_ref),
        load(1, out_hbm, out_ref),
    ]
    for copy in fetched:
        copy.start()

    def cots_in(i, whole):
        s = place.take(i)
        at = (s,) if whole else (s, late.mine, late.side_mine)
        return pltpu.make_async_copy(cots_hbm.at[at], cots_ref.at[at], cot_loads.at[i])

    @pl.loop(0, experts - LATE)
    def _(i):
        cots_in(i, True).start()

    for i in range(experts - LATE, experts):
        cots_in(i, False).start()
    place.greet((other_copy,))
    key_row[...] = slot_keys(routes_ref, slots_ref, capacity, cap)

    def gate_copy(e, landed):
        return move(gate_send.at[e], gate_rows.at[landed], M_GATES, e, landed, place.home(e))

    @pl.loop(1, experts)
    def _(i):
        lows.build(i, key_row, low_ref)
        gate_copy(place.take(i), me).start()

    gate_rows[me] = gate_send[me]

    for copy in fetched:
        copy.wait()

    @pl.loop(0, experts - LATE)
    def _(i):
        cots_in(i, True).wait()

    for i in range(experts - LATE, experts):
        cots_in(i, False).wait()
        late.relay(i)

    lows.build_own(key_row, low_ref)
    pair_tall[...] = jnp.zeros_like(pair_tall)
    grad_out[...] = jnp.zeros_like(grad_out)
    grad_in[...] = jnp.zeros_like(grad_in)
    for k, column in enumerate(widen(key_row[...])):
        key_wide[k] = column
    for k, column in enumerate(widen(routes_ref[...])):
        route_wide[k] = column
    router_pad[...] = jnp.zeros_like(router_pad)
    router_pad[0:experts] = router_ref[...]

    def pair_move(step, s):
        src, dst, row, where = (
            (pair_part, pair_core, M_CORE, place.near),
            (pair_sum, pair_chip, M_CHIP, place.across),
        )[step]
        return move(src.at[s], dst.at[s], row, s, s, where)

    def pair_return(s, landed):
        return move(pair_home.at[s], pair_back.at[landed], M_HOME, s, landed, place.home(s))

    chunk = 256 if units % 256 == 0 else units

    def compute(s, m):
        part = pl.ds(pl.multiple_of(m * half, 16), half)
        left = rows_ref[s, part, :]
        cots = cots_ref[s, part, :]
        gate = gate_tall[part, 0:1]
        pair = jnp.zeros((half, 1), jnp.float32)
        for j in range(units // chunk):
            cols = slice(j * chunk, (j + 1) * chunk)
            pre = dot_rows(left, in_ref[:, cols])
            free = dot_cols(cots, out_ref[cols, :])
            cdf, slope = normal_parts(pre)
            hidden = pre * cdf
            hid_ref[s, part, cols] = (gate * hidden).astype(jnp.bfloat16)
            pre_ref[s, part, cols] = (gate * free * (cdf + slope)).astype(jnp.bfloat16)
            pair += jnp.sum(hidden * free, 1, keepdims=True)
        pair_tall[part, :] = jnp.broadcast_to(pair, (half, 128))

    def second(s):
        dgrad.second(s)
        pair_move(0, s).wait_recv()
        pair_sum[s] = pair_part[s] + pair_core[s]
        pair_move(1, s).start()

    def third(s):
        dgrad.third(s)
        pair_move(1, s).wait_recv()
        line = pair_sum[s] + pair_chip[s]

        @pl.when(s == me)
        def _():
            pair_back[me] = line

        @pl.when(s != me)
        def _():
            pair_home[s] = line
            pair_return(s, me).start()

    def contract(left, right):
        return lax.dot_general(
            left, right, (((0,), (0,)), ((), ())), preferred_element_type=jnp.float32
        )

    def mix_move(s):
        return move(mix_send.at[s], mix_recv.at[s], M_MIX, s, s, place.near)

    def mix_chip(s):
        src = mix_recv.at[s, :, dgrad.side_other]
        return move(src, mix_last.at[s], M_MIX + 1, s, s, place.across)

    def mix_first(s):
        mix_send[s] = dot_rows(hid_ref[s, dgrad.other, :], out_ref[...]).astype(jnp.bfloat16)
        mix_move(s).start()

    def mix_second(s):
        mix_move(s).wait_recv()
        mix_recv[s] = (
            dot_rows(hid_ref[s, dgrad.mine, :], out_ref[...]) + mix_recv[s].astype(jnp.float32)
        ).astype(jnp.bfloat16)

    def mix_third(s):
        mix_chip(s).wait()
        total_part = mix_recv[s, :, dgrad.side_mine].astype(jnp.float32)
        mix_recv[s, :, 0 : dgrad.side] = (total_part + mix_last[s].astype(jnp.float32)).astype(
            jnp.bfloat16
        )

    def work(i, between):
        s = place.take(i)
        gate_tall[...] = jnp.transpose(gate_rows[s])

        @pl.loop(0, 2)
        def _(m):
            compute(s, m)

            @pl.when(m == 0)
            def _():
                between()

        pair_part[s] = jnp.transpose(pair_tall[...])[0:8]
        pair_move(0, s).start()
        dgrad.first(s, lambda part: dot_cols(pre_ref[s, part, :], in_ref[...]))

    def add_out(s):
        grad_out[...] += contract(hid_ref[s], cots_ref[s])

    def add_in(lo, hi):
        @pl.loop(lo, hi)
        def _(i):
            s = place.take(i)
            grad_in[...] += contract(rows_ref[s], pre_ref[s])

    def pass_on(i):
        @pl.when((i > 0) & (i + 1 < experts))
        def _():
            lows.stage_a(i + 1)

    @pl.loop(0, experts)
    def _(i):
        s = place.take(i)

        @pl.when(i > 0)
        def _():
            lows.stage_b(i)
            lows.stage_c(i)
            gate_copy(s, s).wait_recv()

        @pl.when(i >= experts - LATE)
        def _():
            late.stage_c(i)

        work(i, lambda: pass_on(i))

        @pl.when(i == 0)
        def _():
            lows.stage_a(1)

        second(s)

        @pl.when(i == 0)
        def _():
            mix_first(s)
            add_in(0, 1)
            for j in range(experts - LATE, experts):
                late.stage_b(j)

        add_out(s)

        @pl.when(i > 1)
        def _():
            third(place.take(i - 2))

    last = place.take(experts - 1)
    copy_send[...] = grad_out[...].astype(jnp.bfloat16)
    copy_move = move(copy_send, copy_recv, M_PAIR, 0, 0, other_copy)
    copy_move.start()

    @pl.loop(1, experts)
    def _(i):
        mix_first(place.take(i))

    third(place.take(experts - 2))

    @pl.loop(0, MIX_EARLY)
    def _(i):
        s = place.take(i)
        mix_second(s)
        mix_chip(s).start()

    third(last)
    add_in(1, experts)
    early_rows = in_send.shape[0]
    in_send[...] = grad_in[0:early_rows].astype(jnp.bfloat16)
    in_move = move(in_send, in_recv, M_PAIR, 1, 1, other_copy)
    in_move.start()
    streams = 4 + 2 * (2 * images)
    kept_rows = pl.ds(early_rows, width - early_rows)
    late_out = load(streams, grad_in.at[kept_rows, :], grad_in_hbm.at[kept_rows, :])
    late_out.start()
    pair_ref[...] = jnp.zeros_like(pair_ref)

    def build_hot(e):
        lane = lax.broadcasted_iota(jnp.int32, (rows // 4, 128), 1)

        @pl.loop(0, 4)
        def _(m):
            part = pl.ds(pl.multiple_of(m * (rows // 4), 16), rows // 4)
            keys = [key_wide[k, part, :] - e * cap for k in range(2)]
            for low in range(0, cap, 128):
                size = min(128, cap - low)
                hit = (keys[0] == lane + low) | (keys[1] == lane + low)
                hot_ref[part, low : low + size] = jnp.where(hit, 1.0, 0.0).astype(jnp.bfloat16)[
                    :, 0:size
                ]

    my_rows = place.part(place.core, rows // 2, 16)
    total[...] = jnp.zeros_like(total)

    @pl.loop(0, experts)
    def _(i):
        e = place.take(i)
        build_hot(e)
        dgrad.fourth(i)

        @pl.when(i > 0)
        def _():
            pair_return(e, e).wait_recv()

        tall = jnp.transpose(pair_back[e])[0:cap, 0:1]
        high = tall.astype(jnp.bfloat16).astype(jnp.float32)
        middle = (tall - high).astype(jnp.bfloat16).astype(jnp.float32)
        lane = lax.broadcasted_iota(jnp.int32, (cap, 128), 1)
        spelled = jnp.where(
            lane == 0, high, jnp.where(lane == 1, middle, jnp.where(lane == 2, tall - high - middle, 0.0))
        ).astype(jnp.bfloat16)
        found = jnp.sum(dot_rows(hot_ref[...], spelled), 1, keepdims=True)
        lane_rows = lax.broadcasted_iota(jnp.int32, (rows, 128), 1)
        pair_ref[...] += jnp.where(lane_rows == e, found, 0.0)
        dgrad.ready(i)
        total[...] += dot_rows(hot_ref[my_rows, :], back[e])

    ends = Quarters(place, move, M_END, 0, dis_ref)
    dis_ref[ends.rows, ends.mine] = total[...].astype(jnp.bfloat16)
    ends.start()

    @pl.loop(MIX_EARLY, experts)
    def _(i):
        mix_second(place.take(i))

    mixed_in = load(1, mixed_hbm, kept.at[pl.ds(0, rows), :])
    mixed_in.start()
    tile = patches // 2
    router_grad[...] = jnp.zeros_like(router_grad)
    gain_grad[...] = jnp.zeros_like(gain_grad)

    def cot_in(t):
        slot = lax.rem(t, 2)
        part = pl.ds(pl.multiple_of(t * tile, 16), tile)
        return pltpu.make_async_copy(cot_hbm.at[part, :], cot_tile.at[slot], loads.at[2 + slot])

    def rows_out(t, what):
        part = pl.ds(pl.multiple_of(t * tile, 16), tile)
        src, dst = ((kept, mixed_grad_hbm), (dis_ref, att_grad_hbm))[what]
        return pltpu.make_async_copy(src.at[part, :], dst.at[part, :], loads.at[4 + 2 * t + what])

    cot_in(0).start()
    mixed_in.wait()

    def before(t):
        part = pl.ds(pl.multiple_of(t * tile, 16), tile)
        lane = lax.broadcasted_iota(jnp.int32, (tile, 128), 1)
        by_expert = pair_ref[part, :]
        hots = [lane == route_wide[k, part, :] for k in range(2)]
        pair = [jnp.sum(jnp.where(hot, by_expert, 0.0), 1, keepdims=True) for hot in hots]
        weighted = pair[0] * gate_col[part, 0:1] + pair[1] * gate_col[part, 1:2]
        both = gate_col[part, 2:3]
        prob = prob_ref[part, :]
        prob_grad = jnp.where(hots[0], (pair[0] - weighted) / both, 0.0) + jnp.where(
            hots[1], (pair[1] - weighted) / both, 0.0
        )
        logit_grad = prob * (prob_grad - jnp.sum(prob * prob_grad, 1, keepdims=True))
        pair_ref[part, :] = logit_grad
        router_grad[...] += contract(logit_grad.astype(jnp.bfloat16), low_ref[part, :])
        _, hat, scaled = normalize(kept[part, :], flat(gain_ref))
        kept[part, :] = hat
        scale_wide[part, :] = jnp.broadcast_to(scaled, (tile, 128))

    @pl.loop(0, rows // tile)
    def _(t):
        @pl.when(t == 2)
        def _():
            ends.relay()

        before(t)

    ends.ready()
    ends.finish()

    @pl.loop(0, rows // tile)
    def _(t):
        @pl.when(t + 1 < rows // tile)
        def _():
            cot_in(t + 1).start()

        part = pl.ds(pl.multiple_of(t * tile, 16), tile)
        normed_grad = dis_ref[part, :].astype(jnp.float32) + dot_rows(
            pair_ref[part, :].astype(jnp.bfloat16), router_pad[...]
        )
        hat = kept[part, :]
        gain_grad[...] += jnp.sum(normed_grad * hat, 0, keepdims=True)
        grad = normed_grad * flat(gain_ref)
        inner = (
            grad - jnp.mean(grad, -1, keepdims=True) - hat * jnp.mean(grad * hat, -1, keepdims=True)
        )
        cot_in(t).wait()
        full = cot_tile[lax.rem(t, 2)].astype(jnp.float32) + scale_wide[part, 0:1] * inner
        kept[part, :] = full
        rows_out(t, 0).start()
        row = t * tile + lax.broadcasted_iota(jnp.int32, (tile, 1), 0)
        live = lax.rem(row, patches) < jnp.where(t * tile < patches, counts[0], counts[images - 1])
        dis_ref[part, :] = jnp.where(live, full, 0.0).astype(jnp.bfloat16)
        rows_out(t, 1).start()

    @pl.loop(0, MIX_EARLY)
    def _(i):
        mix_third(place.take(i))

    half_out = load(0, mix_recv, half_hbm)
    half_out.start()
    copy_move.wait()
    grad_out[...] += copy_recv[...].astype(jnp.float32)
    out_out = load(streams + 1, grad_out, grad_out_hbm)
    out_out.start()
    in_move.wait()
    grad_in[0:early_rows] += in_recv[...].astype(jnp.float32)
    first_rows = pl.ds(0, early_rows)
    in_out = load(streams + 2, grad_in.at[first_rows, :], grad_in_hbm.at[first_rows, :])
    in_out.start()
    late_out.wait()
    out_out.wait()
    in_out.wait()
    half_out.wait()

    @pl.loop(0, rows // tile)
    def _(t):
        rows_out(t, 0).wait()
        rows_out(t, 1).wait()

    dgrad.finish()
    lows.finish(1, experts)
    late.finish(experts - LATE, experts, False)

    @pl.loop(0, experts)
    def _(i):
        s = place.take(i)
        pair_move(0, s).wait_send()
        pair_move(1, s).wait_send()
        mix_move(s).wait_send()

        @pl.when(i > 0)
        def _():
            pair_return(s, me).wait_send()
            gate_copy(s, me).wait_send()


def middle(
    counts,
    low,
    cot,
    routes,
    slots,
    gates,
    gate_rows,
    weight_in,
    weight_out,
    cots,
    mixed,
    prob,
    gain,
    router,
    experts,
    capacity,
):
    rows, width = low.shape
    units = weight_in.shape[1]
    cap = cots.shape[1]
    half, side, wide_cap = cap // 2, width // 2, round_up(cap, 128)
    bf16, f32 = jnp.bfloat16, jnp.float32
    vmem = pl.BlockSpec(memory_space=pltpu.VMEM)
    hbm = pl.BlockSpec(memory_space=pl.ANY)
    line = pltpu.VMEM((experts, 8, wide_cap), f32)
    halves = pltpu.VMEM((experts, half, width), bf16)
    tile = rows // counts.shape[0] // 2
    return pl.pallas_call(
        functools.partial(middle_kernel, experts, capacity),
        out_shape=[
            jax.ShapeDtypeStruct((experts, half, width), bf16),
            jax.ShapeDtypeStruct((rows, width), f32),
            jax.ShapeDtypeStruct((rows, width), bf16),
            jax.ShapeDtypeStruct((128, width), f32),
            jax.ShapeDtypeStruct((1, width), f32),
            jax.ShapeDtypeStruct((units, width), f32),
            jax.ShapeDtypeStruct((width, units), f32),
        ],
        in_specs=[
            pl.BlockSpec(memory_space=pltpu.SMEM),
            vmem,
            hbm,
            vmem,
            vmem,
            vmem,
            vmem,
            hbm,
            hbm,
            hbm,
            hbm,
            vmem,
            vmem,
            vmem,
        ],
        out_specs=[hbm] * 3 + [vmem] * 2 + [hbm] * 2,
        scratch_shapes=[
            pltpu.VMEM((units, width), f32),
            pltpu.VMEM((width, units), f32),
            pltpu.VMEM((width, units), bf16),
            pltpu.VMEM((units, width), bf16),
            pltpu.VMEM((experts, cap, width), bf16),
            pltpu.VMEM((experts, cap, width), bf16),
            pltpu.VMEM((experts, cap, units), bf16),
            pltpu.VMEM((experts, cap, units), bf16),
            pltpu.VMEM((experts, half, side), bf16),
            line,
            pltpu.VMEM((wide_cap, 8), f32),
            pltpu.VMEM((wide_cap, 128), f32),
            line,
            line,
            line,
            line,
            line,
            line,
            halves,
            halves,
            pltpu.VMEM((max(experts * half, rows), width), f32),
            pltpu.VMEM((experts, half, side), bf16),
            pltpu.VMEM((experts, half, side), bf16),
            pltpu.VMEM((experts, cap, side), bf16),
            halves,
            halves,
            pltpu.VMEM((experts, half, side), bf16),
            pltpu.VMEM((2, rows), jnp.int32),
            pltpu.VMEM((2, rows, 128), jnp.int32),
            pltpu.VMEM((2, rows, 128), jnp.int32),
            pltpu.VMEM((128, width), bf16),
            pltpu.VMEM((rows, cap), bf16),
            pltpu.VMEM((rows // 2, side), f32),
            pltpu.VMEM((rows, 128), f32),
            pltpu.VMEM((rows, width), bf16),
            pltpu.VMEM((units, width), bf16),
            pltpu.VMEM((units, width), bf16),
            pltpu.VMEM((width * GRAD_EARLY // GRAD_PARTS, units), bf16),
            pltpu.VMEM((width * GRAD_EARLY // GRAD_PARTS, units), bf16),
            pltpu.VMEM((2, tile, width), bf16),
            pltpu.VMEM((rows, 128), f32),
            pltpu.SemaphoreType.DMA((7 + 2 * (rows // tile),)),
            pltpu.SemaphoreType.DMA((experts,)),
            pltpu.SemaphoreType.DMA((M_ROWS, experts)),
            pltpu.SemaphoreType.DMA((M_ROWS, experts)),
        ],
        compiler_params=pltpu.CompilerParams(
            collective_id=1, has_side_effects=True, vmem_limit_bytes=VMEM_BYTES
        ),
    )(
        counts,
        low,
        cot,
        routes,
        slots,
        gates,
        gate_rows,
        weight_in,
        weight_out,
        cots,
        mixed,
        prob,
        gain,
        router,
    )


class Fold:
    def __init__(self, place, move, base, core_send, core_recv, kept, chip_send, chip_recv, whole):
        self.place, self.move, self.base = place, move, base
        self.core_send, self.core_recv, self.kept = core_send, core_recv, kept
        self.chip_send, self.chip_recv, self.whole = chip_send, chip_recv, whole
        self.half, self.side = chip_send.shape[1:]
        self.side_mine = place.part(place.chip, self.side, 128)
        self.side_other = place.part(1 - place.chip, self.side, 128)

    def rows(self, image, core):
        start = (2 * image + core) * self.half
        return pl.ds(pl.multiple_of(start, 16), self.half)

    def core_move(self, image):
        return self.move(
            self.core_send.at[image],
            self.core_recv.at[image],
            self.base,
            image,
            image,
            self.place.near,
        )

    def chip_move(self, image):
        return self.move(
            self.chip_send.at[image],
            self.chip_recv.at[image],
            self.base + 1,
            image,
            image,
            self.place.across,
        )

    def share(self, image, step):
        cols = self.side_other if step == 2 else self.side_mine
        ref = self.whole.at[self.rows(image, self.place.core), cols]
        where = self.place.across if step == 0 else self.place.near
        return self.move(ref, ref, self.base + 2 + step, image, image, where)

    def second(self, image):
        self.core_move(image).wait_recv()
        self.chip_send[image] = (
            self.kept[image, :, self.side_other]
            + self.core_recv[image, :, self.side_other].astype(jnp.float32)
        ).astype(jnp.bfloat16)
        self.chip_move(image).start()

    def third(self, image):
        self.chip_move(image).wait_recv()
        self.whole[self.rows(image, self.place.core), self.side_mine] = (
            self.kept[image, :, self.side_mine]
            + self.core_recv[image, :, self.side_mine].astype(jnp.float32)
            + self.chip_recv[image].astype(jnp.float32)
        ).astype(jnp.bfloat16)
        self.share(image, 0).start()
        self.share(image, 1).start()

    def relay(self, image):
        self.share(image, 0).wait_recv()
        self.share(image, 2).start()

    def ready(self, image):
        self.share(image, 1).wait_recv()
        self.share(image, 2).wait_recv()

    def finish(self, images):
        for image in range(images):
            self.core_move(image).wait_send()
            self.chip_move(image).wait_send()
            for step in range(3):
                self.share(image, step).wait_send()


class WideSum:
    def __init__(self, place, move, tables, pair_send, pair_recv, kept, group_send, group_recv, whole):
        self.place, self.move = place, move
        self.pair_sems, self.group_out, self.group_in = tables
        self.pair_send, self.pair_recv, self.kept = pair_send, pair_recv, kept
        self.group_send, self.group_recv, self.whole = group_send, group_recv, whole
        self.rows, self.cols = group_recv.shape[2:]
        self.half = pair_send.shape[1]
        self.real = kept.shape[1]
        self.pair = {"narrow": place.n, "wide": place.w + 1 - 2 * place.parity}

    def pair_move(self, p):
        return self.move[0](
            self.pair_send.at[p], self.pair_recv.at[p], 0, p, p, self.pair
        )

    def chunk(self, e):
        return (
            pl.ds(pl.multiple_of((e // 2) * self.rows, 16), self.rows),
            pl.ds(pl.multiple_of(lax.rem(e, 2) * self.cols, 128), self.cols),
        )

    def group_move(self, p, e, landed):
        rows, cols = self.chunk(e)
        return self.move[1](
            self.group_send.at[p, rows, cols],
            self.group_recv.at[p, landed],
            p,
            e,
            landed,
            self.place.home(e),
        )

    def group_share(self, p, owner, at, landed, where):
        rows, cols = self.chunk(owner)
        ref = self.whole.at[p, self.place.parity, rows, cols]
        pieces = self.pair_send.shape[0]
        return self.move[1](ref, ref, pieces + p, at, landed, where)

    def pair_share(self, p, parity):
        ref = self.whole.at[p, parity]
        return self.move[0](ref, ref, 1, p, p, self.pair)

    def first(self, p, halves):
        @pl.when(self.place.parity == 0)
        def _():
            self.kept[p] = halves[0]
            self.pair_send[p, 0 : self.real] = halves[1].astype(jnp.bfloat16)

        @pl.when(self.place.parity == 1)
        def _():
            self.kept[p] = halves[1]
            self.pair_send[p, 0 : self.real] = halves[0].astype(jnp.bfloat16)

        self.pair_move(p).start()

    def second(self, p):
        self.pair_move(p).wait_recv()
        self.group_send[p, 0 : self.real] = (
            self.kept[p] + self.pair_recv[p, 0 : self.real].astype(jnp.float32)
        ).astype(jnp.bfloat16)

        @pl.loop(1, self.place.experts)
        def _(i):
            self.group_move(p, self.place.take(i), self.place.me).start()

    def third(self, p):
        rows, cols = self.chunk(self.place.me)
        total = self.group_send[p, rows, cols].astype(jnp.float32)
        self.total[...] = total

        @pl.loop(1, self.place.experts)
        def _(i):
            s = self.place.take(i)
            self.group_move(p, s, s).wait_recv()
            self.total[...] += self.group_recv[p, s].astype(jnp.float32)

        self.whole[p, self.place.parity, rows, cols] = self.total[...].astype(jnp.bfloat16)

        @pl.loop(1, self.place.experts)
        def _(i):
            e = self.place.take(i)
            self.group_share(p, self.place.me, e, self.place.me, self.place.home(e)).start()

    def fourth(self, p):
        @pl.loop(1, self.place.experts)
        def _(i):
            s = self.place.take(i)
            self.group_share(p, s, s, s, self.place.home(s)).wait_recv()

        self.pair_share(p, self.place.parity).start()

    def ready(self, p):
        self.pair_share(p, 1 - self.place.parity).wait_recv()

    def finish(self):
        for p in range(self.pair_send.shape[0]):
            self.pair_move(p).wait_send()
            self.pair_share(p, self.place.parity).wait_send()

            @pl.loop(1, self.place.experts)
            def _(i):
                e = self.place.take(i)
                self.group_move(p, e, self.place.me).wait_send()
                self.group_share(p, self.place.me, e, self.place.me, self.place.home(e)).wait_send()


B_MIX, B_ENDMIX, B_FOLD, B_SMALL, B_GRAD = 0, 3, 6, 11, 13
B_ROWS = 14


def back_kernel(
    experts,
    capacity,
    counts,
    att_grad,
    mixed_grad_hbm,
    heads_ref,
    stats_ref,
    attended_ref,
    x_ref,
    gain_ref,
    qkv_w,
    out_w,
    mixed_hbm,
    half_ref,
    routes_ref,
    slots_ref,
    router_part,
    gain2_part,
    grad_hbm,
    out_ref,
    x_grad_hbm,
    in_grad,
    out_grad,
    gain1_out,
    gain2_out,
    router_out,
    grad_sum_hbm,
    small_out,
    grad_sum,
    mixed_part,
    x_grad,
    grad_send,
    grad_recv,
    whole_ref,
    loads,
    low_ref,
    lines,
    head_grad,
    proj_grad,
    key_wide,
    chip_recv,
    back,
    hot_ref,
    total,
    fold_send,
    fold_recv,
    fold_kept,
    fold_chip_send,
    fold_chip_recv,
    normed_ref,
    pair_send,
    pair_recv,
    pair_kept,
    group_send,
    group_recv,
    group_total,
    small_ref,
    small_near,
    small_far,
    small_pair,
    small_group,
    small_steps,
    sent,
    came,
    pair_sent,
    pair_came,
    group_sent,
    group_came,
):
    rows, width = att_grad.shape
    images = counts.shape[0]
    patches = rows // images
    head_cols = attended_ref.shape[1]
    heads = head_cols // HEAD_DIM
    scale = HEAD_DIM ** (-0.5)
    cap = back.shape[1]
    tile = patches // 2
    pieces = heads + 1
    place = Place(experts)
    move = mover(sent, came)
    me = place.me
    wide = WideSum(
        place,
        (mover(pair_sent, pair_came), mover(group_sent, group_came)),
        (None, None, None),
        pair_send,
        pair_recv,
        pair_kept,
        group_send,
        group_recv,
        whole_ref,
    )
    wide.total = group_total
    fold = Fold(
        place,
        move,
        B_FOLD,
        fold_send,
        fold_recv,
        fold_kept,
        fold_chip_send,
        fold_chip_recv,
        normed_ref,
    )
    my_rows = place.part(place.core, rows // 2, 16)
    side_mine = place.part(place.chip, width // 2, 128)

    def load(at, src, dst):
        return pltpu.make_async_copy(src, dst, loads.at[at])

    grad_in = load(0, grad_hbm, grad_sum)
    mixed_in = load(1, mixed_hbm.at[my_rows, side_mine], mixed_part)
    mixed_grad_in = load(2, mixed_grad_hbm, x_grad)
    grad_in.start()
    mixed_in.start()
    mixed_grad_in.start()
    place.greet((wide.pair,))

    def grad_part(k):
        size = grad_sum.shape[0] // GRAD_PARTS
        return pl.ds(k * size, size)

    def grad_move(k):
        part = grad_part(k)
        return move(grad_send.at[part, :], grad_recv.at[part, :], B_GRAD, k, k, wide.pair)

    def grad_go(k):
        part = grad_part(k)
        grad_send[part, :] = grad_sum[part, :].astype(jnp.bfloat16)
        grad_move(k).start()

    def grad_out(k):
        part = grad_part(k)
        return load(3 + 2 * images + k, grad_sum.at[part, :], grad_sum_hbm.at[part, :])

    def grad_end(k):
        part = grad_part(k)
        grad_move(k).wait()
        grad_sum[part, :] += grad_recv[part, :].astype(jnp.float32)
        grad_out(k).start()

    half = half_ref.shape[1]
    side = width // 2
    mine = place.part(place.core, half, 16)
    other = place.part(1 - place.core, half, 16)
    side_other = place.part(1 - place.chip, side, 128)

    def mix_chip(s):
        return move(half_ref.at[s, :, side_other], chip_recv.at[s], B_MIX, s, s, place.across)

    def mix_home(i, landed):
        s = place.take(i)
        early = isinstance(i, int) and i < MIX_EARLY
        src = half_ref.at[s, :, pl.ds(0, side)] if early else chip_recv.at[s]
        return move(src, back.at[landed, mine, :], B_MIX + 1, s, landed, place.home(s))

    def mix_near(e, part):
        ref = back.at[e, part, :]
        return move(ref, ref, B_MIX + 2, e, e, place.near)

    for i in range(1, MIX_EARLY):
        mix_home(i, me).start()

    @pl.loop(MIX_EARLY, experts)
    def _(i):
        mix_chip(place.take(i)).start()

    back[me, mine, :] = half_ref[me, :, 0:side]
    grad_in.wait()
    for k in range(GRAD_EARLY):
        grad_out(k).start()
    grad_go(2)

    def mix_backs():
        @pl.loop(MIX_EARLY, experts)
        def _(i):
            s = place.take(i)
            mix_chip(s).wait_recv()
            chip_recv[s] = (
                half_ref[s, :, side_mine].astype(jnp.float32) + chip_recv[s].astype(jnp.float32)
            ).astype(jnp.bfloat16)
            mix_home(i, me).start()

    def mix_relay(i):
        e = place.take(i)

        @pl.when(e != me)
        def _():
            mix_home(i, e).wait_recv()

        mix_near(e, mine).start()

    def mix_sum(i):
        e = place.take(i)

        lane = lax.broadcasted_iota(jnp.int32, (rows // 4, 128), 1)

        @pl.loop(0, 2)
        def _(m):
            part = pl.ds(pl.multiple_of(m * (rows // 4), 16), rows // 4)
            full = pl.ds(pl.multiple_of((2 * place.core + m) * (rows // 4), 16), rows // 4)
            keys = [key_wide[k, full, :] - e * cap for k in range(2)]
            for low in range(0, cap, 128):
                size = min(128, cap - low)
                hit = (keys[0] == lane + low) | (keys[1] == lane + low)
                hot_ref[part, low : low + size] = jnp.where(hit, 1.0, 0.0).astype(jnp.bfloat16)[
                    :, 0:size
                ]

        mix_near(e, other).wait_recv()
        total[...] += dot_rows(hot_ref[...], back[e])

    ends = Quarters(place, move, B_ENDMIX, 0, out_ref)

    small_sizes = small_ref.shape
    small_ref[...] = jnp.zeros_like(small_ref)
    small_ref[0:experts] = router_part[0:experts]
    small_ref[experts : experts + 1] = gain2_part[...]

    def small_move(step):
        src, dst, where = (
            (small_ref, small_near, place.near),
            (small_steps.at[0], small_far, place.across),
            (small_steps.at[1], small_pair, wide.pair),
        )[step]
        return move(src, dst, B_SMALL, step, step, where)

    def small_home(e, landed):
        return move(
            small_steps.at[2], small_group.at[landed], B_SMALL + 1, e, landed, place.home(e)
        )

    share_row = lax.broadcasted_iota(jnp.int32, small_sizes, 0) == experts + 1

    def small_second():
        small_move(0).wait_recv()
        small_steps[0] = small_ref[...] + jnp.where(share_row, small_near[...], 0.0)
        small_move(1).start()

    def small_third():
        small_move(1).wait_recv()
        small_steps[1] = small_steps[0] + jnp.where(share_row, small_far[...], 0.0)
        small_move(2).start()

    def small_fourth():
        small_move(2).wait_recv()
        small_steps[2] = small_steps[1] + small_pair[...]
        small_group[me] = small_steps[2]

        @pl.loop(1, experts)
        def _(i):
            small_home(place.take(i), me).start()

    def small_last():
        @pl.loop(1, experts)
        def _(i):
            s = place.take(i)
            small_home(s, s).wait_recv()

        small_out[...] = jnp.zeros_like(small_out)

        @pl.loop(0, experts)
        def _(e):
            small_out[...] += small_group[e]

        router_out[...] = small_out[0:experts]
        gain2_out[...] = small_out[experts : experts + 1].reshape(width)
        gain1_out[...] = small_out[experts + 1 : experts + 2].reshape(width)

    real = pair_kept.shape[1]

    def contract(left, right):
        return lax.dot_general(
            left, right, (((0,), (0,)), ((), ())), preferred_element_type=jnp.float32
        )

    def zero_pads():
        if pair_send.shape[1] > real:
            pair_send[:, real:] = jnp.zeros_like(pair_send[:, real:])
            group_send[:, real:] = jnp.zeros_like(group_send[:, real:])

    zero_pads()
    product = contract(attended_ref[...], att_grad[...])
    wide.first(0, (product[0:real], product[real:]))

    @pl.loop(0, rows // tile)
    def _(t):
        part = pl.ds(pl.multiple_of(t * tile, 16), tile)
        normed, _, _ = normalize(x_ref[part, :].astype(jnp.float32), flat(gain_ref))
        low_ref[part, :] = normed.astype(jnp.bfloat16)
        block = dot_cols(att_grad[part, :], out_w[...]).astype(jnp.bfloat16)
        for h in range(heads):
            head_grad[h, part, :] = block[:, h * HEAD_DIM : (h + 1) * HEAD_DIM]

    @pl.loop(0, images)
    def _(image):
        part = pl.ds(pl.multiple_of(image * patches, 16), patches)
        padded = round_up(patches, 128)
        column = jnp.concatenate(
            [stats_ref[part, :], jnp.zeros((padded - patches, 128), jnp.float32)], 0
        )
        lines[image] = jnp.transpose(column)[0:8, :]

    def attend_back(image, h):
        part = pl.ds(pl.multiple_of(image * patches, 16), patches)
        query = heads_ref[0, h, part, :]
        key_rows = heads_ref[1, h, part, :]
        out_grad = head_grad[h, part, :]
        live = lax.broadcasted_iota(jnp.int32, (patches, 1), 0) < counts[image]
        line = lines[image, pl.ds(h, 1), 0:patches]
        scores = jnp.where(live, dot_cols(key_rows, query) * scale, MASKED_SCORE)
        probs = jnp.exp(scores - line)
        change = dot_cols(heads_ref[2, h, part, :], out_grad)
        delta = jnp.sum(probs * change, 0, keepdims=True)
        score_grad = (scale * probs * (change - delta)).astype(jnp.bfloat16)
        proj_grad[2, h, part, :] = dot_rows(probs.astype(jnp.bfloat16), out_grad).astype(
            jnp.bfloat16
        )
        proj_grad[1, h, part, :] = dot_rows(score_grad, query).astype(jnp.bfloat16)
        proj_grad[0, h, part, :] = contract(score_grad, key_rows).astype(jnp.bfloat16)

    def piece(h):
        grads = jnp.concatenate([proj_grad[i, h] for i in range(3)], 1)
        product = contract(grads, low_ref[...])
        wide.first(h + 1, (product[0:real], product[real:]))

    def fold_first(image):
        @pl.loop(0, 2)
        def _(turn):
            part = fold.rows(image, jnp.where(turn == 0, 1 - place.core, place.core))
            normed_part = jnp.zeros((tile, width), jnp.float32)
            for i in range(3):
                grads = jnp.concatenate([proj_grad[i, h, part, :] for h in range(heads)], 1)
                normed_part += dot_rows(grads, qkv_w[i])

            @pl.when(turn == 0)
            def _():
                fold_send[image] = normed_part.astype(jnp.bfloat16)
                fold.core_move(image).start()

            @pl.when(turn == 1)
            def _():
                fold_kept[image] = normed_part

            _, hat, _ = normalize(x_ref[part, :].astype(jnp.float32), flat(gain_ref))
            small_ref[experts + 1 : experts + 2] += jnp.sum(normed_part * hat, 0, keepdims=True)

    for k, column in enumerate(widen(slot_keys(routes_ref, slots_ref, capacity, cap))):
        key_wide[k] = column

    def mix_relays(lo, hi):
        @pl.loop(lo, hi)
        def _(i):
            mix_relay(i)

    def mix_sums(lo, hi):
        @pl.loop(lo, hi)
        def _(i):
            mix_sum(i)

    total[...] = jnp.zeros_like(total)

    def mix_tail():
        mixed_in.wait()
        out_ref[ends.rows, ends.mine] = (mixed_part[...] + total[...]).astype(
            jnp.bfloat16
        )
        ends.start()

    agenda = {
        2: [lambda: mix_backs()],
        3: [lambda: fold.second(0)],
        4: [lambda: wide.second(0)],
        5: [lambda: fold.third(0), lambda: wide.second(1)],
    }

    @pl.loop(0, images * heads)
    def _(step):
        attend_back(step // heads, lax.rem(step, heads))

        @pl.when((step == heads - 1) | (step == 2 * heads - 1))
        def _():
            fold_first(step // heads)

        @pl.when(step >= heads)
        def _():
            piece(step - heads)

        for at, todo in agenda.items():

            @pl.when(step == at)
            def _():
                for act in todo:
                    act()

    small_move(0).start()
    grad_go(3)
    wide.second(2)
    fold.second(1)
    small_second()
    wide.third(0)
    fold.relay(0)
    mix_relays(0, experts)
    wide.third(1)
    wide.second(3)
    small_third()
    mix_sums(0, experts)
    fold.third(1)
    mix_tail()
    wide.third(2)
    wide.fourth(0)
    small_fourth()
    fold.ready(0)
    mixed_grad_in.wait()

    def rows_out(t):
        part = pl.ds(pl.multiple_of(t * tile, 16), tile)
        return load(3 + t, x_grad.at[part, :], x_grad_hbm.at[part, :])

    def input_rows(image):
        @pl.loop(2 * image, 2 * image + 2)
        def _(t):
            part = pl.ds(pl.multiple_of(t * tile, 16), tile)
            _, hat, scaled = normalize(x_ref[part, :].astype(jnp.float32), flat(gain_ref))
            grad = normed_ref[part, :].astype(jnp.float32) * flat(gain_ref)
            inner = (
                grad - jnp.mean(grad, -1, keepdims=True) - hat * jnp.mean(grad * hat, -1, keepdims=True)
            )
            x_grad[part, :] += scaled * inner
            rows_out(t).start()

    input_rows(0)
    wide.fourth(1)
    wide.third(3)
    fold.relay(1)
    wide.fourth(2)
    small_last()
    fold.ready(1)
    input_rows(1)
    wide.fourth(3)
    for k in range(GRAD_EARLY, GRAD_PARTS):
        grad_end(k)
    ends.relay()

    def settle(p):
        wide.ready(p)
        if p == 0:
            for side in range(2):
                out_grad[side * real : (side + 1) * real] = whole_ref[0, side, 0:real].astype(
                    jnp.float32
                )
            return
        lanes = (p - 1) * HEAD_DIM
        for i in range(3):
            row = i * HEAD_DIM
            while row < (i + 1) * HEAD_DIM:
                side, at = row // real, row % real
                size = min((i + 1) * HEAD_DIM - row, real - at)
                put = lanes + row - i * HEAD_DIM
                in_grad[i, put : put + size] = whole_ref[p, side, at : at + size].astype(jnp.float32)
                row += size

    for p in range(pieces):
        settle(p)
    ends.ready()

    @pl.loop(0, rows // tile)
    def _(t):
        rows_out(t).wait()

    for k in range(GRAD_PARTS):
        grad_out(k).wait()
    wide.finish()
    fold.finish(images)
    ends.finish()
    for step in range(3):
        small_move(step).wait_send()

    @pl.loop(0, experts)
    def _(i):
        s = place.take(i)
        mix_near(s, mine).wait_send()

        @pl.when(i > 0)
        def _():
            mix_home(i, me).wait_send()
            small_home(s, me).wait_send()

        @pl.when(i >= MIX_EARLY)
        def _():
            mix_chip(s).wait_send()


def back(
    counts,
    att_grad,
    mixed_grad,
    head_rows,
    stats,
    attended,
    x,
    gain,
    qkv_w,
    out_w,
    mixed,
    halves,
    routes,
    slots,
    router_part,
    gain2_part,
    grad_in,
    capacity,
):
    rows, width = x.shape
    experts, half = halves.shape[:2]
    cap, side = 2 * half, width // 2
    images = counts.shape[0]
    heads = head_rows.shape[1]
    head_cols = out_w.shape[0]
    pieces = heads + 1
    real = head_cols // 2
    split = max(experts // 2, 1)
    chunk_rows = round_up(-(-real // split), 16)
    padded = chunk_rows * split
    part_rows = rows // images // 2
    small = round_up(experts + 2, 8)
    bf16, f32 = jnp.bfloat16, jnp.float32
    vmem = pl.BlockSpec(memory_space=pltpu.VMEM)
    hbm = pl.BlockSpec(memory_space=pl.ANY)
    small_block = pltpu.VMEM((small, width), f32)
    dma = pltpu.SemaphoreType.DMA
    table = max(experts, images, 3, GRAD_PARTS)
    return pl.pallas_call(
        functools.partial(back_kernel, experts, capacity),
        out_shape=[
            jax.ShapeDtypeStruct((rows, width), bf16),
            jax.ShapeDtypeStruct((rows, width), f32),
            jax.ShapeDtypeStruct((3, head_cols, width), f32),
            jax.ShapeDtypeStruct((head_cols, width), f32),
            jax.ShapeDtypeStruct((width,), f32),
            jax.ShapeDtypeStruct((width,), f32),
            jax.ShapeDtypeStruct((experts, width), f32),
            jax.ShapeDtypeStruct(grad_in.shape, f32),
        ],
        in_specs=[pl.BlockSpec(memory_space=pltpu.SMEM), vmem, hbm]
        + [vmem] * 7
        + [hbm]
        + [vmem] * 5
        + [hbm],
        out_specs=[vmem, hbm] + [vmem] * 5 + [hbm],
        scratch_shapes=[
            small_block,
            pltpu.VMEM(grad_in.shape, f32),
            pltpu.VMEM((rows // 2, side), f32),
            pltpu.VMEM((rows, width), f32),
            pltpu.VMEM(grad_in.shape, bf16),
            pltpu.VMEM(grad_in.shape, bf16),
            pltpu.VMEM((pieces, 2, padded, width), bf16),
            dma((3 + 2 * images + GRAD_PARTS,)),
            pltpu.VMEM((rows, width), bf16),
            pltpu.VMEM((images, 8, round_up(rows // images, 128)), f32),
            pltpu.VMEM((heads, rows, HEAD_DIM), bf16),
            pltpu.VMEM((3, heads, rows, HEAD_DIM), bf16),
            pltpu.VMEM((2, rows, 128), jnp.int32),
            pltpu.VMEM((experts, half, side), bf16),
            pltpu.VMEM((experts, cap, side), bf16),
            pltpu.VMEM((rows // 2, cap), bf16),
            pltpu.VMEM((rows // 2, side), f32),
            pltpu.VMEM((images, part_rows, width), bf16),
            pltpu.VMEM((images, part_rows, width), bf16),
            pltpu.VMEM((images, part_rows, width), f32),
            pltpu.VMEM((images, part_rows, side), bf16),
            pltpu.VMEM((images, part_rows, side), bf16),
            pltpu.VMEM((rows, width), bf16),
            pltpu.VMEM((pieces, padded, width), bf16),
            pltpu.VMEM((pieces, padded, width), bf16),
            pltpu.VMEM((pieces, real, width), f32),
            pltpu.VMEM((pieces, padded, width), bf16),
            pltpu.VMEM((pieces, experts, chunk_rows, side), bf16),
            pltpu.VMEM((chunk_rows, side), f32),
            small_block,
            small_block,
            small_block,
            small_block,
            pltpu.VMEM((experts, small, width), f32),
            pltpu.VMEM((3, small, width), f32),
            dma((B_ROWS, table)),
            dma((B_ROWS, table)),
            dma((2, pieces)),
            dma((2, pieces)),
            dma((2 * pieces, experts)),
            dma((2 * pieces, experts)),
        ],
        compiler_params=pltpu.CompilerParams(
            collective_id=3, has_side_effects=True, vmem_limit_bytes=VMEM_BYTES
        ),
    )(
        counts,
        att_grad,
        mixed_grad,
        head_rows,
        stats,
        attended,
        x,
        gain,
        qkv_w,
        out_w,
        mixed,
        halves,
        routes,
        slots,
        router_part,
        gain2_part,
        grad_in,
    )


def body(
    inputs,
    counts,
    routes,
    slot_ids,
    norm_first,
    attn_in,
    attn_out,
    norm_second,
    router,
    expert_in,
    expert_out,
    cotangent,
):
    rows_dev = inputs.shape[0]
    experts = router.shape[1]
    half_slots = (105 * rows_dev + 100 * experts - 1) // (100 * experts)
    capacity = 2 * half_slots
    slot_pad = round_up(capacity, 32)
    routes, slots = routes.T, slot_ids.T
    router_rows, qkv = router.T, attn_in.transpose(0, 2, 1)
    sent_cots, head_rows, attended, stats, mixed, low_second, prob, gates, gate_rows = front(
        counts,
        inputs,
        cotangent,
        routes,
        slots,
        norm_first,
        qkv,
        attn_out,
        norm_second,
        router_rows,
        experts,
        capacity,
        slot_pad,
    )
    halves, mixed_grad, att_grad, router_part, gain_part, expert_out_grad, in_part = middle(
        counts,
        low_second,
        cotangent,
        routes,
        slots,
        gates,
        gate_rows,
        expert_in[0],
        expert_out[0],
        sent_cots,
        mixed,
        prob,
        norm_second,
        router_rows,
        experts,
        capacity,
    )
    output, input_grad, in_grad, attn_out_grad, gain1_grad, gain2_grad, router_grad, expert_in_grad = back(
        counts,
        att_grad,
        mixed_grad,
        head_rows,
        stats,
        attended,
        inputs,
        norm_first,
        qkv,
        attn_out,
        mixed,
        halves,
        routes,
        slots,
        router_part,
        gain_part,
        in_part,
        capacity,
    )
    return (
        output,
        input_grad,
        gain1_grad,
        in_grad.transpose(0, 2, 1),
        attn_out_grad,
        gain2_grad,
        router_grad.T,
        expert_in_grad[None],
        expert_out_grad[None],
    )


def solution(mesh):
    in_specs = (
        P("wide", None),
        P("wide"),
        P("wide", None),
        P("wide", None),
        P(),
        P(None, None, "narrow"),
        P("narrow", None),
        P(),
        P(),
        P("wide", None, "narrow"),
        P("wide", "narrow", None),
        P("wide", None),
    )
    out_specs = (
        P("wide", None),
        P("wide", None),
        P(),
        P(None, None, "narrow"),
        P("narrow", None),
        P(),
        P(),
        P("wide", None, "narrow"),
        P("wide", "narrow", None),
    )
    return jax.shard_map(body, mesh=mesh, in_specs=in_specs, out_specs=out_specs, check_vma=False)
```
